32 devices in a mesh: seq: 8 (over z, y), head: 4 (over x, core).
Axes of the slice: x: 2, y: 2, z: 4, core: 2. Of those that a mesh axis runs over, the one named last changes fastest.
Arguments:
- block_input: bfloat16 [16384, 1024], P('seq'), may hold values from -6 to 6
- first_gain: bfloat16 [1024], P('seq'), may hold values from 0.5 to 1.5
- query_weight: bfloat16 [1024, 1024], P('seq', 'head'), may hold values from -0.1875 to 0.1875
- key_weight: bfloat16 [1024, 1024], P('seq', 'head'), may hold values from -0.1875 to 0.1875
- value_weight: bfloat16 [1024, 1024], P('seq', 'head'), may hold values from -0.1875 to 0.1875
- beta_weight: bfloat16 [1024, 8], P('seq', 'head'), may hold values from -0.1875 to 0.1875
- conv_weight: bfloat16 [3, 4, 1024], P(None, None, 'head'), may hold values from -2.5 to 2.5
- head_gain: bfloat16 [128], replicated, may hold values from 0.5 to 1.5
- output_weight: bfloat16 [1024, 1024], P('seq', 'head'), may hold values from -0.1875 to 0.1875
- second_gain: bfloat16 [1024], P('seq'), may hold values from 0.5 to 1.5
- gate_weight: bfloat16 [1024, 2816], P('seq', 'head'), may hold values from -0.1875 to 0.1875
- up_weight: bfloat16 [1024, 2816], P('seq', 'head'), may hold values from -0.1875 to 0.1875
- down_weight: bfloat16 [1024, 2816], P('seq', 'head'), may hold values from -0.109375 to 0.109375
- lengths: int32 [4], replicated, may hold values from 64 to 8192, as said below
- cotangent: bfloat16 [16384, 1024], P('seq'), may hold values from -6 to 6
Outputs:
- block_output: bfloat16 [16384, 1024], P('seq', 'head')
- input_gradient: float32 [16384, 1024], P('seq', 'head')
- first_gradient: float32 [1024], P('seq')
- query_gradient: float32 [1024, 1024], P('seq', 'head')
- key_gradient: float32 [1024, 1024], P('seq', 'head')
- value_gradient: float32 [1024, 1024], P('seq', 'head')
- beta_gradient: float32 [1024, 8], P('seq', 'head')
- conv_gradient: float32 [3, 4, 1024], P(None, None, 'head')
- headnorm_gradient: float32 [128], replicated
- output_gradient: float32 [1024, 1024], P('seq', 'head')
- second_gradient: float32 [1024], P('seq')
- gate_gradient: float32 [1024, 2816], P('seq', 'head')
- up_gradient: float32 [1024, 2816], P('seq', 'head')
- down_gradient: float32 [1024, 2816], P('seq', 'head')
The draws below stay inside these ranges and needn't reach their ends.
Inputs may be any that keep to these rules, and one draw needn't show every extreme that they name: `lengths`: 4 sequences packed one after another; each length is a multiple of 64, they sum to 16384, and one of them is exactly 8192 tokens long.
All inputs are finite; a program needn't handle non-finite values.
Results may differ from the reference program's by a relative error of at most 0.015.
Values may be sent and summed in bfloat16 or wider, within the bound.
A program may use at most 320 MiB of HBM per device.

```python
import jax
import jax.numpy as jnp
from jax import lax

D = 1024
H = 8
DK = 128
FF = 2816
KCONV = 4
GROUP = 64
NSEQ = 4
HK = 1024
TOKENS = 16384


def draw_lengths(key, part):
    half_groups = TOKENS // GROUP // 2
    picks = jax.random.permutation(jax.random.fold_in(key, 1), half_groups - 1)[:NSEQ - 2] + 1
    cuts = jnp.sort(picks.astype(jnp.int32))
    bounds = jnp.concatenate([jnp.zeros((1,), jnp.int32), cuts, jnp.full((1,), half_groups, jnp.int32)])
    shorter = ((bounds[1:] - bounds[:-1]) * GROUP).astype(jnp.int32)
    longest_at = jax.random.randint(jax.random.fold_in(key, 2), (), 0, NSEQ).astype(jnp.int32)
    places = jnp.arange(NSEQ, dtype=jnp.int32)
    short_index = jnp.clip(places - (places > longest_at).astype(jnp.int32), 0, NSEQ - 2).astype(jnp.int32)
    picked = jnp.sum(jnp.where(short_index[:, None] == jnp.arange(NSEQ - 1, dtype=jnp.int32)[None, :], shorter[None, :], 0), axis=1).astype(jnp.int32)
    return jnp.where(places == longest_at, half_groups * GROUP, picked).astype(jnp.int32)


def block_scale(own_key, extent, cuts, low, largest):
    def one(dim, parts):
        heights = jax.random.uniform(jax.random.fold_in(jax.random.fold_in(own_key, 6), dim), (parts,), jnp.float32, low / len(cuts), largest / len(cuts))
        return jnp.repeat(jnp.exp(heights), extent[dim] // parts).reshape((-1,) + (1,) * (len(extent) - dim - 1))

    level = one(*cuts[0])
    for cut in cuts[1:]:
        level = level * one(*cut)
    return level


def bell_draw(own_key, dims, width, limit, split=(), kind=jnp.bfloat16):
    level = block_scale(own_key, dims, split, -0.22, 0.18) if split else 1.0
    drawn = jax.random.normal(own_key, dims, jnp.float32) * width * level
    return jnp.minimum(jnp.maximum(drawn, -limit), limit).astype(kind)


def setup_inputs(seed: int = 0) -> dict:
    key_of = jax.random.split(jax.random.key(seed), 16)
    block_input = bell_draw(key_of[0], (TOKENS, D), 1.0, 6.0, ((0, 8),))
    first_gain = jnp.clip(1.0 + 0.1 * jax.random.normal(key_of[1], (D,), jnp.float32), 0.5, 1.5).astype(jnp.bfloat16)
    query_weight = bell_draw(key_of[2], (D, HK), D ** -0.5, 0.1875, ((0, 8), (1, 4)))
    key_weight = bell_draw(key_of[3], (D, HK), D ** -0.5, 0.1875, ((0, 8), (1, 4)))
    value_weight = bell_draw(key_of[4], (D, HK), D ** -0.5, 0.1875, ((0, 8), (1, 4)))
    beta_weight = bell_draw(key_of[5], (D, H), D ** -0.5, 0.1875, ((0, 8), (1, 4)))
    conv_weight = bell_draw(key_of[6], (3, KCONV, HK), 0.5, 2.5, ((2, 4),))
    head_gain = jnp.clip(1.0 + 0.1 * jax.random.normal(key_of[7], (DK,), jnp.float32), 0.5, 1.5).astype(jnp.bfloat16)
    output_weight = bell_draw(key_of[8], (D, HK), HK ** -0.5, 0.1875, ((0, 8), (1, 4)))
    second_gain = jnp.clip(1.0 + 0.1 * jax.random.normal(key_of[9], (D,), jnp.float32), 0.5, 1.5).astype(jnp.bfloat16)
    gate_weight = bell_draw(key_of[10], (D, FF), D ** -0.5, 0.1875, ((0, 8), (1, 4)))
    up_weight = bell_draw(key_of[11], (D, FF), D ** -0.5, 0.1875, ((0, 8), (1, 4)))
    down_weight = bell_draw(key_of[12], (D, FF), FF ** -0.5, 0.109375, ((0, 8), (1, 4)))
    lengths = draw_lengths(jax.random.fold_in(key_of[15], 71), 0)
    cotangent = bell_draw(key_of[14], (TOKENS, D), 1.0, 6.0, ((0, 8),))
    return dict(block_input=block_input, first_gain=first_gain, query_weight=query_weight, key_weight=key_weight, value_weight=value_weight, beta_weight=beta_weight, conv_weight=conv_weight, head_gain=head_gain, output_weight=output_weight, second_gain=second_gain, gate_weight=gate_weight, up_weight=up_weight, down_weight=down_weight, lengths=lengths, cotangent=cotangent)


HIGHEST = lax.Precision.HIGHEST

@jax.custom_vjp
def low(v):
    return lax.optimization_barrier(v.astype(jnp.bfloat16)).astype(jnp.float32)

@jax.custom_vjp
def low_back(v):
    return v

def low_keep(v):
    return (low(v), None)

def low_pass(kept, grad):
    return (grad,)

def back_keep(v):
    return (v, None)

def back_low(kept, grad):
    return (low(grad),)
low.defvjp(low_keep, low_pass)
low_back.defvjp(back_keep, back_low)

def exact_dot(left, right):
    return jnp.dot(left, right, precision=HIGHEST, preferred_element_type=jnp.float32)

def precise_product(spec, left, right):
    return jnp.einsum(spec, left, right, precision=HIGHEST)

def rms_scale(values, gain, epsilon):
    return values * lax.rsqrt(lax.optimization_barrier(jnp.mean(values * values, axis=-1, keepdims=True)) + epsilon) * gain

def head_norm(rows, gain, heads):
    shaped = rows.reshape(rows.shape[0], heads, -1)
    return rms_scale(shaped, gain, 1e-05).reshape(rows.shape)

def unit_heads(rows, heads):
    shaped = rows.reshape(rows.shape[0], heads, -1)
    scaled = shaped * lax.rsqrt(lax.optimization_barrier(jnp.sum(shaped * shaped, axis=-1, keepdims=True)) + 1e-06)
    return scaled.reshape(rows.shape)

def activate(padded, table, distance, heads):
    kernel = table.shape[0]
    count = padded.shape[0] - kernel + 1
    mixed = jnp.zeros((count, padded.shape[1]), jnp.float32)
    for offset in range(kernel):
        usable = (kernel - 1 - offset <= distance).astype(jnp.float32)[:, None]
        mixed = mixed + table[offset][None, :] * padded[offset:offset + count] * usable
    silued = jax.nn.silu(mixed)
    third = silued.shape[1] // 3
    return (unit_heads(silued[:, :third], heads), unit_heads(silued[:, third:2 * third], heads), silued[:, 2 * third:])

def tri_inverse(strict):
    eye = jnp.eye(strict.shape[-1], dtype=jnp.float32)
    result = eye - strict
    power = strict
    for rounds in range((strict.shape[-1] - 1).bit_length() - 1):
        power = precise_product('...ij,...jk->...ik', power, power)
        result = precise_product('...ij,...jk->...ik', result, eye + power)
    return result

def group_factors(key_rows, values, beta):
    weighted_keys = key_rows * beta[..., None]
    gram = precise_product('...ik,...jk->...ij', weighted_keys, key_rows)
    inverse = tri_inverse(jnp.tril(gram, -1))
    weight_factor = precise_product('...ij,...jk->...ik', inverse, weighted_keys)
    update_factor = precise_product('...ij,...jk->...ik', inverse, values * beta[..., None])
    return (weight_factor, update_factor)

def group_apply(running_state, pieces):
    query_rows, key_rows, weight_factor, update_factor, reset = pieces
    running_state = running_state * (1.0 - reset)
    fresh_state = update_factor - precise_product('wzu,wuy->wzy', weight_factor, running_state)
    score_matrix = jnp.tril(precise_product('hik,hjk->hij', query_rows, key_rows))
    output_rows = precise_product('wzu,wuy->wzy', query_rows, running_state) + precise_product('dsw,dwo->dso', score_matrix, fresh_state)
    running_state = running_state + precise_product('flp,flt->fpt', key_rows, fresh_state)
    return (running_state, output_rows)

def reference(block_input, first_gain, query_weight, key_weight, value_weight, beta_weight, conv_weight, head_gain, output_weight, second_gain, gate_weight, up_weight, down_weight, lengths, cotangent):
    positions = jnp.arange(TOKENS, dtype=jnp.int32)
    ends = jnp.cumsum(lengths).astype(jnp.int32)
    starts = (ends - lengths).astype(jnp.int32)
    begun = starts[None, :] <= positions[:, None]
    distance = positions - lax.optimization_barrier(jnp.max(jnp.where(begun, starts[None, :], 0), axis=1)).astype(jnp.int32)
    resets = jnp.any(starts[None, :] == positions[::GROUP][:, None], axis=1).astype(jnp.float32)
    groups = TOKENS // GROUP

    def blocks(rows):
        return rows.reshape(groups, GROUP, H, DK).transpose(0, 2, 1, 3)

    def group_step(running_state, pieces):
        query_block, key_block, value_block, beta_block, reset = pieces
        weight_factor, update_factor = group_factors(key_block, value_block, beta_block)
        return group_apply(running_state, (query_block, key_block, weight_factor, update_factor, reset))

    def forward(inputs, gain_one, w_query, w_key, w_value, w_beta, conv_table, gain_head, w_output, gain_two, w_gate, w_up, w_down):
        first_rows = low(rms_scale(inputs, gain_one, 1e-06))
        pre_query = low_back(low(exact_dot(first_rows, w_query)))
        pre_key = low_back(low(exact_dot(first_rows, w_key)))
        pre_value = low_back(low(exact_dot(first_rows, w_value)))
        beta = jax.nn.sigmoid(low_back(exact_dot(first_rows, w_beta)))
        pre_conv = jnp.concatenate([pre_query, pre_key, pre_value], 1)
        padded = jnp.concatenate([jnp.zeros((KCONV - 1, 3 * HK), jnp.float32), pre_conv], 0)
        table = conv_table.transpose(1, 0, 2).reshape(KCONV, 3 * HK)
        query_rows, key_rows, values = activate(padded, table, distance, H)
        query_rows = low(query_rows)
        key_rows = low(key_rows)
        values = low(values)
        beta_blocks = beta.reshape(groups, GROUP, H).transpose(0, 2, 1)
        final, output_rows = lax.scan(jax.checkpoint(group_step), jnp.zeros((H, DK, DK), jnp.float32), (blocks(query_rows), blocks(key_rows), blocks(values), beta_blocks, resets))
        delta_out = output_rows.transpose(0, 2, 1, 3).reshape(TOKENS, HK)
        head_rows = low(head_norm(delta_out, gain_head, H))
        branch = low_back(exact_dot(head_rows, w_output.T))
        middle = inputs + branch
        second_rows = low(rms_scale(middle, gain_two, 1e-06))
        gate = low_back(exact_dot(second_rows, w_gate))
        up_rows = low_back(exact_dot(second_rows, w_up))
        hidden = low(jax.nn.silu(gate) * up_rows)
        return middle + low_back(exact_dot(hidden, w_down.T))
    result, pullback = jax.vjp(forward, block_input.astype(jnp.float32), first_gain.astype(jnp.float32), query_weight.astype(jnp.float32), key_weight.astype(jnp.float32), value_weight.astype(jnp.float32), beta_weight.astype(jnp.float32), conv_weight.astype(jnp.float32), head_gain.astype(jnp.float32), output_weight.astype(jnp.float32), second_gain.astype(jnp.float32), gate_weight.astype(jnp.float32), up_weight.astype(jnp.float32), down_weight.astype(jnp.float32))
    grads = pullback(cotangent.astype(jnp.float32))
    return (result.astype(jnp.bfloat16), grads[0], grads[1], grads[2], grads[3], grads[4], grads[5], grads[6], grads[7], grads[8], grads[9], grads[10], grads[11], grads[12])
```

```python
import functools

import jax
import jax.numpy as jnp
from jax import lax
from jax.experimental import pallas as pl
from jax.experimental.pallas import tpu as pltpu
from jax.sharding import PartitionSpec as P

GROUP = 64
CHUNK = 128
MESH = pl.DeviceIdType.MESH
BF = jnp.bfloat16
F32 = jnp.float32
VMEM_LIMIT = 56 << 20


def nn(left, right):
    return jnp.dot(left.astype(BF), right.astype(BF), preferred_element_type=F32)


def tn(left, right):
    return lax.dot_general(
        left.astype(BF), right.astype(BF), (((0,), (0,)), ((), ())), preferred_element_type=F32
    )


def nt(left, right):
    return lax.dot_general(
        left.astype(BF), right.astype(BF), (((1,), (1,)), ((), ())), preferred_element_type=F32
    )


def sigmoid(v):
    return 0.5 * jnp.tanh(0.5 * v) + 0.5


def side(left, right):
    return jnp.concatenate([left, right], 1)


def stack(top, bottom):
    return jnp.concatenate([top, bottom], 0)


def grid_indices():
    rows = lax.broadcasted_iota(jnp.int32, (CHUNK, CHUNK), 0)
    cols = lax.broadcasted_iota(jnp.int32, (CHUNK, CHUNK), 1)
    return rows, cols


def load_padded(pad_ref, pre_ref, halo_ref, chunk, resets_ref):
    start = pl.multiple_of(chunk * CHUNK, CHUNK)
    before = pl.multiple_of(jnp.maximum(start - 16, 0), 16)
    own = pre_ref[pl.ds(start, CHUNK), :].astype(F32)
    earlier = pre_ref[pl.ds(before, 16), :].astype(F32)[8:]
    halo = halo_ref[...].astype(F32)[8:]
    first = jnp.where(chunk == 0, halo, earlier)
    keep0 = 1.0 - resets_ref[2 * chunk]
    keep1 = 1.0 - resets_ref[2 * chunk + 1]
    pad_ref[0:8] = first * keep0
    pad_ref[8:72] = own[:GROUP]
    pad_ref[72:80] = own[GROUP - 8 : GROUP] * keep1
    pad_ref[80:144] = own[GROUP:]


def tap_rows(pad_ref, tap):
    return stack(pad_ref[5 + tap : 69 + tap], pad_ref[77 + tap : 141 + tap])


def convolve(pad_ref, taps_ref):
    mixed = None
    for tap in range(4):
        term = taps_ref[tap : tap + 1] * tap_rows(pad_ref, tap)
        mixed = term if mixed is None else mixed + term
    return mixed


def inverse_levels(strict, rows, cols, keep1):
    eye = jnp.where(rows == cols, 1.0, 0.0)
    pair = (rows // 2) == (cols // 2)
    results = [eye - jnp.where(pair, a, 0.0) for a in strict]
    width = 2
    while width < CHUNK:
        off = ((rows // (2 * width)) == (cols // (2 * width))) & ((rows // width) != (cols // width))
        lows = [r.astype(BF) for r in results]
        parts = [jnp.where(off, a, 0.0).astype(BF) for a in strict]
        if width == GROUP:
            parts = [jnp.where(off, a * k, 0.0).astype(BF) for a, k in zip(strict, keep1)]
        steps = [nn(r, p) for r, p in zip(lows, parts)]
        results = [r - nn(s, low) for r, s, low in zip(results, steps, lows)]
        width *= 2
    return results


def mixer_forward_kernel(
    heads,
    resets_ref,
    pre_ref,
    halo_ref,
    taps_ref,
    logits_ref,
    qkv_ref,
    inv_ref,
    wu_ref,
    mq_ref,
    start_ref,
    out0_ref,
    total_ref,
    pad_ref,
):
    columns = heads * CHUNK
    rows, cols = grid_indices()
    eye = jnp.where(rows == cols, 1.0, 0.0)
    top = lax.broadcasted_iota(jnp.int32, (CHUNK, 1), 0) < GROUP
    for head in range(heads):
        total_ref[head] = side(eye, jnp.zeros_like(eye))
    batch = pad_ref.shape[0]

    def one(step, carry):
        units = []
        for lane in range(batch):
            chunk = step * batch + lane
            pad = pad_ref.at[lane]
            load_padded(pad, pre_ref, halo_ref, chunk, resets_ref)
            mixed = convolve(pad, taps_ref)
            silued = mixed * sigmoid(mixed)
            keep0 = 1.0 - resets_ref[2 * chunk]
            keep1 = 1.0 - resets_ref[2 * chunk + 1]
            both = keep0 * keep1
            enter = jnp.where(top, keep0, both)
            leave = jnp.where(top, keep1, 1.0)
            at = pl.ds(pl.multiple_of(chunk * CHUNK, CHUNK), CHUNK)
            beta_rows = sigmoid(logits_ref[at, :])
            for head in range(heads):
                window = slice(head * CHUNK, (head + 1) * CHUNK)
                parts = []
                for kind in range(3):
                    part = silued[:, kind * columns + head * CHUNK : kind * columns + (head + 1) * CHUNK]
                    if kind < 2:
                        part = part * lax.rsqrt(jnp.sum(part * part, axis=-1, keepdims=True) + 1e-06)
                    part = part.astype(BF)
                    qkv_ref[at, kind * columns + head * CHUNK : kind * columns + (head + 1) * CHUNK] = part
                    parts.append(part)
                units.append((chunk, head, *parts, beta_rows[:, head : head + 1], keep1, both, enter, leave))
        turned = [u[3].T for u in units]
        strict = [
            jnp.where(rows > cols, u[5] * nn(u[3], t), 0.0) for u, t in zip(units, turned)
        ]
        inverses = [r.astype(BF) for r in inverse_levels(strict, rows, cols, [u[6] for u in units])]
        factors = []
        for u, inverse in zip(units, inverses):
            beta = u[5]
            factors.append(nn(inverse, side(u[3].astype(F32) * beta, u[4].astype(F32) * beta)))
        for u, inverse, factor, t in zip(units, inverses, factors, turned):
            chunk, head, query, key, value, beta, keep1, both, enter, leave = u
            weight, update = factor[:, :CHUNK], factor[:, CHUNK:]
            entering_weight = weight * enter
            inv_ref[chunk, head] = inverse
            wu_ref[chunk, head] = side(entering_weight, update).astype(BF)
            gathered = nn(t, side(weight, update * leave))
            device_map = (both * (eye - gathered[:, :CHUNK])).astype(BF)
            shift = gathered[:, CHUNK:]
            scores = jnp.where(rows >= cols, nn(query, t), 0.0)
            scores = jnp.where((rows >= GROUP) & (cols < GROUP), scores * keep1, scores)
            seen = nn(scores, side(entering_weight, update))
            effective = query.astype(F32) * enter - seen[:, :CHUNK]
            mq_ref[chunk, head] = stack(device_map, effective.astype(BF))
            out0_ref[chunk, head] = seen[:, CHUNK:]
            running = total_ref[head]
            start_ref[chunk, head] = running.astype(BF)
            total_ref[head] = nn(device_map, running) + side(jnp.zeros_like(shift), shift)
        return carry

    lax.fori_loop(0, resets_ref.shape[0] // 2 // batch, one, 0)


def mixer_forward(resets, pre, halo, taps, logits, heads):
    tokens = pre.shape[0]
    chunks = tokens // CHUNK
    columns = heads * CHUNK

    def units(width, kind):
        return jax.ShapeDtypeStruct((chunks, heads, *width), kind)

    return pl.pallas_call(
        functools.partial(mixer_forward_kernel, heads),
        name="mixer_forward",
        out_shape=(
            jax.ShapeDtypeStruct((tokens, 3 * columns), BF),
            units((CHUNK, CHUNK), BF),
            units((CHUNK, 2 * CHUNK), BF),
            units((2 * CHUNK, CHUNK), BF),
            units((CHUNK, 2 * CHUNK), BF),
            units((CHUNK, CHUNK), F32),
            jax.ShapeDtypeStruct((heads, CHUNK, 2 * CHUNK), F32),
        ),
        in_specs=[pl.BlockSpec(memory_space=pltpu.SMEM)] + [pl.BlockSpec(memory_space=pltpu.VMEM)] * 4,
        out_specs=tuple([pl.BlockSpec(memory_space=pltpu.VMEM)] * 7),
        scratch_shapes=[pltpu.VMEM((2, 144, 3 * columns), F32)],
        compiler_params=pltpu.CompilerParams(vmem_limit_bytes=VMEM_LIMIT),
        cost_estimate=pl.CostEstimate(flops=3 * 10**9, bytes_accessed=20 << 20, transcendentals=2 << 20),
    )(resets, pre, halo, taps, logits)


def exchange_kernel(axis, count, window, backward, part_ref, state_ref, slots_ref, send_sem, recv_sem):
    place = lax.axis_index(axis)
    ahead = count - 1 - place if backward else place
    behind = count - 1 - ahead
    sign = -1 if backward else 1
    barrier = pltpu.get_barrier_semaphore()
    for hop in range(1, window + 1):

        @pl.when(ahead >= hop)
        def _():
            pl.semaphore_signal(
                barrier, inc=1, device_id={axis: place - sign * hop}, device_id_type=MESH
            )

    @pl.when(behind > 0)
    def _():
        pl.semaphore_wait(barrier, jnp.minimum(behind, window))

    def copy(hop):
        return pltpu.make_async_remote_copy(
            src_ref=part_ref,
            dst_ref=slots_ref.at[hop - 1],
            send_sem=send_sem.at[hop - 1],
            recv_sem=recv_sem.at[hop - 1],
            device_id={axis: place + sign * hop},
            device_id_type=MESH,
        )

    for hop in range(1, window + 1):

        @pl.when(behind >= hop)
        def _():
            copy(hop).start()

    heads = state_ref.shape[0]
    state_ref[...] = jnp.zeros_like(state_ref)
    for hop in range(window, 0, -1):

        @pl.when(ahead >= hop)
        def _():
            copy(hop).wait_recv()
            for head in range(heads):
                part = slots_ref[hop - 1, head]
                state_ref[head] = nn(part[:, :CHUNK], state_ref[head]) + part[:, CHUNK:].astype(F32)

    for hop in range(1, window + 1):

        @pl.when(behind >= hop)
        def _():
            copy(hop).wait_send()


def exchange(part, axis, backward, collective):
    count = lax.axis_size(axis)
    window = min(count - 1, count // 2)
    heads = part.shape[0]
    return pl.pallas_call(
        functools.partial(exchange_kernel, axis, count, window, backward),
        name="state_backward" if backward else "state_forward",
        out_shape=jax.ShapeDtypeStruct((heads, CHUNK, CHUNK), F32),
        in_specs=[pl.BlockSpec(memory_space=pltpu.VMEM)],
        out_specs=pl.BlockSpec(memory_space=pltpu.VMEM),
        scratch_shapes=[
            pltpu.VMEM((window, heads, CHUNK, 2 * CHUNK), BF),
            pltpu.SemaphoreType.DMA((window,)),
            pltpu.SemaphoreType.DMA((window,)),
        ],
        compiler_params=pltpu.CompilerParams(
            collective_id=collective, has_side_effects=True, vmem_limit_bytes=VMEM_LIMIT
        ),
    )(part)


def mixer_output_kernel(heads, state_ref, start_ref, mq_ref, out0_ref, gain_ref, delta_ref, rows_ref, states_ref):
    batch = 4

    def one(step, carry):
        for lane in range(batch):
            chunk = step * batch + lane
            at = pl.ds(pl.multiple_of(chunk * CHUNK, CHUNK), CHUNK)
            for head in range(heads):
                window = slice(head * CHUNK, (head + 1) * CHUNK)
                begin = start_ref[chunk, head]
                state = nn(begin[:, :CHUNK], state_ref[head]) + begin[:, CHUNK:].astype(F32)
                state = state.astype(BF)
                states_ref[chunk, head] = state
                out = out0_ref[chunk, head] + nn(mq_ref[chunk, head, CHUNK:], state)
                delta_ref[at, window] = out
                scale = lax.rsqrt(jnp.mean(out * out, axis=-1, keepdims=True) + 1e-05)
                rows_ref[at, window] = (out * scale * gain_ref[...]).astype(BF)
        return carry

    lax.fori_loop(0, start_ref.shape[0] // batch, one, 0)


def mixer_output(state, start, mq, out0, gain):
    chunks, heads = start.shape[:2]
    tokens = chunks * CHUNK
    return pl.pallas_call(
        functools.partial(mixer_output_kernel, heads),
        name="mixer_output",
        out_shape=(
            jax.ShapeDtypeStruct((tokens, heads * CHUNK), F32),
            jax.ShapeDtypeStruct((tokens, heads * CHUNK), BF),
            jax.ShapeDtypeStruct((chunks, heads, CHUNK, CHUNK), BF),
        ),
        compiler_params=pltpu.CompilerParams(vmem_limit_bytes=VMEM_LIMIT),
        cost_estimate=pl.CostEstimate(flops=3 * 10**8, bytes_accessed=10 << 20, transcendentals=1 << 14),
    )(state, start, mq, out0, gain)


def mixer_back_state_kernel(heads, dheads_ref, delta_ref, gain_ref, mq_ref, ddelta_ref, gain_grad_ref, shift_ref):
    chunks = mq_ref.shape[0]
    shift_ref[...] = jnp.zeros_like(shift_ref)
    gain_grad_ref[...] = jnp.zeros_like(gain_grad_ref)

    def one(step, carry):
        chunk = chunks - 1 - step
        at = pl.ds(pl.multiple_of(chunk * CHUNK, CHUNK), CHUNK)
        for head in range(heads):
            window = slice(head * CHUNK, (head + 1) * CHUNK)
            out = delta_ref[at, window]
            grad = dheads_ref[at, window].astype(F32)
            scale = lax.rsqrt(jnp.mean(out * out, axis=-1, keepdims=True) + 1e-05)
            unit = out * scale
            gain_grad_ref[...] += jnp.sum((grad * unit).reshape(CHUNK // 8, 8, CHUNK), 0)
            scaled = grad * gain_ref[...]
            back = scale * (scaled - unit * jnp.mean(scaled * unit, axis=-1, keepdims=True))
            back = back.astype(BF)
            ddelta_ref[at, window] = back
            shift_ref[head] = tn(mq_ref[chunk, head], stack(shift_ref[head].astype(BF), back))
        return carry

    lax.fori_loop(0, chunks, one, 0)


def mixer_back_state(dheads, delta, gain, mq):
    chunks, heads = mq.shape[:2]
    tokens = chunks * CHUNK
    return pl.pallas_call(
        functools.partial(mixer_back_state_kernel, heads),
        name="mixer_back_state",
        out_shape=(
            jax.ShapeDtypeStruct((tokens, heads * CHUNK), BF),
            jax.ShapeDtypeStruct((8, CHUNK), F32),
            jax.ShapeDtypeStruct((heads, CHUNK, CHUNK), F32),
        ),
        compiler_params=pltpu.CompilerParams(vmem_limit_bytes=VMEM_LIMIT),
        cost_estimate=pl.CostEstimate(flops=3 * 10**8, bytes_accessed=10 << 20, transcendentals=1 << 14),
    )(dheads, delta, gain, mq)


def mixer_backward_kernel(
    heads,
    resets_ref,
    pre_ref,
    halo_ref,
    taps_ref,
    logits_ref,
    qkv_ref,
    inv_ref,
    wu_ref,
    mq_ref,
    states_ref,
    ddelta_ref,
    arrive_ref,
    dpre_ref,
    tail_ref,
    lead_ref,
    taps_grad_ref,
    dlogits_ref,
    carry_ref,
    pad_ref,
    dpad_ref,
):
    columns = heads * CHUNK
    chunks = mq_ref.shape[0]
    rows, cols = grid_indices()
    top = lax.broadcasted_iota(jnp.int32, (CHUNK, 1), 0) < GROUP
    carry_ref[...] = arrive_ref[...]
    taps_grad_ref[...] = jnp.zeros_like(taps_grad_ref)
    dpad_ref[136:144] = jnp.zeros_like(dpad_ref[136:144])

    def one(step, carry):
        chunk = chunks - 1 - step
        at = pl.ds(pl.multiple_of(chunk * CHUNK, CHUNK), CHUNK)
        keep0 = 1.0 - resets_ref[2 * chunk]
        keep1 = 1.0 - resets_ref[2 * chunk + 1]
        both = keep0 * keep1
        enter = jnp.where(top, keep0, both)
        leave = jnp.where(top, keep1, 1.0)
        load_padded(pad_ref, pre_ref, halo_ref, chunk, resets_ref)
        mixed = convolve(pad_ref, taps_ref)
        gate = sigmoid(mixed)
        slope = gate * (1.0 + mixed * (1.0 - gate))
        silued = mixed * gate
        beta_rows = sigmoid(logits_ref[at, :])
        grads = [[None] * heads for _ in range(3)]
        dlogits = []
        for head in range(heads):
            def part(kind):
                return slice(kind * columns + head * CHUNK, kind * columns + (head + 1) * CHUNK)

            query, key, value = (qkv_ref[at, part(kind)] for kind in range(3))
            beta = beta_rows[:, head : head + 1]
            inverse = inv_ref[chunk, head]
            factors = wu_ref[chunk, head]
            weight, update = factors[:, :CHUNK], factors[:, CHUNK:]
            state = states_ref[chunk, head]
            out_grad = ddelta_ref[at, head * CHUNK : (head + 1) * CHUNK]
            later = carry_ref[head].astype(BF)
            carry_ref[head] = tn(mq_ref[chunk, head], stack(later, out_grad))
            cross = (rows >= GROUP) & (cols < GROUP)
            scores = jnp.where(rows >= cols, nt(query, key), 0.0)
            scores = jnp.where(cross, scores * keep1, scores).astype(BF)
            fresh = (update.astype(F32) - nn(weight, state)).astype(BF)
            fresh_grad = tn(scores, out_grad) + leave * nn(key, later)
            fresh_low = fresh_grad.astype(BF)
            score_grad = jnp.where(rows >= cols, nt(out_grad, fresh), 0.0)
            score_grad = jnp.where(cross, score_grad * keep1, score_grad).astype(BF)
            through = nt(stack(out_grad, fresh_low), state)
            query_grad = enter * through[:CHUNK] + nn(score_grad, key)
            weight_grad = -enter * through[CHUNK:]
            key_grad = tn(score_grad, query) + leave * nt(fresh, later)
            back = tn(inverse, side(weight_grad.astype(BF), fresh_low))
            back_low = back.astype(BF)
            strict = -jnp.where(rows > cols, nt(back_low, side(weight, update)), 0.0)
            strict = jnp.where(cross, strict * keep1, strict).astype(BF)
            yk, zv = back[:, :CHUNK], back[:, CHUNK:]
            key32 = key.astype(F32)
            strict_key = nn(strict, key)
            key_grad = key_grad + beta * (yk + strict_key) + tn(strict, (beta * key32).astype(BF))
            value_grad = beta * zv
            beta_grad = jnp.sum((yk + strict_key) * key32 + zv * value.astype(F32), axis=-1, keepdims=True)
            dlogits.append(beta_grad * beta * (1.0 - beta))
            for kind, grad in ((0, query_grad), (1, key_grad)):
                raw = silued[:, part(kind)]
                inv = lax.rsqrt(jnp.sum(raw * raw, axis=-1, keepdims=True) + 1e-06)
                unit = raw * inv
                grads[kind][head] = (grad - unit * jnp.sum(unit * grad, axis=-1, keepdims=True)) * inv
            grads[2][head] = value_grad
        dlogits_ref[at, :] = jnp.concatenate(dlogits, 1)
        dmixed = jnp.concatenate([g for kind in grads for g in kind], 1) * slope
        dpad_ref[0:GROUP] = dmixed[:GROUP]
        dpad_ref[GROUP : GROUP + 8] = dmixed[GROUP : GROUP + 8] * keep1
        dpad_ref[72 : 72 + GROUP] = dmixed[GROUP:]
        dpre = None
        for tap in range(4):
            back = 3 - tap
            shifted = stack(dpad_ref[back : back + GROUP], dpad_ref[72 + back : 72 + back + GROUP])
            term = taps_ref[tap : tap + 1] * shifted
            dpre = term if dpre is None else dpre + term
            seen = (dmixed * tap_rows(pad_ref, tap)).reshape(CHUNK // 8, 8, 3 * columns)
            taps_grad_ref[tap] += jnp.sum(seen, 0)
        dpre_ref[at, :] = dpre.astype(BF)

        @pl.when(step == 0)
        def _():
            tail_ref[...] = dpre[CHUNK - 8 :]

        dpad_ref[136:144] = dmixed[:8] * keep0
        return carry

    lax.fori_loop(0, chunks, one, 0)
    index = lax.broadcasted_iota(jnp.int32, (8, 1), 0)
    lead = jnp.zeros((8, 3 * columns), F32)
    dpad_ref[0:128] = jnp.zeros_like(dpad_ref[0:128])
    dpad_ref[8:16] = dpad_ref[136:144]
    for tap in range(3):
        back = 3 - tap
        lead = lead + taps_ref[tap : tap + 1] * dpad_ref[back : back + 8]
    lead_ref[...] = lead


def mixer_backward(resets, pre, halo, taps, logits, qkv, inv, wu, mq, states, ddelta, arrive):
    chunks, heads = mq.shape[:2]
    tokens = chunks * CHUNK
    columns = heads * CHUNK
    return pl.pallas_call(
        functools.partial(mixer_backward_kernel, heads),
        name="mixer_backward",
        out_shape=(
            jax.ShapeDtypeStruct((tokens, 3 * columns), BF),
            jax.ShapeDtypeStruct((8, 3 * columns), F32),
            jax.ShapeDtypeStruct((8, 3 * columns), F32),
            jax.ShapeDtypeStruct((4, 8, 3 * columns), F32),
            jax.ShapeDtypeStruct((tokens, heads), F32),
        ),
        in_specs=[pl.BlockSpec(memory_space=pltpu.SMEM)] + [pl.BlockSpec(memory_space=pltpu.VMEM)] * 11,
        out_specs=tuple([pl.BlockSpec(memory_space=pltpu.VMEM)] * 5),
        scratch_shapes=[
            pltpu.VMEM((heads, CHUNK, CHUNK), F32),
            pltpu.VMEM((144, 3 * columns), F32),
            pltpu.VMEM((144, 3 * columns), F32),
        ],
        compiler_params=pltpu.CompilerParams(vmem_limit_bytes=VMEM_LIMIT),
        cost_estimate=pl.CostEstimate(flops=3 * 10**9, bytes_accessed=20 << 20, transcendentals=2 << 20),
    )(resets, pre, halo, taps, logits, qkv, inv, wu, mq, states, ddelta, arrive)


def from_behind(block, axis, distance):
    devices = range(lax.axis_size(axis))
    route = [(i - distance, i) for i in devices if i - distance in devices]
    return lax.ppermute(block, axis, route)


def dot(left, right):
    return jnp.dot(left, right, preferred_element_type=F32)


def dot_rows(left, right):
    return lax.dot_general(left, right, (((0,), (0,)), ((), ())), preferred_element_type=F32)


def dot_cols(left, right):
    return lax.dot_general(left, right, (((1,), (1,)), ((), ())), preferred_element_type=F32)


def gather_seq(block):
    return lax.all_gather(block, "seq", axis=0, tiled=True)


def body(
    block_input,
    first_gain,
    query_weight,
    key_weight,
    value_weight,
    beta_weight,
    conv_weight,
    head_gain,
    output_weight,
    second_gain,
    gate_weight,
    up_weight,
    down_weight,
    lengths,
    cotangent,
):
    tokens, width = block_input.shape
    heads = beta_weight.shape[1]
    columns = query_weight.shape[1]
    hidden_columns = gate_weight.shape[1]
    members = lax.axis_size("seq")
    piece = width // members
    column_start = lax.axis_index("head") * columns
    seq_place = lax.axis_index("seq")

    mixer_pack = gather_seq(
        jnp.concatenate(
            [query_weight, key_weight, value_weight, beta_weight, first_gain[:, None], second_gain[:, None]], 1
        )
    )
    projection = mixer_pack[:, : 3 * columns]
    full_beta = mixer_pack[:, 3 * columns : 3 * columns + heads]
    gain_one = mixer_pack[:, 3 * columns + heads].astype(F32)
    gain_two = mixer_pack[:, 3 * columns + heads + 1].astype(F32)
    full_output = gather_seq(output_weight)
    forward_pack = lax.all_gather(jnp.stack([gate_weight, up_weight, down_weight]), "seq", axis=0)
    full_gate, full_up, full_down = (forward_pack[:, i].reshape(width, hidden_columns) for i in range(3))

    ends = jnp.sum(jnp.where(jnp.arange(4)[:, None] >= jnp.arange(4)[None, :], lengths[None, :], 0), axis=1)
    starts = ends - lengths
    block_starts = seq_place * tokens + GROUP * jnp.arange(tokens // GROUP, dtype=jnp.int32)
    resets = jnp.any(starts[None, :] == block_starts[:, None], axis=1).astype(F32)

    inputs = block_input.astype(F32)
    halo_rows = from_behind(block_input[tokens - 16 :], "seq", 1)
    scale_one = lax.rsqrt(jnp.mean(inputs * inputs, axis=-1, keepdims=True) + 1e-06)
    first_rows = (inputs * scale_one * gain_one).astype(BF)
    halo_in = halo_rows.astype(F32)
    halo_first = (
        halo_in * lax.rsqrt(jnp.mean(halo_in * halo_in, axis=-1, keepdims=True) + 1e-06) * gain_one
    ).astype(BF)
    pre = dot(first_rows, projection).astype(BF)
    halo = dot(halo_first, projection).astype(BF)
    logits = dot(first_rows, full_beta)
    taps = conv_weight.astype(F32).transpose(1, 0, 2).reshape(4, -1)
    qkv, inv, wu, mq, start, out0, total = mixer_forward(resets, pre, halo, taps, logits, heads)
    total_low = total.astype(BF)
    state = exchange(total_low, "seq", False, 0)
    gain_head = head_gain.astype(F32)[None, :]
    delta, head_rows, states = mixer_output(state, start, mq, out0, gain_head)

    branch = lax.psum(dot_cols(head_rows, full_output).astype(BF), "head").astype(F32)
    middle = inputs + branch
    scale_two = lax.rsqrt(jnp.mean(middle * middle, axis=-1, keepdims=True) + 1e-06)
    unit_two = middle * scale_two
    second_rows = (unit_two * gain_two).astype(BF)
    gate = dot(second_rows, full_gate)
    up = dot(second_rows, full_up)
    sig = jax.nn.sigmoid(gate)
    hidden = (gate * sig * up).astype(BF)
    update = lax.psum_scatter(
        dot_cols(hidden, full_down).astype(BF), "head", scatter_dimension=1, tiled=True
    )
    middle_shard = lax.dynamic_slice_in_dim(middle, column_start, columns, 1)
    block_output = (middle_shard + update.astype(F32)).astype(BF)
    down_grad = dot_rows(cotangent, hidden)
    d_hidden = dot(cotangent, full_down)
    d_gate = (d_hidden * up * sig * (1.0 + gate * (1.0 - sig))).astype(BF)
    d_up = (d_hidden * gate * sig).astype(BF)
    gate_grad = dot_rows(second_rows, d_gate)
    up_grad = dot_rows(second_rows, d_up)
    forward_grads = jnp.stack(
        [g.astype(BF).reshape(members, piece, hidden_columns) for g in (gate_grad, up_grad, down_grad)], 1
    )
    forward_sum = lax.psum_scatter(forward_grads, "seq", scatter_dimension=0, tiled=False).astype(F32)
    d_second = lax.psum((dot_cols(d_gate, full_gate) + dot_cols(d_up, full_up)).astype(BF), "head").astype(F32)
    second_part = jnp.sum(d_second * unit_two, 0)
    scaled_two = gain_two * d_second
    d_middle = cotangent.astype(F32) + scale_two * (
        scaled_two - unit_two * jnp.mean(scaled_two * unit_two, axis=-1, keepdims=True)
    )
    d_branch = d_middle.astype(BF)
    output_grad = dot_rows(d_branch, head_rows)
    d_heads = dot(d_branch, full_output).astype(BF)
    ddelta, gain_part, shift = mixer_back_state(d_heads, delta, gain_head, mq)
    back_part = jnp.concatenate([total_low[:, :, :CHUNK].transpose(0, 2, 1), shift.astype(BF)], 2)
    arrive = exchange(back_part, "seq", True, 1)
    d_pre_own, tail, lead, taps_part, d_logits32 = mixer_backward(
        resets, pre, halo, taps, logits, qkv, inv, wu, mq, states, ddelta, arrive
    )
    received = from_behind(lead, "seq", -1)
    d_pre = lax.dynamic_update_slice_in_dim(d_pre_own, (tail + received).astype(BF), tokens - 8, 0)
    d_logits = d_logits32.astype(BF)
    mixer_grads = jnp.concatenate([dot_rows(first_rows, d_pre), dot_rows(d_branch, head_rows)], 1).astype(BF)
    mixer_sum = lax.psum_scatter(mixer_grads, "seq", scatter_dimension=0, tiled=True).astype(F32)
    beta_part = dot_rows(first_rows, d_logits)
    d_first_part = dot_cols(d_pre, projection) + dot_cols(d_logits, full_beta)
    d_first = lax.psum(d_first_part.astype(BF), "head").astype(F32)
    unit_one = inputs * scale_one
    first_part = jnp.sum(d_first * unit_one, 0)
    scaled_one = gain_one * d_first
    d_input = d_middle + scale_one * (
        scaled_one - unit_one * jnp.mean(scaled_one * unit_one, axis=-1, keepdims=True)
    )
    input_gradient = lax.dynamic_slice_in_dim(d_input, column_start, columns, 1)

    seq_small = jnp.concatenate(
        [
            jnp.sum(taps_part, 1).reshape(-1),
            beta_part.reshape(-1),
            first_part,
            second_part,
        ]
    )
    gain_sum = lax.psum(jnp.sum(gain_part, 0), ("seq", "head"))
    small = lax.psum(seq_small, "seq")
    edge = 12 * columns
    conv_gradient = small[:edge].reshape(4, 3, columns).transpose(1, 0, 2)
    row_start = seq_place * piece
    beta_all = small[edge : edge + width * heads].reshape(width, heads)
    beta_gradient = lax.dynamic_slice_in_dim(beta_all, row_start, piece, 0)
    edge += width * heads
    first_gradient = lax.dynamic_slice_in_dim(small, edge + row_start, piece, 0)
    second_gradient = lax.dynamic_slice_in_dim(small, edge + width + row_start, piece, 0)
    return (
        block_output,
        input_gradient,
        first_gradient,
        mixer_sum[:, :columns],
        mixer_sum[:, columns : 2 * columns],
        mixer_sum[:, 2 * columns : 3 * columns],
        beta_gradient,
        conv_gradient,
        gain_sum,
        mixer_sum[:, 3 * columns :],
        second_gradient,
        forward_sum[0],
        forward_sum[1],
        forward_sum[2],
    )


def solution(mesh):
    return jax.shard_map(
        body,
        mesh=mesh,
        in_specs=(
            P("seq", None),
            P("seq"),
            P("seq", "head"),
            P("seq", "head"),
            P("seq", "head"),
            P("seq", "head"),
            P(None, None, "head"),
            P(),
            P("seq", "head"),
            P("seq"),
            P("seq", "head"),
            P("seq", "head"),
            P("seq", "head"),
            P(),
            P("seq", None),
        ),
        out_specs=(
            P("seq", "head"),
            P("seq", "head"),
            P("seq"),
            P("seq", "head"),
            P("seq", "head"),
            P("seq", "head"),
            P("seq", "head"),
            P(None, None, "head"),
            P(),
            P("seq", "head"),
            P("seq"),
            P("seq", "head"),
            P("seq", "head"),
            P("seq", "head"),
        ),
        check_vma=False,
    )
```

```python
import functools

import jax
import jax.numpy as jnp
from jax import lax
from jax.experimental import pallas as pl
from jax.experimental.pallas import tpu as pltpu
from jax.sharding import PartitionSpec as P

GROUP = 64
CHUNK = 128
MESH = pl.DeviceIdType.MESH
BF = jnp.bfloat16
F32 = jnp.float32
VMEM_LIMIT = 56 << 20


def nn(left, right):
    return jnp.dot(left.astype(BF), right.astype(BF), preferred_element_type=F32)


def tn(left, right):
    return lax.dot_general(
        left.astype(BF), right.astype(BF), (((0,), (0,)), ((), ())), preferred_element_type=F32
    )


def nt(left, right):
    return lax.dot_general(
        left.astype(BF), right.astype(BF), (((1,), (1,)), ((), ())), preferred_element_type=F32
    )


def sigmoid(v):
    return 0.5 * jnp.tanh(0.5 * v) + 0.5


def side(left, right):
    return jnp.concatenate([left, right], 1)


def stack(top, bottom):
    return jnp.concatenate([top, bottom], 0)


def grid_indices():
    rows = lax.broadcasted_iota(jnp.int32, (CHUNK, CHUNK), 0)
    cols = lax.broadcasted_iota(jnp.int32, (CHUNK, CHUNK), 1)
    return rows, cols


def load_padded(pad_ref, pre_ref, halo_ref, chunk, resets_ref):
    start = pl.multiple_of(chunk * CHUNK, CHUNK)
    before = pl.multiple_of(jnp.maximum(start - 16, 0), 16)
    own = pre_ref[pl.ds(start, CHUNK), :].astype(F32)
    earlier = pre_ref[pl.ds(before, 16), :].astype(F32)[8:]
    halo = halo_ref[...].astype(F32)[8:]
    first = jnp.where(chunk == 0, halo, earlier)
    keep0 = 1.0 - resets_ref[2 * chunk]
    keep1 = 1.0 - resets_ref[2 * chunk + 1]
    pad_ref[0:8] = first * keep0
    pad_ref[8:72] = own[:GROUP]
    pad_ref[72:80] = own[GROUP - 8 : GROUP] * keep1
    pad_ref[80:144] = own[GROUP:]


def tap_rows(pad_ref, tap):
    return stack(pad_ref[5 + tap : 69 + tap], pad_ref[77 + tap : 141 + tap])


def convolve(pad_ref, taps_ref):
    mixed = None
    for tap in range(4):
        term = taps_ref[tap : tap + 1] * tap_rows(pad_ref, tap)
        mixed = term if mixed is None else mixed + term
    return mixed


def inverse_levels(strict, rows, cols, keep1):
    eye = jnp.where(rows == cols, 1.0, 0.0)
    pair = (rows // 2) == (cols // 2)
    results = [eye - jnp.where(pair, a, 0.0) for a in strict]
    width = 2
    while width < CHUNK:
        off = ((rows // (2 * width)) == (cols // (2 * width))) & ((rows // width) != (cols // width))
        lows = [r.astype(BF) for r in results]
        parts = [jnp.where(off, a, 0.0).astype(BF) for a in strict]
        if width == GROUP:
            parts = [jnp.where(off, a * k, 0.0).astype(BF) for a, k in zip(strict, keep1)]
        steps = [nn(r, p) for r, p in zip(lows, parts)]
        results = [r - nn(s, low) for r, s, low in zip(results, steps, lows)]
        width *= 2
    return results


def mixer_forward_kernel(
    heads,
    resets_ref,
    pre_ref,
    halo_ref,
    taps_ref,
    logits_ref,
    qkv_ref,
    inv_ref,
    wu_ref,
    mq_ref,
    start_ref,
    out0_ref,
    total_ref,
    pad_ref,
):
    columns = heads * CHUNK
    rows, cols = grid_indices()
    eye = jnp.where(rows == cols, 1.0, 0.0)
    top = lax.broadcasted_iota(jnp.int32, (CHUNK, 1), 0) < GROUP
    for head in range(heads):
        total_ref[head] = side(eye, jnp.zeros_like(eye))
    batch = pad_ref.shape[0]

    def one(step, carry):
        units = []
        for lane in range(batch):
            chunk = step * batch + lane
            pad = pad_ref.at[lane]
            load_padded(pad, pre_ref, halo_ref, chunk, resets_ref)
            mixed = convolve(pad, taps_ref)
            silued = mixed * sigmoid(mixed)
            keep0 = 1.0 - resets_ref[2 * chunk]
            keep1 = 1.0 - resets_ref[2 * chunk + 1]
            both = keep0 * keep1
            enter = jnp.where(top, keep0, both)
            leave = jnp.where(top, keep1, 1.0)
            at = pl.ds(pl.multiple_of(chunk * CHUNK, CHUNK), CHUNK)
            beta_rows = sigmoid(logits_ref[at, :])
            for head in range(heads):
                window = slice(head * CHUNK, (head + 1) * CHUNK)
                parts = []
                for kind in range(3):
                    part = silued[:, kind * columns + head * CHUNK : kind * columns + (head + 1) * CHUNK]
                    if kind < 2:
                        part = part * lax.rsqrt(jnp.sum(part * part, axis=-1, keepdims=True) + 1e-06)
                    part = part.astype(BF)
                    qkv_ref[at, kind * columns + head * CHUNK : kind * columns + (head + 1) * CHUNK] = part
                    parts.append(part)
                units.append((chunk, head, *parts, beta_rows[:, head : head + 1], keep1, both, enter, leave))
        turned = [u[3].T for u in units]
        strict = [
            jnp.where(rows > cols, u[5] * nn(u[3], t), 0.0) for u, t in zip(units, turned)
        ]
        inverses = [r.astype(BF) for r in inverse_levels(strict, rows, cols, [u[6] for u in units])]
        factors = []
        for u, inverse in zip(units, inverses):
            beta = u[5]
            factors.append(nn(inverse, side(u[3].astype(F32) * beta, u[4].astype(F32) * beta)))
        for u, inverse, factor, t in zip(units, inverses, factors, turned):
            chunk, head, query, key, value, beta, keep1, both, enter, leave = u
            weight, update = factor[:, :CHUNK], factor[:, CHUNK:]
            entering_weight = weight * enter
            inv_ref[chunk, head] = inverse
            wu_ref[chunk, head] = side(entering_weight, update).astype(BF)
            gathered = nn(t, side(weight, update * leave))
            device_map = (both * (eye - gathered[:, :CHUNK])).astype(BF)
            shift = gathered[:, CHUNK:]
            scores = jnp.where(rows >= cols, nn(query, t), 0.0)
            scores = jnp.where((rows >= GROUP) & (cols < GROUP), scores * keep1, scores)
            seen = nn(scores, side(entering_weight, update))
            effective = query.astype(F32) * enter - seen[:, :CHUNK]
            mq_ref[chunk, head] = stack(device_map, effective.astype(BF))
            out0_ref[chunk, head] = seen[:, CHUNK:]
            running = total_ref[head]
            start_ref[chunk, head] = running.astype(BF)
            total_ref[head] = nn(device_map, running) + side(jnp.zeros_like(shift), shift)
        return carry

    lax.fori_loop(0, resets_ref.shape[0] // 2 // batch, one, 0)


def mixer_forward(resets, pre, halo, taps, logits, heads):
    tokens = pre.shape[0]
    chunks = tokens // CHUNK
    columns = heads * CHUNK

    def units(width, kind):
        return jax.ShapeDtypeStruct((chunks, heads, *width), kind)

    return pl.pallas_call(
        functools.partial(mixer_forward_kernel, heads),
        name="mixer_forward",
        out_shape=(
            jax.ShapeDtypeStruct((tokens, 3 * columns), BF),
            units((CHUNK, CHUNK), BF),
            units((CHUNK, 2 * CHUNK), BF),
            units((2 * CHUNK, CHUNK), BF),
            units((CHUNK, 2 * CHUNK), BF),
            units((CHUNK, CHUNK), F32),
            jax.ShapeDtypeStruct((heads, CHUNK, 2 * CHUNK), F32),
        ),
        in_specs=[pl.BlockSpec(memory_space=pltpu.SMEM)] + [pl.BlockSpec(memory_space=pltpu.VMEM)] * 4,
        out_specs=tuple([pl.BlockSpec(memory_space=pltpu.VMEM)] * 7),
        scratch_shapes=[pltpu.VMEM((2, 144, 3 * columns), F32)],
        compiler_params=pltpu.CompilerParams(vmem_limit_bytes=VMEM_LIMIT),
        cost_estimate=pl.CostEstimate(flops=3 * 10**9, bytes_accessed=20 << 20, transcendentals=2 << 20),
    )(resets, pre, halo, taps, logits)


def exchange_kernel(axis, count, window, backward, gathers, *refs):
    if gathers:
        part_ref, own_ref, state_ref, others_ref, slots_ref, send_sem, recv_sem, head_send, head_recv = refs
        _, _, near, far = head_peers()
    else:
        part_ref, state_ref, slots_ref, send_sem, recv_sem = refs
    place = lax.axis_index(axis)
    ahead = count - 1 - place if backward else place
    behind = count - 1 - ahead
    sign = -1 if backward else 1
    barrier = pltpu.get_barrier_semaphore()
    for hop in range(1, window + 1):

        @pl.when(ahead >= hop)
        def _():
            pl.semaphore_signal(
                barrier, inc=1, device_id={axis: place - sign * hop}, device_id_type=MESH
            )

    extra = 0
    if gathers:
        extra = 2
        for target in (near, far):
            pl.semaphore_signal(barrier, inc=1, device_id={"head": target}, device_id_type=MESH)

        def near_copy():
            return push(own_ref, others_ref.at[0], head_send.at[0], head_recv.at[0], "head", near)

        def far_copy():
            return push(own_ref, others_ref.at[1], head_send.at[1], head_recv.at[1], "head", far)

        def pass_copy():
            return push(others_ref.at[1], others_ref.at[2], head_send.at[2], head_recv.at[2], "head", near)

    if gathers:
        pl.semaphore_wait(barrier, jnp.minimum(behind, window) + extra)
    else:

        @pl.when(behind > 0)
        def _():
            pl.semaphore_wait(barrier, jnp.minimum(behind, window))

    def copy(hop):
        return push(
            part_ref,
            slots_ref.at[hop - 1],
            send_sem.at[hop - 1],
            recv_sem.at[hop - 1],
            axis,
            place + sign * hop,
        )

    for hop in range(1, window + 1):

        @pl.when(behind >= hop)
        def _():
            copy(hop).start()

    if gathers:
        far_copy().start()
        near_copy().start()
    heads = state_ref.shape[0]
    state_ref[...] = jnp.zeros_like(state_ref)
    for hop in range(window, 0, -1):

        @pl.when(ahead >= hop)
        def _():
            copy(hop).wait_recv()
            for head in range(heads):
                part = slots_ref[hop - 1, head]
                state_ref[head] = nn(part[:, :CHUNK], state_ref[head]) + part[:, CHUNK:].astype(F32)

    if gathers:
        far_copy().wait_recv()
        pass_copy().start()
        near_copy().wait()
        far_copy().wait_send()
        pass_copy().wait()
    for hop in range(1, window + 1):

        @pl.when(behind >= hop)
        def _():
            copy(hop).wait_send()


def exchange(part, own, axis, backward, collective):
    count = lax.axis_size(axis)
    window = min(count - 1, count // 2)
    heads = part.shape[0]
    whole = pl.BlockSpec(memory_space=pltpu.VMEM)
    gathers = own is not None
    out_shape = [jax.ShapeDtypeStruct((heads, CHUNK, CHUNK), F32)]
    scratch = [
        pltpu.VMEM((window, heads, CHUNK, 2 * CHUNK), BF),
        pltpu.SemaphoreType.DMA((window,)),
        pltpu.SemaphoreType.DMA((window,)),
    ]
    if gathers:
        out_shape.append(jax.ShapeDtypeStruct((3, *own.shape), own.dtype))
        scratch += [pltpu.SemaphoreType.DMA((3,))] * 2
    return pl.pallas_call(
        functools.partial(exchange_kernel, axis, count, window, backward, gathers),
        name="state_backward" if backward else "state_forward",
        out_shape=out_shape,
        in_specs=[whole] * (2 if gathers else 1),
        out_specs=[whole] * len(out_shape),
        scratch_shapes=scratch,
        compiler_params=pltpu.CompilerParams(
            collective_id=collective, has_side_effects=True, vmem_limit_bytes=VMEM_LIMIT
        ),
        cost_estimate=pl.CostEstimate(flops=10**9, bytes_accessed=20 << 20, transcendentals=0),
    )(*((part, own) if gathers else (part,)))


def mixer_output_kernel(heads, state_ref, start_ref, mq_ref, out0_ref, gain_ref, delta_ref, rows_ref, states_ref):
    batch = 4

    def one(step, carry):
        for lane in range(batch):
            chunk = step * batch + lane
            at = pl.ds(pl.multiple_of(chunk * CHUNK, CHUNK), CHUNK)
            for head in range(heads):
                window = slice(head * CHUNK, (head + 1) * CHUNK)
                begin = start_ref[chunk, head]
                state = nn(begin[:, :CHUNK], state_ref[head]) + begin[:, CHUNK:].astype(F32)
                state = state.astype(BF)
                states_ref[chunk, head] = state
                out = out0_ref[chunk, head] + nn(mq_ref[chunk, head, CHUNK:], state)
                delta_ref[at, window] = out
                scale = lax.rsqrt(jnp.mean(out * out, axis=-1, keepdims=True) + 1e-05)
                rows_ref[at, window] = (out * scale * gain_ref[...]).astype(BF)
        return carry

    lax.fori_loop(0, start_ref.shape[0] // batch, one, 0)


def mixer_output(state, start, mq, out0, gain):
    chunks, heads = start.shape[:2]
    tokens = chunks * CHUNK
    return pl.pallas_call(
        functools.partial(mixer_output_kernel, heads),
        name="mixer_output",
        out_shape=(
            jax.ShapeDtypeStruct((tokens, heads * CHUNK), F32),
            jax.ShapeDtypeStruct((tokens, heads * CHUNK), BF),
            jax.ShapeDtypeStruct((chunks, heads, CHUNK, CHUNK), BF),
        ),
        compiler_params=pltpu.CompilerParams(vmem_limit_bytes=VMEM_LIMIT),
        cost_estimate=pl.CostEstimate(flops=3 * 10**8, bytes_accessed=10 << 20, transcendentals=1 << 14),
    )(state, start, mq, out0, gain)


def mixer_back_state_kernel(heads, dheads_ref, delta_ref, gain_ref, mq_ref, ddelta_ref, gain_grad_ref, shift_ref):
    chunks = mq_ref.shape[0]
    shift_ref[...] = jnp.zeros_like(shift_ref)
    gain_grad_ref[...] = jnp.zeros_like(gain_grad_ref)

    def one(step, carry):
        chunk = chunks - 1 - step
        at = pl.ds(pl.multiple_of(chunk * CHUNK, CHUNK), CHUNK)
        for head in range(heads):
            window = slice(head * CHUNK, (head + 1) * CHUNK)
            out = delta_ref[at, window]
            grad = dheads_ref[at, window].astype(F32)
            scale = lax.rsqrt(jnp.mean(out * out, axis=-1, keepdims=True) + 1e-05)
            unit = out * scale
            gain_grad_ref[...] += jnp.sum((grad * unit).reshape(CHUNK // 8, 8, CHUNK), 0)
            scaled = grad * gain_ref[...]
            back = scale * (scaled - unit * jnp.mean(scaled * unit, axis=-1, keepdims=True))
            back = back.astype(BF)
            ddelta_ref[at, window] = back
            shift_ref[head] = tn(mq_ref[chunk, head], stack(shift_ref[head].astype(BF), back))
        return carry

    lax.fori_loop(0, chunks, one, 0)


def mixer_back_state(dheads, delta, gain, mq):
    chunks, heads = mq.shape[:2]
    tokens = chunks * CHUNK
    return pl.pallas_call(
        functools.partial(mixer_back_state_kernel, heads),
        name="mixer_back_state",
        out_shape=(
            jax.ShapeDtypeStruct((tokens, heads * CHUNK), BF),
            jax.ShapeDtypeStruct((8, CHUNK), F32),
            jax.ShapeDtypeStruct((heads, CHUNK, CHUNK), F32),
        ),
        compiler_params=pltpu.CompilerParams(vmem_limit_bytes=VMEM_LIMIT),
        cost_estimate=pl.CostEstimate(flops=3 * 10**8, bytes_accessed=10 << 20, transcendentals=1 << 14),
    )(dheads, delta, gain, mq)


def mixer_backward_kernel(
    heads,
    resets_ref,
    pre_ref,
    halo_ref,
    taps_ref,
    logits_ref,
    qkv_ref,
    inv_ref,
    wu_ref,
    mq_ref,
    states_ref,
    ddelta_ref,
    arrive_ref,
    dpre_ref,
    tail_ref,
    lead_ref,
    taps_grad_ref,
    dlogits_ref,
    carry_ref,
    pad_ref,
    dpad_ref,
):
    columns = heads * CHUNK
    chunks = mq_ref.shape[0]
    rows, cols = grid_indices()
    top = lax.broadcasted_iota(jnp.int32, (CHUNK, 1), 0) < GROUP
    carry_ref[...] = arrive_ref[...]
    taps_grad_ref[...] = jnp.zeros_like(taps_grad_ref)
    dpad_ref[136:144] = jnp.zeros_like(dpad_ref[136:144])

    def one(step, carry):
        chunk = chunks - 1 - step
        at = pl.ds(pl.multiple_of(chunk * CHUNK, CHUNK), CHUNK)
        keep0 = 1.0 - resets_ref[2 * chunk]
        keep1 = 1.0 - resets_ref[2 * chunk + 1]
        both = keep0 * keep1
        enter = jnp.where(top, keep0, both)
        leave = jnp.where(top, keep1, 1.0)
        load_padded(pad_ref, pre_ref, halo_ref, chunk, resets_ref)
        mixed = convolve(pad_ref, taps_ref)
        gate = sigmoid(mixed)
        slope = gate * (1.0 + mixed * (1.0 - gate))
        silued = mixed * gate
        beta_rows = sigmoid(logits_ref[at, :])
        grads = [[None] * heads for _ in range(3)]
        dlogits = []
        for head in range(heads):
            def part(kind):
                return slice(kind * columns + head * CHUNK, kind * columns + (head + 1) * CHUNK)

            query, key, value = (qkv_ref[at, part(kind)] for kind in range(3))
            beta = beta_rows[:, head : head + 1]
            inverse = inv_ref[chunk, head]
            factors = wu_ref[chunk, head]
            weight, update = factors[:, :CHUNK], factors[:, CHUNK:]
            state = states_ref[chunk, head]
            out_grad = ddelta_ref[at, head * CHUNK : (head + 1) * CHUNK]
            later = carry_ref[head].astype(BF)
            carry_ref[head] = tn(mq_ref[chunk, head], stack(later, out_grad))
            cross = (rows >= GROUP) & (cols < GROUP)
            scores = jnp.where(rows >= cols, nt(query, key), 0.0)
            scores = jnp.where(cross, scores * keep1, scores).astype(BF)
            fresh = (update.astype(F32) - nn(weight, state)).astype(BF)
            fresh_grad = tn(scores, out_grad) + leave * nn(key, later)
            fresh_low = fresh_grad.astype(BF)
            score_grad = jnp.where(rows >= cols, nt(out_grad, fresh), 0.0)
            score_grad = jnp.where(cross, score_grad * keep1, score_grad).astype(BF)
            through = nt(stack(out_grad, fresh_low), state)
            query_grad = enter * through[:CHUNK] + nn(score_grad, key)
            weight_grad = -enter * through[CHUNK:]
            key_grad = tn(score_grad, query) + leave * nt(fresh, later)
            back = tn(inverse, side(weight_grad.astype(BF), fresh_low))
            back_low = back.astype(BF)
            strict = -jnp.where(rows > cols, nt(back_low, side(weight, update)), 0.0)
            strict = jnp.where(cross, strict * keep1, strict).astype(BF)
            yk, zv = back[:, :CHUNK], back[:, CHUNK:]
            key32 = key.astype(F32)
            strict_key = nn(strict, key)
            key_grad = key_grad + beta * (yk + strict_key) + tn(strict, (beta * key32).astype(BF))
            value_grad = beta * zv
            beta_grad = jnp.sum((yk + strict_key) * key32 + zv * value.astype(F32), axis=-1, keepdims=True)
            dlogits.append(beta_grad * beta * (1.0 - beta))
            for kind, grad in ((0, query_grad), (1, key_grad)):
                raw = silued[:, part(kind)]
                inv = lax.rsqrt(jnp.sum(raw * raw, axis=-1, keepdims=True) + 1e-06)
                unit = raw * inv
                grads[kind][head] = (grad - unit * jnp.sum(unit * grad, axis=-1, keepdims=True)) * inv
            grads[2][head] = value_grad
        dlogits_ref[at, :] = jnp.concatenate(dlogits, 1)
        dmixed = jnp.concatenate([g for kind in grads for g in kind], 1) * slope
        dpad_ref[0:GROUP] = dmixed[:GROUP]
        dpad_ref[GROUP : GROUP + 8] = dmixed[GROUP : GROUP + 8] * keep1
        dpad_ref[72 : 72 + GROUP] = dmixed[GROUP:]
        dpre = None
        for tap in range(4):
            back = 3 - tap
            shifted = stack(dpad_ref[back : back + GROUP], dpad_ref[72 + back : 72 + back + GROUP])
            term = taps_ref[tap : tap + 1] * shifted
            dpre = term if dpre is None else dpre + term
            seen = (dmixed * tap_rows(pad_ref, tap)).reshape(CHUNK // 8, 8, 3 * columns)
            taps_grad_ref[tap] += jnp.sum(seen, 0)
        dpre_ref[at, :] = dpre.astype(BF)

        @pl.when(step == 0)
        def _():
            tail_ref[...] = dpre[CHUNK - 8 :]

        dpad_ref[136:144] = dmixed[:8] * keep0
        return carry

    lax.fori_loop(0, chunks, one, 0)
    index = lax.broadcasted_iota(jnp.int32, (8, 1), 0)
    lead = jnp.zeros((8, 3 * columns), F32)
    dpad_ref[0:128] = jnp.zeros_like(dpad_ref[0:128])
    dpad_ref[8:16] = dpad_ref[136:144]
    for tap in range(3):
        back = 3 - tap
        lead = lead + taps_ref[tap : tap + 1] * dpad_ref[back : back + 8]
    lead_ref[...] = lead


def mixer_backward(resets, pre, halo, taps, logits, qkv, inv, wu, mq, states, ddelta, arrive):
    chunks, heads = mq.shape[:2]
    tokens = chunks * CHUNK
    columns = heads * CHUNK
    return pl.pallas_call(
        functools.partial(mixer_backward_kernel, heads),
        name="mixer_backward",
        out_shape=(
            jax.ShapeDtypeStruct((tokens, 3 * columns), BF),
            jax.ShapeDtypeStruct((8, 3 * columns), F32),
            jax.ShapeDtypeStruct((8, 3 * columns), F32),
            jax.ShapeDtypeStruct((4, 8, 3 * columns), F32),
            jax.ShapeDtypeStruct((tokens, heads), F32),
        ),
        in_specs=[pl.BlockSpec(memory_space=pltpu.SMEM)] + [pl.BlockSpec(memory_space=pltpu.VMEM)] * 11,
        out_specs=tuple([pl.BlockSpec(memory_space=pltpu.VMEM)] * 5),
        scratch_shapes=[
            pltpu.VMEM((heads, CHUNK, CHUNK), F32),
            pltpu.VMEM((144, 3 * columns), F32),
            pltpu.VMEM((144, 3 * columns), F32),
        ],
        compiler_params=pltpu.CompilerParams(vmem_limit_bytes=VMEM_LIMIT),
        cost_estimate=pl.CostEstimate(flops=3 * 10**9, bytes_accessed=20 << 20, transcendentals=2 << 20),
    )(resets, pre, halo, taps, logits, qkv, inv, wu, mq, states, ddelta, arrive)


def head_peers():
    place = lax.axis_index("head")
    low = lax.rem(place, 2)
    high = lax.rem(lax.div(place, 2), 2)
    return place, low, place + 1 - 2 * low, place + 2 - 4 * high


def push(src, dst, send_sem, recv_sem, axis, target):
    return pltpu.make_async_remote_copy(
        src_ref=src,
        dst_ref=dst,
        send_sem=send_sem,
        recv_sem=recv_sem,
        device_id={axis: target},
        device_id_type=MESH,
    )


def greet(axis, targets):
    barrier = pltpu.get_barrier_semaphore()
    for target in targets:
        pl.semaphore_signal(barrier, inc=1, device_id={axis: target}, device_id_type=MESH)
    pl.semaphore_wait(barrier, len(targets))


def middle_kernel(
    steps,
    hidden,
    rows_ref,
    weights_ref,
    others_ref,
    input_ref,
    ct_ref,
    late_ct_ref,
    gain_ref,
    dheads_ref,
    update_ref,
    mid_ref,
    dmid_ref,
    grads_ref,
    gain_grad_ref,
    full_ref,
    acc_ref,
    part_ref,
    pair_ref,
    far_ref,
    sum_ref,
    keep_ref,
    scale_ref,
    shard_ref,
    row_near_send,
    row_near_recv,
    row_far_send,
    row_far_recv,
    row_pass_send,
    row_pass_recv,
    pair_send,
    pair_recv,
    far_send,
    far_recv,
    last_send,
    last_recv,
):
    step = pl.program_id(0)
    place, low, near, far = head_peers()
    chunk, width = input_ref.shape
    columns = rows_ref.shape[1]
    half = width // 2
    mine = pl.ds(pl.multiple_of(low * half, 128), half)
    theirs = pl.ds(pl.multiple_of((1 - low) * half, 128), half)
    own_columns = pl.ds(pl.multiple_of(place * columns, 128), columns)

    def at(index):
        return pl.ds(pl.multiple_of(index * chunk, chunk), chunk)

    def near_rows(index):
        return push(
            rows_ref.at[at(index)], full_ref.at[0, at(index)], row_near_send.at[index], row_near_recv.at[index], "head", near
        )

    def far_rows(index):
        return push(
            rows_ref.at[at(index)], full_ref.at[1, at(index)], row_far_send.at[index], row_far_recv.at[index], "head", far
        )

    def pass_rows(index):
        return push(
            full_ref.at[1, at(index)], full_ref.at[2, at(index)], row_pass_send.at[index], row_pass_recv.at[index], "head", near
        )

    def pair(index):
        return push(
            part_ref.at[lax.rem(index, 2), :, theirs], pair_ref.at[index], pair_send.at[index], pair_recv.at[index], "head", near
        )

    def across(index):
        return push(pair_ref.at[index], far_ref.at[index], far_send.at[index], far_recv.at[index], "head", far)

    def last(index):
        return push(
            sum_ref.at[index, :, mine], sum_ref.at[index, :, mine], last_send.at[index], last_recv.at[index], "head", near
        )

    @pl.when(step == 0)
    def _():
        greet("head", (near, far))

        @pl.loop(0, steps)
        def _(index):
            far_rows(index).start()
            near_rows(index).start()

        acc_ref[...] = jnp.zeros_like(acc_ref)
        gain_grad_ref[...] = jnp.zeros_like(gain_grad_ref)

    @pl.when(step < steps)
    def _():
        ct = ct_ref[...]
        d_hidden = nn(ct, weights_ref[:, columns + 2 * hidden :])

        @pl.when(step == 0)
        def _():
            far_rows(step).wait_recv()
            pass_rows(step).start()

        near_rows(step).wait_recv()
        pass_rows(step).wait_recv()
        rows = jnp.concatenate(
            [rows_ref[at(step)], full_ref[0, at(step)], full_ref[1, at(step)], full_ref[2, at(step)]], 1
        )
        output = jnp.concatenate([weights_ref[:, :columns], others_ref[0], others_ref[1], others_ref[2]], 1)
        middle = input_ref[...].astype(F32) + nt(rows, output)
        keep_ref[lax.rem(step, 2)] = middle
        mid_ref[...] = keep_ref[lax.rem(step, 2), :, own_columns]
        scale = lax.rsqrt(jnp.mean(middle * middle, axis=-1, keepdims=True) + 1e-06)
        scale_ref[lax.rem(step, 2)] = scale
        second = (middle * scale * gain_ref[...]).astype(BF)
        both = nn(second, weights_ref[:, columns : columns + 2 * hidden])
        gate, up = both[:, :hidden], both[:, hidden:]
        sig = sigmoid(gate)
        silu = gate * sig
        active = (silu * up).astype(BF)
        d_gate = (d_hidden * up * (sig + silu * (1.0 - sig))).astype(BF)
        d_up = (d_hidden * silu).astype(BF)
        d_both = jnp.concatenate([d_gate, d_up], 1)

        @pl.when(step >= 2)
        def _():
            pair(step - 2).wait_send()

        part_ref[lax.rem(step, 2)] = nt(d_both, weights_ref[:, columns : columns + 2 * hidden]).astype(BF)
        pair(step).start()

        @pl.when(step + 1 < steps)
        def _():
            far_rows(step + 1).wait_recv()
            pass_rows(step + 1).start()

        update_ref[...] = nt(active, weights_ref[:, columns + 2 * hidden :]).astype(BF)
        acc_ref[:, columns : columns + 2 * hidden] += tn(second, d_both)
        acc_ref[:, columns + 2 * hidden :] += tn(ct, active)

    @pl.when(step > 0)
    def _():
        done = step - 1
        across(done).wait_recv()
        across(done).wait_send()
        total = pair_ref[done].astype(F32) + far_ref[done].astype(F32)
        sum_ref[done, :, mine] = total.astype(BF)
        last(done).start()

    @pl.when(step < steps)
    def _():
        pair(step).wait_recv()
        both = part_ref[lax.rem(step, 2), :, mine].astype(F32) + pair_ref[step].astype(F32)
        pair_ref[step] = both.astype(BF)
        across(step).start()

    @pl.when(step > 0)
    def _():
        done = step - 1
        last(done).wait_recv()
        grad = sum_ref[done].astype(F32)
        middle = keep_ref[lax.rem(done, 2)]
        scale = scale_ref[lax.rem(done, 2)]
        unit = middle * scale
        gain_grad_ref[...] += jnp.sum((grad * unit).reshape(chunk // 8, 8, width), 0)
        scaled = grad * gain_ref[...]
        d_middle = late_ct_ref[...].astype(F32) + scale * (
            scaled - unit * jnp.mean(scaled * unit, axis=-1, keepdims=True)
        )
        shard_ref[...] = d_middle
        dmid_ref[...] = shard_ref[:, own_columns]
        d_branch = d_middle.astype(BF)
        dheads_ref[...] = nn(d_branch, weights_ref[:, :columns]).astype(BF)
        acc_ref[:, :columns] += tn(d_branch, rows_ref[at(done)])

    @pl.when(step == steps)
    def _():
        grads_ref[...] = acc_ref[...].astype(BF)

        @pl.loop(0, steps)
        def _(index):
            near_rows(index).wait_send()
            far_rows(index).wait_send()
            pass_rows(index).wait_send()
            last(index).wait_send()

        for index in range(max(steps - 2, 0), steps):
            pair(index).wait_send()


def middle_stage(head_rows, weights, others, inputs, cotangent, gain, hidden, collective):
    tokens, width = inputs.shape
    columns = head_rows.shape[1]
    chunk = min(256, tokens // 2)
    steps = tokens // chunk
    whole = pl.BlockSpec(memory_space=pltpu.VMEM)

    def early(wide):
        return pl.BlockSpec((chunk, wide), lambda s: (jnp.minimum(s, steps - 1), 0))

    def late(wide):
        return pl.BlockSpec((chunk, wide), lambda s: (jnp.maximum(s - 1, 0), 0))

    dma = pltpu.SemaphoreType.DMA((steps,))
    return pl.pallas_call(
        functools.partial(middle_kernel, steps, hidden),
        name="middle",
        grid=(steps + 1,),
        out_shape=(
            jax.ShapeDtypeStruct((tokens, columns), BF),
            jax.ShapeDtypeStruct((tokens, width), BF),
            jax.ShapeDtypeStruct((tokens, columns), F32),
            jax.ShapeDtypeStruct((tokens, columns), F32),
            jax.ShapeDtypeStruct(weights.shape, BF),
            jax.ShapeDtypeStruct((8, width), F32),
        ),
        in_specs=[whole, whole, whole, early(width), early(width), late(width), whole],
        out_specs=(late(columns), early(width), early(columns), late(columns), whole, whole),
        scratch_shapes=[
            pltpu.VMEM((3, tokens, columns), BF),
            pltpu.VMEM(weights.shape, F32),
            pltpu.VMEM((2, chunk, width), BF),
            pltpu.VMEM((steps, chunk, width // 2), BF),
            pltpu.VMEM((steps, chunk, width // 2), BF),
            pltpu.VMEM((steps, chunk, width), BF),
            pltpu.VMEM((2, chunk, width), F32),
            pltpu.VMEM((2, chunk, 1), F32),
            pltpu.VMEM((chunk, width), F32),
        ]
        + [dma] * 12,
        compiler_params=pltpu.CompilerParams(
            collective_id=collective,
            has_side_effects=True,
            vmem_limit_bytes=VMEM_LIMIT,
            dimension_semantics=("arbitrary",),
        ),
        cost_estimate=pl.CostEstimate(flops=30 * 10**9, bytes_accessed=30 << 20, transcendentals=2 << 20),
    )(head_rows, weights, others, inputs, cotangent, cotangent, gain)


def from_behind(block, axis, distance):
    devices = range(lax.axis_size(axis))
    route = [(i - distance, i) for i in devices if i - distance in devices]
    return lax.ppermute(block, axis, route)


def dot(left, right):
    return jnp.dot(left, right, preferred_element_type=F32)


def dot_rows(left, right):
    return lax.dot_general(left, right, (((0,), (0,)), ((), ())), preferred_element_type=F32)


def dot_cols(left, right):
    return lax.dot_general(left, right, (((1,), (1,)), ((), ())), preferred_element_type=F32)


def gather_seq(block):
    return lax.all_gather(block, "seq", axis=0, tiled=True)


def body(
    block_input,
    first_gain,
    query_weight,
    key_weight,
    value_weight,
    beta_weight,
    conv_weight,
    head_gain,
    output_weight,
    second_gain,
    gate_weight,
    up_weight,
    down_weight,
    lengths,
    cotangent,
):
    tokens, width = block_input.shape
    heads = beta_weight.shape[1]
    columns = query_weight.shape[1]
    hidden_columns = gate_weight.shape[1]
    members = lax.axis_size("seq")
    piece = width // members
    column_start = lax.axis_index("head") * columns
    seq_place = lax.axis_index("seq")

    mixer_pack = gather_seq(
        jnp.concatenate(
            [query_weight, key_weight, value_weight, beta_weight, first_gain[:, None], second_gain[:, None]], 1
        )
    )
    projection = mixer_pack[:, : 3 * columns]
    full_beta = mixer_pack[:, 3 * columns : 3 * columns + heads]
    gain_one = mixer_pack[:, 3 * columns + heads].astype(F32)
    gain_two = mixer_pack[:, 3 * columns + heads + 1].astype(F32)
    spare = -hidden_columns % 128
    hidden_wide = hidden_columns + spare

    def widen(block):
        return jnp.pad(block, ((0, 0), (0, spare)))

    weights = gather_seq(
        jnp.concatenate([output_weight, widen(gate_weight), widen(up_weight), widen(down_weight)], 1)
    )

    ends = jnp.sum(jnp.where(jnp.arange(4)[:, None] >= jnp.arange(4)[None, :], lengths[None, :], 0), axis=1)
    starts = ends - lengths
    block_starts = seq_place * tokens + GROUP * jnp.arange(tokens // GROUP, dtype=jnp.int32)
    resets = jnp.any(starts[None, :] == block_starts[:, None], axis=1).astype(F32)

    inputs = block_input.astype(F32)
    halo_rows = from_behind(block_input[tokens - 16 :], "seq", 1)
    scale_one = lax.rsqrt(jnp.mean(inputs * inputs, axis=-1, keepdims=True) + 1e-06)
    first_rows = (inputs * scale_one * gain_one).astype(BF)
    halo_in = halo_rows.astype(F32)
    halo_first = (
        halo_in * lax.rsqrt(jnp.mean(halo_in * halo_in, axis=-1, keepdims=True) + 1e-06) * gain_one
    ).astype(BF)
    pre = dot(first_rows, projection).astype(BF)
    halo = dot(halo_first, projection).astype(BF)
    logits = dot(first_rows, full_beta)
    taps = conv_weight.astype(F32).transpose(1, 0, 2).reshape(4, -1)
    qkv, inv, wu, mq, start, out0, total = mixer_forward(resets, pre, halo, taps, logits, heads)
    total_low = total.astype(BF)
    state, others = exchange(total_low, weights[:, :columns], "seq", False, 0)
    gain_head = head_gain.astype(F32)[None, :]
    delta, head_rows, states = mixer_output(state, start, mq, out0, gain_head)

    d_heads, update_part, middle_shard, d_middle_shard, grads, second_grad = middle_stage(
        head_rows, weights, others, block_input, cotangent, gain_two[None, :], hidden_wide, 2
    )
    update = lax.psum_scatter(update_part, "head", scatter_dimension=1, tiled=True)
    block_output = (middle_shard + update.astype(F32)).astype(BF)
    forward_sum = lax.psum_scatter(grads, "seq", scatter_dimension=0, tiled=True).astype(F32)
    second_part = jnp.sum(second_grad, 0)
    ddelta, gain_part, shift = mixer_back_state(d_heads, delta, gain_head, mq)
    back_part = jnp.concatenate([total_low[:, :, :CHUNK].transpose(0, 2, 1), shift.astype(BF)], 2)
    (arrive,) = exchange(back_part, None, "seq", True, 1)
    d_pre_own, tail, lead, taps_part, d_logits32 = mixer_backward(
        resets, pre, halo, taps, logits, qkv, inv, wu, mq, states, ddelta, arrive
    )
    received = from_behind(lead, "seq", -1)
    d_pre = lax.dynamic_update_slice_in_dim(d_pre_own, (tail + received).astype(BF), tokens - 8, 0)
    d_logits = d_logits32.astype(BF)
    mixer_grads = dot_rows(first_rows, d_pre).astype(BF)
    mixer_sum = lax.psum_scatter(mixer_grads, "seq", scatter_dimension=0, tiled=True).astype(F32)
    beta_part = dot_rows(first_rows, d_logits)
    d_first_part = dot_cols(d_pre, projection) + dot_cols(d_logits, full_beta)
    d_first = lax.psum_scatter(d_first_part.astype(BF), "head", scatter_dimension=1, tiled=True).astype(F32)
    unit_one = inputs * scale_one
    row_part = jnp.sum(d_first_part * gain_one * unit_one, axis=-1)
    row_mean = lax.psum(row_part, "head") / width
    unit_shard = lax.dynamic_slice_in_dim(unit_one, column_start, columns, 1)
    gain_shard = lax.dynamic_slice_in_dim(gain_one, column_start, columns, 0)
    first_shard = jnp.sum(d_first * unit_shard, 0)
    first_part = lax.dynamic_update_slice_in_dim(jnp.zeros((width,), F32), first_shard, column_start, 0)
    input_gradient = d_middle_shard + scale_one * (d_first * gain_shard - unit_shard * row_mean[:, None])

    first_gathered = lax.psum(jnp.concatenate([first_part, jnp.sum(gain_part, 0)]), ("seq", "head"))
    gain_sum = first_gathered[width:]
    small = lax.psum(jnp.concatenate([jnp.sum(taps_part, 1).reshape(-1), beta_part.reshape(-1), second_part]), "seq")
    edge = 12 * columns
    conv_gradient = small[:edge].reshape(4, 3, columns).transpose(1, 0, 2)
    row_start = seq_place * piece
    beta_all = small[edge : edge + width * heads].reshape(width, heads)
    beta_gradient = lax.dynamic_slice_in_dim(beta_all, row_start, piece, 0)
    edge += width * heads
    first_gradient = lax.dynamic_slice_in_dim(first_gathered, row_start, piece, 0)
    second_gradient = lax.dynamic_slice_in_dim(small, edge + row_start, piece, 0)
    return (
        block_output,
        input_gradient,
        first_gradient,
        mixer_sum[:, :columns],
        mixer_sum[:, columns : 2 * columns],
        mixer_sum[:, 2 * columns : 3 * columns],
        beta_gradient,
        conv_gradient,
        gain_sum,
        forward_sum[:, :columns],
        second_gradient,
        *(
            forward_sum[:, columns + i * hidden_wide : columns + i * hidden_wide + hidden_columns]
            for i in range(3)
        ),
    )


def solution(mesh):
    return jax.shard_map(
        body,
        mesh=mesh,
        in_specs=(
            P("seq", None),
            P("seq"),
            P("seq", "head"),
            P("seq", "head"),
            P("seq", "head"),
            P("seq", "head"),
            P(None, None, "head"),
            P(),
            P("seq", "head"),
            P("seq"),
            P("seq", "head"),
            P("seq", "head"),
            P("seq", "head"),
            P(),
            P("seq", None),
        ),
        out_specs=(
            P("seq", "head"),
            P("seq", "head"),
            P("seq"),
            P("seq", "head"),
            P("seq", "head"),
            P("seq", "head"),
            P("seq", "head"),
            P(None, None, "head"),
            P(),
            P("seq", "head"),
            P("seq"),
            P("seq", "head"),
            P("seq", "head"),
            P("seq", "head"),
        ),
        check_vma=False,
    )
```

```python
import functools

import jax
import jax.numpy as jnp
from jax import lax
from jax.experimental import pallas as pl
from jax.experimental.pallas import tpu as pltpu
from jax.sharding import PartitionSpec as P

GROUP = 64
CHUNK = 128
MESH = pl.DeviceIdType.MESH
BF = jnp.bfloat16
F32 = jnp.float32
VMEM_LIMIT = 56 << 20


def nn(left, right):
    return jnp.dot(left.astype(BF), right.astype(BF), preferred_element_type=F32)


def tn(left, right):
    return lax.dot_general(
        left.astype(BF), right.astype(BF), (((0,), (0,)), ((), ())), preferred_element_type=F32
    )


def nt(left, right):
    return lax.dot_general(
        left.astype(BF), right.astype(BF), (((1,), (1,)), ((), ())), preferred_element_type=F32
    )


def sigmoid(v):
    return 0.5 * jnp.tanh(0.5 * v) + 0.5


def side(left, right):
    return jnp.concatenate([left, right], 1)


def stack(top, bottom):
    return jnp.concatenate([top, bottom], 0)


def grid_indices():
    rows = lax.broadcasted_iota(jnp.int32, (CHUNK, CHUNK), 0)
    cols = lax.broadcasted_iota(jnp.int32, (CHUNK, CHUNK), 1)
    return rows, cols


def load_padded(pad_ref, pre_ref, halo_ref, chunk, resets_ref):
    start = pl.multiple_of(chunk * CHUNK, CHUNK)
    before = pl.multiple_of(jnp.maximum(start - 16, 0), 16)
    own = pre_ref[pl.ds(start, CHUNK), :].astype(F32)
    earlier = pre_ref[pl.ds(before, 16), :].astype(F32)[8:]
    halo = halo_ref[...].astype(F32)[8:]
    first = jnp.where(chunk == 0, halo, earlier)
    keep0 = 1.0 - resets_ref[2 * chunk]
    keep1 = 1.0 - resets_ref[2 * chunk + 1]
    pad_ref[0:8] = first * keep0
    pad_ref[8:72] = own[:GROUP]
    pad_ref[72:80] = own[GROUP - 8 : GROUP] * keep1
    pad_ref[80:144] = own[GROUP:]


def tap_rows(pad_ref, tap):
    return stack(pad_ref[5 + tap : 69 + tap], pad_ref[77 + tap : 141 + tap])


def convolve(pad_ref, taps_ref):
    mixed = None
    for tap in range(4):
        term = taps_ref[tap : tap + 1] * tap_rows(pad_ref, tap)
        mixed = term if mixed is None else mixed + term
    return mixed


def inverse_levels(strict, rows, cols, keep1):
    eye = jnp.where(rows == cols, 1.0, 0.0)
    pair = (rows // 2) == (cols // 2)
    results = [eye - jnp.where(pair, a, 0.0) for a in strict]
    width = 2
    while width < CHUNK:
        off = ((rows // (2 * width)) == (cols // (2 * width))) & ((rows // width) != (cols // width))
        lows = [r.astype(BF) for r in results]
        parts = [jnp.where(off, a, 0.0).astype(BF) for a in strict]
        if width == GROUP:
            parts = [jnp.where(off, a * k, 0.0).astype(BF) for a, k in zip(strict, keep1)]
        steps = [nn(r, p) for r, p in zip(lows, parts)]
        results = [r - nn(s, low) for r, s, low in zip(results, steps, lows)]
        width *= 2
    return results


def mixer_forward_kernel(
    heads,
    resets_ref,
    pre_ref,
    halo_ref,
    taps_ref,
    logits_ref,
    qkv_ref,
    inv_ref,
    wu_ref,
    mq_ref,
    start_ref,
    out0_ref,
    total_ref,
    pad_ref,
):
    columns = heads * CHUNK
    rows, cols = grid_indices()
    eye = jnp.where(rows == cols, 1.0, 0.0)
    top = lax.broadcasted_iota(jnp.int32, (CHUNK, 1), 0) < GROUP
    for head in range(heads):
        total_ref[head] = side(eye, jnp.zeros_like(eye))
    batch = pad_ref.shape[0]

    def one(step, carry):
        units = []
        for lane in range(batch):
            chunk = step * batch + lane
            pad = pad_ref.at[lane]
            load_padded(pad, pre_ref, halo_ref, chunk, resets_ref)
            mixed = convolve(pad, taps_ref)
            silued = mixed * sigmoid(mixed)
            keep0 = 1.0 - resets_ref[2 * chunk]
            keep1 = 1.0 - resets_ref[2 * chunk + 1]
            both = keep0 * keep1
            enter = jnp.where(top, keep0, both)
            leave = jnp.where(top, keep1, 1.0)
            at = pl.ds(pl.multiple_of(chunk * CHUNK, CHUNK), CHUNK)
            beta_rows = sigmoid(logits_ref[at, :])
            for head in range(heads):
                window = slice(head * CHUNK, (head + 1) * CHUNK)
                parts = []
                for kind in range(3):
                    part = silued[:, kind * columns + head * CHUNK : kind * columns + (head + 1) * CHUNK]
                    if kind < 2:
                        part = part * lax.rsqrt(jnp.sum(part * part, axis=-1, keepdims=True) + 1e-06)
                    part = part.astype(BF)
                    qkv_ref[at, kind * columns + head * CHUNK : kind * columns + (head + 1) * CHUNK] = part
                    parts.append(part)
                units.append((chunk, head, *parts, beta_rows[:, head : head + 1], keep1, both, enter, leave))
        turned = [u[3].T for u in units]
        strict = [
            jnp.where(rows > cols, u[5] * nn(u[3], t), 0.0) for u, t in zip(units, turned)
        ]
        inverses = [r.astype(BF) for r in inverse_levels(strict, rows, cols, [u[6] for u in units])]
        factors = []
        for u, inverse in zip(units, inverses):
            beta = u[5]
            factors.append(nn(inverse, side(u[3].astype(F32) * beta, u[4].astype(F32) * beta)))
        for u, inverse, factor, t in zip(units, inverses, factors, turned):
            chunk, head, query, key, value, beta, keep1, both, enter, leave = u
            weight, update = factor[:, :CHUNK], factor[:, CHUNK:]
            entering_weight = weight * enter
            inv_ref[chunk, head] = inverse
            wu_ref[chunk, head] = side(entering_weight, update).astype(BF)
            gathered = nn(t, side(weight, update * leave))
            device_map = (both * (eye - gathered[:, :CHUNK])).astype(BF)
            shift = gathered[:, CHUNK:]
            scores = jnp.where(rows >= cols, nn(query, t), 0.0)
            scores = jnp.where((rows >= GROUP) & (cols < GROUP), scores * keep1, scores)
            seen = nn(scores, side(entering_weight, update))
            effective = query.astype(F32) * enter - seen[:, :CHUNK]
            mq_ref[chunk, head] = stack(device_map, effective.astype(BF))
            out0_ref[chunk, head] = seen[:, CHUNK:]
            running = total_ref[head]
            start_ref[chunk, head] = running.astype(BF)
            total_ref[head] = nn(device_map, running) + side(jnp.zeros_like(shift), shift)
        return carry

    lax.fori_loop(0, resets_ref.shape[0] // 2 // batch, one, 0)


def mixer_forward(resets, pre, halo, taps, logits, heads):
    tokens = pre.shape[0]
    chunks = tokens // CHUNK
    columns = heads * CHUNK

    def units(width, kind):
        return jax.ShapeDtypeStruct((chunks, heads, *width), kind)

    return pl.pallas_call(
        functools.partial(mixer_forward_kernel, heads),
        name="mixer_forward",
        out_shape=(
            jax.ShapeDtypeStruct((tokens, 3 * columns), BF),
            units((CHUNK, CHUNK), BF),
            units((CHUNK, 2 * CHUNK), BF),
            units((2 * CHUNK, CHUNK), BF),
            units((CHUNK, 2 * CHUNK), BF),
            units((CHUNK, CHUNK), F32),
            jax.ShapeDtypeStruct((heads, CHUNK, 2 * CHUNK), F32),
        ),
        in_specs=[pl.BlockSpec(memory_space=pltpu.SMEM)] + [pl.BlockSpec(memory_space=pltpu.VMEM)] * 4,
        out_specs=tuple([pl.BlockSpec(memory_space=pltpu.VMEM)] * 7),
        scratch_shapes=[pltpu.VMEM((2, 144, 3 * columns), F32)],
        compiler_params=pltpu.CompilerParams(vmem_limit_bytes=VMEM_LIMIT),
        cost_estimate=pl.CostEstimate(flops=3 * 10**9, bytes_accessed=20 << 20, transcendentals=2 << 20),
    )(resets, pre, halo, taps, logits)


def exchange_kernel(axis, count, window, backward, gathers, *refs):
    if backward:
        (
            part_ref, update_ref, mid_ref, state_ref, block_ref, slots_ref, send_sem, recv_sem,
            near_ref, relay_ref, far_ref, *sems,
        ) = refs
        _, _, near, far = head_peers()
        chunk = 256
        steps = update_ref.shape[0] // chunk
        at, _, start_pair, pass_on, own_sum, finish = head_scatter_copies(
            chunk, update_ref, near_ref, relay_ref, far_ref, sems
        )
    elif gathers:
        part_ref, own_ref, state_ref, others_ref, slots_ref, send_sem, recv_sem, head_send, head_recv = refs
        _, _, near, far = head_peers()
    else:
        part_ref, state_ref, slots_ref, send_sem, recv_sem = refs
    place = lax.axis_index(axis)
    ahead = count - 1 - place if backward else place
    behind = count - 1 - ahead
    sign = -1 if backward else 1
    barrier = pltpu.get_barrier_semaphore()
    for hop in range(1, window + 1):

        @pl.when(ahead >= hop)
        def _():
            pl.semaphore_signal(
                barrier, inc=1, device_id={axis: place - sign * hop}, device_id_type=MESH
            )

    extra = 0
    if gathers or backward:
        extra = 2
        for target in (near, far):
            pl.semaphore_signal(barrier, inc=1, device_id={"head": target}, device_id_type=MESH)

    if gathers:

        def near_copy():
            return push(own_ref, others_ref.at[0], head_send.at[0], head_recv.at[0], "head", near)

        def far_copy():
            return push(own_ref, others_ref.at[1], head_send.at[1], head_recv.at[1], "head", far)

        def pass_copy():
            return push(others_ref.at[1], others_ref.at[2], head_send.at[2], head_recv.at[2], "head", near)

    pl.semaphore_wait(barrier, jnp.minimum(behind, window) + extra)

    def copy(hop):
        return push(
            part_ref,
            slots_ref.at[hop - 1],
            send_sem.at[hop - 1],
            recv_sem.at[hop - 1],
            axis,
            place + sign * hop,
        )

    for hop in range(1, window + 1):

        @pl.when(behind >= hop)
        def _():
            copy(hop).start()

    if gathers:
        far_copy().start()
        near_copy().start()
    if backward:

        @pl.loop(0, steps)
        def _(index):
            start_pair(index)

        @pl.loop(0, steps)
        def _(index):
            pass_on(index)

    heads = state_ref.shape[0]
    state_ref[...] = jnp.zeros_like(state_ref)
    for hop in range(window, 0, -1):

        @pl.when(ahead >= hop)
        def _():
            copy(hop).wait_recv()
            for head in range(heads):
                part = slots_ref[hop - 1, head]
                state_ref[head] = nn(part[:, :CHUNK], state_ref[head]) + part[:, CHUNK:].astype(F32)

    if gathers:
        far_copy().wait_recv()
        pass_copy().start()
        near_copy().wait()
        far_copy().wait_send()
        pass_copy().wait()
    if backward:

        @pl.loop(0, steps)
        def _(index):
            block_ref[at(index)] = (mid_ref[at(index)] + own_sum(index)).astype(BF)
            finish(index)

    for hop in range(1, window + 1):

        @pl.when(behind >= hop)
        def _():
            copy(hop).wait_send()


def exchange(part, extras, axis, backward, collective):
    count = lax.axis_size(axis)
    window = min(count - 1, count // 2)
    heads = part.shape[0]
    whole = pl.BlockSpec(memory_space=pltpu.VMEM)
    gathers = not backward
    out_shape = [jax.ShapeDtypeStruct((heads, CHUNK, CHUNK), F32)]
    scratch = [
        pltpu.VMEM((window, heads, CHUNK, 2 * CHUNK), BF),
        pltpu.SemaphoreType.DMA((window,)),
        pltpu.SemaphoreType.DMA((window,)),
    ]
    if gathers:
        out_shape.append(jax.ShapeDtypeStruct((3, *extras[0].shape), extras[0].dtype))
        scratch += [pltpu.SemaphoreType.DMA((3,))] * 2
    else:
        tokens, columns = extras[1].shape
        out_shape.append(jax.ShapeDtypeStruct((tokens, columns), BF))
        scratch += head_scatter_scratch(tokens, columns, tokens // 256)
    return pl.pallas_call(
        functools.partial(exchange_kernel, axis, count, window, backward, gathers),
        name="state_backward" if backward else "state_forward",
        out_shape=out_shape,
        in_specs=[whole] * (1 + len(extras)),
        out_specs=[whole] * len(out_shape),
        scratch_shapes=scratch,
        compiler_params=pltpu.CompilerParams(
            collective_id=collective, has_side_effects=True, vmem_limit_bytes=VMEM_LIMIT
        ),
        cost_estimate=pl.CostEstimate(flops=10**9, bytes_accessed=20 << 20, transcendentals=0),
    )(part, *extras)


def mixer_output_kernel(heads, state_ref, start_ref, mq_ref, out0_ref, gain_ref, delta_ref, rows_ref, states_ref):
    batch = 4

    def one(step, carry):
        for lane in range(batch):
            chunk = step * batch + lane
            at = pl.ds(pl.multiple_of(chunk * CHUNK, CHUNK), CHUNK)
            for head in range(heads):
                window = slice(head * CHUNK, (head + 1) * CHUNK)
                begin = start_ref[chunk, head]
                state = nn(begin[:, :CHUNK], state_ref[head]) + begin[:, CHUNK:].astype(F32)
                state = state.astype(BF)
                states_ref[chunk, head] = state
                out = out0_ref[chunk, head] + nn(mq_ref[chunk, head, CHUNK:], state)
                delta_ref[at, window] = out
                scale = lax.rsqrt(jnp.mean(out * out, axis=-1, keepdims=True) + 1e-05)
                rows_ref[at, window] = (out * scale * gain_ref[...]).astype(BF)
        return carry

    lax.fori_loop(0, start_ref.shape[0] // batch, one, 0)


def mixer_output(state, start, mq, out0, gain):
    chunks, heads = start.shape[:2]
    tokens = chunks * CHUNK
    return pl.pallas_call(
        functools.partial(mixer_output_kernel, heads),
        name="mixer_output",
        out_shape=(
            jax.ShapeDtypeStruct((tokens, heads * CHUNK), F32),
            jax.ShapeDtypeStruct((tokens, heads * CHUNK), BF),
            jax.ShapeDtypeStruct((chunks, heads, CHUNK, CHUNK), BF),
        ),
        compiler_params=pltpu.CompilerParams(vmem_limit_bytes=VMEM_LIMIT),
        cost_estimate=pl.CostEstimate(flops=3 * 10**8, bytes_accessed=10 << 20, transcendentals=1 << 14),
    )(state, start, mq, out0, gain)


def mixer_back_state_kernel(heads, dheads_ref, delta_ref, gain_ref, mq_ref, ddelta_ref, gain_grad_ref, shift_ref):
    chunks = mq_ref.shape[0]
    shift_ref[...] = jnp.zeros_like(shift_ref)
    gain_grad_ref[...] = jnp.zeros_like(gain_grad_ref)

    def one(step, carry):
        chunk = chunks - 1 - step
        at = pl.ds(pl.multiple_of(chunk * CHUNK, CHUNK), CHUNK)
        for head in range(heads):
            window = slice(head * CHUNK, (head + 1) * CHUNK)
            out = delta_ref[at, window]
            grad = dheads_ref[at, window].astype(F32)
            scale = lax.rsqrt(jnp.mean(out * out, axis=-1, keepdims=True) + 1e-05)
            unit = out * scale
            gain_grad_ref[...] += jnp.sum((grad * unit).reshape(CHUNK // 8, 8, CHUNK), 0)
            scaled = grad * gain_ref[...]
            back = scale * (scaled - unit * jnp.mean(scaled * unit, axis=-1, keepdims=True))
            back = back.astype(BF)
            ddelta_ref[at, window] = back
            shift_ref[head] = tn(mq_ref[chunk, head], stack(shift_ref[head].astype(BF), back))
        return carry

    lax.fori_loop(0, chunks, one, 0)


def mixer_back_state(dheads, delta, gain, mq):
    chunks, heads = mq.shape[:2]
    tokens = chunks * CHUNK
    return pl.pallas_call(
        functools.partial(mixer_back_state_kernel, heads),
        name="mixer_back_state",
        out_shape=(
            jax.ShapeDtypeStruct((tokens, heads * CHUNK), BF),
            jax.ShapeDtypeStruct((8, CHUNK), F32),
            jax.ShapeDtypeStruct((heads, CHUNK, CHUNK), F32),
        ),
        compiler_params=pltpu.CompilerParams(vmem_limit_bytes=VMEM_LIMIT),
        cost_estimate=pl.CostEstimate(flops=3 * 10**8, bytes_accessed=10 << 20, transcendentals=1 << 14),
    )(dheads, delta, gain, mq)


def mixer_backward_kernel(
    heads,
    resets_ref,
    pre_ref,
    halo_ref,
    taps_ref,
    logits_ref,
    qkv_ref,
    inv_ref,
    wu_ref,
    mq_ref,
    states_ref,
    ddelta_ref,
    arrive_ref,
    dpre_ref,
    taps_grad_ref,
    carry_ref,
    pad_ref,
    dpad_ref,
    tail_ref,
    lead_ref,
    edge_ref,
    send_sem,
    recv_sem,
):
    member, members = lax.axis_index("seq"), lax.axis_size("seq")
    barrier = pltpu.get_barrier_semaphore()

    @pl.when(member + 1 < members)
    def _():
        pl.semaphore_signal(barrier, inc=1, device_id={"seq": member + 1}, device_id_type=MESH)

    columns = heads * CHUNK
    chunks = mq_ref.shape[0]
    rows, cols = grid_indices()
    top = lax.broadcasted_iota(jnp.int32, (CHUNK, 1), 0) < GROUP
    carry_ref[...] = arrive_ref[...]
    taps_grad_ref[...] = jnp.zeros_like(taps_grad_ref)
    dpad_ref[136:144] = jnp.zeros_like(dpad_ref[136:144])

    def one(step, carry):
        chunk = chunks - 1 - step
        at = pl.ds(pl.multiple_of(chunk * CHUNK, CHUNK), CHUNK)
        keep0 = 1.0 - resets_ref[2 * chunk]
        keep1 = 1.0 - resets_ref[2 * chunk + 1]
        both = keep0 * keep1
        enter = jnp.where(top, keep0, both)
        leave = jnp.where(top, keep1, 1.0)
        load_padded(pad_ref, pre_ref, halo_ref, chunk, resets_ref)
        mixed = convolve(pad_ref, taps_ref)
        gate = sigmoid(mixed)
        slope = gate * (1.0 + mixed * (1.0 - gate))
        silued = mixed * gate
        beta_rows = sigmoid(logits_ref[at, :])
        grads = [[None] * heads for _ in range(3)]
        dlogits = []
        for head in range(heads):
            def part(kind):
                return slice(kind * columns + head * CHUNK, kind * columns + (head + 1) * CHUNK)

            query, key, value = (qkv_ref[at, part(kind)] for kind in range(3))
            beta = beta_rows[:, head : head + 1]
            inverse = inv_ref[chunk, head]
            factors = wu_ref[chunk, head]
            weight, update = factors[:, :CHUNK], factors[:, CHUNK:]
            state = states_ref[chunk, head]
            out_grad = ddelta_ref[at, head * CHUNK : (head + 1) * CHUNK]
            later = carry_ref[head].astype(BF)
            carry_ref[head] = tn(mq_ref[chunk, head], stack(later, out_grad))
            cross = (rows >= GROUP) & (cols < GROUP)
            scores = jnp.where(rows >= cols, nt(query, key), 0.0)
            scores = jnp.where(cross, scores * keep1, scores).astype(BF)
            fresh = (update.astype(F32) - nn(weight, state)).astype(BF)
            fresh_grad = tn(scores, out_grad) + leave * nn(key, later)
            fresh_low = fresh_grad.astype(BF)
            score_grad = jnp.where(rows >= cols, nt(out_grad, fresh), 0.0)
            score_grad = jnp.where(cross, score_grad * keep1, score_grad).astype(BF)
            through = nt(stack(out_grad, fresh_low), state)
            query_grad = enter * through[:CHUNK] + nn(score_grad, key)
            weight_grad = -enter * through[CHUNK:]
            key_grad = tn(score_grad, query) + leave * nt(fresh, later)
            back = tn(inverse, side(weight_grad.astype(BF), fresh_low))
            back_low = back.astype(BF)
            strict = -jnp.where(rows > cols, nt(back_low, side(weight, update)), 0.0)
            strict = jnp.where(cross, strict * keep1, strict).astype(BF)
            yk, zv = back[:, :CHUNK], back[:, CHUNK:]
            key32 = key.astype(F32)
            strict_key = nn(strict, key)
            key_grad = key_grad + beta * (yk + strict_key) + tn(strict, (beta * key32).astype(BF))
            value_grad = beta * zv
            beta_grad = jnp.sum((yk + strict_key) * key32 + zv * value.astype(F32), axis=-1, keepdims=True)
            dlogits.append(beta_grad * beta * (1.0 - beta))
            for kind, grad in ((0, query_grad), (1, key_grad)):
                raw = silued[:, part(kind)]
                inv = lax.rsqrt(jnp.sum(raw * raw, axis=-1, keepdims=True) + 1e-06)
                unit = raw * inv
                grads[kind][head] = (grad - unit * jnp.sum(unit * grad, axis=-1, keepdims=True)) * inv
            grads[2][head] = value_grad
        lanes = lax.broadcasted_iota(jnp.int32, (CHUNK, CHUNK), 1)
        spread = jnp.zeros((CHUNK, CHUNK), F32)
        for head in range(heads):
            spread = jnp.where(lanes == head, dlogits[head], spread)
        dpre_ref[at, 3 * columns :] = spread.astype(BF)
        dmixed = jnp.concatenate([g for kind in grads for g in kind], 1) * slope
        dpad_ref[0:GROUP] = dmixed[:GROUP]
        dpad_ref[GROUP : GROUP + 8] = dmixed[GROUP : GROUP + 8] * keep1
        dpad_ref[72 : 72 + GROUP] = dmixed[GROUP:]
        dpre = None
        for tap in range(4):
            back = 3 - tap
            shifted = stack(dpad_ref[back : back + GROUP], dpad_ref[72 + back : 72 + back + GROUP])
            term = taps_ref[tap : tap + 1] * shifted
            dpre = term if dpre is None else dpre + term
            seen = (dmixed * tap_rows(pad_ref, tap)).reshape(CHUNK // 8, 8, 3 * columns)
            taps_grad_ref[tap] += jnp.sum(seen, 0)
        dpre_ref[at, : 3 * columns] = dpre.astype(BF)

        @pl.when(step == 0)
        def _():
            tail_ref[...] = dpre[CHUNK - 16 :]

        dpad_ref[136:144] = dmixed[:8] * keep0
        return carry

    lax.fori_loop(0, chunks, one, 0)
    index = lax.broadcasted_iota(jnp.int32, (8, 1), 0)
    lead = jnp.zeros((8, 3 * columns), F32)
    dpad_ref[0:128] = jnp.zeros_like(dpad_ref[0:128])
    dpad_ref[8:16] = dpad_ref[136:144]
    for tap in range(3):
        back = 3 - tap
        lead = lead + taps_ref[tap : tap + 1] * dpad_ref[back : back + 8]
    lead_ref[...] = lead

    def to_previous(target):
        return push(lead_ref, edge_ref, send_sem, recv_sem, "seq", target)

    @pl.when(member > 0)
    def _():
        pl.semaphore_wait(barrier, 1)
        to_previous(member - 1).start()

    @pl.when(member + 1 < members)
    def _():
        to_previous(member).wait_recv()
        last = pl.ds(dpre_ref.shape[0] - 16, 16)
        late = stack(tail_ref[0:8], tail_ref[8:16] + edge_ref[...])
        dpre_ref[last, : 3 * columns] = late.astype(BF)

    @pl.when(member > 0)
    def _():
        to_previous(member - 1).wait_send()


def mixer_backward(resets, pre, halo, taps, logits, qkv, inv, wu, mq, states, ddelta, arrive, collective):
    chunks, heads = mq.shape[:2]
    tokens = chunks * CHUNK
    columns = heads * CHUNK
    return pl.pallas_call(
        functools.partial(mixer_backward_kernel, heads),
        name="mixer_backward",
        out_shape=(
            jax.ShapeDtypeStruct((tokens, 3 * columns + CHUNK), BF),
            jax.ShapeDtypeStruct((4, 8, 3 * columns), F32),
        ),
        in_specs=[pl.BlockSpec(memory_space=pltpu.SMEM)] + [pl.BlockSpec(memory_space=pltpu.VMEM)] * 11,
        out_specs=tuple([pl.BlockSpec(memory_space=pltpu.VMEM)] * 2),
        scratch_shapes=[
            pltpu.VMEM((heads, CHUNK, CHUNK), F32),
            pltpu.VMEM((144, 3 * columns), F32),
            pltpu.VMEM((144, 3 * columns), F32),
            pltpu.VMEM((16, 3 * columns), F32),
            pltpu.VMEM((8, 3 * columns), F32),
            pltpu.VMEM((8, 3 * columns), F32),
            pltpu.SemaphoreType.DMA,
            pltpu.SemaphoreType.DMA,
        ],
        compiler_params=pltpu.CompilerParams(
            collective_id=collective, has_side_effects=True, vmem_limit_bytes=VMEM_LIMIT
        ),
        cost_estimate=pl.CostEstimate(flops=3 * 10**9, bytes_accessed=20 << 20, transcendentals=2 << 20),
    )(resets, pre, halo, taps, logits, qkv, inv, wu, mq, states, ddelta, arrive)


def head_peers():
    place = lax.axis_index("head")
    low = lax.rem(place, 2)
    high = lax.rem(lax.div(place, 2), 2)
    return place, low, place + 1 - 2 * low, place + 2 - 4 * high


def push(src, dst, send_sem, recv_sem, axis, target):
    return pltpu.make_async_remote_copy(
        src_ref=src,
        dst_ref=dst,
        send_sem=send_sem,
        recv_sem=recv_sem,
        device_id={axis: target},
        device_id_type=MESH,
    )


def greet(axis, targets):
    barrier = pltpu.get_barrier_semaphore()
    for target in targets:
        pl.semaphore_signal(barrier, inc=1, device_id={axis: target}, device_id_type=MESH)
    pl.semaphore_wait(barrier, len(targets))


def middle_kernel(
    steps,
    hidden,
    rows_ref,
    weights_ref,
    others_ref,
    input_ref,
    ct_ref,
    late_ct_ref,
    gain_ref,
    dheads_ref,
    update_ref,
    mid_ref,
    dmid_ref,
    grads_ref,
    gain_grad_ref,
    full_ref,
    acc_ref,
    part_ref,
    pair_ref,
    far_ref,
    sum_ref,
    keep_ref,
    scale_ref,
    shard_ref,
    row_near_send,
    row_near_recv,
    row_far_send,
    row_far_recv,
    row_pass_send,
    row_pass_recv,
    pair_send,
    pair_recv,
    far_send,
    far_recv,
    last_send,
    last_recv,
):
    step = pl.program_id(0)
    place, low, near, far = head_peers()
    chunk, width = input_ref.shape
    columns = rows_ref.shape[1]
    half = width // 2
    mine = pl.ds(pl.multiple_of(low * half, 128), half)
    theirs = pl.ds(pl.multiple_of((1 - low) * half, 128), half)
    own_columns = pl.ds(pl.multiple_of(place * columns, 128), columns)

    def at(index):
        return pl.ds(pl.multiple_of(index * chunk, chunk), chunk)

    def near_rows(index):
        return push(
            rows_ref.at[at(index)], full_ref.at[0, at(index)], row_near_send.at[index], row_near_recv.at[index], "head", near
        )

    def far_rows(index):
        return push(
            rows_ref.at[at(index)], full_ref.at[1, at(index)], row_far_send.at[index], row_far_recv.at[index], "head", far
        )

    def pass_rows(index):
        return push(
            full_ref.at[1, at(index)], full_ref.at[2, at(index)], row_pass_send.at[index], row_pass_recv.at[index], "head", near
        )

    def pair(index):
        return push(
            part_ref.at[lax.rem(index, 2), :, theirs], pair_ref.at[index], pair_send.at[index], pair_recv.at[index], "head", near
        )

    def across(index):
        return push(pair_ref.at[index], far_ref.at[index], far_send.at[index], far_recv.at[index], "head", far)

    def last(index):
        return push(
            sum_ref.at[index, :, mine], sum_ref.at[index, :, mine], last_send.at[index], last_recv.at[index], "head", near
        )

    @pl.when(step == 0)
    def _():
        greet("head", (near, far))

        @pl.loop(0, steps)
        def _(index):
            far_rows(index).start()
            near_rows(index).start()

        acc_ref[...] = jnp.zeros_like(acc_ref)
        gain_grad_ref[...] = jnp.zeros_like(gain_grad_ref)

    @pl.when(step < steps)
    def _():
        ct = ct_ref[...]
        d_hidden = nn(ct, weights_ref[:, columns + 2 * hidden :])

        @pl.when(step == 0)
        def _():
            far_rows(step).wait_recv()
            pass_rows(step).start()

        near_rows(step).wait_recv()
        pass_rows(step).wait_recv()
        rows = jnp.concatenate(
            [rows_ref[at(step)], full_ref[0, at(step)], full_ref[1, at(step)], full_ref[2, at(step)]], 1
        )
        output = jnp.concatenate([weights_ref[:, :columns], others_ref[0], others_ref[1], others_ref[2]], 1)
        middle = input_ref[...].astype(F32) + nt(rows, output)
        keep_ref[lax.rem(step, 2)] = middle
        mid_ref[...] = keep_ref[lax.rem(step, 2), :, own_columns]
        scale = lax.rsqrt(jnp.mean(middle * middle, axis=-1, keepdims=True) + 1e-06)
        scale_ref[lax.rem(step, 2)] = scale
        second = (middle * scale * gain_ref[...]).astype(BF)
        both = nn(second, weights_ref[:, columns : columns + 2 * hidden])
        gate, up = both[:, :hidden], both[:, hidden:]
        sig = sigmoid(gate)
        silu = gate * sig
        active = (silu * up).astype(BF)
        d_gate = (d_hidden * up * (sig + silu * (1.0 - sig))).astype(BF)
        d_up = (d_hidden * silu).astype(BF)
        d_both = jnp.concatenate([d_gate, d_up], 1)

        @pl.when(step >= 2)
        def _():
            pair(step - 2).wait_send()

        part_ref[lax.rem(step, 2)] = nt(d_both, weights_ref[:, columns : columns + 2 * hidden]).astype(BF)
        pair(step).start()

        @pl.when(step + 1 < steps)
        def _():
            far_rows(step + 1).wait_recv()
            pass_rows(step + 1).start()

        update_ref[...] = nt(active, weights_ref[:, columns + 2 * hidden :]).astype(BF)
        acc_ref[:, columns : columns + 2 * hidden] += tn(second, d_both)
        acc_ref[:, columns + 2 * hidden :] += tn(ct, active)

    @pl.when(step > 0)
    def _():
        done = step - 1
        across(done).wait_recv()
        across(done).wait_send()
        total = pair_ref[done].astype(F32) + far_ref[done].astype(F32)
        sum_ref[done, :, mine] = total.astype(BF)
        last(done).start()

    @pl.when(step < steps)
    def _():
        pair(step).wait_recv()
        both = part_ref[lax.rem(step, 2), :, mine].astype(F32) + pair_ref[step].astype(F32)
        pair_ref[step] = both.astype(BF)
        across(step).start()

    @pl.when(step > 0)
    def _():
        done = step - 1
        last(done).wait_recv()
        grad = sum_ref[done].astype(F32)
        middle = keep_ref[lax.rem(done, 2)]
        scale = scale_ref[lax.rem(done, 2)]
        unit = middle * scale
        gain_grad_ref[...] += jnp.sum((grad * unit).reshape(chunk // 8, 8, width), 0)
        scaled = grad * gain_ref[...]
        d_middle = late_ct_ref[...].astype(F32) + scale * (
            scaled - unit * jnp.mean(scaled * unit, axis=-1, keepdims=True)
        )
        shard_ref[...] = d_middle
        dmid_ref[...] = shard_ref[:, own_columns]
        d_branch = d_middle.astype(BF)
        dheads_ref[...] = nn(d_branch, weights_ref[:, :columns]).astype(BF)
        acc_ref[:, :columns] += tn(d_branch, rows_ref[at(done)])

    @pl.when(step == steps)
    def _():
        grads_ref[...] = acc_ref[...].astype(BF)

        @pl.loop(0, steps)
        def _(index):
            near_rows(index).wait_send()
            far_rows(index).wait_send()
            pass_rows(index).wait_send()
            last(index).wait_send()

        for index in range(max(steps - 2, 0), steps):
            pair(index).wait_send()


def middle_stage(head_rows, weights, others, inputs, cotangent, gain, hidden, collective):
    tokens, width = inputs.shape
    columns = head_rows.shape[1]
    chunk = min(256, tokens // 2)
    steps = tokens // chunk
    whole = pl.BlockSpec(memory_space=pltpu.VMEM)

    def early(wide):
        return pl.BlockSpec((chunk, wide), lambda s: (jnp.minimum(s, steps - 1), 0))

    def late(wide):
        return pl.BlockSpec((chunk, wide), lambda s: (jnp.maximum(s - 1, 0), 0))

    dma = pltpu.SemaphoreType.DMA((steps,))
    return pl.pallas_call(
        functools.partial(middle_kernel, steps, hidden),
        name="middle",
        grid=(steps + 1,),
        out_shape=(
            jax.ShapeDtypeStruct((tokens, columns), BF),
            jax.ShapeDtypeStruct((tokens, width), BF),
            jax.ShapeDtypeStruct((tokens, columns), F32),
            jax.ShapeDtypeStruct((tokens, columns), F32),
            jax.ShapeDtypeStruct(weights.shape, BF),
            jax.ShapeDtypeStruct((8, width), F32),
        ),
        in_specs=[whole, whole, whole, early(width), early(width), late(width), whole],
        out_specs=(late(columns), early(width), early(columns), late(columns), whole, whole),
        scratch_shapes=[
            pltpu.VMEM((3, tokens, columns), BF),
            pltpu.VMEM(weights.shape, F32),
            pltpu.VMEM((2, chunk, width), BF),
            pltpu.VMEM((steps, chunk, width // 2), BF),
            pltpu.VMEM((steps, chunk, width // 2), BF),
            pltpu.VMEM((steps, chunk, width), BF),
            pltpu.VMEM((2, chunk, width), F32),
            pltpu.VMEM((2, chunk, 1), F32),
            pltpu.VMEM((chunk, width), F32),
        ]
        + [dma] * 12,
        compiler_params=pltpu.CompilerParams(
            collective_id=collective,
            has_side_effects=True,
            vmem_limit_bytes=VMEM_LIMIT,
            dimension_semantics=("arbitrary",),
        ),
        cost_estimate=pl.CostEstimate(flops=30 * 10**9, bytes_accessed=30 << 20, transcendentals=2 << 20),
    )(head_rows, weights, others, inputs, cotangent, cotangent, gain)


def zeros_below(value):
    return (value & -value).bit_length() - 1


def flip(place, mask):
    bit = 1
    while bit <= mask:
        if mask & bit:
            place = place + bit - 2 * bit * lax.rem(lax.div(place, bit), 2)
        bit *= 2
    return place


def head_scatter_copies(chunk, part_ref, near_ref, send_ref, far_ref, sems):
    place, low, near, far = head_peers()
    high = lax.rem(lax.div(place, 2), 2)
    columns = far_ref.shape[-1]
    near_send, near_recv, far_send, far_recv = sems

    def at(index):
        return pl.ds(pl.multiple_of(index * chunk, chunk), chunk)

    def cols(owner):
        return pl.ds(pl.multiple_of(owner * columns, 128), columns)

    def pair(index, side_):
        return push(
            part_ref.at[at(index), cols(2 * side_ + 1 - low)],
            near_ref.at[side_, at(index)],
            near_send.at[side_, index],
            near_recv.at[side_, index],
            "head",
            near,
        )

    def across(index):
        return push(send_ref.at[at(index)], far_ref.at[at(index)], far_send.at[index], far_recv.at[index], "head", far)

    def start_pair(index):
        pair(index, 0).start()
        pair(index, 1).start()

    def pass_on(index):
        pair(index, 0).wait_recv()
        pair(index, 1).wait_recv()
        total = part_ref[at(index), cols(2 * (1 - high) + low)].astype(F32) + near_ref[1 - high, at(index)].astype(F32)
        send_ref[at(index)] = total.astype(BF)
        across(index).start()

    def own_sum(index):
        across(index).wait_recv()
        near_part = part_ref[at(index), cols(place)].astype(F32) + near_ref[high, at(index)].astype(F32)
        return near_part + far_ref[at(index)].astype(F32)

    def finish(index):
        pair(index, 0).wait_send()
        pair(index, 1).wait_send()
        across(index).wait_send()

    return at, cols, start_pair, pass_on, own_sum, finish


def head_scatter_scratch(tokens, columns, steps):
    return [
        pltpu.VMEM((2, tokens, columns), BF),
        pltpu.VMEM((tokens, columns), BF),
        pltpu.VMEM((tokens, columns), BF),
        pltpu.SemaphoreType.DMA((2, steps)),
        pltpu.SemaphoreType.DMA((2, steps)),
        pltpu.SemaphoreType.DMA((steps,)),
        pltpu.SemaphoreType.DMA((steps,)),
    ]


def final_kernel(
    members,
    chunk,
    rows_ref,
    dpre_ref,
    pack_ref,
    input_ref,
    scale_ref,
    gain_ref,
    dmid_ref,
    small_ref,
    ingrad_ref,
    piece_ref,
    sums_ref,
    acc_ref,
    out_ref,
    slots_ref,
    part_ref,
    near_ref,
    send_ref,
    far_ref,
    near_send,
    near_recv,
    far_send,
    far_recv,
    stat_ref,
    stat_slots,
    small_slots,
    piece_send,
    piece_recv,
    stat_send,
    stat_recv,
    small_send,
    small_recv,
):
    tokens, width = input_ref.shape
    steps = tokens // chunk
    place, low, near, far = head_peers()
    member = lax.axis_index("seq")
    rows = width // members
    stages = (members - 1).bit_length()
    at, cols, start_pair, pass_on, own_sum, finish = head_scatter_copies(
        chunk, part_ref, near_ref, send_ref, far_ref, (near_send, near_recv, far_send, far_recv)
    )

    barrier = pltpu.get_barrier_semaphore()
    for target in (near, far):
        pl.semaphore_signal(barrier, inc=1, device_id={"head": target}, device_id_type=MESH)
    for stage in range(stages):
        pl.semaphore_signal(barrier, inc=1, device_id={"seq": flip(member, 1 << stage)}, device_id_type=MESH)
    pl.semaphore_wait(barrier, 2 + stages)

    order = sorted(range(members), key=lambda r: zeros_below(r) if r else stages)
    sent = [r for r in order if r]
    events = {}
    for r in order:
        for stage in range(zeros_below(r) if r else stages):
            events[stage, r] = len(events)

    def give(r):
        stage = zeros_below(r)
        slot = events[stage, r ^ (1 << stage)]
        return push(
            out_ref.at[r],
            slots_ref.at[slot],
            piece_send.at[r],
            piece_recv.at[slot],
            "seq",
            flip(member, 1 << stage),
        )

    def take(stage, r):
        slot = events[stage, r]
        return push(
            out_ref.at[0], slots_ref.at[slot], piece_send.at[0], piece_recv.at[slot], "seq", flip(member, 1 << stage)
        )

    def send_piece(r):
        out_ref[r] = acc_ref[flip(member, r)].astype(BF)
        give(r).start()

    def receive(r):
        index = flip(member, r)
        for stage in range(zeros_below(r) if r else stages):
            take(stage, r).wait_recv()
            acc_ref[index] += slots_ref[events[stage, r]].astype(F32)
        if r:
            send_piece(r)

    first = sorted([r for r in range(members) if r % 2], key=lambda r: order.index(r ^ 1))
    evens = [r for r in order if r % 2 == 0]
    if rows % 128 == 0:
        for r in first + evens:
            index = flip(member, r)
            columns = pl.ds(pl.multiple_of(index * rows, 128), rows)
            acc_ref[index] = tn(rows_ref[:, columns], dpre_ref[...])
            if r % 2:
                send_piece(r)
    else:
        per = 128 // rows
        for unit in range(width // 128):
            block = tn(rows_ref[:, unit * 128 : (unit + 1) * 128], dpre_ref[...])
            acc_ref[unit * per : (unit + 1) * per] = block.reshape(per, rows, block.shape[1])
        for r in first:
            send_piece(r)

    small_slots[0] = small_ref[...]
    diagonal = lax.broadcasted_iota(jnp.int32, (128, 128), 0) == lax.broadcasted_iota(jnp.int32, (128, 128), 1)

    def project(index):
        part = nt(dpre_ref[at(index)], pack_ref[...])
        part_ref[at(index)] = part.astype(BF)
        start_pair(index)
        seen = part * (input_ref[at(index)].astype(F32) * scale_ref[at(index)])
        small_slots[0, 0:1] += jnp.sum(seen, 0, keepdims=True)
        stat = jnp.sum(seen * gain_ref[...], axis=-1, keepdims=True)
        for block in range(chunk // 128):
            line = jnp.where(diagonal, stat[block * 128 : (block + 1) * 128], 0.0)
            stat_ref[index * (chunk // 128) + block] = jnp.sum(line, 0, keepdims=True)

    receives = list(evens)
    for group in range(steps // 2):

        @pl.loop(2 * group, 2 * group + 2)
        def _(index):
            project(index)

            @pl.when(index > 0)
            def _():
                pass_on(index - 1)

        if group and len(receives) > 2:
            receive(receives.pop(0))
    pass_on(steps - 1)

    def stat_copy(stage):
        target = (near, far)[stage]
        return push(stat_ref, stat_slots.at[stage], stat_send.at[stage], stat_recv.at[stage], "head", target)

    def head_copy(stage):
        target = (near, far)[stage]
        return push(
            small_slots.at[stage, pl.ds(0, 8)],
            small_slots.at[2 + stage, pl.ds(0, 8)],
            small_send.at[stage],
            small_recv.at[stage],
            "head",
            target,
        )

    stat_copy(0).start()
    head_copy(0).start()
    stat_copy(0).wait()
    head_copy(0).wait()
    stat_ref[...] += stat_slots[0]
    small_slots[1] = small_slots[0]
    small_slots[1, 0:8] += small_slots[2, 0:8]
    stat_copy(1).start()
    head_copy(1).start()
    while len(receives) > 1:
        receive(receives.pop(0))
    stat_copy(1).wait()
    head_copy(1).wait()
    stat_ref[...] += stat_slots[1]
    small_slots[4] = small_slots[1]
    small_slots[4, 0:8] += small_slots[3, 0:8]

    bits = list(range(1, stages)) + [0]

    def seq_copy(turn):
        return push(
            small_slots.at[4 + 2 * turn],
            small_slots.at[5 + 2 * turn],
            small_send.at[2 + turn],
            small_recv.at[2 + turn],
            "seq",
            flip(member, 1 << bits[turn]),
        )

    def seq_add(turn):
        seq_copy(turn).wait()
        small_slots[6 + 2 * turn] = small_slots[4 + 2 * turn] + small_slots[5 + 2 * turn]

    seq_copy(0).start()

    def result(index):
        grad = own_sum(index)
        scale = scale_ref[at(index)]
        unit = input_ref[at(index), cols(place)].astype(F32) * scale
        means = []
        for block in range(chunk // 128):
            line = jnp.where(diagonal, stat_ref[index * (chunk // 128) + block], 0.0)
            means.append(jnp.sum(line, axis=-1, keepdims=True))
        mean = jnp.concatenate(means, 0) * (1.0 / width)
        ingrad_ref[at(index)] = dmid_ref[at(index)] + scale * (grad * gain_ref[:, cols(place)] - unit * mean)

    for turn in range(stages):
        start, stop = turn * steps // stages, (turn + 1) * steps // stages
        if stop > start:

            @pl.loop(start, stop)
            def _(index):
                result(index)

        seq_add(turn)
        if turn + 1 < stages:
            seq_copy(turn + 1).start()
    receive(0)
    piece_ref[...] = acc_ref[member]
    sums_ref[...] = small_slots[4 + 2 * stages]

    @pl.loop(0, steps)
    def _(index):
        finish(index)

    for r in sent:
        give(r).wait_send()


def final_stage(first_rows, dpre, pack, inputs, scale, gain, dmid, small, members, collective):
    tokens, width = inputs.shape
    columns = dmid.shape[1]
    chunk = 256
    steps = tokens // chunk
    stages = (members - 1).bit_length()
    rows = width // members
    wide = dpre.shape[1]
    whole = pl.BlockSpec(memory_space=pltpu.VMEM)
    return pl.pallas_call(
        functools.partial(final_kernel, members, chunk),
        name="final",
        out_shape=(
            jax.ShapeDtypeStruct((tokens, columns), F32),
            jax.ShapeDtypeStruct((rows, wide), F32),
            jax.ShapeDtypeStruct(small.shape, F32),
        ),
        in_specs=[whole] * 8,
        out_specs=(whole,) * 3,
        scratch_shapes=[
            pltpu.VMEM((members, rows, wide), F32),
            pltpu.VMEM((members, rows, wide), BF),
            pltpu.VMEM((members - 1, rows, wide), BF),
            pltpu.VMEM((tokens, width), BF),
        ]
        + head_scatter_scratch(tokens, columns, steps)
        + [
            pltpu.VMEM((tokens // 128, 1, 128), F32),
            pltpu.VMEM((2, tokens // 128, 1, 128), F32),
            pltpu.VMEM((5 + 2 * stages, *small.shape), F32),
            pltpu.SemaphoreType.DMA((members,)),
            pltpu.SemaphoreType.DMA((members - 1,)),
            pltpu.SemaphoreType.DMA((2,)),
            pltpu.SemaphoreType.DMA((2,)),
            pltpu.SemaphoreType.DMA((2 + stages,)),
            pltpu.SemaphoreType.DMA((2 + stages,)),
        ],
        compiler_params=pltpu.CompilerParams(
            collective_id=collective, has_side_effects=True, vmem_limit_bytes=VMEM_LIMIT
        ),
        cost_estimate=pl.CostEstimate(flops=8 * 10**9, bytes_accessed=30 << 20, transcendentals=0),
    )(first_rows, dpre, pack, inputs, scale, gain, dmid, small)


def from_behind(block, axis, distance):
    devices = range(lax.axis_size(axis))
    route = [(i - distance, i) for i in devices if i - distance in devices]
    return lax.ppermute(block, axis, route)


def dot(left, right):
    return jnp.dot(left, right, preferred_element_type=F32)


def dot_rows(left, right):
    return lax.dot_general(left, right, (((0,), (0,)), ((), ())), preferred_element_type=F32)


def dot_cols(left, right):
    return lax.dot_general(left, right, (((1,), (1,)), ((), ())), preferred_element_type=F32)


def gather_seq(block):
    return lax.all_gather(block, "seq", axis=0, tiled=True)


def body(
    block_input,
    first_gain,
    query_weight,
    key_weight,
    value_weight,
    beta_weight,
    conv_weight,
    head_gain,
    output_weight,
    second_gain,
    gate_weight,
    up_weight,
    down_weight,
    lengths,
    cotangent,
):
    tokens, width = block_input.shape
    heads = beta_weight.shape[1]
    columns = query_weight.shape[1]
    hidden_columns = gate_weight.shape[1]
    members = lax.axis_size("seq")
    piece = width // members
    seq_place = lax.axis_index("seq")

    mixer_pack = gather_seq(
        jnp.concatenate(
            [
                query_weight,
                key_weight,
                value_weight,
                beta_weight,
                first_gain[:, None],
                second_gain[:, None],
                jnp.zeros((piece, CHUNK - heads - 2), BF),
            ],
            1,
        )
    )
    projection = mixer_pack[:, : 3 * columns]
    full_beta = mixer_pack[:, 3 * columns : 3 * columns + heads]
    gain_one = mixer_pack[:, 3 * columns + heads].astype(F32)
    gain_two = mixer_pack[:, 3 * columns + heads + 1].astype(F32)
    spare = -hidden_columns % 128
    hidden_wide = hidden_columns + spare

    def widen(block):
        return jnp.pad(block, ((0, 0), (0, spare)))

    weights = gather_seq(
        jnp.concatenate([output_weight, widen(gate_weight), widen(up_weight), widen(down_weight)], 1)
    )

    ends = jnp.sum(jnp.where(jnp.arange(4)[:, None] >= jnp.arange(4)[None, :], lengths[None, :], 0), axis=1)
    starts = ends - lengths
    block_starts = seq_place * tokens + GROUP * jnp.arange(tokens // GROUP, dtype=jnp.int32)
    resets = jnp.any(starts[None, :] == block_starts[:, None], axis=1).astype(F32)

    inputs = block_input.astype(F32)
    halo_rows = from_behind(block_input[tokens - 16 :], "seq", 1)
    scale_one = lax.rsqrt(jnp.mean(inputs * inputs, axis=-1, keepdims=True) + 1e-06)
    first_rows = (inputs * scale_one * gain_one).astype(BF)
    halo_in = halo_rows.astype(F32)
    halo_first = (
        halo_in * lax.rsqrt(jnp.mean(halo_in * halo_in, axis=-1, keepdims=True) + 1e-06) * gain_one
    ).astype(BF)
    pre = dot(first_rows, projection).astype(BF)
    halo = dot(halo_first, projection).astype(BF)
    logits = dot(first_rows, full_beta)
    taps = conv_weight.astype(F32).transpose(1, 0, 2).reshape(4, -1)
    qkv, inv, wu, mq, start, out0, total = mixer_forward(resets, pre, halo, taps, logits, heads)
    total_low = total.astype(BF)
    state, others = exchange(total_low, (weights[:, :columns],), "seq", False, 0)
    gain_head = head_gain.astype(F32)[None, :]
    delta, head_rows, states = mixer_output(state, start, mq, out0, gain_head)

    d_heads, update_part, middle_shard, d_middle_shard, grads, second_grad = middle_stage(
        head_rows, weights, others, block_input, cotangent, gain_two[None, :], hidden_wide, 2
    )
    forward_sum = lax.psum_scatter(grads, "seq", scatter_dimension=0, tiled=True).astype(F32)
    second_part = jnp.sum(second_grad, 0)
    ddelta, gain_part, shift = mixer_back_state(d_heads, delta, gain_head, mq)
    back_part = jnp.concatenate([total_low[:, :, :CHUNK].transpose(0, 2, 1), shift.astype(BF)], 2)
    arrive, block_output = exchange(back_part, (update_part, middle_shard), "seq", True, 1)
    d_pre, taps_part = mixer_backward(
        resets, pre, halo, taps, logits, qkv, inv, wu, mq, states, ddelta, arrive, 3
    )
    small = jnp.concatenate(
        [
            jnp.zeros((1, width), F32),
            jnp.pad(jnp.sum(gain_part, 0, keepdims=True), ((0, 0), (0, width - CHUNK))),
            jnp.zeros((6, width), F32),
            jnp.sum(second_grad, 0, keepdims=True),
            jnp.sum(taps_part, 1).reshape(-1, width),
            jnp.zeros((7 - 12 * columns // width, width), F32),
        ]
    )
    input_gradient, mixer_sum, sums = final_stage(
        first_rows, d_pre, mixer_pack, block_input, scale_one, gain_one[None, :], d_middle_shard, small, members, 4
    )
    gain_sum = sums[1, :CHUNK]
    conv_gradient = sums[9 : 9 + 12 * columns // width].reshape(4, 3, columns).transpose(1, 0, 2)
    row_start = seq_place * piece
    first_gradient = lax.dynamic_slice_in_dim(sums[0], row_start, piece, 0)
    second_gradient = lax.dynamic_slice_in_dim(sums[8], row_start, piece, 0)
    beta_gradient = mixer_sum[:, 3 * columns : 3 * columns + heads]
    return (
        block_output,
        input_gradient,
        first_gradient,
        mixer_sum[:, :columns],
        mixer_sum[:, columns : 2 * columns],
        mixer_sum[:, 2 * columns : 3 * columns],
        beta_gradient,
        conv_gradient,
        gain_sum,
        forward_sum[:, :columns],
        second_gradient,
        *(
            forward_sum[:, columns + i * hidden_wide : columns + i * hidden_wide + hidden_columns]
            for i in range(3)
        ),
    )


def solution(mesh):
    return jax.shard_map(
        body,
        mesh=mesh,
        in_specs=(
            P("seq", None),
            P("seq"),
            P("seq", "head"),
            P("seq", "head"),
            P("seq", "head"),
            P("seq", "head"),
            P(None, None, "head"),
            P(),
            P("seq", "head"),
            P("seq"),
            P("seq", "head"),
            P("seq", "head"),
            P("seq", "head"),
            P(),
            P("seq", None),
        ),
        out_specs=(
            P("seq", "head"),
            P("seq", "head"),
            P("seq"),
            P("seq", "head"),
            P("seq", "head"),
            P("seq", "head"),
            P("seq", "head"),
            P(None, None, "head"),
            P(),
            P("seq", "head"),
            P("seq"),
            P("seq", "head"),
            P("seq", "head"),
            P("seq", "head"),
        ),
        check_vma=False,
    )
```

```python
import functools

import jax
import jax.numpy as jnp
from jax import lax
from jax.experimental import pallas as pl
from jax.experimental.pallas import tpu as pltpu
from jax.sharding import PartitionSpec as P

GROUP = 64
CHUNK = 128
MESH = pl.DeviceIdType.MESH
BF = jnp.bfloat16
F32 = jnp.float32
VMEM_LIMIT = 56 << 20


def nn(left, right):
    return jnp.dot(left.astype(BF), right.astype(BF), preferred_element_type=F32)


def tn(left, right):
    return lax.dot_general(
        left.astype(BF), right.astype(BF), (((0,), (0,)), ((), ())), preferred_element_type=F32
    )


def nt(left, right):
    return lax.dot_general(
        left.astype(BF), right.astype(BF), (((1,), (1,)), ((), ())), preferred_element_type=F32
    )


def sigmoid(v):
    return 0.5 * jnp.tanh(0.5 * v) + 0.5


def side(left, right):
    return jnp.concatenate([left, right], 1)


def stack(top, bottom):
    return jnp.concatenate([top, bottom], 0)


def grid_indices():
    rows = lax.broadcasted_iota(jnp.int32, (CHUNK, CHUNK), 0)
    cols = lax.broadcasted_iota(jnp.int32, (CHUNK, CHUNK), 1)
    return rows, cols


def load_padded(pad_ref, pre_ref, halo_ref, chunk, resets_ref):
    start = pl.multiple_of(chunk * CHUNK, CHUNK)
    before = pl.multiple_of(jnp.maximum(start - 16, 0), 16)
    own = pre_ref[pl.ds(start, CHUNK), :].astype(F32)
    earlier = pre_ref[pl.ds(before, 16), :].astype(F32)[8:]
    halo = halo_ref[...].astype(F32)[8:]
    first = jnp.where(chunk == 0, halo, earlier)
    keep0 = 1.0 - resets_ref[2 * chunk]
    keep1 = 1.0 - resets_ref[2 * chunk + 1]
    pad_ref[0:8] = first * keep0
    pad_ref[8:72] = own[:GROUP]
    pad_ref[72:80] = own[GROUP - 8 : GROUP] * keep1
    pad_ref[80:144] = own[GROUP:]


def tap_rows(pad_ref, tap):
    return stack(pad_ref[5 + tap : 69 + tap], pad_ref[77 + tap : 141 + tap])


def convolve(pad_ref, taps_ref):
    mixed = None
    for tap in range(4):
        term = taps_ref[tap : tap + 1] * tap_rows(pad_ref, tap)
        mixed = term if mixed is None else mixed + term
    return mixed


def inverse_levels(strict, rows, cols, keep1):
    eye = jnp.where(rows == cols, 1.0, 0.0)
    pair = (rows // 2) == (cols // 2)
    results = [eye - jnp.where(pair, a, 0.0) for a in strict]
    width = 2
    while width < CHUNK:
        off = ((rows // (2 * width)) == (cols // (2 * width))) & ((rows // width) != (cols // width))
        lows = [r.astype(BF) for r in results]
        parts = [jnp.where(off, a, 0.0).astype(BF) for a in strict]
        if width == GROUP:
            parts = [jnp.where(off, a * k, 0.0).astype(BF) for a, k in zip(strict, keep1)]
        steps = [nn(r, p) for r, p in zip(lows, parts)]
        results = [r - nn(s, low) for r, s, low in zip(results, steps, lows)]
        width *= 2
    return results


def exchange_kernel(axis, count, window, backward, *refs):
    if backward:
        (
            part_ref, update_ref, mid_ref, grads_ref, state_ref, block_ref, total_ref, slots_ref, send_sem, recv_sem,
            near_ref, relay_ref, far_ref, *sems, piece_relay, piece_slots, piece_send, piece_recv,
        ) = refs
        begin, receive, jobs, end = piece_scatter(
            grads_ref, piece_relay, piece_slots, total_ref, piece_send, piece_recv, count
        )
        _, _, near, far = head_peers()
        chunk = 256
        steps = update_ref.shape[0] // chunk
        at, _, start_pair, pass_on, own_sum, finish = head_scatter_copies(
            chunk, update_ref, near_ref, relay_ref, far_ref, sems
        )
    else:
        part_ref, state_ref, slots_ref, send_sem, recv_sem = refs
    place = lax.axis_index(axis)
    ahead = count - 1 - place if backward else place
    behind = count - 1 - ahead
    sign = -1 if backward else 1
    barrier = pltpu.get_barrier_semaphore()
    for hop in range(1, window + 1):

        @pl.when(ahead >= hop)
        def _():
            pl.semaphore_signal(
                barrier, inc=1, device_id={axis: place - sign * hop}, device_id_type=MESH
            )

    extra = 0
    if backward:
        extra = 2 + greet_seq(count)[1]
        for target in (near, far):
            pl.semaphore_signal(barrier, inc=1, device_id={"head": target}, device_id_type=MESH)

    if extra:
        pl.semaphore_wait(barrier, jnp.minimum(behind, window) + extra)
    else:

        @pl.when(behind > 0)
        def _():
            pl.semaphore_wait(barrier, jnp.minimum(behind, window))

    def copy(hop):
        return push(
            part_ref,
            slots_ref.at[hop - 1],
            send_sem.at[hop - 1],
            recv_sem.at[hop - 1],
            axis,
            place + sign * hop,
        )

    for hop in range(1, window + 1):

        @pl.when(behind >= hop)
        def _():
            copy(hop).start()

    if backward:

        @pl.loop(0, steps)
        def _(index):
            start_pair(index)

        begin()

        @pl.loop(0, steps)
        def _(index):
            pass_on(index)

        for job in jobs[: len(jobs) // 2]:
            receive(*job)

    heads = state_ref.shape[0]
    state_ref[...] = jnp.zeros_like(state_ref)
    for hop in range(window, 0, -1):

        @pl.when(ahead >= hop)
        def _():
            copy(hop).wait_recv()
            for head in range(heads):
                part = slots_ref[hop - 1, head]
                state_ref[head] = nn(part[:, :CHUNK], state_ref[head]) + part[:, CHUNK:].astype(F32)

    if backward:
        for job in jobs[len(jobs) // 2 :]:
            receive(*job)

        @pl.loop(0, steps)
        def _(index):
            block_ref[at(index)] = (mid_ref[at(index)] + own_sum(index)).astype(BF)
            finish(index)

        end()

    for hop in range(1, window + 1):

        @pl.when(behind >= hop)
        def _():
            copy(hop).wait_send()


def exchange(part, extras, axis, backward, collective):
    count = lax.axis_size(axis)
    window = min(count - 1, count // 2)
    heads = part.shape[0]
    whole = pl.BlockSpec(memory_space=pltpu.VMEM)
    out_shape = [jax.ShapeDtypeStruct((heads, CHUNK, CHUNK), F32)]
    scratch = [
        pltpu.VMEM((window, heads, CHUNK, 2 * CHUNK), BF),
        pltpu.SemaphoreType.DMA((window,)),
        pltpu.SemaphoreType.DMA((window,)),
    ]
    if backward:
        tokens, columns = extras[1].shape
        out_shape.append(jax.ShapeDtypeStruct((tokens, columns), BF))
        scratch += head_scatter_scratch(tokens, columns, tokens // 256)
        parts, _, *piece = extras[2].shape
        out_shape.append(jax.ShapeDtypeStruct((parts, *piece), F32))
        scratch += piece_scatter_scratch(parts, count, piece)
    return pl.pallas_call(
        functools.partial(exchange_kernel, axis, count, window, backward),
        name="state_backward" if backward else "state_forward",
        out_shape=out_shape,
        in_specs=[whole] * (1 + len(extras)),
        out_specs=[whole] * len(out_shape),
        scratch_shapes=scratch,
        compiler_params=pltpu.CompilerParams(
            collective_id=collective, has_side_effects=True, vmem_limit_bytes=VMEM_LIMIT
        ),
        cost_estimate=pl.CostEstimate(flops=10**9, bytes_accessed=20 << 20, transcendentals=0),
    )(part, *extras)


def mixer_output_kernel(heads, state_ref, start_ref, mq_ref, out0_ref, gain_ref, delta_ref, rows_ref, states_ref):
    batch = 4

    def one(step, carry):
        for lane in range(batch):
            chunk = step * batch + lane
            at = pl.ds(pl.multiple_of(chunk * CHUNK, CHUNK), CHUNK)
            for head in range(heads):
                window = slice(head * CHUNK, (head + 1) * CHUNK)
                begin = start_ref[chunk, head]
                state = nn(begin[:, :CHUNK], state_ref[head]) + begin[:, CHUNK:].astype(F32)
                state = state.astype(BF)
                states_ref[chunk, head] = state
                out = out0_ref[chunk, head] + nn(mq_ref[chunk, head, CHUNK:], state)
                delta_ref[at, window] = out
                scale = lax.rsqrt(jnp.mean(out * out, axis=-1, keepdims=True) + 1e-05)
                rows_ref[at, window] = (out * scale * gain_ref[...]).astype(BF)
        return carry

    lax.fori_loop(0, start_ref.shape[0] // batch, one, 0)


def mixer_output(state, start, mq, out0, gain):
    chunks, heads = start.shape[:2]
    tokens = chunks * CHUNK
    return pl.pallas_call(
        functools.partial(mixer_output_kernel, heads),
        name="mixer_output",
        out_shape=(
            jax.ShapeDtypeStruct((tokens, heads * CHUNK), F32),
            jax.ShapeDtypeStruct((tokens, heads * CHUNK), BF),
            jax.ShapeDtypeStruct((chunks, heads, CHUNK, CHUNK), BF),
        ),
        compiler_params=pltpu.CompilerParams(vmem_limit_bytes=VMEM_LIMIT),
        cost_estimate=pl.CostEstimate(flops=3 * 10**8, bytes_accessed=10 << 20, transcendentals=1 << 14),
    )(state, start, mq, out0, gain)


def mixer_back_state_kernel(heads, dheads_ref, delta_ref, gain_ref, mq_ref, ddelta_ref, gain_grad_ref, shift_ref):
    chunks = mq_ref.shape[0]
    shift_ref[...] = jnp.zeros_like(shift_ref)
    gain_grad_ref[...] = jnp.zeros_like(gain_grad_ref)

    def one(step, carry):
        chunk = chunks - 1 - step
        at = pl.ds(pl.multiple_of(chunk * CHUNK, CHUNK), CHUNK)
        for head in range(heads):
            window = slice(head * CHUNK, (head + 1) * CHUNK)
            out = delta_ref[at, window]
            grad = dheads_ref[at, window].astype(F32)
            scale = lax.rsqrt(jnp.mean(out * out, axis=-1, keepdims=True) + 1e-05)
            unit = out * scale
            gain_grad_ref[...] += jnp.sum((grad * unit).reshape(CHUNK // 8, 8, CHUNK), 0)
            scaled = grad * gain_ref[...]
            back = scale * (scaled - unit * jnp.mean(scaled * unit, axis=-1, keepdims=True))
            back = back.astype(BF)
            ddelta_ref[at, window] = back
            shift_ref[head] = tn(mq_ref[chunk, head], stack(shift_ref[head].astype(BF), back))
        return carry

    lax.fori_loop(0, chunks, one, 0)


def mixer_back_state(dheads, delta, gain, mq):
    chunks, heads = mq.shape[:2]
    tokens = chunks * CHUNK
    return pl.pallas_call(
        functools.partial(mixer_back_state_kernel, heads),
        name="mixer_back_state",
        out_shape=(
            jax.ShapeDtypeStruct((tokens, heads * CHUNK), BF),
            jax.ShapeDtypeStruct((8, CHUNK), F32),
            jax.ShapeDtypeStruct((heads, CHUNK, CHUNK), F32),
        ),
        compiler_params=pltpu.CompilerParams(vmem_limit_bytes=VMEM_LIMIT),
        cost_estimate=pl.CostEstimate(flops=3 * 10**8, bytes_accessed=10 << 20, transcendentals=1 << 14),
    )(dheads, delta, gain, mq)


def piece_scatter_scratch(parts, members, piece):
    return [
        pltpu.VMEM((parts, max(members // 2 - 1, 1), *piece), BF),
        pltpu.VMEM((parts, members - 1, *piece), BF),
        pltpu.SemaphoreType.DMA((parts, members)),
        pltpu.SemaphoreType.DMA((parts, members)),
    ]


def piece_scatter(own_ref, relay_ref, slots_ref, total_ref, send, recv, members):
    member = lax.axis_index("seq")
    parts = own_ref.shape[0]
    stages = (members - 1).bit_length()
    order = sorted(range(members), key=lambda r: zeros_below(r) if r else stages)
    levels = {r: list(range(zeros_below(r) if r else stages)) for r in order}
    events = {}
    for r in order:
        for stage in levels[r]:
            events[r, stage] = len(events)
    kept = [r for r in order if r and r % 2 == 0]

    def source(part, r):
        return own_ref.at[part, flip(member, r)] if r % 2 else relay_ref.at[part, kept.index(r)]

    def give(part, r):
        stage = zeros_below(r)
        slot = events[r ^ (1 << stage), stage]
        return push(
            source(part, r), slots_ref.at[part, slot], send.at[part, r], recv.at[part, slot], "seq", flip(member, 1 << stage)
        )

    def take(part, r, stage):
        slot = events[r, stage]
        return push(
            own_ref.at[part, flip(member, 1)], slots_ref.at[part, slot], send.at[part, 0], recv.at[part, slot], "seq", flip(member, 1 << stage)
        )

    jobs = [(part, r) for r in order if r % 2 == 0 for part in range(parts)]

    def begin():
        for part, r in jobs:
            give(part, r ^ 1).start()

    def receive(part, r):
        total = own_ref[part, flip(member, r)].astype(F32)
        for stage in levels[r]:
            take(part, r, stage).wait_recv()
            total = total + slots_ref[part, events[r, stage]].astype(F32)
        if r:
            relay_ref[part, kept.index(r)] = total.astype(BF)
            give(part, r).start()
        else:
            total_ref[part] = total

    def finish():
        for part in range(parts):
            for r in order:
                if r:
                    give(part, r).wait_send()

    return begin, receive, jobs, finish


def mixer_backward_kernel(
    heads,
    resets_ref,
    pre_ref,
    halo_ref,
    taps_ref,
    logits_ref,
    qkv_ref,
    inv_ref,
    wu_ref,
    mq_ref,
    states_ref,
    ddelta_ref,
    arrive_ref,
    grads_ref,
    dpre_ref,
    taps_grad_ref,
    total_ref,
    carry_ref,
    pad_ref,
    dpad_ref,
    tail_ref,
    lead_ref,
    edge_ref,
    send_sem,
    recv_sem,
    relay_ref,
    slots_ref,
    piece_send,
    piece_recv,
):
    member, members = lax.axis_index("seq"), lax.axis_size("seq")
    barrier, stages = greet_seq(members)
    begin, receive, order, finish = piece_scatter(
        grads_ref, relay_ref, slots_ref, total_ref, piece_send, piece_recv, members
    )

    @pl.when(member + 1 < members)
    def _():
        pl.semaphore_signal(barrier, inc=1, device_id={"seq": member + 1}, device_id_type=MESH)

    columns = heads * CHUNK
    chunks = mq_ref.shape[0]
    rows, cols = grid_indices()
    top = lax.broadcasted_iota(jnp.int32, (CHUNK, 1), 0) < GROUP
    pl.semaphore_wait(barrier, stages + jnp.minimum(member, 1))
    begin()
    carry_ref[...] = arrive_ref[...]
    taps_grad_ref[...] = jnp.zeros_like(taps_grad_ref)
    dpad_ref[136:144] = jnp.zeros_like(dpad_ref[136:144])

    def one(step, carry):
        chunk = chunks - 1 - step
        at = pl.ds(pl.multiple_of(chunk * CHUNK, CHUNK), CHUNK)
        keep0 = 1.0 - resets_ref[2 * chunk]
        keep1 = 1.0 - resets_ref[2 * chunk + 1]
        both = keep0 * keep1
        enter = jnp.where(top, keep0, both)
        leave = jnp.where(top, keep1, 1.0)
        load_padded(pad_ref, pre_ref, halo_ref, chunk, resets_ref)
        mixed = convolve(pad_ref, taps_ref)
        gate = sigmoid(mixed)
        slope = gate * (1.0 + mixed * (1.0 - gate))
        silued = mixed * gate
        beta_rows = sigmoid(logits_ref[at, :])
        grads = [[None] * heads for _ in range(3)]
        dlogits = []
        cross = (rows >= GROUP) & (cols < GROUP)

        def part(kind, head):
            return slice(kind * columns + head * CHUNK, kind * columns + (head + 1) * CHUNK)

        def masked(product, keep):
            lower = jnp.where(keep, product, 0.0)
            return jnp.where(cross, lower * keep1, lower).astype(BF)

        every = range(heads)
        query = [qkv_ref[at, part(0, h)] for h in every]
        key = [qkv_ref[at, part(1, h)] for h in every]
        value = [qkv_ref[at, part(2, h)] for h in every]
        key32 = [k.astype(F32) for k in key]
        beta = [beta_rows[:, h : h + 1] for h in every]
        inverse = [inv_ref[chunk, h] for h in every]
        weight = [wu_ref[chunk, h, :, :CHUNK] for h in every]
        factors = [wu_ref[chunk, h] for h in every]
        update = [wu_ref[chunk, h, :, CHUNK:] for h in every]
        state = [states_ref[chunk, h] for h in every]
        out_grad = [ddelta_ref[at, h * CHUNK : (h + 1) * CHUNK] for h in every]
        later = [carry_ref[h].astype(BF) for h in every]
        carried = [tn(mq_ref[chunk, h], stack(later[h], out_grad[h])) for h in every]
        scores = [masked(nt(query[h], key[h]), rows >= cols) for h in every]
        fresh = [(update[h].astype(F32) - nn(weight[h], state[h])).astype(BF) for h in every]
        fresh_low = [(tn(scores[h], out_grad[h]) + leave * nn(key[h], later[h])).astype(BF) for h in every]
        score_grad = [masked(nt(out_grad[h], fresh[h]), rows >= cols) for h in every]
        through = [nt(stack(out_grad[h], fresh_low[h]), state[h]) for h in every]
        weight_grad = [(-enter * through[h][CHUNK:]).astype(BF) for h in every]
        back = [tn(inverse[h], side(weight_grad[h], fresh_low[h])) for h in every]
        query_grad = [enter * through[h][:CHUNK] + nn(score_grad[h], key[h]) for h in every]
        key_grad = [tn(score_grad[h], query[h]) + leave * nt(fresh[h], later[h]) for h in every]
        strict = [masked(-nt(back[h].astype(BF), factors[h]), rows > cols) for h in every]
        strict_key = [nn(strict[h], key[h]) for h in every]
        turned = [tn(strict[h], (beta[h] * key32[h]).astype(BF)) for h in every]
        for h in every:
            carry_ref[h] = carried[h]
            yk, zv = back[h][:, :CHUNK], back[h][:, CHUNK:]
            both_key = yk + strict_key[h]
            key_grad[h] = key_grad[h] + beta[h] * both_key + turned[h]
            grads[2][h] = beta[h] * zv
            beta_grad = jnp.sum(both_key * key32[h] + zv * value[h].astype(F32), axis=-1, keepdims=True)
            dlogits.append(beta_grad * beta[h] * (1.0 - beta[h]))
        for kind, grad in ((0, query_grad), (1, key_grad)):
            raw = [silued[:, part(kind, h)] for h in every]
            norm = [lax.rsqrt(jnp.sum(raw[h] * raw[h], axis=-1, keepdims=True) + 1e-06) for h in every]
            unit = [raw[h] * norm[h] for h in every]
            inner = [jnp.sum(unit[h] * grad[h], axis=-1, keepdims=True) for h in every]
            grads[kind] = [(grad[h] - unit[h] * inner[h]) * norm[h] for h in every]
        lanes = lax.broadcasted_iota(jnp.int32, (CHUNK, CHUNK), 1)
        spread = jnp.zeros((CHUNK, CHUNK), F32)
        for head in range(heads):
            spread = jnp.where(lanes == head, dlogits[head], spread)
        dpre_ref[at, 3 * columns :] = spread.astype(BF)
        dmixed = jnp.concatenate([g for kind in grads for g in kind], 1) * slope
        dpad_ref[0:GROUP] = dmixed[:GROUP]
        dpad_ref[GROUP : GROUP + 8] = dmixed[GROUP : GROUP + 8] * keep1
        dpad_ref[72 : 72 + GROUP] = dmixed[GROUP:]
        dpre = None
        for tap in range(4):
            back = 3 - tap
            shifted = stack(dpad_ref[back : back + GROUP], dpad_ref[72 + back : 72 + back + GROUP])
            term = taps_ref[tap : tap + 1] * shifted
            dpre = term if dpre is None else dpre + term
            seen = (dmixed * tap_rows(pad_ref, tap)).reshape(CHUNK // 8, 8, 3 * columns)
            taps_grad_ref[tap] += jnp.sum(seen, 0)
        dpre_ref[at, : 3 * columns] = dpre.astype(BF)

        @pl.when(step == 0)
        def _():
            tail_ref[...] = dpre[CHUNK - 16 :]

        dpad_ref[136:144] = dmixed[:8] * keep0
        for place, job in enumerate(order):

            @pl.when(step == (place + 1) * (chunks - 1) // len(order))
            def _():
                receive(*job)

        return carry

    lax.fori_loop(0, chunks, one, 0)
    index = lax.broadcasted_iota(jnp.int32, (8, 1), 0)
    lead = jnp.zeros((8, 3 * columns), F32)
    dpad_ref[0:128] = jnp.zeros_like(dpad_ref[0:128])
    dpad_ref[8:16] = dpad_ref[136:144]
    for tap in range(3):
        back = 3 - tap
        lead = lead + taps_ref[tap : tap + 1] * dpad_ref[back : back + 8]
    lead_ref[...] = lead

    def to_previous(target):
        return push(lead_ref, edge_ref, send_sem, recv_sem, "seq", target)

    @pl.when(member > 0)
    def _():
        to_previous(member - 1).start()

    @pl.when(member + 1 < members)
    def _():
        to_previous(member).wait_recv()
        last = pl.ds(dpre_ref.shape[0] - 16, 16)
        late = stack(tail_ref[0:8], tail_ref[8:16] + edge_ref[...])
        dpre_ref[last, : 3 * columns] = late.astype(BF)

    @pl.when(member > 0)
    def _():
        to_previous(member - 1).wait_send()

    finish()


def mixer_backward(resets, pre, halo, taps, logits, qkv, inv, wu, mq, states, ddelta, arrive, grads, collective):
    chunks, heads = mq.shape[:2]
    tokens = chunks * CHUNK
    columns = heads * CHUNK
    parts, members = grads.shape[:2]
    piece = grads.shape[2:]
    return pl.pallas_call(
        functools.partial(mixer_backward_kernel, heads),
        name="mixer_backward",
        out_shape=(
            jax.ShapeDtypeStruct((tokens, 3 * columns + CHUNK), BF),
            jax.ShapeDtypeStruct((4, 8, 3 * columns), F32),
            jax.ShapeDtypeStruct((parts, *piece), F32),
        ),
        in_specs=[pl.BlockSpec(memory_space=pltpu.SMEM)] + [pl.BlockSpec(memory_space=pltpu.VMEM)] * 12,
        out_specs=tuple([pl.BlockSpec(memory_space=pltpu.VMEM)] * 3),
        scratch_shapes=[
            pltpu.VMEM((heads, CHUNK, CHUNK), F32),
            pltpu.VMEM((144, 3 * columns), F32),
            pltpu.VMEM((144, 3 * columns), F32),
            pltpu.VMEM((16, 3 * columns), F32),
            pltpu.VMEM((8, 3 * columns), F32),
            pltpu.VMEM((8, 3 * columns), F32),
            pltpu.SemaphoreType.DMA,
            pltpu.SemaphoreType.DMA,
        ]
        + piece_scatter_scratch(parts, members, piece),
        compiler_params=pltpu.CompilerParams(
            collective_id=collective, has_side_effects=True, vmem_limit_bytes=VMEM_LIMIT
        ),
        cost_estimate=pl.CostEstimate(flops=3 * 10**9, bytes_accessed=20 << 20, transcendentals=2 << 20),
    )(resets, pre, halo, taps, logits, qkv, inv, wu, mq, states, ddelta, arrive, grads)


def head_peers():
    place = lax.axis_index("head")
    low = lax.rem(place, 2)
    high = lax.rem(lax.div(place, 2), 2)
    return place, low, place + 1 - 2 * low, place + 2 - 4 * high


def push(src, dst, send_sem, recv_sem, axis, target):
    return pltpu.make_async_remote_copy(
        src_ref=src,
        dst_ref=dst,
        send_sem=send_sem,
        recv_sem=recv_sem,
        device_id={axis: target},
        device_id_type=MESH,
    )


def greet(axis, targets):
    barrier = pltpu.get_barrier_semaphore()
    for target in targets:
        pl.semaphore_signal(barrier, inc=1, device_id={axis: target}, device_id_type=MESH)
    pl.semaphore_wait(barrier, len(targets))


def middle_kernel(
    steps,
    rows_ref,
    full_hbm,
    turned_hbm,
    others_hbm,
    input_ref,
    ct_ref,
    late_ct_ref,
    gain_ref,
    dheads_ref,
    update_ref,
    mid_ref,
    dmid_ref,
    first_grads_ref,
    second_grads_ref,
    third_grads_ref,
    gain_grad_ref,
    gate_ref,
    up_ref,
    down_ref,
    turned_ref,
    others_ref,
    load_sem,
    full_ref,
    acc_ref,
    part_ref,
    pair_ref,
    far_ref,
    sum_ref,
    keep_ref,
    scale_ref,
    shard_ref,
    row_near_send,
    row_near_recv,
    row_far_send,
    row_far_recv,
    row_pass_send,
    row_pass_recv,
    pair_send,
    pair_recv,
    far_send,
    far_recv,
    last_send,
    last_recv,
):
    step = pl.program_id(0)
    place, low, near, far = head_peers()
    chunk, width = input_ref.shape
    columns = rows_ref.shape[1]
    hidden = gate_ref.shape[0]
    half = width // 2
    mine = pl.ds(pl.multiple_of(low * half, 128), half)
    theirs = pl.ds(pl.multiple_of((1 - low) * half, 128), half)
    own_columns = pl.ds(pl.multiple_of(place * columns, 128), columns)

    def at(index):
        return pl.ds(pl.multiple_of(index * chunk, chunk), chunk)

    def near_rows(index):
        return push(
            rows_ref.at[at(index)], full_ref.at[0, at(index)], row_near_send.at[index], row_near_recv.at[index], "head", near
        )

    def far_rows(index):
        return push(
            rows_ref.at[at(index)], full_ref.at[1, at(index)], row_far_send.at[index], row_far_recv.at[index], "head", far
        )

    def pass_rows(index):
        return push(
            full_ref.at[1, at(index)], full_ref.at[2, at(index)], row_pass_send.at[index], row_pass_recv.at[index], "head", near
        )

    def pair(index):
        return push(
            part_ref.at[lax.rem(index, 2), :, theirs], pair_ref.at[index], pair_send.at[index], pair_recv.at[index], "head", near
        )

    def across(index):
        return push(pair_ref.at[index], far_ref.at[index], far_send.at[index], far_recv.at[index], "head", far)

    def last(index):
        return push(
            sum_ref.at[index, :, mine], sum_ref.at[index, :, mine], last_send.at[index], last_recv.at[index], "head", near
        )

    def loads():
        targets = [
            (full_hbm.at[0], gate_ref),
            (full_hbm.at[1], up_ref),
            (full_hbm.at[2], down_ref),
            (turned_hbm, turned_ref),
        ] + [(others_hbm.at[other], others_ref.at[other]) for other in range(3)]
        for number, (source, target) in enumerate(targets):
            for piece in range(width // 128):
                yield pltpu.make_async_copy(
                    source.at[piece], target.at[:, piece * 128 : (piece + 1) * 128], load_sem.at[number, piece]
                )

    @pl.when(step == 0)
    def _():
        for load in loads():
            load.start()
        greet("head", (near, far))

        @pl.loop(0, steps)
        def _(index):
            far_rows(index).start()
            near_rows(index).start()

        acc_ref[...] = jnp.zeros_like(acc_ref)
        gain_grad_ref[...] = jnp.zeros_like(gain_grad_ref)
        for load in loads():
            load.wait()

    @pl.when(step < steps)
    def _():
        ct = ct_ref[...]
        d_hidden = nt(ct, down_ref[...])

        @pl.when(step == 0)
        def _():
            far_rows(step).wait_recv()
            pass_rows(step).start()

        near_rows(step).wait_recv()
        pass_rows(step).wait_recv()
        branch = nn(rows_ref[at(step)], turned_ref[...])
        for other in range(3):
            branch = branch + nn(full_ref[other, at(step)], others_ref[other])
        middle = input_ref[...].astype(F32) + branch
        keep_ref[lax.rem(step, 3)] = middle
        mid_ref[...] = keep_ref[lax.rem(step, 3), :, own_columns]
        scale = lax.rsqrt(jnp.mean(middle * middle, axis=-1, keepdims=True) + 1e-06)
        scale_ref[lax.rem(step, 3)] = scale
        second = (middle * scale * gain_ref[...]).astype(BF)
        gate, up = nt(second, gate_ref[...]), nt(second, up_ref[...])
        sig = sigmoid(gate)
        silu = gate * sig
        active = (silu * up).astype(BF)
        d_gate = (d_hidden * up * (sig + silu * (1.0 - sig))).astype(BF)
        d_up = (d_hidden * silu).astype(BF)

        @pl.when(step >= 2)
        def _():
            pair(step - 2).wait_send()

        part_ref[lax.rem(step, 2)] = (nn(d_gate, gate_ref[...]) + nn(d_up, up_ref[...])).astype(BF)
        pair(step).start()

        @pl.when(step + 1 < steps)
        def _():
            far_rows(step + 1).wait_recv()
            pass_rows(step + 1).start()

        update_ref[...] = nn(active, down_ref[...]).astype(BF)
        acc_ref[:hidden] += tn(d_gate, second)
        acc_ref[hidden : 2 * hidden] += tn(d_up, second)
        acc_ref[2 * hidden : 3 * hidden] += tn(active, ct)

    @pl.when(step < steps)
    def _():
        pair(step).wait_recv()
        both = part_ref[lax.rem(step, 2), :, mine].astype(F32) + pair_ref[step].astype(F32)
        pair_ref[step] = both.astype(BF)
        across(step).start()

    @pl.when((step > 0) & (step <= steps))
    def _():
        done = step - 1
        across(done).wait_recv()
        across(done).wait_send()
        total = pair_ref[done].astype(F32) + far_ref[done].astype(F32)
        sum_ref[done, :, mine] = total.astype(BF)
        last(done).start()

    @pl.when(step > 1)
    def _():
        done = step - 2
        last(done).wait_recv()
        grad = sum_ref[done].astype(F32)
        middle = keep_ref[lax.rem(done, 3)]
        scale = scale_ref[lax.rem(done, 3)]
        unit = middle * scale
        gain_grad_ref[...] += jnp.sum((grad * unit).reshape(chunk // 8, 8, width), 0)
        scaled = grad * gain_ref[...]
        d_middle = late_ct_ref[...].astype(F32) + scale * (
            scaled - unit * jnp.mean(scaled * unit, axis=-1, keepdims=True)
        )
        shard_ref[...] = d_middle
        dmid_ref[...] = shard_ref[:, own_columns]
        d_branch = d_middle.astype(BF)
        dheads_ref[...] = nt(d_branch, turned_ref[...]).astype(BF)
        acc_ref[3 * hidden :] += tn(rows_ref[at(done)], d_branch)

    @pl.when(step == steps + 1)
    def _():
        for piece in range(width // 128):
            lanes = slice(piece * 128, (piece + 1) * 128)
            begin = 0
            for grads_ref in (first_grads_ref, second_grads_ref, third_grads_ref):
                rows = grads_ref.shape[2]
                for part in range(2):
                    grads_ref[part, piece] = acc_ref[begin : begin + rows, lanes].astype(BF)
                    begin += rows

        @pl.loop(0, steps)
        def _(index):
            near_rows(index).wait_send()
            far_rows(index).wait_send()
            pass_rows(index).wait_send()
            last(index).wait_send()

        for index in range(max(steps - 2, 0), steps):
            pair(index).wait_send()


def middle_stage(head_rows, full, turned, others, inputs, cotangent, gain, collective):
    tokens, width = inputs.shape
    columns = head_rows.shape[1]
    chunk = min(256, tokens // 2)
    steps = tokens // chunk
    whole = pl.BlockSpec(memory_space=pltpu.VMEM)
    outside = pl.BlockSpec(memory_space=pl.ANY)
    hidden = full.shape[2]
    units = (3 * hidden + columns) // 32
    shares = [16 * (units * 36 // 74), 0, 16 * (units * 25 // 74)]
    shares[1] = 16 * units - sum(shares)

    def early(wide):
        return pl.BlockSpec((chunk, wide), lambda s: (jnp.minimum(s, steps - 1), 0))

    def late(wide):
        return pl.BlockSpec((chunk, wide), lambda s: (jnp.maximum(s - 2, 0), 0))

    dma = pltpu.SemaphoreType.DMA((steps,))
    return pl.pallas_call(
        functools.partial(middle_kernel, steps),
        name="middle",
        grid=(steps + 2,),
        out_shape=(
            jax.ShapeDtypeStruct((tokens, columns), BF),
            jax.ShapeDtypeStruct((tokens, width), BF),
            jax.ShapeDtypeStruct((tokens, columns), F32),
            jax.ShapeDtypeStruct((tokens, columns), F32),
            *(jax.ShapeDtypeStruct((2, width // 128, rows, 128), BF) for rows in shares),
            jax.ShapeDtypeStruct((8, width), F32),
        ),
        in_specs=[whole] + [outside] * 3 + [early(width), early(width), late(width), whole],
        out_specs=(late(columns), early(width), early(columns), late(columns), whole, whole, whole, whole),
        scratch_shapes=[
            pltpu.VMEM((hidden, width), BF),
            pltpu.VMEM((hidden, width), BF),
            pltpu.VMEM((hidden, width), BF),
            pltpu.VMEM((columns, width), BF),
            pltpu.VMEM((3, columns, width), BF),
            pltpu.SemaphoreType.DMA((7, width // 128)),
            pltpu.VMEM((3, tokens, columns), BF),
            pltpu.VMEM((3 * hidden + columns, width), F32),
            pltpu.VMEM((2, chunk, width), BF),
            pltpu.VMEM((steps, chunk, width // 2), BF),
            pltpu.VMEM((steps, chunk, width // 2), BF),
            pltpu.VMEM((steps, chunk, width), BF),
            pltpu.VMEM((3, chunk, width), F32),
            pltpu.VMEM((3, chunk, 1), F32),
            pltpu.VMEM((chunk, width), F32),
        ]
        + [dma] * 12,
        compiler_params=pltpu.CompilerParams(
            collective_id=collective,
            has_side_effects=True,
            vmem_limit_bytes=VMEM_LIMIT,
            dimension_semantics=("arbitrary",),
        ),
        cost_estimate=pl.CostEstimate(flops=30 * 10**9, bytes_accessed=30 << 20, transcendentals=2 << 20),
    )(head_rows, full, turned, others, inputs, cotangent, cotangent, gain)


def zeros_below(value):
    return (value & -value).bit_length() - 1


def flip(place, mask):
    bit = 1
    while bit <= mask:
        if mask & bit:
            place = place + bit - 2 * bit * lax.rem(lax.div(place, bit), 2)
        bit *= 2
    return place


def head_scatter_copies(chunk, part_ref, near_ref, send_ref, far_ref, sems):
    place, low, near, far = head_peers()
    high = lax.rem(lax.div(place, 2), 2)
    columns = far_ref.shape[-1]
    near_send, near_recv, far_send, far_recv = sems

    def at(index):
        return pl.ds(pl.multiple_of(index * chunk, chunk), chunk)

    def cols(owner):
        return pl.ds(pl.multiple_of(owner * columns, 128), columns)

    def pair(index, side_):
        return push(
            part_ref.at[at(index), cols(2 * side_ + 1 - low)],
            near_ref.at[side_, at(index)],
            near_send.at[side_, index],
            near_recv.at[side_, index],
            "head",
            near,
        )

    def across(index):
        return push(send_ref.at[at(index)], far_ref.at[at(index)], far_send.at[index], far_recv.at[index], "head", far)

    def start_pair(index):
        pair(index, 0).start()
        pair(index, 1).start()

    def pass_on(index):
        pair(index, 0).wait_recv()
        pair(index, 1).wait_recv()
        total = part_ref[at(index), cols(2 * (1 - high) + low)].astype(F32) + near_ref[1 - high, at(index)].astype(F32)
        send_ref[at(index)] = total.astype(BF)
        across(index).start()

    def own_sum(index):
        across(index).wait_recv()
        near_part = part_ref[at(index), cols(place)].astype(F32) + near_ref[high, at(index)].astype(F32)
        return near_part + far_ref[at(index)].astype(F32)

    def finish(index):
        pair(index, 0).wait_send()
        pair(index, 1).wait_send()
        across(index).wait_send()

    return at, cols, start_pair, pass_on, own_sum, finish


def head_scatter_scratch(tokens, columns, steps):
    return [
        pltpu.VMEM((2, tokens, columns), BF),
        pltpu.VMEM((tokens, columns), BF),
        pltpu.VMEM((tokens, columns), BF),
        pltpu.SemaphoreType.DMA((2, steps)),
        pltpu.SemaphoreType.DMA((2, steps)),
        pltpu.SemaphoreType.DMA((steps,)),
        pltpu.SemaphoreType.DMA((steps,)),
    ]


def final_kernel(
    members,
    chunk,
    rows_ref,
    dpre_ref,
    pack_ref,
    input_ref,
    scale_ref,
    gain_ref,
    dmid_ref,
    small_ref,
    rest_ref,
    ingrad_ref,
    piece_ref,
    sums_ref,
    total_ref,
    acc_ref,
    out_ref,
    slots_ref,
    part_ref,
    near_ref,
    send_ref,
    far_ref,
    near_send,
    near_recv,
    far_send,
    far_recv,
    stat_ref,
    stat_slots,
    small_slots,
    piece_send,
    piece_recv,
    stat_send,
    stat_recv,
    small_send,
    small_recv,
    rest_relay,
    rest_slots,
    rest_send,
    rest_recv,
):
    tokens, width = input_ref.shape
    steps = tokens // chunk
    place, low, near, far = head_peers()
    member = lax.axis_index("seq")
    rows = width // members
    stages = (members - 1).bit_length()
    at, cols, start_pair, pass_on, own_sum, finish = head_scatter_copies(
        chunk, part_ref, near_ref, send_ref, far_ref, (near_send, near_recv, far_send, far_recv)
    )

    barrier = pltpu.get_barrier_semaphore()
    opposite = near + far - place
    for target in (near, far, opposite):
        pl.semaphore_signal(barrier, inc=1, device_id={"head": target}, device_id_type=MESH)
    for stage in range(stages):
        pl.semaphore_signal(barrier, inc=1, device_id={"seq": flip(member, 1 << stage)}, device_id_type=MESH)
    begin, rest_receive, rest_jobs, rest_end = piece_scatter(
        rest_ref, rest_relay, rest_slots, total_ref, rest_send, rest_recv, members
    )
    pl.semaphore_wait(barrier, 3 + stages)
    order = sorted(range(members), key=lambda r: zeros_below(r) if r else stages)
    sent = [r for r in order if r]
    events = {}
    for r in order:
        for stage in range(zeros_below(r) if r else stages):
            events[stage, r] = len(events)

    def give(r):
        stage = zeros_below(r)
        slot = events[stage, r ^ (1 << stage)]
        return push(
            out_ref.at[r],
            slots_ref.at[slot],
            piece_send.at[r],
            piece_recv.at[slot],
            "seq",
            flip(member, 1 << stage),
        )

    def take(stage, r):
        slot = events[stage, r]
        return push(
            out_ref.at[0], slots_ref.at[slot], piece_send.at[0], piece_recv.at[slot], "seq", flip(member, 1 << stage)
        )

    def send_piece(r):
        out_ref[r] = acc_ref[flip(member, r)].astype(BF)
        give(r).start()

    def receive(r):
        index = flip(member, r)
        for stage in range(zeros_below(r) if r else stages):
            take(stage, r).wait_recv()
            acc_ref[index] += slots_ref[events[stage, r]].astype(F32)
        if r:
            send_piece(r)

    first = sorted([r for r in range(members) if r % 2], key=lambda r: order.index(r ^ 1))
    evens = [r for r in order if r % 2 == 0]
    if rows % 128 == 0:
        for r in first:
            even = 2 * lax.div(flip(member, r), 2)
            columns = pl.ds(pl.multiple_of(even * rows, 128), 2 * rows)
            block = tn(rows_ref[:, columns], dpre_ref[...])
            acc_ref[even] = block[:rows]
            acc_ref[even + 1] = block[rows:]
            send_piece(r)
        begin()
    else:
        per = 128 // rows
        for unit in range(width // 128):
            block = tn(rows_ref[:, unit * 128 : (unit + 1) * 128], dpre_ref[...])
            acc_ref[unit * per : (unit + 1) * per] = block.reshape(per, rows, block.shape[1])
        for r in first:
            send_piece(r)
        begin()

    small_slots[0] = small_ref[...]
    diagonal = lax.broadcasted_iota(jnp.int32, (128, 128), 0) == lax.broadcasted_iota(jnp.int32, (128, 128), 1)

    def project(index):
        part = nt(dpre_ref[at(index)], pack_ref[...])
        part_ref[at(index)] = part.astype(BF)
        start_pair(index)
        seen = part * (input_ref[at(index)].astype(F32) * scale_ref[at(index)])
        small_slots[0, 0:1] += jnp.sum(seen, 0, keepdims=True)
        stat = jnp.sum(seen * gain_ref[...], axis=-1, keepdims=True)
        for block in range(chunk // 128):
            line = jnp.where(diagonal, stat[block * 128 : (block + 1) * 128], 0.0)
            stat_ref[index * (chunk // 128) + block] = jnp.sum(line, 0, keepdims=True)

    early = steps // 2
    receives = list(evens)
    for half in range(2):

        @pl.loop(half * early, (half + 1) * early)
        def _(index):
            project(index)

            @pl.when(lax.rem(index, 2) == 1)
            def _():
                pass_on(lax.div(index, 2))

        if len(receives) > 1:
            receive(receives.pop(0))

    def stat_copy(turn):
        target = (near, far, opposite)[turn]
        return push(stat_ref, stat_slots.at[turn], stat_send.at[turn], stat_recv.at[turn], "head", target)

    def head_copy(turn):
        target = (near, far, opposite)[turn]
        return push(
            small_slots.at[0, pl.ds(0, 8)],
            small_slots.at[1 + turn, pl.ds(0, 8)],
            small_send.at[turn],
            small_recv.at[turn],
            "head",
            target,
        )

    for turn in (1, 2, 0):
        head_copy(turn).start()
        stat_copy(turn).start()
    for index in range(early, steps):
        pass_on(index)
    while len(receives) > 1:
        receive(receives.pop(0))
    for turn in range(3):
        head_copy(turn).wait()
    small_slots[4] = small_slots[0]
    small_slots[4, 0:8] += small_slots[1, 0:8] + small_slots[2, 0:8] + small_slots[3, 0:8]

    bits = list(range(1, stages)) + [0]

    def seq_copy(turn):
        return push(
            small_slots.at[4 + 2 * turn],
            small_slots.at[5 + 2 * turn],
            small_send.at[3 + turn],
            small_recv.at[3 + turn],
            "seq",
            flip(member, 1 << bits[turn]),
        )

    def seq_add(turn):
        seq_copy(turn).wait()
        small_slots[6 + 2 * turn] = small_slots[4 + 2 * turn] + small_slots[5 + 2 * turn]

    seq_copy(0).start()
    for turn in range(3):
        stat_copy(turn).wait()
    stat_ref[...] += stat_slots[0] + stat_slots[1] + stat_slots[2]

    def result(index):
        grad = own_sum(index)
        scale = scale_ref[at(index)]
        unit = input_ref[at(index), cols(place)].astype(F32) * scale
        means = []
        for block in range(chunk // 128):
            line = jnp.where(diagonal, stat_ref[index * (chunk // 128) + block], 0.0)
            means.append(jnp.sum(line, axis=-1, keepdims=True))
        mean = jnp.concatenate(means, 0) * (1.0 / width)
        ingrad_ref[at(index)] = dmid_ref[at(index)] + scale * (grad * gain_ref[:, cols(place)] - unit * mean)

    rests = list(rest_jobs)
    for turn in range(stages):
        start, stop = turn * steps // stages, (turn + 1) * steps // stages
        if stop > start:

            @pl.loop(start, stop)
            def _(index):
                result(index)

        share = (len(rests) - 1) // (stages - turn)
        for job in rests[:share]:
            rest_receive(*job)
        rests = rests[share:]
        seq_add(turn)
        if turn + 1 < stages:
            seq_copy(turn + 1).start()
    receive(0)
    for job in rests:
        rest_receive(*job)
    piece_ref[...] = acc_ref[member]
    sums_ref[...] = small_slots[4 + 2 * stages]

    @pl.loop(0, steps)
    def _(index):
        finish(index)

    for r in sent:
        give(r).wait_send()
    rest_end()


def final_stage(first_rows, dpre, pack, inputs, scale, gain, dmid, small, rest, members, collective):
    tokens, width = inputs.shape
    columns = dmid.shape[1]
    chunk = 256
    steps = tokens // chunk
    stages = (members - 1).bit_length()
    rows = width // members
    wide = dpre.shape[1]
    whole = pl.BlockSpec(memory_space=pltpu.VMEM)
    return pl.pallas_call(
        functools.partial(final_kernel, members, chunk),
        name="final",
        out_shape=(
            jax.ShapeDtypeStruct((tokens, columns), F32),
            jax.ShapeDtypeStruct((rows, wide), F32),
            jax.ShapeDtypeStruct(small.shape, F32),
            jax.ShapeDtypeStruct((rest.shape[0], *rest.shape[2:]), F32),
        ),
        in_specs=[whole] * 9,
        out_specs=(whole,) * 4,
        scratch_shapes=[
            pltpu.VMEM((members, rows, wide), F32),
            pltpu.VMEM((members, rows, wide), BF),
            pltpu.VMEM((members - 1, rows, wide), BF),
            pltpu.VMEM((tokens, width), BF),
        ]
        + head_scatter_scratch(tokens, columns, steps)
        + [
            pltpu.VMEM((tokens // 128, 1, 128), F32),
            pltpu.VMEM((3, tokens // 128, 1, 128), F32),
            pltpu.VMEM((5 + 2 * stages, *small.shape), F32),
            pltpu.SemaphoreType.DMA((members,)),
            pltpu.SemaphoreType.DMA((members - 1,)),
            pltpu.SemaphoreType.DMA((3,)),
            pltpu.SemaphoreType.DMA((3,)),
            pltpu.SemaphoreType.DMA((3 + stages,)),
            pltpu.SemaphoreType.DMA((3 + stages,)),
        ]
        + piece_scatter_scratch(rest.shape[0], members, rest.shape[2:]),
        compiler_params=pltpu.CompilerParams(
            collective_id=collective, has_side_effects=True, vmem_limit_bytes=VMEM_LIMIT
        ),
        cost_estimate=pl.CostEstimate(flops=8 * 10**9, bytes_accessed=30 << 20, transcendentals=0),
    )(first_rows, dpre, pack, inputs, scale, gain, dmid, small, rest)
def turn_column(column):
    diagonal = lax.broadcasted_iota(jnp.int32, (128, 128), 0) == lax.broadcasted_iota(jnp.int32, (128, 128), 1)
    lines = []
    for block in range(column.shape[0] // 128):
        lines.append(jnp.sum(jnp.where(diagonal, column[block * 128 : (block + 1) * 128], 0.0), 0, keepdims=True))
    return jnp.concatenate(lines, 1)


def piece_gather(full_ref, send, recv, members):
    member = lax.axis_index("seq")
    parts = full_ref.shape[0]
    stages = (members - 1).bit_length()

    def give(part, r, stage):
        owner = flip(member, r)
        mark = r ^ (1 << stage)
        return push(
            full_ref.at[part, owner],
            full_ref.at[part, owner],
            send.at[part, mark],
            recv.at[part, mark],
            "seq",
            flip(member, 1 << stage),
        )

    def take(part, r):
        owner = flip(member, r)
        return push(
            full_ref.at[part, owner],
            full_ref.at[part, owner],
            send.at[part, r],
            recv.at[part, r],
            "seq",
            flip(member, r & -r),
        )

    def begin(part=0, levels=None):
        for stage in reversed(range(stages)) if levels is None else levels:
            give(part, 0, stage).start()

    def relay(part, r):
        take(part, r).wait_recv()
        for stage in reversed(range(zeros_below(r))):
            give(part, r, stage).start()
        if r == 1 << (stages - 1) and part + 1 < parts:
            begin(part + 1)

    order = sorted([r for r in range(1, members) if r % 2 == 0], key=lambda r: (-zeros_below(r), r))
    def when(part, r):
        return 2 * part + 3 * (bin(r).count("1") - 1), part, -zeros_below(r), r

    relays = sorted([(part, r) for r in order for part in range(parts)], key=lambda job: when(*job))

    def arrive():
        for part in range(parts):
            for r in range(1, members, 2):
                take(part, r).wait_recv()

    def finish():
        for part in range(parts):
            for r in [0] + order:
                for stage in range(zeros_below(r) if r else stages):
                    give(part, r, stage).wait_send()

    return begin, relay, relays, arrive, finish


def greet_seq(members):
    member = lax.axis_index("seq")
    stages = (members - 1).bit_length()
    barrier = pltpu.get_barrier_semaphore()
    for stage in range(stages):
        pl.semaphore_signal(barrier, inc=1, device_id={"seq": flip(member, 1 << stage)}, device_id_type=MESH)
    return barrier, stages


def front_kernel(
    members,
    heads,
    resets_ref,
    input_ref,
    query_ref,
    key_ref,
    value_ref,
    extra_ref,
    out_weight_ref,
    own_ref,
    taps_ref,
    pack_ref,
    first_ref,
    pre_ref,
    logits_ref,
    halo_ref,
    scale_ref,
    gains_ref,
    turned_ref,
    full_ref,
    others_ref,
    qkv_ref,
    inv_ref,
    wu_ref,
    mq_ref,
    start_ref,
    out0_ref,
    total_ref,
    pad_ref,
    edge_ref,
    pack_send,
    pack_recv,
    edge_send,
    edge_recv,
    turned_send,
    turned_recv,
    full_send,
    full_recv,
    head_send,
    head_recv,
):
    tokens, width = input_ref.shape
    columns = heads * CHUNK
    member = lax.axis_index("seq")
    _, _, near, far = head_peers()
    barrier, stages = greet_seq(members)
    for target in (near, far):
        pl.semaphore_signal(barrier, inc=1, device_id={"head": target}, device_id_type=MESH)

    @pl.when(member > 0)
    def _():
        pl.semaphore_signal(barrier, inc=1, device_id={"seq": member - 1}, device_id_type=MESH)

    pack_ref[0, member, :, :columns] = query_ref[...]
    pack_ref[0, member, :, columns : 2 * columns] = key_ref[...]
    pack_ref[0, member, :, 2 * columns : 3 * columns] = value_ref[...]
    pack_ref[0, member, :, 3 * columns :] = extra_ref[...]
    turned_ref[0, member] = out_weight_ref[...]
    for part in range(full_ref.shape[0]):
        full_ref[part, member] = own_ref[part]
    pack = piece_gather(pack_ref, pack_send, pack_recv, members)
    turned = piece_gather(turned_ref, turned_send, turned_recv, members)
    full = piece_gather(full_ref, full_send, full_recv, members)
    near_copy = push(turned_ref.at[0], others_ref.at[0], head_send.at[0], head_recv.at[0], "head", near)
    far_copy = push(turned_ref.at[0], others_ref.at[1], head_send.at[1], head_recv.at[1], "head", far)
    pass_copy = push(others_ref.at[1], others_ref.at[2], head_send.at[2], head_recv.at[2], "head", near)
    pl.semaphore_wait(barrier, stages + 2 + jnp.minimum(members - 1 - member, 1))
    pack[0]()
    turned[0]()
    full[0](0, [stages - 1, 0])

    last_rows = pl.ds(tokens - 16, 16)

    def edge(target):
        return push(input_ref.at[last_rows], edge_ref, edge_send, edge_recv, "seq", target)

    @pl.when(member + 1 < members)
    def _():
        edge(member + 1).start()

    chunk = 256

    def at(index):
        return pl.ds(pl.multiple_of(index * chunk, chunk), chunk)

    def measure(index):
        block = input_ref[at(index)].astype(F32)
        scale_ref[at(index)] = lax.rsqrt(jnp.mean(block * block, axis=-1, keepdims=True) + 1e-06)

    pl.loop(0, tokens // chunk)(measure)
    for job in pack[2]:
        pack[1](*job)
    for job in turned[2]:
        turned[1](*job)
    full[0](0, range(1, stages - 1))
    pack[3]()
    projection = pack_ref[0].reshape(width, pack_ref.shape[3])
    extras = projection[:, 3 * columns :].astype(F32)
    gains_ref[0:1] = turn_column(extras[:, heads : heads + 1])
    gains_ref[1:2] = turn_column(extras[:, heads + 1 : heads + 2])

    def project(index):
        first = (input_ref[at(index)].astype(F32) * scale_ref[at(index)] * gains_ref[0:1]).astype(BF)
        first_ref[at(index)] = first
        both = nn(first, pack_ref[0].reshape(width, pack_ref.shape[3]))
        pre_ref[at(index)] = both[:, : 3 * columns].astype(BF)
        logits_ref[at(index)] = both[:, 3 * columns :]

    pl.loop(0, tokens // chunk)(project)

    @pl.when(member == 0)
    def _():
        halo_ref[...] = jnp.zeros_like(halo_ref)

    @pl.when(member > 0)
    def _():
        edge(member).wait_recv()
        block = edge_ref[...].astype(F32)
        scale = lax.rsqrt(jnp.mean(block * block, axis=-1, keepdims=True) + 1e-06)
        first = (block * scale * gains_ref[0:1]).astype(BF)
        halo_ref[...] = nn(first, pack_ref[0].reshape(width, pack_ref.shape[3])[:, : 3 * columns]).astype(BF)

    turned[3]()
    near_copy.start()
    far_copy.start()
    rows, cols = grid_indices()
    eye = jnp.where(rows == cols, 1.0, 0.0)
    top = lax.broadcasted_iota(jnp.int32, (CHUNK, 1), 0) < GROUP
    for head in range(heads):
        total_ref[head] = side(eye, jnp.zeros_like(eye))
    batch = pad_ref.shape[0]

    def one(step, carry):
        units = []
        for lane in range(batch):
            chunk = step * batch + lane
            pad = pad_ref.at[lane]
            load_padded(pad, pre_ref, halo_ref, chunk, resets_ref)
            mixed = convolve(pad, taps_ref)
            silued = mixed * sigmoid(mixed)
            keep0 = 1.0 - resets_ref[2 * chunk]
            keep1 = 1.0 - resets_ref[2 * chunk + 1]
            both = keep0 * keep1
            enter = jnp.where(top, keep0, both)
            leave = jnp.where(top, keep1, 1.0)
            at = pl.ds(pl.multiple_of(chunk * CHUNK, CHUNK), CHUNK)
            beta_rows = sigmoid(logits_ref[at, :])
            for head in range(heads):
                window = slice(head * CHUNK, (head + 1) * CHUNK)
                parts = []
                for kind in range(3):
                    part = silued[:, kind * columns + head * CHUNK : kind * columns + (head + 1) * CHUNK]
                    if kind < 2:
                        part = part * lax.rsqrt(jnp.sum(part * part, axis=-1, keepdims=True) + 1e-06)
                    part = part.astype(BF)
                    qkv_ref[at, kind * columns + head * CHUNK : kind * columns + (head + 1) * CHUNK] = part
                    parts.append(part)
                units.append((chunk, head, *parts, beta_rows[:, head : head + 1], keep1, both, enter, leave))
        turned = [u[3].T for u in units]
        strict = [
            jnp.where(rows > cols, u[5] * nn(u[3], t), 0.0) for u, t in zip(units, turned)
        ]
        inverses = [r.astype(BF) for r in inverse_levels(strict, rows, cols, [u[6] for u in units])]
        factors = []
        for u, inverse in zip(units, inverses):
            beta = u[5]
            factors.append(nn(inverse, side(u[3].astype(F32) * beta, u[4].astype(F32) * beta)))
        for u, inverse, factor, t in zip(units, inverses, factors, turned):
            chunk, head, query, key, value, beta, keep1, both, enter, leave = u
            weight, update = factor[:, :CHUNK], factor[:, CHUNK:]
            entering_weight = weight * enter
            inv_ref[chunk, head] = inverse
            wu_ref[chunk, head] = side(entering_weight, update).astype(BF)
            gathered = nn(t, side(weight, update * leave))
            device_map = (both * (eye - gathered[:, :CHUNK])).astype(BF)
            shift = gathered[:, CHUNK:]
            scores = jnp.where(rows >= cols, nn(query, t), 0.0)
            scores = jnp.where((rows >= GROUP) & (cols < GROUP), scores * keep1, scores)
            seen = nn(scores, side(entering_weight, update))
            effective = query.astype(F32) * enter - seen[:, :CHUNK]
            mq_ref[chunk, head] = stack(device_map, effective.astype(BF))
            out0_ref[chunk, head] = seen[:, CHUNK:]
            running = total_ref[head]
            start_ref[chunk, head] = running.astype(BF)
            total_ref[head] = nn(device_map, running) + side(jnp.zeros_like(shift), shift)
        return carry

    count = resets_ref.shape[0] // 2 // batch
    relays = full[2]

    def pumped(step, carry):
        carry = one(step, carry)
        for turn in range(count):
            jobs = [job for place, job in enumerate(relays) if place * count // len(relays) == turn]
            if not jobs and turn != count // 2:
                continue

            @pl.when(step == turn)
            def _():
                for job in jobs:
                    full[1](*job)
                if turn == count // 2:
                    far_copy.wait_recv()
                    pass_copy.start()

        return carry

    lax.fori_loop(0, count, pumped, 0)
    near_copy.wait()
    far_copy.wait_send()
    pass_copy.wait()
    full[3]()

    @pl.when(member + 1 < members)
    def _():
        edge(member + 1).wait_send()

    for gather in (pack, turned, full):
        gather[4]()


def front_stage(resets, inputs, query, key, value, extra, out_weight, own, taps, members, heads, collective):
    tokens, width = inputs.shape
    columns = heads * CHUNK
    chunks = tokens // CHUNK
    whole = pl.BlockSpec(memory_space=pltpu.VMEM)
    piece = width // members

    def units(wide, kind):
        return jax.ShapeDtypeStruct((chunks, heads, *wide), kind)

    def dma(*shape):
        return [pltpu.SemaphoreType.DMA(shape)] * 2

    return pl.pallas_call(
        functools.partial(front_kernel, members, heads),
        name="front",
        out_shape=(
            jax.ShapeDtypeStruct((1, members, piece, 3 * columns + CHUNK), BF),
            jax.ShapeDtypeStruct((tokens, width), BF),
            jax.ShapeDtypeStruct((tokens, 3 * columns), BF),
            jax.ShapeDtypeStruct((tokens, CHUNK), F32),
            jax.ShapeDtypeStruct((16, 3 * columns), BF),
            jax.ShapeDtypeStruct((tokens, 1), F32),
            jax.ShapeDtypeStruct((2, width), F32),
            jax.ShapeDtypeStruct((1, members, *out_weight.shape), BF),
            jax.ShapeDtypeStruct((own.shape[0], members, *own.shape[1:]), BF),
            jax.ShapeDtypeStruct((3, members, *out_weight.shape), BF),
            jax.ShapeDtypeStruct((tokens, 3 * columns), BF),
            units((CHUNK, CHUNK), BF),
            units((CHUNK, 2 * CHUNK), BF),
            units((2 * CHUNK, CHUNK), BF),
            units((CHUNK, 2 * CHUNK), BF),
            units((CHUNK, CHUNK), F32),
            jax.ShapeDtypeStruct((heads, CHUNK, 2 * CHUNK), F32),
        ),
        in_specs=[pl.BlockSpec(memory_space=pltpu.SMEM)] + [whole] * 8,
        out_specs=(whole,) * 17,
        scratch_shapes=[pltpu.VMEM((2, 144, 3 * columns), F32), pltpu.VMEM((16, width), BF)]
        + dma(1, members)
        + dma()
        + dma(1, members)
        + dma(own.shape[0], members)
        + dma(3),
        compiler_params=pltpu.CompilerParams(
            collective_id=collective, has_side_effects=True, vmem_limit_bytes=VMEM_LIMIT
        ),
        cost_estimate=pl.CostEstimate(flops=8 * 10**9, bytes_accessed=40 << 20, transcendentals=2 << 20),
    )(resets, inputs, query, key, value, extra, out_weight, own, taps)


def lanes_whole(pieces):
    places, rows, piece = pieces.shape
    if piece >= 128:
        return pieces
    group = 128 // piece
    return pieces.reshape(places // group, group, rows, piece).transpose(0, 2, 1, 3).reshape(places // group, rows, 128)


def lanes_split(blocks, piece):
    count, rows, lanes = blocks.shape
    if piece >= 128:
        return blocks
    group = 128 // piece
    return blocks.reshape(count, rows, group, piece).transpose(0, 2, 1, 3).reshape(count * group, rows, piece)


def body(
    block_input,
    first_gain,
    query_weight,
    key_weight,
    value_weight,
    beta_weight,
    conv_weight,
    head_gain,
    output_weight,
    second_gain,
    gate_weight,
    up_weight,
    down_weight,
    lengths,
    cotangent,
):
    tokens, width = block_input.shape
    heads = beta_weight.shape[1]
    columns = query_weight.shape[1]
    hidden_columns = gate_weight.shape[1]
    members = lax.axis_size("seq")
    piece = width // members
    seq_place = lax.axis_index("seq")

    extra = jnp.concatenate(
        [beta_weight, first_gain[:, None], second_gain[:, None], jnp.zeros((piece, CHUNK - heads - 2), BF)], 1
    )
    ends = jnp.sum(jnp.where(jnp.arange(4)[:, None] >= jnp.arange(4)[None, :], lengths[None, :], 0), axis=1)
    starts = ends - lengths
    block_starts = seq_place * tokens + GROUP * jnp.arange(tokens // GROUP, dtype=jnp.int32)
    resets = jnp.any(starts[None, :] == block_starts[:, None], axis=1).astype(F32)

    taps = conv_weight.astype(F32).transpose(1, 0, 2).reshape(4, -1)
    own = jnp.stack([gate_weight.T, up_weight.T, down_weight.T])
    split = piece < 128
    (
        mixer_pack,
        first_rows,
        pre,
        logits,
        halo,
        scale_one,
        gains,
        turned,
        full,
        others,
        qkv,
        inv,
        wu,
        mq,
        start,
        out0,
        total,
    ) = front_stage(
        resets,
        block_input,
        query_weight,
        key_weight,
        value_weight,
        extra,
        output_weight.T,
        own[:1, :16] if split else own,
        taps,
        members,
        heads,
        5,
    )
    mixer_pack = mixer_pack.reshape(width, -1)
    if split:
        gathered = lax.all_gather(own, "seq", axis=1)
        full = jnp.stack([lanes_whole(gathered[i]) for i in range(3)])
    turned = lanes_whole(turned[0])
    others = jnp.stack([lanes_whole(others[i]) for i in range(3)]) if split else others
    total_low = total.astype(BF)
    (state,) = exchange(total_low, (), "seq", False, 0)
    gain_head = head_gain.astype(F32)[None, :]
    delta, head_rows, states = mixer_output(state, start, mq, out0, gain_head)

    d_heads, update_part, middle_shard, d_middle_shard, *grads, second_grad = middle_stage(
        head_rows, full, turned, others, block_input, cotangent, gains[1:2], 2
    )
    second_part = jnp.sum(second_grad, 0)
    ddelta, gain_part, shift = mixer_back_state(d_heads, delta, gain_head, mq)
    back_part = jnp.concatenate([total_low[:, :, :CHUNK].transpose(0, 2, 1), shift.astype(BF)], 2)
    if split:
        pieces = jnp.concatenate([part for pair in grads for part in pair], 1)
        whole_sum = lax.psum_scatter(lanes_split(pieces, piece), "seq", scatter_dimension=0, tiled=False).astype(F32)
        grads = [jnp.zeros((1, members, 16, 128), BF)] * 3
    arrive, block_output, third_sum = exchange(back_part, (update_part, middle_shard, grads[2]), "seq", True, 1)
    d_pre, taps_part, first_sum = mixer_backward(
        resets, pre, halo, taps, logits, qkv, inv, wu, mq, states, ddelta, arrive, grads[0], 3
    )
    small = jnp.concatenate(
        [
            jnp.zeros((1, width), F32),
            jnp.pad(jnp.sum(gain_part, 0, keepdims=True), ((0, 0), (0, width - CHUNK))),
            jnp.zeros((6, width), F32),
            jnp.sum(second_grad, 0, keepdims=True),
            jnp.sum(taps_part, 1).reshape(-1, width),
            jnp.zeros((7 - 12 * columns // width, width), F32),
        ]
    )
    input_gradient, mixer_sum, sums, second_sum = final_stage(
        first_rows, d_pre, mixer_pack, block_input, scale_one, gains[0:1], d_middle_shard, small, grads[1], members, 4
    )
    if not split:
        whole_sum = jnp.concatenate([s.reshape(-1, 128) for s in (first_sum, second_sum, third_sum)])
    gain_sum = sums[1, :CHUNK]
    conv_gradient = sums[9 : 9 + 12 * columns // width].reshape(4, 3, columns).transpose(1, 0, 2)
    row_start = seq_place * piece
    first_gradient = lax.dynamic_slice_in_dim(sums[0], row_start, piece, 0)
    second_gradient = lax.dynamic_slice_in_dim(sums[8], row_start, piece, 0)
    beta_gradient = mixer_sum[:, 3 * columns : 3 * columns + heads]
    return (
        block_output,
        input_gradient,
        first_gradient,
        mixer_sum[:, :columns],
        mixer_sum[:, columns : 2 * columns],
        mixer_sum[:, 2 * columns : 3 * columns],
        beta_gradient,
        conv_gradient,
        gain_sum,
        whole_sum[3 * hidden_columns :].T,
        second_gradient,
        whole_sum[:hidden_columns].T,
        whole_sum[hidden_columns : 2 * hidden_columns].T,
        whole_sum[2 * hidden_columns : 3 * hidden_columns].T,
    )


def solution(mesh):
    return jax.shard_map(
        body,
        mesh=mesh,
        in_specs=(
            P("seq", None),
            P("seq"),
            P("seq", "head"),
            P("seq", "head"),
            P("seq", "head"),
            P("seq", "head"),
            P(None, None, "head"),
            P(),
            P("seq", "head"),
            P("seq"),
            P("seq", "head"),
            P("seq", "head"),
            P("seq", "head"),
            P(),
            P("seq", None),
        ),
        out_specs=(
            P("seq", "head"),
            P("seq", "head"),
            P("seq"),
            P("seq", "head"),
            P("seq", "head"),
            P("seq", "head"),
            P("seq", "head"),
            P(None, None, "head"),
            P(),
            P("seq", "head"),
            P("seq"),
            P("seq", "head"),
            P("seq", "head"),
            P("seq", "head"),
        ),
        check_vma=False,
    )
```

```python
import functools

import jax
import jax.numpy as jnp
from jax import lax
from jax.experimental import pallas as pl
from jax.experimental.pallas import tpu as pltpu
from jax.sharding import PartitionSpec as P

GROUP = 64
CHUNK = 128
MESH = pl.DeviceIdType.MESH
BF = jnp.bfloat16
F32 = jnp.float32
VMEM_LIMIT = 59 << 20


def nn(left, right):
    return jnp.dot(left.astype(BF), right.astype(BF), preferred_element_type=F32)


def tn(left, right):
    return lax.dot_general(
        left.astype(BF), right.astype(BF), (((0,), (0,)), ((), ())), preferred_element_type=F32
    )


def nt(left, right):
    return lax.dot_general(
        left.astype(BF), right.astype(BF), (((1,), (1,)), ((), ())), preferred_element_type=F32
    )


def sigmoid(v):
    return 0.5 * jnp.tanh(0.5 * v) + 0.5


def side(left, right):
    return jnp.concatenate([left, right], 1)


def stack(top, bottom):
    return jnp.concatenate([top, bottom], 0)


def grid_indices():
    rows = lax.broadcasted_iota(jnp.int32, (CHUNK, CHUNK), 0)
    cols = lax.broadcasted_iota(jnp.int32, (CHUNK, CHUNK), 1)
    return rows, cols


def load_padded(pad_ref, pre_ref, halo_ref, chunk, resets_ref):
    start = pl.multiple_of(chunk * CHUNK, CHUNK)
    before = pl.multiple_of(jnp.maximum(start - 16, 0), 16)
    own = pre_ref[pl.ds(start, CHUNK), :].astype(F32)
    earlier = pre_ref[pl.ds(before, 16), :].astype(F32)[8:]
    halo = halo_ref[...].astype(F32)[8:]
    first = jnp.where(chunk == 0, halo, earlier)
    keep0 = 1.0 - resets_ref[2 * chunk]
    keep1 = 1.0 - resets_ref[2 * chunk + 1]
    pad_ref[0:8] = first * keep0
    pad_ref[8:72] = own[:GROUP]
    pad_ref[72:80] = own[GROUP - 8 : GROUP] * keep1
    pad_ref[80:144] = own[GROUP:]


def tap_rows(pad_ref, tap):
    return stack(pad_ref[5 + tap : 69 + tap], pad_ref[77 + tap : 141 + tap])


def convolve(pad_ref, taps_ref):
    mixed = None
    for tap in range(4):
        term = taps_ref[tap : tap + 1] * tap_rows(pad_ref, tap)
        mixed = term if mixed is None else mixed + term
    return mixed


def inverse_levels(strict, rows, cols, keep1):
    eye = jnp.where(rows == cols, 1.0, 0.0)
    pair = (rows // 2) == (cols // 2)
    results = [eye - jnp.where(pair, a, 0.0) for a in strict]
    width = 2
    while width < CHUNK:
        off = ((rows // (2 * width)) == (cols // (2 * width))) & ((rows // width) != (cols // width))
        lows = [r.astype(BF) for r in results]
        parts = [jnp.where(off, a, 0.0).astype(BF) for a in strict]
        if width == GROUP:
            parts = [jnp.where(off, a * k, 0.0).astype(BF) for a, k in zip(strict, keep1)]
        steps = [nn(r, p) for r, p in zip(lows, parts)]
        results = [r - nn(s, low) for r, s, low in zip(results, steps, lows)]
        width *= 2
    return results


def exchange_kernel(axis, count, window, backward, *refs):
    if backward:
        (
            part_ref, update_ref, mid_ref, grads_ref, state_ref, block_ref, total_ref, slots_ref, send_sem, recv_sem,
            near_ref, relay_ref, far_ref, *sems, piece_relay, piece_slots, piece_send, piece_recv,
        ) = refs
        begin, receive, jobs, end = piece_scatter(
            grads_ref, piece_relay, piece_slots, total_ref, piece_send, piece_recv, count
        )
        _, _, near, far = head_peers()
        chunk = 256
        steps = update_ref.shape[0] // chunk
        at, _, start_pair, pass_on, own_sum, finish = head_scatter_copies(
            chunk, update_ref, near_ref, relay_ref, far_ref, sems
        )
    else:
        part_ref, state_ref, slots_ref, send_sem, recv_sem = refs
    place = lax.axis_index(axis)
    ahead = count - 1 - place if backward else place
    behind = count - 1 - ahead
    sign = -1 if backward else 1
    barrier = pltpu.get_barrier_semaphore()
    for hop in range(1, window + 1):

        @pl.when(ahead >= hop)
        def _():
            pl.semaphore_signal(
                barrier, inc=1, device_id={axis: place - sign * hop}, device_id_type=MESH
            )

    extra = 0
    if backward:
        extra = 2 + greet_seq(count)[1]
        for target in (near, far):
            pl.semaphore_signal(barrier, inc=1, device_id={"head": target}, device_id_type=MESH)

    if extra:
        pl.semaphore_wait(barrier, jnp.minimum(behind, window) + extra)
    else:

        @pl.when(behind > 0)
        def _():
            pl.semaphore_wait(barrier, jnp.minimum(behind, window))

    def copy(hop):
        return push(
            part_ref,
            slots_ref.at[hop - 1],
            send_sem.at[hop - 1],
            recv_sem.at[hop - 1],
            axis,
            place + sign * hop,
        )

    for hop in range(1, window + 1):

        @pl.when(behind >= hop)
        def _():
            copy(hop).start()

    if backward:

        @pl.loop(0, steps)
        def _(index):
            start_pair(index)

        begin()

        @pl.loop(0, steps)
        def _(index):
            pass_on(index)

        for job in jobs[: len(jobs) // 2]:
            receive(*job)

    heads = state_ref.shape[0]
    state_ref[...] = jnp.zeros_like(state_ref)
    for hop in range(window, 0, -1):

        @pl.when(ahead >= hop)
        def _():
            copy(hop).wait_recv()
            for head in range(heads):
                part = slots_ref[hop - 1, head]
                state_ref[head] = nn(part[:, :CHUNK], state_ref[head]) + part[:, CHUNK:].astype(F32)

    if backward:
        for job in jobs[len(jobs) // 2 :]:
            receive(*job)

        @pl.loop(0, steps)
        def _(index):
            block_ref[at(index)] = (mid_ref[at(index)] + own_sum(index)).astype(BF)
            finish(index)

        end()

    for hop in range(1, window + 1):

        @pl.when(behind >= hop)
        def _():
            copy(hop).wait_send()


def exchange(part, extras, axis, backward, collective):
    count = lax.axis_size(axis)
    window = min(count - 1, count // 2)
    heads = part.shape[0]
    whole = pl.BlockSpec(memory_space=pltpu.VMEM)
    out_shape = [jax.ShapeDtypeStruct((heads, CHUNK, CHUNK), F32)]
    scratch = [
        pltpu.VMEM((window, heads, CHUNK, 2 * CHUNK), BF),
        pltpu.SemaphoreType.DMA((window,)),
        pltpu.SemaphoreType.DMA((window,)),
    ]
    if backward:
        tokens, columns = extras[1].shape
        out_shape.append(jax.ShapeDtypeStruct((tokens, columns), BF))
        scratch += head_scatter_scratch(tokens, columns, tokens // 256)
        parts, _, *piece = extras[2].shape
        out_shape.append(jax.ShapeDtypeStruct((parts, *piece), F32))
        scratch += piece_scatter_scratch(parts, count, piece)
    return pl.pallas_call(
        functools.partial(exchange_kernel, axis, count, window, backward),
        name="state_backward" if backward else "state_forward",
        out_shape=out_shape,
        in_specs=[whole] * (1 + len(extras)),
        out_specs=[whole] * len(out_shape),
        scratch_shapes=scratch,
        compiler_params=pltpu.CompilerParams(
            collective_id=collective, has_side_effects=True, vmem_limit_bytes=VMEM_LIMIT
        ),
        cost_estimate=pl.CostEstimate(flops=10**9, bytes_accessed=20 << 20, transcendentals=0),
    )(part, *extras)


def mixer_back_state_kernel(heads, dheads_ref, delta_ref, gain_ref, mq_ref, ddelta_ref, gain_grad_ref, shift_ref):
    chunks = mq_ref.shape[0]
    shift_ref[...] = jnp.zeros_like(shift_ref)
    gain_grad_ref[...] = jnp.zeros_like(gain_grad_ref)

    def one(step, carry):
        chunk = chunks - 1 - step
        at = pl.ds(pl.multiple_of(chunk * CHUNK, CHUNK), CHUNK)
        for head in range(heads):
            window = slice(head * CHUNK, (head + 1) * CHUNK)
            out = delta_ref[at, window]
            grad = dheads_ref[at, window].astype(F32)
            scale = lax.rsqrt(jnp.mean(out * out, axis=-1, keepdims=True) + 1e-05)
            unit = out * scale
            gain_grad_ref[...] += jnp.sum((grad * unit).reshape(CHUNK // 8, 8, CHUNK), 0)
            scaled = grad * gain_ref[...]
            back = scale * (scaled - unit * jnp.mean(scaled * unit, axis=-1, keepdims=True))
            back = back.astype(BF)
            ddelta_ref[at, window] = back
            shift_ref[head] = tn(mq_ref[chunk, head], stack(shift_ref[head].astype(BF), back))
        return carry

    lax.fori_loop(0, chunks, one, 0)


def mixer_back_state(dheads, delta, gain, mq):
    chunks, heads = mq.shape[:2]
    tokens = chunks * CHUNK
    return pl.pallas_call(
        functools.partial(mixer_back_state_kernel, heads),
        name="mixer_back_state",
        out_shape=(
            jax.ShapeDtypeStruct((tokens, heads * CHUNK), BF),
            jax.ShapeDtypeStruct((8, CHUNK), F32),
            jax.ShapeDtypeStruct((heads, CHUNK, CHUNK), F32),
        ),
        compiler_params=pltpu.CompilerParams(vmem_limit_bytes=VMEM_LIMIT),
        cost_estimate=pl.CostEstimate(flops=3 * 10**8, bytes_accessed=10 << 20, transcendentals=1 << 14),
    )(dheads, delta, gain, mq)


def piece_scatter_scratch(parts, members, piece):
    return [
        pltpu.VMEM((parts, max(members // 2 - 1, 1), *piece), BF),
        pltpu.VMEM((parts, members - 1, *piece), BF),
        pltpu.SemaphoreType.DMA((parts, members)),
        pltpu.SemaphoreType.DMA((parts, members)),
    ]


def piece_scatter(own_ref, relay_ref, slots_ref, total_ref, send, recv, members):
    member = lax.axis_index("seq")
    parts = own_ref.shape[0]
    stages = (members - 1).bit_length()
    order = sorted(range(members), key=lambda r: zeros_below(r) if r else stages)
    levels = {r: list(range(zeros_below(r) if r else stages)) for r in order}
    events = {}
    for r in order:
        for stage in levels[r]:
            events[r, stage] = len(events)
    kept = [r for r in order if r and r % 2 == 0]

    def source(part, r):
        return own_ref.at[part, flip(member, r)] if r % 2 else relay_ref.at[part, kept.index(r)]

    def give(part, r):
        stage = zeros_below(r)
        slot = events[r ^ (1 << stage), stage]
        return push(
            source(part, r), slots_ref.at[part, slot], send.at[part, r], recv.at[part, slot], "seq", flip(member, 1 << stage)
        )

    def take(part, r, stage):
        slot = events[r, stage]
        return push(
            own_ref.at[part, flip(member, 1)], slots_ref.at[part, slot], send.at[part, 0], recv.at[part, slot], "seq", flip(member, 1 << stage)
        )

    jobs = [(part, r) for r in order if r % 2 == 0 for part in range(parts)]

    def begin():
        for part, r in jobs:
            give(part, r ^ 1).start()

    def receive(part, r):
        total = own_ref[part, flip(member, r)].astype(F32)
        for stage in levels[r]:
            take(part, r, stage).wait_recv()
            total = total + slots_ref[part, events[r, stage]].astype(F32)
        if r:
            relay_ref[part, kept.index(r)] = total.astype(BF)
            give(part, r).start()
        else:
            total_ref[part] = total

    def finish():
        for part in range(parts):
            for r in order:
                if r:
                    give(part, r).wait_send()

    return begin, receive, jobs, finish


def mixer_backward_kernel(
    heads,
    resets_ref,
    pre_ref,
    halo_ref,
    taps_ref,
    logits_ref,
    qkv_ref,
    inv_ref,
    wu_ref,
    mq_ref,
    states_ref,
    ddelta_ref,
    arrive_ref,
    grads_ref,
    dpre_ref,
    taps_grad_ref,
    total_ref,
    carry_ref,
    pad_ref,
    dpad_ref,
    tail_ref,
    lead_ref,
    edge_ref,
    send_sem,
    recv_sem,
    relay_ref,
    slots_ref,
    piece_send,
    piece_recv,
):
    member, members = lax.axis_index("seq"), lax.axis_size("seq")
    barrier, stages = greet_seq(members)
    begin, receive, order, finish = piece_scatter(
        grads_ref, relay_ref, slots_ref, total_ref, piece_send, piece_recv, members
    )

    @pl.when(member + 1 < members)
    def _():
        pl.semaphore_signal(barrier, inc=1, device_id={"seq": member + 1}, device_id_type=MESH)

    columns = heads * CHUNK
    chunks = mq_ref.shape[0]
    rows, cols = grid_indices()
    top = lax.broadcasted_iota(jnp.int32, (CHUNK, 1), 0) < GROUP
    pl.semaphore_wait(barrier, stages + jnp.minimum(member, 1))
    begin()
    carry_ref[...] = arrive_ref[...]
    taps_grad_ref[...] = jnp.zeros_like(taps_grad_ref)
    dpad_ref[136:144] = jnp.zeros_like(dpad_ref[136:144])

    def one(step, carry):
        chunk = chunks - 1 - step
        at = pl.ds(pl.multiple_of(chunk * CHUNK, CHUNK), CHUNK)
        keep0 = 1.0 - resets_ref[2 * chunk]
        keep1 = 1.0 - resets_ref[2 * chunk + 1]
        both = keep0 * keep1
        enter = jnp.where(top, keep0, both)
        leave = jnp.where(top, keep1, 1.0)
        load_padded(pad_ref, pre_ref, halo_ref, chunk, resets_ref)
        mixed = convolve(pad_ref, taps_ref)
        gate = sigmoid(mixed)
        slope = gate * (1.0 + mixed * (1.0 - gate))
        silued = mixed * gate
        beta_rows = sigmoid(logits_ref[at, :])
        grads = [[None] * heads for _ in range(3)]
        dlogits = []
        cross = (rows >= GROUP) & (cols < GROUP)

        def part(kind, head):
            return slice(kind * columns + head * CHUNK, kind * columns + (head + 1) * CHUNK)

        def masked(product, keep):
            lower = jnp.where(keep, product, 0.0)
            return jnp.where(cross, lower * keep1, lower).astype(BF)

        every = range(heads)
        query = [qkv_ref[at, part(0, h)] for h in every]
        key = [qkv_ref[at, part(1, h)] for h in every]
        value = [qkv_ref[at, part(2, h)] for h in every]
        key32 = [k.astype(F32) for k in key]
        beta = [beta_rows[:, h : h + 1] for h in every]
        inverse = [inv_ref[chunk, h] for h in every]
        weight = [wu_ref[chunk, h, :, :CHUNK] for h in every]
        factors = [wu_ref[chunk, h] for h in every]
        update = [wu_ref[chunk, h, :, CHUNK:] for h in every]
        state = [states_ref[chunk, h] for h in every]
        out_grad = [ddelta_ref[at, h * CHUNK : (h + 1) * CHUNK] for h in every]
        later = [carry_ref[h].astype(BF) for h in every]
        carried = [tn(mq_ref[chunk, h], stack(later[h], out_grad[h])) for h in every]
        scores = [masked(nt(query[h], key[h]), rows >= cols) for h in every]
        fresh = [(update[h].astype(F32) - nn(weight[h], state[h])).astype(BF) for h in every]
        fresh_low = [(tn(scores[h], out_grad[h]) + leave * nn(key[h], later[h])).astype(BF) for h in every]
        score_grad = [masked(nt(out_grad[h], fresh[h]), rows >= cols) for h in every]
        through = [nt(stack(out_grad[h], fresh_low[h]), state[h]) for h in every]
        weight_grad = [(-enter * through[h][CHUNK:]).astype(BF) for h in every]
        back = [tn(inverse[h], side(weight_grad[h], fresh_low[h])) for h in every]
        query_grad = [enter * through[h][:CHUNK] + nn(score_grad[h], key[h]) for h in every]
        key_grad = [tn(score_grad[h], query[h]) + leave * nt(fresh[h], later[h]) for h in every]
        strict = [masked(-nt(back[h].astype(BF), factors[h]), rows > cols) for h in every]
        strict_key = [nn(strict[h], key[h]) for h in every]
        turned = [tn(strict[h], (beta[h] * key32[h]).astype(BF)) for h in every]
        for h in every:
            carry_ref[h] = carried[h]
            yk, zv = back[h][:, :CHUNK], back[h][:, CHUNK:]
            both_key = yk + strict_key[h]
            key_grad[h] = key_grad[h] + beta[h] * both_key + turned[h]
            grads[2][h] = beta[h] * zv
            beta_grad = jnp.sum(both_key * key32[h] + zv * value[h].astype(F32), axis=-1, keepdims=True)
            dlogits.append(beta_grad * beta[h] * (1.0 - beta[h]))
        for kind, grad in ((0, query_grad), (1, key_grad)):
            raw = [silued[:, part(kind, h)] for h in every]
            norm = [lax.rsqrt(jnp.sum(raw[h] * raw[h], axis=-1, keepdims=True) + 1e-06) for h in every]
            unit = [raw[h] * norm[h] for h in every]
            inner = [jnp.sum(unit[h] * grad[h], axis=-1, keepdims=True) for h in every]
            grads[kind] = [(grad[h] - unit[h] * inner[h]) * norm[h] for h in every]
        lanes = lax.broadcasted_iota(jnp.int32, (CHUNK, CHUNK), 1)
        spread = jnp.zeros((CHUNK, CHUNK), F32)
        for head in range(heads):
            spread = jnp.where(lanes == head, dlogits[head], spread)
        dpre_ref[at, 3 * columns :] = spread.astype(BF)
        dmixed = jnp.concatenate([g for kind in grads for g in kind], 1) * slope
        dpad_ref[0:GROUP] = dmixed[:GROUP]
        dpad_ref[GROUP : GROUP + 8] = dmixed[GROUP : GROUP + 8] * keep1
        dpad_ref[72 : 72 + GROUP] = dmixed[GROUP:]
        dpre = None
        for tap in range(4):
            back = 3 - tap
            shifted = stack(dpad_ref[back : back + GROUP], dpad_ref[72 + back : 72 + back + GROUP])
            term = taps_ref[tap : tap + 1] * shifted
            dpre = term if dpre is None else dpre + term
            seen = (dmixed * tap_rows(pad_ref, tap)).reshape(CHUNK // 8, 8, 3 * columns)
            taps_grad_ref[tap] += jnp.sum(seen, 0)
        dpre_ref[at, : 3 * columns] = dpre.astype(BF)

        @pl.when(step == 0)
        def _():
            tail_ref[...] = dpre[CHUNK - 16 :]

        dpad_ref[136:144] = dmixed[:8] * keep0
        for place, job in enumerate(order):

            @pl.when(step == (place + 1) * (chunks - 1) // len(order))
            def _():
                receive(*job)

        return carry

    lax.fori_loop(0, chunks, one, 0)
    index = lax.broadcasted_iota(jnp.int32, (8, 1), 0)
    lead = jnp.zeros((8, 3 * columns), F32)
    dpad_ref[0:128] = jnp.zeros_like(dpad_ref[0:128])
    dpad_ref[8:16] = dpad_ref[136:144]
    for tap in range(3):
        back = 3 - tap
        lead = lead + taps_ref[tap : tap + 1] * dpad_ref[back : back + 8]
    lead_ref[...] = lead

    def to_previous(target):
        return push(lead_ref, edge_ref, send_sem, recv_sem, "seq", target)

    @pl.when(member > 0)
    def _():
        to_previous(member - 1).start()

    @pl.when(member + 1 < members)
    def _():
        to_previous(member).wait_recv()
        last = pl.ds(dpre_ref.shape[0] - 16, 16)
        late = stack(tail_ref[0:8], tail_ref[8:16] + edge_ref[...])
        dpre_ref[last, : 3 * columns] = late.astype(BF)

    @pl.when(member > 0)
    def _():
        to_previous(member - 1).wait_send()

    finish()


def mixer_backward(resets, pre, halo, taps, logits, qkv, inv, wu, mq, states, ddelta, arrive, grads, collective):
    chunks, heads = mq.shape[:2]
    tokens = chunks * CHUNK
    columns = heads * CHUNK
    parts, members = grads.shape[:2]
    piece = grads.shape[2:]
    return pl.pallas_call(
        functools.partial(mixer_backward_kernel, heads),
        name="mixer_backward",
        out_shape=(
            jax.ShapeDtypeStruct((tokens, 3 * columns + CHUNK), BF),
            jax.ShapeDtypeStruct((4, 8, 3 * columns), F32),
            jax.ShapeDtypeStruct((parts, *piece), F32),
        ),
        in_specs=[pl.BlockSpec(memory_space=pltpu.SMEM)] + [pl.BlockSpec(memory_space=pltpu.VMEM)] * 12,
        out_specs=tuple([pl.BlockSpec(memory_space=pltpu.VMEM)] * 3),
        scratch_shapes=[
            pltpu.VMEM((heads, CHUNK, CHUNK), F32),
            pltpu.VMEM((144, 3 * columns), F32),
            pltpu.VMEM((144, 3 * columns), F32),
            pltpu.VMEM((16, 3 * columns), F32),
            pltpu.VMEM((8, 3 * columns), F32),
            pltpu.VMEM((8, 3 * columns), F32),
            pltpu.SemaphoreType.DMA,
            pltpu.SemaphoreType.DMA,
        ]
        + piece_scatter_scratch(parts, members, piece),
        compiler_params=pltpu.CompilerParams(
            collective_id=collective, has_side_effects=True, vmem_limit_bytes=VMEM_LIMIT
        ),
        cost_estimate=pl.CostEstimate(flops=3 * 10**9, bytes_accessed=20 << 20, transcendentals=2 << 20),
    )(resets, pre, halo, taps, logits, qkv, inv, wu, mq, states, ddelta, arrive, grads)


def head_peers():
    place = lax.axis_index("head")
    low = lax.rem(place, 2)
    high = lax.rem(lax.div(place, 2), 2)
    return place, low, place + 1 - 2 * low, place + 2 - 4 * high


def push(src, dst, send_sem, recv_sem, axis, target):
    return pltpu.make_async_remote_copy(
        src_ref=src,
        dst_ref=dst,
        send_sem=send_sem,
        recv_sem=recv_sem,
        device_id={axis: target},
        device_id_type=MESH,
    )


def greet(axis, targets):
    barrier = pltpu.get_barrier_semaphore()
    for target in targets:
        pl.semaphore_signal(barrier, inc=1, device_id={axis: target}, device_id_type=MESH)
    pl.semaphore_wait(barrier, len(targets))


def middle_kernel(
    steps,
    rows_ref,
    late_rows_ref,
    far_rows_ref,
    full_hbm,
    turned_hbm,
    others_hbm,
    input_ref,
    ct_ref,
    late_ct_ref,
    gain_ref,
    dheads_ref,
    update_ref,
    mid_ref,
    dmid_ref,
    first_grads_ref,
    second_grads_ref,
    third_grads_ref,
    gain_grad_ref,
    gate_ref,
    up_ref,
    down_ref,
    turned_ref,
    others_ref,
    load_sem,
    acc_ref,
    part_ref,
    pair_ref,
    far_ref,
    sum_ref,
    keep_ref,
    scale_ref,
    shard_ref,
    pair_send,
    pair_recv,
    far_send,
    far_recv,
    last_send,
    last_recv,
):
    step = pl.program_id(0)
    place, low, near, far = head_peers()
    chunk, width = input_ref.shape
    columns = rows_ref.shape[1]
    hidden = gate_ref.shape[0]
    half = width // 2
    mine = pl.ds(pl.multiple_of(low * half, 128), half)
    theirs = pl.ds(pl.multiple_of((1 - low) * half, 128), half)
    own_columns = pl.ds(pl.multiple_of(place * columns, 128), columns)

    def pair(index):
        return push(
            part_ref.at[lax.rem(index, 2), :, theirs], pair_ref.at[index], pair_send.at[index], pair_recv.at[index], "head", near
        )

    def across(index):
        return push(pair_ref.at[index], far_ref.at[index], far_send.at[index], far_recv.at[index], "head", far)

    def last(index):
        return push(
            sum_ref.at[index, :, mine], sum_ref.at[index, :, mine], last_send.at[index], last_recv.at[index], "head", near
        )

    def loads():
        targets = [
            (full_hbm.at[0], gate_ref),
            (full_hbm.at[1], up_ref),
            (full_hbm.at[2], down_ref),
            (turned_hbm, turned_ref),
        ] + [(others_hbm.at[other], others_ref.at[other]) for other in range(3)]
        for number, (source, target) in enumerate(targets):
            for piece in range(width // 128):
                yield pltpu.make_async_copy(
                    source.at[piece], target.at[:, piece * 128 : (piece + 1) * 128], load_sem.at[number, piece]
                )

    @pl.when(step == 0)
    def _():
        for load in loads():
            load.start()
        greet("head", (near, far))

        acc_ref[...] = jnp.zeros_like(acc_ref)
        gain_grad_ref[...] = jnp.zeros_like(gain_grad_ref)
        for load in loads():
            load.wait()

    @pl.when(step < steps)
    def _():
        ct = ct_ref[...]
        d_hidden = nt(ct, down_ref[...])

        branch = nn(rows_ref[...], turned_ref[...])
        for other in range(3):
            branch = branch + nn(far_rows_ref[other], others_ref[other])
        middle = input_ref[...].astype(F32) + branch
        keep_ref[lax.rem(step, 4)] = middle
        mid_ref[...] = keep_ref[lax.rem(step, 4), :, own_columns]
        scale = lax.rsqrt(jnp.mean(middle * middle, axis=-1, keepdims=True) + 1e-06)
        scale_ref[lax.rem(step, 4)] = scale
        second = (middle * scale * gain_ref[...]).astype(BF)
        gate, up = nt(second, gate_ref[...]), nt(second, up_ref[...])
        sig = sigmoid(gate)
        silu = gate * sig
        active = (silu * up).astype(BF)
        d_gate = (d_hidden * up * (sig + silu * (1.0 - sig))).astype(BF)
        d_up = (d_hidden * silu).astype(BF)

        @pl.when(step >= 2)
        def _():
            pair(step - 2).wait_send()

        part_ref[lax.rem(step, 2)] = (nn(d_gate, gate_ref[...]) + nn(d_up, up_ref[...])).astype(BF)
        pair(step).start()

        update_ref[...] = nn(active, down_ref[...]).astype(BF)
        acc_ref[:hidden] += tn(d_gate, second)
        acc_ref[hidden : 2 * hidden] += tn(d_up, second)
        acc_ref[2 * hidden : 3 * hidden] += tn(active, ct)

    @pl.when(step < steps)
    def _():
        pair(step).wait_recv()
        both = part_ref[lax.rem(step, 2), :, mine].astype(F32) + pair_ref[step].astype(F32)
        pair_ref[step] = both.astype(BF)
        across(step).start()

    @pl.when((step > 1) & (step < steps + 2))
    def _():
        done = step - 2
        across(done).wait_recv()
        across(done).wait_send()
        total = pair_ref[done].astype(F32) + far_ref[done].astype(F32)
        sum_ref[done, :, mine] = total.astype(BF)
        last(done).start()

    @pl.when(step > 2)
    def _():
        done = step - 3
        last(done).wait_recv()
        grad = sum_ref[done].astype(F32)
        middle = keep_ref[lax.rem(done, 4)]
        scale = scale_ref[lax.rem(done, 4)]
        unit = middle * scale
        gain_grad_ref[...] += jnp.sum((grad * unit).reshape(chunk // 8, 8, width), 0)
        scaled = grad * gain_ref[...]
        d_middle = late_ct_ref[...].astype(F32) + scale * (
            scaled - unit * jnp.mean(scaled * unit, axis=-1, keepdims=True)
        )
        shard_ref[...] = d_middle
        dmid_ref[...] = shard_ref[:, own_columns]
        d_branch = d_middle.astype(BF)
        dheads_ref[...] = nt(d_branch, turned_ref[...]).astype(BF)
        acc_ref[3 * hidden :] += tn(late_rows_ref[...], d_branch)

    @pl.when(step == steps + 2)
    def _():
        for piece in range(width // 128):
            lanes = slice(piece * 128, (piece + 1) * 128)
            begin = 0
            for grads_ref in (first_grads_ref, second_grads_ref, third_grads_ref):
                rows = grads_ref.shape[2]
                for part in range(2):
                    grads_ref[part, piece] = acc_ref[begin : begin + rows, lanes].astype(BF)
                    begin += rows

        @pl.loop(0, steps)
        def _(index):
            last(index).wait_send()

        for index in range(max(steps - 2, 0), steps):
            pair(index).wait_send()


def middle_stage(head_rows, far_rows, full, turned, others, inputs, cotangent, gain, collective):
    tokens, width = inputs.shape
    columns = head_rows.shape[1]
    chunk = min(256, tokens // 2)
    steps = tokens // chunk
    whole = pl.BlockSpec(memory_space=pltpu.VMEM)
    outside = pl.BlockSpec(memory_space=pl.ANY)
    hidden = full.shape[2]
    units = (3 * hidden + columns) // 32
    shares = [16 * (units * 36 // 74), 0, 16 * (units * 25 // 74)]
    shares[1] = 16 * units - sum(shares)

    def early(wide):
        return pl.BlockSpec((chunk, wide), lambda s: (jnp.minimum(s, steps - 1), 0))

    def late(wide):
        return pl.BlockSpec((chunk, wide), lambda s: (jnp.maximum(s - 3, 0), 0))

    far = pl.BlockSpec((3, chunk, columns), lambda s: (0, jnp.minimum(s, steps - 1), 0))
    dma = pltpu.SemaphoreType.DMA((steps,))
    return pl.pallas_call(
        functools.partial(middle_kernel, steps),
        name="middle",
        grid=(steps + 3,),
        out_shape=(
            jax.ShapeDtypeStruct((tokens, columns), BF),
            jax.ShapeDtypeStruct((tokens, width), BF),
            jax.ShapeDtypeStruct((tokens, columns), F32),
            jax.ShapeDtypeStruct((tokens, columns), F32),
            *(jax.ShapeDtypeStruct((2, width // 128, rows, 128), BF) for rows in shares),
            jax.ShapeDtypeStruct((8, width), F32),
        ),
        in_specs=[early(columns), late(columns), far] + [outside] * 3 + [early(width), early(width), late(width), whole],
        out_specs=(late(columns), early(width), early(columns), late(columns), whole, whole, whole, whole),
        scratch_shapes=[
            pltpu.VMEM((hidden, width), BF),
            pltpu.VMEM((hidden, width), BF),
            pltpu.VMEM((hidden, width), BF),
            pltpu.VMEM((columns, width), BF),
            pltpu.VMEM((3, columns, width), BF),
            pltpu.SemaphoreType.DMA((7, width // 128)),
            pltpu.VMEM((3 * hidden + columns, width), F32),
            pltpu.VMEM((2, chunk, width), BF),
            pltpu.VMEM((steps, chunk, width // 2), BF),
            pltpu.VMEM((steps, chunk, width // 2), BF),
            pltpu.VMEM((steps, chunk, width), BF),
            pltpu.VMEM((4, chunk, width), F32),
            pltpu.VMEM((4, chunk, 1), F32),
            pltpu.VMEM((chunk, width), F32),
        ]
        + [dma] * 6,
        compiler_params=pltpu.CompilerParams(
            collective_id=collective,
            has_side_effects=True,
            vmem_limit_bytes=VMEM_LIMIT,
            dimension_semantics=("arbitrary",),
        ),
        cost_estimate=pl.CostEstimate(flops=30 * 10**9, bytes_accessed=30 << 20, transcendentals=2 << 20),
    )(head_rows, head_rows, far_rows, full, turned, others, inputs, cotangent, cotangent, gain)


def zeros_below(value):
    return (value & -value).bit_length() - 1


def flip(place, mask):
    bit = 1
    while bit <= mask:
        if mask & bit:
            place = place + bit - 2 * bit * lax.rem(lax.div(place, bit), 2)
        bit *= 2
    return place


def head_scatter_copies(chunk, part_ref, near_ref, send_ref, far_ref, sems):
    place, low, near, far = head_peers()
    high = lax.rem(lax.div(place, 2), 2)
    columns = far_ref.shape[-1]
    near_send, near_recv, far_send, far_recv = sems

    def at(index):
        return pl.ds(pl.multiple_of(index * chunk, chunk), chunk)

    def cols(owner):
        return pl.ds(pl.multiple_of(owner * columns, 128), columns)

    def pair(index, side_):
        return push(
            part_ref.at[at(index), cols(2 * side_ + 1 - low)],
            near_ref.at[side_, at(index)],
            near_send.at[side_, index],
            near_recv.at[side_, index],
            "head",
            near,
        )

    def across(index):
        return push(send_ref.at[at(index)], far_ref.at[at(index)], far_send.at[index], far_recv.at[index], "head", far)

    def start_pair(index):
        pair(index, 0).start()
        pair(index, 1).start()

    def pass_on(index):
        pair(index, 0).wait_recv()
        pair(index, 1).wait_recv()
        total = part_ref[at(index), cols(2 * (1 - high) + low)].astype(F32) + near_ref[1 - high, at(index)].astype(F32)
        send_ref[at(index)] = total.astype(BF)
        across(index).start()

    def own_sum(index):
        across(index).wait_recv()
        near_part = part_ref[at(index), cols(place)].astype(F32) + near_ref[high, at(index)].astype(F32)
        return near_part + far_ref[at(index)].astype(F32)

    def finish(index):
        pair(index, 0).wait_send()
        pair(index, 1).wait_send()
        across(index).wait_send()

    return at, cols, start_pair, pass_on, own_sum, finish


def head_scatter_scratch(tokens, columns, steps):
    return [
        pltpu.VMEM((2, tokens, columns), BF),
        pltpu.VMEM((tokens, columns), BF),
        pltpu.VMEM((tokens, columns), BF),
        pltpu.SemaphoreType.DMA((2, steps)),
        pltpu.SemaphoreType.DMA((2, steps)),
        pltpu.SemaphoreType.DMA((steps,)),
        pltpu.SemaphoreType.DMA((steps,)),
    ]


def final_kernel(
    members,
    chunk,
    rows_ref,
    dpre_ref,
    pack_ref,
    input_ref,
    scale_ref,
    gain_ref,
    dmid_ref,
    small_ref,
    rest_ref,
    ingrad_ref,
    piece_ref,
    sums_ref,
    total_ref,
    acc_ref,
    out_ref,
    slots_ref,
    part_ref,
    near_ref,
    send_ref,
    far_ref,
    near_send,
    near_recv,
    far_send,
    far_recv,
    stat_ref,
    stat_slots,
    small_slots,
    piece_send,
    piece_recv,
    stat_send,
    stat_recv,
    small_send,
    small_recv,
    rest_relay,
    rest_slots,
    rest_send,
    rest_recv,
):
    tokens, width = input_ref.shape
    steps = tokens // chunk
    place, low, near, far = head_peers()
    member = lax.axis_index("seq")
    rows = width // members
    stages = (members - 1).bit_length()
    at, cols, start_pair, pass_on, own_sum, finish = head_scatter_copies(
        chunk, part_ref, near_ref, send_ref, far_ref, (near_send, near_recv, far_send, far_recv)
    )

    barrier = pltpu.get_barrier_semaphore()
    opposite = near + far - place
    for target in (near, far, opposite):
        pl.semaphore_signal(barrier, inc=1, device_id={"head": target}, device_id_type=MESH)
    for stage in range(stages):
        pl.semaphore_signal(barrier, inc=1, device_id={"seq": flip(member, 1 << stage)}, device_id_type=MESH)
    begin, rest_receive, rest_jobs, rest_end = piece_scatter(
        rest_ref, rest_relay, rest_slots, total_ref, rest_send, rest_recv, members
    )
    pl.semaphore_wait(barrier, 3 + stages)
    order = sorted(range(members), key=lambda r: zeros_below(r) if r else stages)
    sent = [r for r in order if r]
    events = {}
    for r in order:
        for stage in range(zeros_below(r) if r else stages):
            events[stage, r] = len(events)

    def give(r):
        stage = zeros_below(r)
        slot = events[stage, r ^ (1 << stage)]
        return push(
            out_ref.at[r],
            slots_ref.at[slot],
            piece_send.at[r],
            piece_recv.at[slot],
            "seq",
            flip(member, 1 << stage),
        )

    def take(stage, r):
        slot = events[stage, r]
        return push(
            out_ref.at[0], slots_ref.at[slot], piece_send.at[0], piece_recv.at[slot], "seq", flip(member, 1 << stage)
        )

    def send_piece(r):
        out_ref[r] = acc_ref[flip(member, r)].astype(BF)
        give(r).start()

    def receive(r):
        index = flip(member, r)
        for stage in range(zeros_below(r) if r else stages):
            take(stage, r).wait_recv()
            acc_ref[index] += slots_ref[events[stage, r]].astype(F32)
        if r:
            send_piece(r)

    first = sorted([r for r in range(members) if r % 2], key=lambda r: order.index(r ^ 1))
    evens = [r for r in order if r % 2 == 0]
    if rows % 128 == 0:
        for r in first:
            even = 2 * lax.div(flip(member, r), 2)
            columns = pl.ds(pl.multiple_of(even * rows, 128), 2 * rows)
            block = tn(rows_ref[:, columns], dpre_ref[...])
            acc_ref[even] = block[:rows]
            acc_ref[even + 1] = block[rows:]
            send_piece(r)
        begin()
    else:
        per = 128 // rows
        for unit in range(width // 128):
            block = tn(rows_ref[:, unit * 128 : (unit + 1) * 128], dpre_ref[...])
            acc_ref[unit * per : (unit + 1) * per] = block.reshape(per, rows, block.shape[1])
        for r in first:
            send_piece(r)
        begin()

    small_slots[0] = small_ref[...]
    diagonal = lax.broadcasted_iota(jnp.int32, (128, 128), 0) == lax.broadcasted_iota(jnp.int32, (128, 128), 1)

    def project(index):
        part = nt(dpre_ref[at(index)], pack_ref[...])
        part_ref[at(index)] = part.astype(BF)
        start_pair(index)
        seen = part * (input_ref[at(index)].astype(F32) * scale_ref[at(index)])
        small_slots[0, 0:1] += jnp.sum(seen, 0, keepdims=True)
        stat = jnp.sum(seen * gain_ref[...], axis=-1, keepdims=True)
        for block in range(chunk // 128):
            line = jnp.where(diagonal, stat[block * 128 : (block + 1) * 128], 0.0)
            stat_ref[index * (chunk // 128) + block] = jnp.sum(line, 0, keepdims=True)

    early = steps // 2
    receives = list(evens)
    for half in range(2):

        @pl.loop(half * early, (half + 1) * early)
        def _(index):
            project(index)

            @pl.when(lax.rem(index, 2) == 1)
            def _():
                pass_on(lax.div(index, 2))

        if len(receives) > 1:
            receive(receives.pop(0))

    def stat_copy(turn):
        target = (near, far, opposite)[turn]
        return push(stat_ref, stat_slots.at[turn], stat_send.at[turn], stat_recv.at[turn], "head", target)

    def head_copy(turn):
        target = (near, far, opposite)[turn]
        return push(
            small_slots.at[0, pl.ds(0, 8)],
            small_slots.at[1 + turn, pl.ds(0, 8)],
            small_send.at[turn],
            small_recv.at[turn],
            "head",
            target,
        )

    for turn in (1, 2, 0):
        head_copy(turn).start()
        stat_copy(turn).start()
    for index in range(early, steps):
        pass_on(index)
    while len(receives) > 1:
        receive(receives.pop(0))
    for turn in range(3):
        head_copy(turn).wait()
    small_slots[4] = small_slots[0]
    small_slots[4, 0:8] += small_slots[1, 0:8] + small_slots[2, 0:8] + small_slots[3, 0:8]

    bits = list(range(1, stages)) + [0]

    def seq_copy(turn):
        return push(
            small_slots.at[4 + 2 * turn],
            small_slots.at[5 + 2 * turn],
            small_send.at[3 + turn],
            small_recv.at[3 + turn],
            "seq",
            flip(member, 1 << bits[turn]),
        )

    def seq_add(turn):
        seq_copy(turn).wait()
        small_slots[6 + 2 * turn] = small_slots[4 + 2 * turn] + small_slots[5 + 2 * turn]

    seq_copy(0).start()
    for turn in range(3):
        stat_copy(turn).wait()
    stat_ref[...] += stat_slots[0] + stat_slots[1] + stat_slots[2]

    def result(index):
        grad = own_sum(index)
        scale = scale_ref[at(index)]
        unit = input_ref[at(index), cols(place)].astype(F32) * scale
        means = []
        for block in range(chunk // 128):
            line = jnp.where(diagonal, stat_ref[index * (chunk // 128) + block], 0.0)
            means.append(jnp.sum(line, axis=-1, keepdims=True))
        mean = jnp.concatenate(means, 0) * (1.0 / width)
        ingrad_ref[at(index)] = dmid_ref[at(index)] + scale * (grad * gain_ref[:, cols(place)] - unit * mean)

    rests = list(rest_jobs)
    for turn in range(stages):
        start, stop = turn * steps // stages, (turn + 1) * steps // stages
        if stop > start:

            @pl.loop(start, stop)
            def _(index):
                result(index)

        share = (len(rests) - 1) // (stages - turn)
        for job in rests[:share]:
            rest_receive(*job)
        rests = rests[share:]
        seq_add(turn)
        if turn + 1 < stages:
            seq_copy(turn + 1).start()
    receive(0)
    for job in rests:
        rest_receive(*job)
    piece_ref[...] = acc_ref[member]
    sums_ref[...] = small_slots[4 + 2 * stages]

    @pl.loop(0, steps)
    def _(index):
        finish(index)

    for r in sent:
        give(r).wait_send()
    rest_end()


def final_stage(first_rows, dpre, pack, inputs, scale, gain, dmid, small, rest, members, collective):
    tokens, width = inputs.shape
    columns = dmid.shape[1]
    chunk = 256
    steps = tokens // chunk
    stages = (members - 1).bit_length()
    rows = width // members
    wide = dpre.shape[1]
    whole = pl.BlockSpec(memory_space=pltpu.VMEM)
    return pl.pallas_call(
        functools.partial(final_kernel, members, chunk),
        name="final",
        out_shape=(
            jax.ShapeDtypeStruct((tokens, columns), F32),
            jax.ShapeDtypeStruct((rows, wide), F32),
            jax.ShapeDtypeStruct(small.shape, F32),
            jax.ShapeDtypeStruct((rest.shape[0], *rest.shape[2:]), F32),
        ),
        in_specs=[whole] * 9,
        out_specs=(whole,) * 4,
        scratch_shapes=[
            pltpu.VMEM((members, rows, wide), F32),
            pltpu.VMEM((members, rows, wide), BF),
            pltpu.VMEM((members - 1, rows, wide), BF),
            pltpu.VMEM((tokens, width), BF),
        ]
        + head_scatter_scratch(tokens, columns, steps)
        + [
            pltpu.VMEM((tokens // 128, 1, 128), F32),
            pltpu.VMEM((3, tokens // 128, 1, 128), F32),
            pltpu.VMEM((5 + 2 * stages, *small.shape), F32),
            pltpu.SemaphoreType.DMA((members,)),
            pltpu.SemaphoreType.DMA((members - 1,)),
            pltpu.SemaphoreType.DMA((3,)),
            pltpu.SemaphoreType.DMA((3,)),
            pltpu.SemaphoreType.DMA((3 + stages,)),
            pltpu.SemaphoreType.DMA((3 + stages,)),
        ]
        + piece_scatter_scratch(rest.shape[0], members, rest.shape[2:]),
        compiler_params=pltpu.CompilerParams(
            collective_id=collective, has_side_effects=True, vmem_limit_bytes=VMEM_LIMIT
        ),
        cost_estimate=pl.CostEstimate(flops=8 * 10**9, bytes_accessed=30 << 20, transcendentals=0),
    )(first_rows, dpre, pack, inputs, scale, gain, dmid, small, rest)
def turn_column(column):
    diagonal = lax.broadcasted_iota(jnp.int32, (128, 128), 0) == lax.broadcasted_iota(jnp.int32, (128, 128), 1)
    lines = []
    for block in range(column.shape[0] // 128):
        lines.append(jnp.sum(jnp.where(diagonal, column[block * 128 : (block + 1) * 128], 0.0), 0, keepdims=True))
    return jnp.concatenate(lines, 1)


def piece_gather(full_ref, send, recv, members):
    member = lax.axis_index("seq")
    parts = full_ref.shape[0]
    stages = (members - 1).bit_length()

    def give(part, r, stage):
        owner = flip(member, r)
        mark = r ^ (1 << stage)
        return push(
            full_ref.at[part, owner],
            full_ref.at[part, owner],
            send.at[part, mark],
            recv.at[part, mark],
            "seq",
            flip(member, 1 << stage),
        )

    def take(part, r):
        owner = flip(member, r)
        return push(
            full_ref.at[part, owner],
            full_ref.at[part, owner],
            send.at[part, r],
            recv.at[part, r],
            "seq",
            flip(member, r & -r),
        )

    def begin(part=0, levels=None):
        for stage in reversed(range(stages)) if levels is None else levels:
            give(part, 0, stage).start()

    def relay(part, r):
        take(part, r).wait_recv()
        for stage in reversed(range(zeros_below(r))):
            give(part, r, stage).start()
        if r == 1 << (stages - 1) and part + 1 < parts:
            begin(part + 1)

    order = sorted([r for r in range(1, members) if r % 2 == 0], key=lambda r: (-zeros_below(r), r))
    def when(part, r):
        return 2 * part + 3 * (bin(r).count("1") - 1), part, -zeros_below(r), r

    relays = sorted([(part, r) for r in order for part in range(parts)], key=lambda job: when(*job))

    def arrive():
        for part in range(parts):
            for r in range(1, members, 2):
                take(part, r).wait_recv()

    def finish():
        for part in range(parts):
            for r in [0] + order:
                for stage in range(zeros_below(r) if r else stages):
                    give(part, r, stage).wait_send()

    return begin, relay, relays, arrive, finish


def greet_seq(members):
    member = lax.axis_index("seq")
    stages = (members - 1).bit_length()
    barrier = pltpu.get_barrier_semaphore()
    for stage in range(stages):
        pl.semaphore_signal(barrier, inc=1, device_id={"seq": flip(member, 1 << stage)}, device_id_type=MESH)
    return barrier, stages


def front_kernel(
    members,
    heads,
    resets_ref,
    input_ref,
    query_ref,
    key_ref,
    value_ref,
    extra_ref,
    out_weight_ref,
    own_ref,
    taps_ref,
    head_gain_ref,
    pack_ref,
    first_ref,
    pre_ref,
    logits_ref,
    halo_ref,
    scale_ref,
    gains_ref,
    turned_ref,
    full_ref,
    others_ref,
    qkv_ref,
    inv_ref,
    wu_ref,
    mq_ref,
    total_ref,
    delta_ref,
    rows_ref,
    far_rows_ref,
    states_ref,
    start_ref,
    out0_ref,
    state_ref,
    part_ref,
    slots_ref,
    pad_ref,
    edge_ref,
    pack_send,
    pack_recv,
    edge_send,
    edge_recv,
    turned_send,
    turned_recv,
    full_send,
    full_recv,
    head_send,
    head_recv,
    state_send,
    state_recv,
    row_near_send,
    row_near_recv,
    row_far_send,
    row_far_recv,
    row_pass_send,
    row_pass_recv,
):
    tokens, width = input_ref.shape
    columns = heads * CHUNK
    member = lax.axis_index("seq")
    _, _, near, far = head_peers()
    barrier, stages = greet_seq(members)
    for target in (near, far):
        pl.semaphore_signal(barrier, inc=1, device_id={"head": target}, device_id_type=MESH)

    @pl.when(member > 0)
    def _():
        pl.semaphore_signal(barrier, inc=1, device_id={"seq": member - 1}, device_id_type=MESH)

    window = slots_ref.shape[0]
    behind = members - 1 - member
    for hop in range(1, window + 1):

        @pl.when(member >= hop)
        def _():
            pl.semaphore_signal(barrier, inc=1, device_id={"seq": member - hop}, device_id_type=MESH)

    def state_copy(hop):
        return push(
            part_ref, slots_ref.at[hop - 1], state_send.at[hop - 1], state_recv.at[hop - 1], "seq", member + hop
        )

    pack_ref[0, member, :, :columns] = query_ref[...]
    pack_ref[0, member, :, columns : 2 * columns] = key_ref[...]
    pack_ref[0, member, :, 2 * columns : 3 * columns] = value_ref[...]
    pack_ref[0, member, :, 3 * columns :] = extra_ref[...]
    turned_ref[0, member] = out_weight_ref[...]
    for part in range(full_ref.shape[0]):
        full_ref[part, member] = own_ref[part]
    pack = piece_gather(pack_ref, pack_send, pack_recv, members)
    turned = piece_gather(turned_ref, turned_send, turned_recv, members)
    full = piece_gather(full_ref, full_send, full_recv, members)
    near_copy = push(turned_ref.at[0], others_ref.at[0], head_send.at[0], head_recv.at[0], "head", near)
    far_copy = push(turned_ref.at[0], others_ref.at[1], head_send.at[1], head_recv.at[1], "head", far)
    pass_copy = push(others_ref.at[1], others_ref.at[2], head_send.at[2], head_recv.at[2], "head", near)
    pl.semaphore_wait(barrier, stages + 2 + jnp.minimum(behind, 1) + jnp.minimum(behind, window))
    pack[0]()
    turned[0]()
    full[0](0, [stages - 1, 0])

    last_rows = pl.ds(tokens - 16, 16)

    def edge(target):
        return push(input_ref.at[last_rows], edge_ref, edge_send, edge_recv, "seq", target)

    @pl.when(member + 1 < members)
    def _():
        edge(member + 1).start()

    chunk = 256

    def at(index):
        return pl.ds(pl.multiple_of(index * chunk, chunk), chunk)

    def measure(index):
        block = input_ref[at(index)].astype(F32)
        scale_ref[at(index)] = lax.rsqrt(jnp.mean(block * block, axis=-1, keepdims=True) + 1e-06)

    pl.loop(0, tokens // chunk)(measure)
    for job in pack[2]:
        pack[1](*job)
    for job in turned[2]:
        turned[1](*job)
    full[0](0, range(1, stages - 1))
    pack[3]()
    projection = pack_ref[0].reshape(width, pack_ref.shape[3])
    extras = projection[:, 3 * columns :].astype(F32)
    gains_ref[0:1] = turn_column(extras[:, heads : heads + 1])
    gains_ref[1:2] = turn_column(extras[:, heads + 1 : heads + 2])

    def project(index):
        first = (input_ref[at(index)].astype(F32) * scale_ref[at(index)] * gains_ref[0:1]).astype(BF)
        first_ref[at(index)] = first
        both = nn(first, pack_ref[0].reshape(width, pack_ref.shape[3]))
        pre_ref[at(index)] = both[:, : 3 * columns].astype(BF)
        logits_ref[at(index)] = both[:, 3 * columns :]

    pl.loop(0, tokens // chunk)(project)

    @pl.when(member == 0)
    def _():
        halo_ref[...] = jnp.zeros_like(halo_ref)

    @pl.when(member > 0)
    def _():
        edge(member).wait_recv()
        block = edge_ref[...].astype(F32)
        scale = lax.rsqrt(jnp.mean(block * block, axis=-1, keepdims=True) + 1e-06)
        first = (block * scale * gains_ref[0:1]).astype(BF)
        halo_ref[...] = nn(first, pack_ref[0].reshape(width, pack_ref.shape[3])[:, : 3 * columns]).astype(BF)

    turned[3]()
    near_copy.start()
    far_copy.start()
    rows, cols = grid_indices()
    eye = jnp.where(rows == cols, 1.0, 0.0)
    top = lax.broadcasted_iota(jnp.int32, (CHUNK, 1), 0) < GROUP
    for head in range(heads):
        total_ref[head] = side(eye, jnp.zeros_like(eye))
    batch = pad_ref.shape[0]

    def one(step, carry):
        units = []
        for lane in range(batch):
            chunk = step * batch + lane
            pad = pad_ref.at[lane]
            load_padded(pad, pre_ref, halo_ref, chunk, resets_ref)
            mixed = convolve(pad, taps_ref)
            silued = mixed * sigmoid(mixed)
            keep0 = 1.0 - resets_ref[2 * chunk]
            keep1 = 1.0 - resets_ref[2 * chunk + 1]
            both = keep0 * keep1
            enter = jnp.where(top, keep0, both)
            leave = jnp.where(top, keep1, 1.0)
            at = pl.ds(pl.multiple_of(chunk * CHUNK, CHUNK), CHUNK)
            beta_rows = sigmoid(logits_ref[at, :])
            for head in range(heads):
                window = slice(head * CHUNK, (head + 1) * CHUNK)
                parts = []
                for kind in range(3):
                    part = silued[:, kind * columns + head * CHUNK : kind * columns + (head + 1) * CHUNK]
                    if kind < 2:
                        part = part * lax.rsqrt(jnp.sum(part * part, axis=-1, keepdims=True) + 1e-06)
                    part = part.astype(BF)
                    qkv_ref[at, kind * columns + head * CHUNK : kind * columns + (head + 1) * CHUNK] = part
                    parts.append(part)
                units.append((chunk, head, *parts, beta_rows[:, head : head + 1], keep1, both, enter, leave))
        turned = [u[3].T for u in units]
        strict = [
            jnp.where(rows > cols, u[5] * nn(u[3], t), 0.0) for u, t in zip(units, turned)
        ]
        inverses = [r.astype(BF) for r in inverse_levels(strict, rows, cols, [u[6] for u in units])]
        factors = []
        for u, inverse in zip(units, inverses):
            beta = u[5]
            factors.append(nn(inverse, side(u[3].astype(F32) * beta, u[4].astype(F32) * beta)))
        for u, inverse, factor, t in zip(units, inverses, factors, turned):
            chunk, head, query, key, value, beta, keep1, both, enter, leave = u
            weight, update = factor[:, :CHUNK], factor[:, CHUNK:]
            entering_weight = weight * enter
            inv_ref[chunk, head] = inverse
            wu_ref[chunk, head] = side(entering_weight, update).astype(BF)
            gathered = nn(t, side(weight, update * leave))
            device_map = (both * (eye - gathered[:, :CHUNK])).astype(BF)
            shift = gathered[:, CHUNK:]
            scores = jnp.where(rows >= cols, nn(query, t), 0.0)
            scores = jnp.where((rows >= GROUP) & (cols < GROUP), scores * keep1, scores)
            seen = nn(scores, side(entering_weight, update))
            effective = query.astype(F32) * enter - seen[:, :CHUNK]
            mq_ref[chunk, head] = stack(device_map, effective.astype(BF))
            out0_ref[chunk, head] = seen[:, CHUNK:]
            running = total_ref[head]
            start_ref[chunk, head] = running.astype(BF)
            total_ref[head] = nn(device_map, running) + side(jnp.zeros_like(shift), shift)
        return carry

    count = resets_ref.shape[0] // 2 // batch
    held = 3 if len(full[2]) > 3 else 0
    relays = full[2][: len(full[2]) - held]

    def pumped(step, carry):
        carry = one(step, carry)
        for turn in range(count):
            jobs = [job for place, job in enumerate(relays) if place * count // len(relays) == turn]
            if not jobs and turn != count // 2:
                continue

            @pl.when(step == turn)
            def _():
                for job in jobs:
                    full[1](*job)
                if turn == count // 2:
                    far_copy.wait_recv()
                    pass_copy.start()

        return carry

    lax.fori_loop(0, count, pumped, 0)
    part_ref[...] = total_ref[...].astype(BF)
    for hop in range(1, window + 1):

        @pl.when(behind >= hop)
        def _():
            state_copy(hop).start()

    for job in full[2][len(full[2]) - held :]:
        full[1](*job)
    state_ref[...] = jnp.zeros_like(state_ref)
    for hop in range(window, 0, -1):

        @pl.when(member >= hop)
        def _():
            state_copy(hop).wait_recv()
            for head in range(heads):
                part = slots_ref[hop - 1, head]
                state_ref[head] = nn(part[:, :CHUNK], state_ref[head]) + part[:, CHUNK:].astype(F32)

    def near_rows(index):
        return push(
            rows_ref.at[at(index)], far_rows_ref.at[0, at(index)], row_near_send.at[index], row_near_recv.at[index], "head", near
        )

    def far_rows(index):
        return push(
            rows_ref.at[at(index)], far_rows_ref.at[1, at(index)], row_far_send.at[index], row_far_recv.at[index], "head", far
        )

    def pass_rows(index):
        return push(
            far_rows_ref.at[1, at(index)], far_rows_ref.at[2, at(index)], row_pass_send.at[index], row_pass_recv.at[index], "head", near
        )

    def finished(index):
        for lane in range(chunk // CHUNK):
            place_ = index * (chunk // CHUNK) + lane
            rows_at = pl.ds(pl.multiple_of(place_ * CHUNK, CHUNK), CHUNK)
            begins = [start_ref[place_, head] for head in range(heads)]
            states = [
                (nn(begins[head][:, :CHUNK], state_ref[head]) + begins[head][:, CHUNK:].astype(F32)).astype(BF)
                for head in range(heads)
            ]
            outs = [out0_ref[place_, head] + nn(mq_ref[place_, head, CHUNK:], states[head]) for head in range(heads)]
            for head in range(heads):
                lanes = slice(head * CHUNK, (head + 1) * CHUNK)
                states_ref[place_, head] = states[head]
                delta_ref[rows_at, lanes] = outs[head]
                scale = lax.rsqrt(jnp.mean(outs[head] * outs[head], axis=-1, keepdims=True) + 1e-05)
                rows_ref[rows_at, lanes] = (outs[head] * scale * head_gain_ref[...]).astype(BF)
        far_rows(index).start()
        near_rows(index).start()

    pl.loop(0, tokens // chunk)(finished)

    @pl.loop(0, tokens // chunk)
    def _(index):
        far_rows(index).wait_recv()
        pass_rows(index).start()

    near_copy.wait()
    far_copy.wait_send()
    pass_copy.wait()
    full[3]()

    @pl.when(member + 1 < members)
    def _():
        edge(member + 1).wait_send()

    for hop in range(1, window + 1):

        @pl.when(behind >= hop)
        def _():
            state_copy(hop).wait_send()

    @pl.loop(0, tokens // chunk)
    def _(index):
        near_rows(index).wait()
        far_rows(index).wait_send()
        pass_rows(index).wait()

    for gather in (pack, turned, full):
        gather[4]()


def front_stage(resets, inputs, query, key, value, extra, out_weight, own, taps, head_gain, members, heads, collective):
    tokens, width = inputs.shape
    columns = heads * CHUNK
    chunks = tokens // CHUNK
    whole = pl.BlockSpec(memory_space=pltpu.VMEM)
    piece = width // members
    window = min(members - 1, members // 2)

    def units(wide, kind):
        return jax.ShapeDtypeStruct((chunks, heads, *wide), kind)

    def dma(*shape):
        return [pltpu.SemaphoreType.DMA(shape)] * 2

    return pl.pallas_call(
        functools.partial(front_kernel, members, heads),
        name="front",
        out_shape=(
            jax.ShapeDtypeStruct((1, members, piece, 3 * columns + CHUNK), BF),
            jax.ShapeDtypeStruct((tokens, width), BF),
            jax.ShapeDtypeStruct((tokens, 3 * columns), BF),
            jax.ShapeDtypeStruct((tokens, CHUNK), F32),
            jax.ShapeDtypeStruct((16, 3 * columns), BF),
            jax.ShapeDtypeStruct((tokens, 1), F32),
            jax.ShapeDtypeStruct((2, width), F32),
            jax.ShapeDtypeStruct((1, members, *out_weight.shape), BF),
            jax.ShapeDtypeStruct((own.shape[0], members, *own.shape[1:]), BF),
            jax.ShapeDtypeStruct((3, members, *out_weight.shape), BF),
            jax.ShapeDtypeStruct((tokens, 3 * columns), BF),
            units((CHUNK, CHUNK), BF),
            units((CHUNK, 2 * CHUNK), BF),
            units((2 * CHUNK, CHUNK), BF),
            jax.ShapeDtypeStruct((heads, CHUNK, 2 * CHUNK), F32),
            jax.ShapeDtypeStruct((tokens, columns), F32),
            jax.ShapeDtypeStruct((tokens, columns), BF),
            jax.ShapeDtypeStruct((3, tokens, columns), BF),
            units((CHUNK, CHUNK), BF),
        ),
        in_specs=[pl.BlockSpec(memory_space=pltpu.SMEM)] + [whole] * 9,
        out_specs=(whole,) * 19,
        scratch_shapes=[
            pltpu.VMEM((chunks, heads, CHUNK, 2 * CHUNK), BF),
            pltpu.VMEM((chunks, heads, CHUNK, CHUNK), F32),
            pltpu.VMEM((heads, CHUNK, CHUNK), F32),
            pltpu.VMEM((heads, CHUNK, 2 * CHUNK), BF),
            pltpu.VMEM((window, heads, CHUNK, 2 * CHUNK), BF),
            pltpu.VMEM((2, 144, 3 * columns), F32),
            pltpu.VMEM((16, width), BF),
        ]
        + dma(1, members)
        + dma()
        + dma(1, members)
        + dma(own.shape[0], members)
        + dma(3)
        + dma(window)
        + dma(tokens // 256) * 3,
        compiler_params=pltpu.CompilerParams(
            collective_id=collective, has_side_effects=True, vmem_limit_bytes=VMEM_LIMIT
        ),
        cost_estimate=pl.CostEstimate(flops=8 * 10**9, bytes_accessed=40 << 20, transcendentals=2 << 20),
    )(resets, inputs, query, key, value, extra, out_weight, own, taps, head_gain)


def lanes_whole(pieces):
    places, rows, piece = pieces.shape
    if piece >= 128:
        return pieces
    group = 128 // piece
    return pieces.reshape(places // group, group, rows, piece).transpose(0, 2, 1, 3).reshape(places // group, rows, 128)


def lanes_split(blocks, piece):
    count, rows, lanes = blocks.shape
    if piece >= 128:
        return blocks
    group = 128 // piece
    return blocks.reshape(count, rows, group, piece).transpose(0, 2, 1, 3).reshape(count * group, rows, piece)


def body(
    block_input,
    first_gain,
    query_weight,
    key_weight,
    value_weight,
    beta_weight,
    conv_weight,
    head_gain,
    output_weight,
    second_gain,
    gate_weight,
    up_weight,
    down_weight,
    lengths,
    cotangent,
):
    tokens, width = block_input.shape
    heads = beta_weight.shape[1]
    columns = query_weight.shape[1]
    hidden_columns = gate_weight.shape[1]
    members = lax.axis_size("seq")
    piece = width // members
    seq_place = lax.axis_index("seq")

    extra = jnp.concatenate(
        [beta_weight, first_gain[:, None], second_gain[:, None], jnp.zeros((piece, CHUNK - heads - 2), BF)], 1
    )
    ends = jnp.sum(jnp.where(jnp.arange(4)[:, None] >= jnp.arange(4)[None, :], lengths[None, :], 0), axis=1)
    starts = ends - lengths
    block_starts = seq_place * tokens + GROUP * jnp.arange(tokens // GROUP, dtype=jnp.int32)
    resets = jnp.any(starts[None, :] == block_starts[:, None], axis=1).astype(F32)

    taps = conv_weight.astype(F32).transpose(1, 0, 2).reshape(4, -1)
    gain_head = head_gain.astype(F32)[None, :]
    own = jnp.stack([gate_weight.T, up_weight.T, down_weight.T])
    split = piece < 128
    (
        mixer_pack,
        first_rows,
        pre,
        logits,
        halo,
        scale_one,
        gains,
        turned,
        full,
        others,
        qkv,
        inv,
        wu,
        mq,
        total,
        delta,
        head_rows,
        far_rows,
        states,
    ) = front_stage(
        resets,
        block_input,
        query_weight,
        key_weight,
        value_weight,
        extra,
        output_weight.T,
        own[:1, :16] if split else own,
        taps,
        gain_head,
        members,
        heads,
        5,
    )
    mixer_pack = mixer_pack.reshape(width, -1)
    if split:
        gathered = lax.all_gather(own, "seq", axis=1)
        full = jnp.stack([lanes_whole(gathered[i]) for i in range(3)])
    turned = lanes_whole(turned[0])
    others = jnp.stack([lanes_whole(others[i]) for i in range(3)]) if split else others
    total_low = total.astype(BF)
    d_heads, update_part, middle_shard, d_middle_shard, *grads, second_grad = middle_stage(
        head_rows, far_rows, full, turned, others, block_input, cotangent, gains[1:2], 2
    )
    second_part = jnp.sum(second_grad, 0)
    ddelta, gain_part, shift = mixer_back_state(d_heads, delta, gain_head, mq)
    back_part = jnp.concatenate([total_low[:, :, :CHUNK].transpose(0, 2, 1), shift.astype(BF)], 2)
    if split:
        pieces = jnp.concatenate([part for pair in grads for part in pair], 1)
        whole_sum = lax.psum_scatter(lanes_split(pieces, piece), "seq", scatter_dimension=0, tiled=False).astype(F32)
        grads = [jnp.zeros((1, members, 16, 128), BF)] * 3
    arrive, block_output, third_sum = exchange(back_part, (update_part, middle_shard, grads[2]), "seq", True, 1)
    d_pre, taps_part, first_sum = mixer_backward(
        resets, pre, halo, taps, logits, qkv, inv, wu, mq, states, ddelta, arrive, grads[0], 3
    )
    small = jnp.concatenate(
        [
            jnp.zeros((1, width), F32),
            jnp.pad(jnp.sum(gain_part, 0, keepdims=True), ((0, 0), (0, width - CHUNK))),
            jnp.zeros((6, width), F32),
            jnp.sum(second_grad, 0, keepdims=True),
            jnp.sum(taps_part, 1).reshape(-1, width),
            jnp.zeros((7 - 12 * columns // width, width), F32),
        ]
    )
    input_gradient, mixer_sum, sums, second_sum = final_stage(
        first_rows, d_pre, mixer_pack, block_input, scale_one, gains[0:1], d_middle_shard, small, grads[1], members, 4
    )
    if not split:
        whole_sum = jnp.concatenate([s.reshape(-1, 128) for s in (first_sum, second_sum, third_sum)])
    gain_sum = sums[1, :CHUNK]
    conv_gradient = sums[9 : 9 + 12 * columns // width].reshape(4, 3, columns).transpose(1, 0, 2)
    row_start = seq_place * piece
    first_gradient = lax.dynamic_slice_in_dim(sums[0], row_start, piece, 0)
    second_gradient = lax.dynamic_slice_in_dim(sums[8], row_start, piece, 0)
    beta_gradient = mixer_sum[:, 3 * columns : 3 * columns + heads]
    return (
        block_output,
        input_gradient,
        first_gradient,
        mixer_sum[:, :columns],
        mixer_sum[:, columns : 2 * columns],
        mixer_sum[:, 2 * columns : 3 * columns],
        beta_gradient,
        conv_gradient,
        gain_sum,
        whole_sum[3 * hidden_columns :].T,
        second_gradient,
        whole_sum[:hidden_columns].T,
        whole_sum[hidden_columns : 2 * hidden_columns].T,
        whole_sum[2 * hidden_columns : 3 * hidden_columns].T,
    )


def solution(mesh):
    return jax.shard_map(
        body,
        mesh=mesh,
        in_specs=(
            P("seq", None),
            P("seq"),
            P("seq", "head"),
            P("seq", "head"),
            P("seq", "head"),
            P("seq", "head"),
            P(None, None, "head"),
            P(),
            P("seq", "head"),
            P("seq"),
            P("seq", "head"),
            P("seq", "head"),
            P("seq", "head"),
            P(),
            P("seq", None),
        ),
        out_specs=(
            P("seq", "head"),
            P("seq", "head"),
            P("seq"),
            P("seq", "head"),
            P("seq", "head"),
            P("seq", "head"),
            P("seq", "head"),
            P(None, None, "head"),
            P(),
            P("seq", "head"),
            P("seq"),
            P("seq", "head"),
            P("seq", "head"),
            P("seq", "head"),
        ),
        check_vma=False,
    )
```

```python
import functools

import jax
import jax.numpy as jnp
from jax import lax
from jax.experimental import pallas as pl
from jax.experimental.pallas import tpu as pltpu
from jax.sharding import PartitionSpec as P

GROUP = 64
CHUNK = 128
MESH = pl.DeviceIdType.MESH
BF = jnp.bfloat16
F32 = jnp.float32
VMEM_LIMIT = 59 << 20


def nn(left, right):
    return jnp.dot(left.astype(BF), right.astype(BF), preferred_element_type=F32)


def tn(left, right):
    return lax.dot_general(
        left.astype(BF), right.astype(BF), (((0,), (0,)), ((), ())), preferred_element_type=F32
    )


def nt(left, right):
    return lax.dot_general(
        left.astype(BF), right.astype(BF), (((1,), (1,)), ((), ())), preferred_element_type=F32
    )


def sigmoid(v):
    return 0.5 * jnp.tanh(0.5 * v) + 0.5


def side(left, right):
    return jnp.concatenate([left, right], 1)


def stack(top, bottom):
    return jnp.concatenate([top, bottom], 0)


def grid_indices():
    rows = lax.broadcasted_iota(jnp.int32, (CHUNK, CHUNK), 0)
    cols = lax.broadcasted_iota(jnp.int32, (CHUNK, CHUNK), 1)
    return rows, cols


def fill_resets(lengths_ref, resets_ref, tokens):
    base = lax.axis_index("seq") * tokens

    @pl.loop(0, tokens // GROUP)
    def _(block):
        position = base + block * GROUP
        value = jnp.float32(0.0)
        start = jnp.int32(0)
        for index in range(lengths_ref.shape[0]):
            value = jnp.where(start == position, 1.0, value)
            start = start + lengths_ref[index]
        resets_ref[block] = value


def fill_taps(conv_ref, taps_ref):
    columns = conv_ref.shape[2]
    for kind in range(3):
        taps_ref[:, kind * columns : (kind + 1) * columns] = conv_ref[kind].astype(F32)


def load_padded(pad_ref, pre_ref, halo_ref, chunk, resets_ref):
    start = pl.multiple_of(chunk * CHUNK, CHUNK)
    before = pl.multiple_of(jnp.maximum(start - 16, 0), 16)
    own = pre_ref[pl.ds(start, CHUNK), :].astype(F32)
    earlier = pre_ref[pl.ds(before, 16), :].astype(F32)[8:]
    halo = halo_ref[...].astype(F32)[8:]
    first = jnp.where(chunk == 0, halo, earlier)
    keep0 = 1.0 - resets_ref[2 * chunk]
    keep1 = 1.0 - resets_ref[2 * chunk + 1]
    pad_ref[0:8] = first * keep0
    pad_ref[8:72] = own[:GROUP]
    pad_ref[72:80] = own[GROUP - 8 : GROUP] * keep1
    pad_ref[80:144] = own[GROUP:]


def tap_rows(pad_ref, tap):
    return stack(pad_ref[5 + tap : 69 + tap], pad_ref[77 + tap : 141 + tap])


def convolve(pad_ref, taps_ref):
    mixed = None
    for tap in range(4):
        term = taps_ref[tap : tap + 1] * tap_rows(pad_ref, tap)
        mixed = term if mixed is None else mixed + term
    return mixed


def inverse_levels(strict, rows, cols, keep1):
    eye = jnp.where(rows == cols, 1.0, 0.0)
    pair = (rows // 2) == (cols // 2)
    results = [eye - jnp.where(pair, a, 0.0) for a in strict]
    width = 2
    while width < CHUNK:
        off = ((rows // (2 * width)) == (cols // (2 * width))) & ((rows // width) != (cols // width))
        lows = [r.astype(BF) for r in results]
        parts = [jnp.where(off, a, 0.0).astype(BF) for a in strict]
        if width == GROUP:
            parts = [jnp.where(off, a * k, 0.0).astype(BF) for a, k in zip(strict, keep1)]
        steps = [nn(r, p) for r, p in zip(lows, parts)]
        results = [r - nn(s, low) for r, s, low in zip(results, steps, lows)]
        width *= 2
    return results


def state_backward_kernel(
    heads,
    window,
    dheads_ref,
    delta_ref,
    gain_ref,
    mq_ref,
    total_ref,
    update_ref,
    mid_ref,
    grads_ref,
    ddelta_ref,
    gain_grad_ref,
    state_ref,
    block_ref,
    sum_ref,
    shift_ref,
    part_ref,
    slots_ref,
    send_sem,
    recv_sem,
    near_ref,
    relay_ref,
    far_ref,
    near_send,
    near_recv,
    far_send,
    far_recv,
    piece_relay,
    piece_slots,
    piece_send,
    piece_recv,
):
    member, members = lax.axis_index("seq"), lax.axis_size("seq")
    _, _, near, far = head_peers()
    chunk = 256
    steps = update_ref.shape[0] // chunk
    chunks = mq_ref.shape[0]
    behind = members - 1 - member
    at, _, start_pair, pass_on, own_sum, finish = head_scatter_copies(
        chunk, update_ref, near_ref, relay_ref, far_ref, (near_send, near_recv, far_send, far_recv)
    )
    begin, receive, jobs, end = piece_scatter(
        grads_ref, piece_relay, piece_slots, sum_ref, piece_send, piece_recv, members
    )
    barrier, stages = greet_seq(members)
    for hop in range(1, window + 1):

        @pl.when(behind >= hop)
        def _():
            pl.semaphore_signal(barrier, inc=1, device_id={"seq": member + hop}, device_id_type=MESH)

    for target in (near, far):
        pl.semaphore_signal(barrier, inc=1, device_id={"head": target}, device_id_type=MESH)
    pl.semaphore_wait(barrier, stages + 2 + jnp.minimum(member, window))

    @pl.loop(0, steps)
    def _(index):
        start_pair(index)

    for head in range(heads):
        part_ref[0, head] = total_ref[head, :, :CHUNK].T.astype(BF)

    def copy(kind, hop):
        return push(
            part_ref.at[kind],
            slots_ref.at[kind, hop - 1],
            send_sem.at[kind, hop - 1],
            recv_sem.at[kind, hop - 1],
            "seq",
            member - hop,
        )

    def send(kind):
        for hop in range(1, window + 1):

            @pl.when(member >= hop)
            def _():
                copy(kind, hop).start()

    send(0)
    half = len(jobs) // 4
    begin(jobs[:half])
    shift_ref[...] = jnp.zeros_like(shift_ref)
    gain_grad_ref[...] = jnp.zeros_like(gain_grad_ref)

    def one(step, carry):
        index = chunks - 1 - step
        rows = pl.ds(pl.multiple_of(index * CHUNK, CHUNK), CHUNK)
        for head in range(heads):
            lanes = slice(head * CHUNK, (head + 1) * CHUNK)
            out = delta_ref[rows, lanes]
            grad = dheads_ref[rows, lanes].astype(F32)
            scale = lax.rsqrt(jnp.mean(out * out, axis=-1, keepdims=True) + 1e-05)
            unit = out * scale
            gain_grad_ref[...] += jnp.sum((grad * unit).reshape(CHUNK // 8, 8, CHUNK), 0)
            scaled = grad * gain_ref[...]
            back = scale * (scaled - unit * jnp.mean(scaled * unit, axis=-1, keepdims=True))
            back = back.astype(BF)
            ddelta_ref[rows, lanes] = back
            shift_ref[head] = tn(mq_ref[index, head], stack(shift_ref[head].astype(BF), back))

        @pl.when(lax.rem(step, 2) == 1)
        def _():
            pass_on(lax.div(step, 2))

        return carry

    lax.fori_loop(0, chunks, one, 0)
    for head in range(heads):
        part_ref[1, head] = shift_ref[head].astype(BF)
    send(1)
    begin(jobs[half:])
    for job in jobs[: len(jobs) // 2]:
        receive(*job)
    state_ref[...] = jnp.zeros_like(state_ref)
    for hop in range(window, 0, -1):

        @pl.when(behind >= hop)
        def _():
            copy(0, hop).wait_recv()
            copy(1, hop).wait_recv()
            for head in range(heads):
                state_ref[head] = nn(slots_ref[0, hop - 1, head], state_ref[head]) + slots_ref[1, hop - 1, head].astype(F32)

    for job in jobs[len(jobs) // 2 :]:
        receive(*job)

    @pl.loop(0, steps)
    def _(index):
        block_ref[at(index)] = (mid_ref[at(index)] + own_sum(index)).astype(BF)
        finish(index)

    end()
    for hop in range(1, window + 1):

        @pl.when(member >= hop)
        def _():
            copy(0, hop).wait_send()
            copy(1, hop).wait_send()


def state_backward(dheads, delta, gain, mq, total, update, mid, grads, members, collective):
    chunks, heads = mq.shape[:2]
    tokens, columns = mid.shape
    window = min(members - 1, members // 2)
    whole = pl.BlockSpec(memory_space=pltpu.VMEM)
    parts, _, *piece = grads.shape
    return pl.pallas_call(
        functools.partial(state_backward_kernel, heads, window),
        name="state_backward",
        out_shape=(
            jax.ShapeDtypeStruct((tokens, columns), BF),
            jax.ShapeDtypeStruct((8, CHUNK), F32),
            jax.ShapeDtypeStruct((heads, CHUNK, CHUNK), F32),
            jax.ShapeDtypeStruct((tokens, columns), BF),
            jax.ShapeDtypeStruct((parts, *piece), F32),
        ),
        in_specs=[whole] * 8,
        out_specs=(whole,) * 5,
        scratch_shapes=[
            pltpu.VMEM((heads, CHUNK, CHUNK), F32),
            pltpu.VMEM((2, heads, CHUNK, CHUNK), BF),
            pltpu.VMEM((2, window, heads, CHUNK, CHUNK), BF),
            pltpu.SemaphoreType.DMA((2, window)),
            pltpu.SemaphoreType.DMA((2, window)),
        ]
        + head_scatter_scratch(tokens, columns, tokens // 256)
        + piece_scatter_scratch(parts, members, piece),
        compiler_params=pltpu.CompilerParams(
            collective_id=collective, has_side_effects=True, vmem_limit_bytes=VMEM_LIMIT
        ),
        cost_estimate=pl.CostEstimate(flops=10**9, bytes_accessed=30 << 20, transcendentals=0),
    )(dheads, delta, gain, mq, total, update, mid, grads)


def piece_scatter_scratch(parts, members, piece):
    return [
        pltpu.VMEM((parts, max(members // 2 - 1, 1), *piece), BF),
        pltpu.VMEM((parts, members - 1, *piece), BF),
        pltpu.SemaphoreType.DMA((parts, members)),
        pltpu.SemaphoreType.DMA((parts, members)),
    ]


def piece_scatter(own_ref, relay_ref, slots_ref, total_ref, send, recv, members):
    member = lax.axis_index("seq")
    parts = own_ref.shape[0]
    stages = (members - 1).bit_length()
    order = sorted(range(members), key=lambda r: zeros_below(r) if r else stages)
    levels = {r: list(range(zeros_below(r) if r else stages)) for r in order}
    events = {}
    for r in order:
        for stage in levels[r]:
            events[r, stage] = len(events)
    kept = [r for r in order if r and r % 2 == 0]

    def source(part, r):
        return own_ref.at[part, flip(member, r)] if r % 2 else relay_ref.at[part, kept.index(r)]

    def give(part, r):
        stage = zeros_below(r)
        slot = events[r ^ (1 << stage), stage]
        return push(
            source(part, r), slots_ref.at[part, slot], send.at[part, r], recv.at[part, slot], "seq", flip(member, 1 << stage)
        )

    def take(part, r, stage):
        slot = events[r, stage]
        return push(
            own_ref.at[part, flip(member, 1)], slots_ref.at[part, slot], send.at[part, 0], recv.at[part, slot], "seq", flip(member, 1 << stage)
        )

    jobs = [(part, r) for r in order if r % 2 == 0 for part in range(parts)]

    def begin(some=None):
        for part, r in jobs if some is None else some:
            give(part, r ^ 1).start()

    def receive(part, r):
        total = own_ref[part, flip(member, r)].astype(F32)
        for stage in levels[r]:
            take(part, r, stage).wait_recv()
            total = total + slots_ref[part, events[r, stage]].astype(F32)
        if r:
            relay_ref[part, kept.index(r)] = total.astype(BF)
            give(part, r).start()
        else:
            total_ref[part] = total

    def finish():
        for part in range(parts):
            for r in order:
                if r:
                    give(part, r).wait_send()

    return begin, receive, jobs, finish


def mixer_backward_kernel(
    heads,
    lengths_ref,
    pre_hbm,
    halo_ref,
    conv_ref,
    logits_hbm,
    qkv_hbm,
    inv_hbm,
    wu_hbm,
    mq_hbm,
    states_hbm,
    ddelta_hbm,
    arrive_ref,
    grads_ref,
    dpre_ref,
    taps_grad_ref,
    total_ref,
    pre_ref,
    logits_ref,
    qkv_ref,
    inv_ref,
    wu_ref,
    mq_ref,
    states_ref,
    ddelta_ref,
    load_sem,
    resets_ref,
    taps_ref,
    carry_ref,
    pad_ref,
    dpad_ref,
    tail_ref,
    lead_ref,
    edge_ref,
    send_sem,
    recv_sem,
    relay_ref,
    slots_ref,
    piece_send,
    piece_recv,
):
    member, members = lax.axis_index("seq"), lax.axis_size("seq")
    barrier, stages = greet_seq(members)
    begin, receive, order, finish = piece_scatter(
        grads_ref, relay_ref, slots_ref, total_ref, piece_send, piece_recv, members
    )

    @pl.when(member + 1 < members)
    def _():
        pl.semaphore_signal(barrier, inc=1, device_id={"seq": member + 1}, device_id_type=MESH)

    columns = heads * CHUNK
    chunks = mq_ref.shape[0]
    fill_resets(lengths_ref, resets_ref, pre_ref.shape[0])
    fill_taps(conv_ref, taps_ref)
    quarter = chunks // 4
    sources = (pre_hbm, logits_hbm, qkv_hbm, ddelta_hbm, inv_hbm, wu_hbm, mq_hbm, states_hbm)
    targets = (pre_ref, logits_ref, qkv_ref, ddelta_ref, inv_ref, wu_ref, mq_ref, states_ref)

    def load(number, turn):
        unit = CHUNK if number < 4 else 1
        reach = pl.ds((chunks - (turn + 1) * quarter) * unit, quarter * unit)
        return pltpu.make_async_copy(
            sources[number].at[reach], targets[number].at[reach], load_sem.at[number, turn]
        )

    for turn in range(4):
        for number in range(8):
            load(number, turn).start()
    load(0, 0).wait()
    rows, cols = grid_indices()
    top = lax.broadcasted_iota(jnp.int32, (CHUNK, 1), 0) < GROUP
    pl.semaphore_wait(barrier, stages + jnp.minimum(member, 1))
    begin()
    carry_ref[...] = arrive_ref[...]
    taps_grad_ref[...] = jnp.zeros_like(taps_grad_ref)
    dpad_ref[136:144] = jnp.zeros_like(dpad_ref[136:144])

    def one(step, carry):
        chunk = chunks - 1 - step
        at = pl.ds(pl.multiple_of(chunk * CHUNK, CHUNK), CHUNK)
        for turn in range(4):

            @pl.when(step == turn * quarter)
            def _():
                for number in range(1, 8):
                    load(number, turn).wait()
                if turn < 3:
                    load(0, turn + 1).wait()

        keep0 = 1.0 - resets_ref[2 * chunk]
        keep1 = 1.0 - resets_ref[2 * chunk + 1]
        both = keep0 * keep1
        enter = jnp.where(top, keep0, both)
        leave = jnp.where(top, keep1, 1.0)
        load_padded(pad_ref, pre_ref, halo_ref, chunk, resets_ref)
        mixed = convolve(pad_ref, taps_ref)
        gate = sigmoid(mixed)
        slope = gate * (1.0 + mixed * (1.0 - gate))
        silued = mixed * gate
        beta_rows = sigmoid(logits_ref[at, :])
        grads = [[None] * heads for _ in range(3)]
        dlogits = []
        cross = (rows >= GROUP) & (cols < GROUP)

        def part(kind, head):
            return slice(kind * columns + head * CHUNK, kind * columns + (head + 1) * CHUNK)

        def masked(product, keep):
            lower = jnp.where(keep, product, 0.0)
            return jnp.where(cross, lower * keep1, lower).astype(BF)

        every = range(heads)
        query = [qkv_ref[at, part(0, h)] for h in every]
        key = [qkv_ref[at, part(1, h)] for h in every]
        value = [qkv_ref[at, part(2, h)] for h in every]
        key32 = [k.astype(F32) for k in key]
        beta = [beta_rows[:, h : h + 1] for h in every]
        inverse = [inv_ref[chunk, h] for h in every]
        weight = [wu_ref[chunk, h, :, :CHUNK] for h in every]
        factors = [wu_ref[chunk, h] for h in every]
        update = [wu_ref[chunk, h, :, CHUNK:] for h in every]
        state = [states_ref[chunk, h] for h in every]
        out_grad = [ddelta_ref[at, h * CHUNK : (h + 1) * CHUNK] for h in every]
        later = [carry_ref[h].astype(BF) for h in every]
        carried = [tn(mq_ref[chunk, h], stack(later[h], out_grad[h])) for h in every]
        scores = [masked(nt(query[h], key[h]), rows >= cols) for h in every]
        fresh = [(update[h].astype(F32) - nn(weight[h], state[h])).astype(BF) for h in every]
        fresh_low = [(tn(scores[h], out_grad[h]) + leave * nn(key[h], later[h])).astype(BF) for h in every]
        score_grad = [masked(nt(out_grad[h], fresh[h]), rows >= cols) for h in every]
        through = [nt(stack(out_grad[h], fresh_low[h]), state[h]) for h in every]
        weight_grad = [(-enter * through[h][CHUNK:]).astype(BF) for h in every]
        back = [tn(inverse[h], side(weight_grad[h], fresh_low[h])) for h in every]
        query_grad = [enter * through[h][:CHUNK] + nn(score_grad[h], key[h]) for h in every]
        key_grad = [tn(score_grad[h], query[h]) + leave * nt(fresh[h], later[h]) for h in every]
        strict = [masked(-nt(back[h].astype(BF), factors[h]), rows > cols) for h in every]
        strict_key = [nn(strict[h], key[h]) for h in every]
        turned = [tn(strict[h], (beta[h] * key32[h]).astype(BF)) for h in every]
        for h in every:
            carry_ref[h] = carried[h]
            yk, zv = back[h][:, :CHUNK], back[h][:, CHUNK:]
            both_key = yk + strict_key[h]
            key_grad[h] = key_grad[h] + beta[h] * both_key + turned[h]
            grads[2][h] = beta[h] * zv
            beta_grad = jnp.sum(both_key * key32[h] + zv * value[h].astype(F32), axis=-1, keepdims=True)
            dlogits.append(beta_grad * beta[h] * (1.0 - beta[h]))
        for kind, grad in ((0, query_grad), (1, key_grad)):
            raw = [silued[:, part(kind, h)] for h in every]
            norm = [lax.rsqrt(jnp.sum(raw[h] * raw[h], axis=-1, keepdims=True) + 1e-06) for h in every]
            unit = [raw[h] * norm[h] for h in every]
            inner = [jnp.sum(unit[h] * grad[h], axis=-1, keepdims=True) for h in every]
            grads[kind] = [(grad[h] - unit[h] * inner[h]) * norm[h] for h in every]
        lanes = lax.broadcasted_iota(jnp.int32, (CHUNK, CHUNK), 1)
        spread = jnp.zeros((CHUNK, CHUNK), F32)
        for head in range(heads):
            spread = jnp.where(lanes == head, dlogits[head], spread)
        dpre_ref[at, 3 * columns :] = spread.astype(BF)
        dmixed = jnp.concatenate([g for kind in grads for g in kind], 1) * slope
        dpad_ref[0:GROUP] = dmixed[:GROUP]
        dpad_ref[GROUP : GROUP + 8] = dmixed[GROUP : GROUP + 8] * keep1
        dpad_ref[72 : 72 + GROUP] = dmixed[GROUP:]
        dpre = None
        for tap in range(4):
            back = 3 - tap
            shifted = stack(dpad_ref[back : back + GROUP], dpad_ref[72 + back : 72 + back + GROUP])
            term = taps_ref[tap : tap + 1] * shifted
            dpre = term if dpre is None else dpre + term
            seen = (dmixed * tap_rows(pad_ref, tap)).reshape(CHUNK // 8, 8, 3 * columns)
            taps_grad_ref[tap] += jnp.sum(seen, 0)
        dpre_ref[at, : 3 * columns] = dpre.astype(BF)

        @pl.when(step == 0)
        def _():
            tail_ref[...] = dpre[CHUNK - 16 :]

        dpad_ref[136:144] = dmixed[:8] * keep0
        for place, job in enumerate(order):

            @pl.when(step == (place + 1) * (chunks - 1) // len(order))
            def _():
                receive(*job)

        return carry

    lax.fori_loop(0, chunks, one, 0)
    index = lax.broadcasted_iota(jnp.int32, (8, 1), 0)
    lead = jnp.zeros((8, 3 * columns), F32)
    dpad_ref[0:128] = jnp.zeros_like(dpad_ref[0:128])
    dpad_ref[8:16] = dpad_ref[136:144]
    for tap in range(3):
        back = 3 - tap
        lead = lead + taps_ref[tap : tap + 1] * dpad_ref[back : back + 8]
    lead_ref[...] = lead

    def to_previous(target):
        return push(lead_ref, edge_ref, send_sem, recv_sem, "seq", target)

    @pl.when(member > 0)
    def _():
        to_previous(member - 1).start()

    @pl.when(member + 1 < members)
    def _():
        to_previous(member).wait_recv()
        last = pl.ds(dpre_ref.shape[0] - 16, 16)
        late = stack(tail_ref[0:8], tail_ref[8:16] + edge_ref[...])
        dpre_ref[last, : 3 * columns] = late.astype(BF)

    @pl.when(member > 0)
    def _():
        to_previous(member - 1).wait_send()

    finish()


def mixer_backward(lengths, pre, halo, conv, logits, qkv, inv, wu, mq, states, ddelta, arrive, grads, collective):
    chunks, heads = mq.shape[:2]
    tokens = chunks * CHUNK
    columns = heads * CHUNK
    parts, members = grads.shape[:2]
    piece = grads.shape[2:]
    whole, outside = pl.BlockSpec(memory_space=pltpu.VMEM), pl.BlockSpec(memory_space=pl.ANY)
    streamed = (pre, logits, qkv, inv, wu, mq, states, ddelta)
    return pl.pallas_call(
        functools.partial(mixer_backward_kernel, heads),
        name="mixer_backward",
        out_shape=(
            jax.ShapeDtypeStruct((tokens, 3 * columns + CHUNK), BF),
            jax.ShapeDtypeStruct((4, 8, 3 * columns), F32),
            jax.ShapeDtypeStruct((parts, *piece), F32),
        ),
        in_specs=[pl.BlockSpec(memory_space=pltpu.SMEM), outside, whole, whole] + [outside] * 7 + [whole] * 2,
        out_specs=tuple([pl.BlockSpec(memory_space=pltpu.VMEM)] * 3),
        scratch_shapes=[pltpu.VMEM(a.shape, a.dtype) for a in streamed]
        + [
            pltpu.SemaphoreType.DMA((8, 4)),
            pltpu.SMEM((tokens // GROUP,), F32),
            pltpu.VMEM((4, 3 * columns), F32),
            pltpu.VMEM((heads, CHUNK, CHUNK), F32),
            pltpu.VMEM((144, 3 * columns), F32),
            pltpu.VMEM((144, 3 * columns), F32),
            pltpu.VMEM((16, 3 * columns), F32),
            pltpu.VMEM((8, 3 * columns), F32),
            pltpu.VMEM((8, 3 * columns), F32),
            pltpu.SemaphoreType.DMA,
            pltpu.SemaphoreType.DMA,
        ]
        + piece_scatter_scratch(parts, members, piece),
        compiler_params=pltpu.CompilerParams(
            collective_id=collective, has_side_effects=True, vmem_limit_bytes=VMEM_LIMIT
        ),
        cost_estimate=pl.CostEstimate(flops=3 * 10**9, bytes_accessed=20 << 20, transcendentals=2 << 20),
    )(lengths, pre, halo, conv, logits, qkv, inv, wu, mq, states, ddelta, arrive, grads)


def head_peers():
    place = lax.axis_index("head")
    low = lax.rem(place, 2)
    high = lax.rem(lax.div(place, 2), 2)
    return place, low, place + 1 - 2 * low, place + 2 - 4 * high


def push(src, dst, send_sem, recv_sem, axis, target):
    return pltpu.make_async_remote_copy(
        src_ref=src,
        dst_ref=dst,
        send_sem=send_sem,
        recv_sem=recv_sem,
        device_id={axis: target},
        device_id_type=MESH,
    )


def greet(axis, targets):
    barrier = pltpu.get_barrier_semaphore()
    for target in targets:
        pl.semaphore_signal(barrier, inc=1, device_id={axis: target}, device_id_type=MESH)
    pl.semaphore_wait(barrier, len(targets))


def middle_kernel(
    steps,
    rows_ref,
    late_rows_ref,
    far_rows_ref,
    full_hbm,
    turned_hbm,
    others_hbm,
    input_ref,
    ct_ref,
    late_ct_ref,
    gain_ref,
    dheads_ref,
    update_ref,
    mid_ref,
    dmid_ref,
    first_grads_ref,
    second_grads_ref,
    third_grads_ref,
    gain_grad_ref,
    gate_ref,
    up_ref,
    down_ref,
    turned_ref,
    others_ref,
    load_sem,
    acc_ref,
    part_ref,
    pair_ref,
    far_ref,
    sum_ref,
    keep_ref,
    scale_ref,
    shard_ref,
    pair_send,
    pair_recv,
    far_send,
    far_recv,
    last_send,
    last_recv,
):
    step = pl.program_id(0)
    place, low, near, far = head_peers()
    chunk, width = input_ref.shape
    columns = rows_ref.shape[1]
    hidden = gate_ref.shape[0]
    half = width // 2
    mine = pl.ds(pl.multiple_of(low * half, 128), half)
    theirs = pl.ds(pl.multiple_of((1 - low) * half, 128), half)
    own_columns = pl.ds(pl.multiple_of(place * columns, 128), columns)

    def pair(index):
        return push(
            part_ref.at[lax.rem(index, 2), :, theirs], pair_ref.at[index], pair_send.at[index], pair_recv.at[index], "head", near
        )

    def across(index):
        return push(pair_ref.at[index], far_ref.at[index], far_send.at[index], far_recv.at[index], "head", far)

    def last(index):
        return push(
            sum_ref.at[index, :, mine], sum_ref.at[index, :, mine], last_send.at[index], last_recv.at[index], "head", near
        )

    def loads():
        targets = [
            (full_hbm.at[0], gate_ref),
            (full_hbm.at[1], up_ref),
            (full_hbm.at[2], down_ref),
            (turned_hbm, turned_ref),
        ] + [(others_hbm.at[other], others_ref.at[other]) for other in range(3)]
        for number, (source, target) in enumerate(targets):
            for piece in range(width // 128):
                yield pltpu.make_async_copy(
                    source.at[piece], target.at[:, piece * 128 : (piece + 1) * 128], load_sem.at[number, piece]
                )

    @pl.when(step == 0)
    def _():
        for load in loads():
            load.start()
        greet("head", (near, far))

        acc_ref[...] = jnp.zeros_like(acc_ref)
        gain_grad_ref[...] = jnp.zeros_like(gain_grad_ref)
        for load in loads():
            load.wait()

    @pl.when(step < steps)
    def _():
        ct = ct_ref[...]
        d_hidden = nt(ct, down_ref[...])

        branch = nn(rows_ref[...], turned_ref[...])
        for other in range(3):
            branch = branch + nn(far_rows_ref[other], others_ref[other])
        middle = input_ref[...].astype(F32) + branch
        keep_ref[lax.rem(step, 4)] = middle
        mid_ref[...] = keep_ref[lax.rem(step, 4), :, own_columns]
        scale = lax.rsqrt(jnp.mean(middle * middle, axis=-1, keepdims=True) + 1e-06)
        scale_ref[lax.rem(step, 4)] = scale
        second = (middle * scale * gain_ref[1:2]).astype(BF)
        gate, up = nt(second, gate_ref[...]), nt(second, up_ref[...])
        sig = sigmoid(gate)
        silu = gate * sig
        active = (silu * up).astype(BF)
        d_gate = (d_hidden * up * (sig + silu * (1.0 - sig))).astype(BF)
        d_up = (d_hidden * silu).astype(BF)

        @pl.when(step >= 2)
        def _():
            pair(step - 2).wait_send()

        part_ref[lax.rem(step, 2)] = (nn(d_gate, gate_ref[...]) + nn(d_up, up_ref[...])).astype(BF)
        pair(step).start()

        update_ref[...] = nn(active, down_ref[...]).astype(BF)
        acc_ref[:hidden] += tn(d_gate, second)
        acc_ref[hidden : 2 * hidden] += tn(d_up, second)
        acc_ref[2 * hidden : 3 * hidden] += tn(active, ct)

    @pl.when(step < steps)
    def _():
        pair(step).wait_recv()
        both = part_ref[lax.rem(step, 2), :, mine].astype(F32) + pair_ref[step].astype(F32)
        pair_ref[step] = both.astype(BF)
        across(step).start()

    @pl.when((step > 1) & (step < steps + 2))
    def _():
        done = step - 2
        across(done).wait_recv()
        across(done).wait_send()
        total = pair_ref[done].astype(F32) + far_ref[done].astype(F32)
        sum_ref[done, :, mine] = total.astype(BF)
        last(done).start()

    @pl.when(step > 2)
    def _():
        done = step - 3
        last(done).wait_recv()
        grad = sum_ref[done].astype(F32)
        middle = keep_ref[lax.rem(done, 4)]
        scale = scale_ref[lax.rem(done, 4)]
        unit = middle * scale
        gain_grad_ref[...] += jnp.sum((grad * unit).reshape(chunk // 8, 8, width), 0)
        scaled = grad * gain_ref[1:2]
        d_middle = late_ct_ref[...].astype(F32) + scale * (
            scaled - unit * jnp.mean(scaled * unit, axis=-1, keepdims=True)
        )
        shard_ref[...] = d_middle
        dmid_ref[...] = shard_ref[:, own_columns]
        d_branch = d_middle.astype(BF)
        dheads_ref[...] = nt(d_branch, turned_ref[...]).astype(BF)
        acc_ref[3 * hidden :] += tn(late_rows_ref[...], d_branch)

    @pl.when(step == steps + 2)
    def _():
        for piece in range(width // 128):
            lanes = slice(piece * 128, (piece + 1) * 128)
            begin = 0
            for grads_ref in (first_grads_ref, second_grads_ref, third_grads_ref):
                rows = grads_ref.shape[2]
                for part in range(2):
                    grads_ref[part, piece] = acc_ref[begin : begin + rows, lanes].astype(BF)
                    begin += rows

        @pl.loop(0, steps)
        def _(index):
            last(index).wait_send()

        for index in range(max(steps - 2, 0), steps):
            pair(index).wait_send()


def middle_stage(head_rows, far_rows, full, turned, others, inputs, cotangent, gain, collective):
    tokens, width = inputs.shape
    columns = head_rows.shape[1]
    chunk = min(256, tokens // 2)
    steps = tokens // chunk
    whole = pl.BlockSpec(memory_space=pltpu.VMEM)
    outside = pl.BlockSpec(memory_space=pl.ANY)
    hidden = full.shape[2]
    units = (3 * hidden + columns) // 32
    shares = [16 * (units * 36 // 74), 0, 16 * (units * 25 // 74)]
    shares[1] = 16 * units - sum(shares)

    def early(wide):
        return pl.BlockSpec((chunk, wide), lambda s: (jnp.minimum(s, steps - 1), 0))

    def late(wide):
        return pl.BlockSpec((chunk, wide), lambda s: (jnp.maximum(s - 3, 0), 0))

    far = pl.BlockSpec((3, chunk, columns), lambda s: (0, jnp.minimum(s, steps - 1), 0))
    dma = pltpu.SemaphoreType.DMA((steps,))
    return pl.pallas_call(
        functools.partial(middle_kernel, steps),
        name="middle",
        grid=(steps + 3,),
        out_shape=(
            jax.ShapeDtypeStruct((tokens, columns), BF),
            jax.ShapeDtypeStruct((tokens, width), BF),
            jax.ShapeDtypeStruct((tokens, columns), F32),
            jax.ShapeDtypeStruct((tokens, columns), F32),
            *(jax.ShapeDtypeStruct((2, width // 128, rows, 128), BF) for rows in shares),
            jax.ShapeDtypeStruct((8, width), F32),
        ),
        in_specs=[early(columns), late(columns), far] + [outside] * 3 + [early(width), early(width), late(width), whole],
        out_specs=(late(columns), early(width), early(columns), late(columns), whole, whole, whole, whole),
        scratch_shapes=[
            pltpu.VMEM((hidden, width), BF),
            pltpu.VMEM((hidden, width), BF),
            pltpu.VMEM((hidden, width), BF),
            pltpu.VMEM((columns, width), BF),
            pltpu.VMEM((3, columns, width), BF),
            pltpu.SemaphoreType.DMA((7, width // 128)),
            pltpu.VMEM((3 * hidden + columns, width), F32),
            pltpu.VMEM((2, chunk, width), BF),
            pltpu.VMEM((steps, chunk, width // 2), BF),
            pltpu.VMEM((steps, chunk, width // 2), BF),
            pltpu.VMEM((steps, chunk, width), BF),
            pltpu.VMEM((4, chunk, width), F32),
            pltpu.VMEM((4, chunk, 1), F32),
            pltpu.VMEM((chunk, width), F32),
        ]
        + [dma] * 6,
        compiler_params=pltpu.CompilerParams(
            collective_id=collective,
            has_side_effects=True,
            vmem_limit_bytes=VMEM_LIMIT,
            dimension_semantics=("arbitrary",),
        ),
        cost_estimate=pl.CostEstimate(flops=30 * 10**9, bytes_accessed=30 << 20, transcendentals=2 << 20),
    )(head_rows, head_rows, far_rows, full, turned, others, inputs, cotangent, cotangent, gain)


def zeros_below(value):
    return (value & -value).bit_length() - 1


def flip(place, mask):
    bit = 1
    while bit <= mask:
        if mask & bit:
            place = place + bit - 2 * bit * lax.rem(lax.div(place, bit), 2)
        bit *= 2
    return place


def head_scatter_copies(chunk, part_ref, near_ref, send_ref, far_ref, sems):
    place, low, near, far = head_peers()
    high = lax.rem(lax.div(place, 2), 2)
    columns = far_ref.shape[-1]
    near_send, near_recv, far_send, far_recv = sems

    def at(index):
        return pl.ds(pl.multiple_of(index * chunk, chunk), chunk)

    def cols(owner):
        return pl.ds(pl.multiple_of(owner * columns, 128), columns)

    def pair(index, side_):
        return push(
            part_ref.at[at(index), cols(2 * side_ + 1 - low)],
            near_ref.at[side_, at(index)],
            near_send.at[side_, index],
            near_recv.at[side_, index],
            "head",
            near,
        )

    def across(index):
        return push(send_ref.at[at(index)], far_ref.at[at(index)], far_send.at[index], far_recv.at[index], "head", far)

    def start_pair(index):
        pair(index, 0).start()
        pair(index, 1).start()

    def pass_on(index):
        pair(index, 0).wait_recv()
        pair(index, 1).wait_recv()
        total = part_ref[at(index), cols(2 * (1 - high) + low)].astype(F32) + near_ref[1 - high, at(index)].astype(F32)
        send_ref[at(index)] = total.astype(BF)
        across(index).start()

    def own_sum(index):
        across(index).wait_recv()
        near_part = part_ref[at(index), cols(place)].astype(F32) + near_ref[high, at(index)].astype(F32)
        return near_part + far_ref[at(index)].astype(F32)

    def finish(index):
        pair(index, 0).wait_send()
        pair(index, 1).wait_send()
        across(index).wait_send()

    return at, cols, start_pair, pass_on, own_sum, finish


def head_scatter_scratch(tokens, columns, steps):
    return [
        pltpu.VMEM((2, tokens, columns), BF),
        pltpu.VMEM((tokens, columns), BF),
        pltpu.VMEM((tokens, columns), BF),
        pltpu.SemaphoreType.DMA((2, steps)),
        pltpu.SemaphoreType.DMA((2, steps)),
        pltpu.SemaphoreType.DMA((steps,)),
        pltpu.SemaphoreType.DMA((steps,)),
    ]


def final_kernel(
    members,
    chunk,
    rows_ref,
    dpre_ref,
    pack_hbm,
    input_hbm,
    scale_hbm,
    gain_ref,
    dmid_hbm,
    head_part_ref,
    second_part_ref,
    taps_part_ref,
    rest_ref,
    ingrad_ref,
    piece_ref,
    sums_ref,
    total_ref,
    pack_ref,
    input_ref,
    scale_ref,
    dmid_ref,
    load_sem,
    acc_ref,
    out_ref,
    slots_ref,
    part_ref,
    near_ref,
    send_ref,
    far_ref,
    near_send,
    near_recv,
    far_send,
    far_recv,
    stat_ref,
    stat_slots,
    small_slots,
    piece_send,
    piece_recv,
    stat_send,
    stat_recv,
    small_send,
    small_recv,
    rest_relay,
    rest_slots,
    rest_send,
    rest_recv,
):
    tokens, width = input_ref.shape
    steps = tokens // chunk
    loads = [
        pltpu.make_async_copy(source, target, load_sem.at[number])
        for number, (source, target) in enumerate(
            ((pack_hbm, pack_ref), (input_hbm, input_ref), (scale_hbm, scale_ref), (dmid_hbm, dmid_ref))
        )
    ]
    for load in loads:
        load.start()
    place, low, near, far = head_peers()
    member = lax.axis_index("seq")
    rows = width // members
    stages = (members - 1).bit_length()
    at, cols, start_pair, pass_on, own_sum, finish = head_scatter_copies(
        chunk, part_ref, near_ref, send_ref, far_ref, (near_send, near_recv, far_send, far_recv)
    )

    barrier = pltpu.get_barrier_semaphore()
    opposite = near + far - place
    for target in (near, far, opposite):
        pl.semaphore_signal(barrier, inc=1, device_id={"head": target}, device_id_type=MESH)
    for stage in range(stages):
        pl.semaphore_signal(barrier, inc=1, device_id={"seq": flip(member, 1 << stage)}, device_id_type=MESH)
    begin, rest_receive, rest_jobs, rest_end = piece_scatter(
        rest_ref, rest_relay, rest_slots, total_ref, rest_send, rest_recv, members
    )
    pl.semaphore_wait(barrier, 3 + stages)
    order = sorted(range(members), key=lambda r: zeros_below(r) if r else stages)
    sent = [r for r in order if r]
    events = {}
    for r in order:
        for stage in range(zeros_below(r) if r else stages):
            events[stage, r] = len(events)

    def give(r):
        stage = zeros_below(r)
        slot = events[stage, r ^ (1 << stage)]
        return push(
            out_ref.at[r],
            slots_ref.at[slot],
            piece_send.at[r],
            piece_recv.at[slot],
            "seq",
            flip(member, 1 << stage),
        )

    def take(stage, r):
        slot = events[stage, r]
        return push(
            out_ref.at[0], slots_ref.at[slot], piece_send.at[0], piece_recv.at[slot], "seq", flip(member, 1 << stage)
        )

    def send_piece(r):
        out_ref[r] = acc_ref[flip(member, r)].astype(BF)
        give(r).start()

    def receive(r):
        index = flip(member, r)
        for stage in range(zeros_below(r) if r else stages):
            take(stage, r).wait_recv()
            acc_ref[index] += slots_ref[events[stage, r]].astype(F32)
        if r:
            send_piece(r)

    first = sorted([r for r in range(members) if r % 2], key=lambda r: order.index(r ^ 1))
    evens = [r for r in order if r % 2 == 0]
    if rows % 128 == 0:
        for r in first:
            even = 2 * lax.div(flip(member, r), 2)
            columns = pl.ds(pl.multiple_of(even * rows, 128), 2 * rows)
            block = tn(rows_ref[:, columns], dpre_ref[...])
            acc_ref[even] = block[:rows]
            acc_ref[even + 1] = block[rows:]
            send_piece(r)
        begin()
    else:
        per = 128 // rows
        for unit in range(width // 128):
            block = tn(rows_ref[:, unit * 128 : (unit + 1) * 128], dpre_ref[...])
            acc_ref[unit * per : (unit + 1) * per] = block.reshape(per, rows, block.shape[1])
        for r in first:
            send_piece(r)
        begin()

    small_slots[0] = jnp.zeros_like(small_slots[0])
    small_slots[0, 1:2, :CHUNK] = jnp.sum(head_part_ref[...], 0, keepdims=True)
    small_slots[0, 8:9] = jnp.sum(second_part_ref[...], 0, keepdims=True)
    columns3 = taps_part_ref.shape[2]
    for tap in range(4):
        taps_sum = jnp.sum(taps_part_ref[tap], 0, keepdims=True)
        for block in range(3):
            flat = tap * columns3 + block * (columns3 // 3)
            line, lane = 9 + flat // width, flat % width
            small_slots[0, line : line + 1, lane : lane + columns3 // 3] = taps_sum[
                :, block * (columns3 // 3) : (block + 1) * (columns3 // 3)
            ]
    for load in loads:
        load.wait()
    diagonal = lax.broadcasted_iota(jnp.int32, (128, 128), 0) == lax.broadcasted_iota(jnp.int32, (128, 128), 1)

    def project(index):
        part = nt(dpre_ref[at(index)], pack_ref[...])
        part_ref[at(index)] = part.astype(BF)
        start_pair(index)
        seen = part * (input_ref[at(index)].astype(F32) * scale_ref[at(index)])
        small_slots[0, 0:1] += jnp.sum(seen, 0, keepdims=True)
        stat = jnp.sum(seen * gain_ref[0:1], axis=-1, keepdims=True)
        for block in range(chunk // 128):
            line = jnp.where(diagonal, stat[block * 128 : (block + 1) * 128], 0.0)
            stat_ref[index * (chunk // 128) + block] = jnp.sum(line, 0, keepdims=True)

    early = steps // 2
    receives = list(evens)
    for half in range(2):

        @pl.loop(half * early, (half + 1) * early)
        def _(index):
            project(index)

            @pl.when(lax.rem(index, 2) == 1)
            def _():
                pass_on(lax.div(index, 2))

        if len(receives) > 1:
            receive(receives.pop(0))

    def stat_copy(turn):
        target = (near, far, opposite)[turn]
        return push(stat_ref, stat_slots.at[turn], stat_send.at[turn], stat_recv.at[turn], "head", target)

    def head_copy(turn):
        target = (near, far, opposite)[turn]
        return push(
            small_slots.at[0, pl.ds(0, 8)],
            small_slots.at[1 + turn, pl.ds(0, 8)],
            small_send.at[turn],
            small_recv.at[turn],
            "head",
            target,
        )

    for turn in (1, 2, 0):
        head_copy(turn).start()
        stat_copy(turn).start()
    for index in range(early, steps):
        pass_on(index)
    while len(receives) > 1:
        receive(receives.pop(0))
    for turn in range(3):
        head_copy(turn).wait()
    small_slots[4] = small_slots[0]
    small_slots[4, 0:8] += small_slots[1, 0:8] + small_slots[2, 0:8] + small_slots[3, 0:8]

    bits = list(range(1, stages)) + [0]

    def seq_copy(turn):
        return push(
            small_slots.at[4 + 2 * turn],
            small_slots.at[5 + 2 * turn],
            small_send.at[3 + turn],
            small_recv.at[3 + turn],
            "seq",
            flip(member, 1 << bits[turn]),
        )

    def seq_add(turn):
        seq_copy(turn).wait()
        small_slots[6 + 2 * turn] = small_slots[4 + 2 * turn] + small_slots[5 + 2 * turn]

    seq_copy(0).start()
    for turn in range(3):
        stat_copy(turn).wait()
    stat_ref[...] += stat_slots[0] + stat_slots[1] + stat_slots[2]

    def result(index):
        grad = own_sum(index)
        scale = scale_ref[at(index)]
        unit = input_ref[at(index), cols(place)].astype(F32) * scale
        means = []
        for block in range(chunk // 128):
            line = jnp.where(diagonal, stat_ref[index * (chunk // 128) + block], 0.0)
            means.append(jnp.sum(line, axis=-1, keepdims=True))
        mean = jnp.concatenate(means, 0) * (1.0 / width)
        ingrad_ref[at(index)] = dmid_ref[at(index)] + scale * (grad * gain_ref[0:1, cols(place)] - unit * mean)

    rests = list(rest_jobs)
    for turn in range(stages):
        start, stop = turn * steps // stages, (turn + 1) * steps // stages
        if stop > start:

            @pl.loop(start, stop)
            def _(index):
                result(index)

        share = (len(rests) - 1) // (stages - turn)
        for job in rests[:share]:
            rest_receive(*job)
        rests = rests[share:]
        seq_add(turn)
        if turn + 1 < stages:
            seq_copy(turn + 1).start()
    receive(0)
    for job in rests:
        rest_receive(*job)
    piece_ref[...] = acc_ref[member]
    sums_ref[...] = small_slots[4 + 2 * stages]

    @pl.loop(0, steps)
    def _(index):
        finish(index)

    for r in sent:
        give(r).wait_send()
    rest_end()


def final_stage(first_rows, dpre, pack, inputs, scale, gain, dmid, parts, rest, members, collective):
    tokens, width = inputs.shape
    columns = dmid.shape[1]
    chunk = 256
    steps = tokens // chunk
    stages = (members - 1).bit_length()
    rows = width // members
    wide = dpre.shape[1]
    whole, outside = pl.BlockSpec(memory_space=pltpu.VMEM), pl.BlockSpec(memory_space=pl.ANY)
    return pl.pallas_call(
        functools.partial(final_kernel, members, chunk),
        name="final",
        out_shape=(
            jax.ShapeDtypeStruct((tokens, columns), F32),
            jax.ShapeDtypeStruct((rows, wide), F32),
            jax.ShapeDtypeStruct((16, width), F32),
            jax.ShapeDtypeStruct((rest.shape[0], *rest.shape[2:]), F32),
        ),
        in_specs=[whole, whole, outside, outside, outside, whole, outside] + [whole] * 4,
        out_specs=(whole,) * 4,
        scratch_shapes=[pltpu.VMEM(a.shape, a.dtype) for a in (pack, inputs, scale, dmid)]
        + [
            pltpu.SemaphoreType.DMA((4,)),
            pltpu.VMEM((members, rows, wide), F32),
            pltpu.VMEM((members, rows, wide), BF),
            pltpu.VMEM((members - 1, rows, wide), BF),
            pltpu.VMEM((tokens, width), BF),
        ]
        + head_scatter_scratch(tokens, columns, steps)
        + [
            pltpu.VMEM((tokens // 128, 1, 128), F32),
            pltpu.VMEM((3, tokens // 128, 1, 128), F32),
            pltpu.VMEM((5 + 2 * stages, 16, width), F32),
            pltpu.SemaphoreType.DMA((members,)),
            pltpu.SemaphoreType.DMA((members - 1,)),
            pltpu.SemaphoreType.DMA((3,)),
            pltpu.SemaphoreType.DMA((3,)),
            pltpu.SemaphoreType.DMA((3 + stages,)),
            pltpu.SemaphoreType.DMA((3 + stages,)),
        ]
        + piece_scatter_scratch(rest.shape[0], members, rest.shape[2:]),
        compiler_params=pltpu.CompilerParams(
            collective_id=collective, has_side_effects=True, vmem_limit_bytes=VMEM_LIMIT
        ),
        cost_estimate=pl.CostEstimate(flops=8 * 10**9, bytes_accessed=30 << 20, transcendentals=0),
    )(first_rows, dpre, pack, inputs, scale, gain, dmid, *parts, rest)


def finish_kernel(
    hidden,
    block_ref,
    ingrad_ref,
    piece_ref,
    sums_ref,
    first_ref,
    second_ref,
    third_ref,
    block_out,
    ingrad_out,
    first_gain_out,
    query_out,
    key_out,
    value_out,
    beta_out,
    conv_out,
    head_gain_out,
    output_out,
    second_gain_out,
    gate_out,
    up_out,
    down_out,
    turn_ref,
    strip_ref,
    sems,
):
    rows, columns = query_out.shape
    member = lax.axis_index("seq")
    pieces = [(block_ref, block_out), (ingrad_ref, ingrad_out)]
    for kind, target in enumerate((query_out, key_out, value_out)):
        pieces.append((piece_ref.at[:, pl.ds(kind * columns, columns)], target))
    pieces.append((piece_ref.at[:, pl.ds(3 * columns, CHUNK)], strip_ref))
    spans = []
    place = 0
    for source in (first_ref, second_ref, third_ref):
        for part in range(2):
            spans.append((place, source, part))
            place += source.shape[1]
    goal = 0
    for target, count in ((gate_out, hidden), (up_out, hidden), (down_out, hidden), (turn_ref, columns)):
        for begin, source, part in spans:
            low, high = max(begin, goal), min(begin + source.shape[1], goal + count)
            if low < high:
                pieces.append(
                    (source.at[part, pl.ds(low - begin, high - low)], target.at[pl.ds(low - goal, high - low)])
                )
        goal += count
    copies = [pltpu.make_async_copy(source, target, sems.at[number]) for number, (source, target) in enumerate(pieces)]
    for copy in copies:
        copy.start()
    window = pl.ds(pl.multiple_of(member * rows, 128), rows)
    first_gain_out[...] = sums_ref[0:1, window]
    second_gain_out[...] = sums_ref[8:9, window]
    head_gain_out[...] = sums_ref[1:2, :CHUNK]
    width = sums_ref.shape[1]
    for kind in range(3):
        for tap in range(4):
            flat = (3 * tap + kind) * columns
            line, lane = 9 + flat // width, flat % width
            conv_out[kind, tap : tap + 1] = sums_ref[line : line + 1, lane : lane + columns]
    for copy in copies:
        copy.wait()
    output_out[...] = turn_ref[...].T
    beta_out[...] = strip_ref[...].T[: beta_out.shape[0]]


def finish_stage(block, ingrad, piece, sums, first, second, third, hidden, heads):
    tokens, columns = ingrad.shape
    rows = piece.shape[0]
    whole, outside = pl.BlockSpec(memory_space=pltpu.VMEM), pl.BlockSpec(memory_space=pl.ANY)

    def made(*shape):
        return jax.ShapeDtypeStruct(shape, F32)

    return pl.pallas_call(
        functools.partial(finish_kernel, hidden),
        name="finish",
        out_shape=(
            jax.ShapeDtypeStruct((tokens, columns), BF),
            made(tokens, columns),
            made(1, rows),
            made(rows, columns),
            made(rows, columns),
            made(rows, columns),
            made(heads, rows),
            made(3, 4, columns),
            made(1, CHUNK),
            made(rows, columns),
            made(1, rows),
            made(hidden, rows),
            made(hidden, rows),
            made(hidden, rows),
        ),
        in_specs=[outside] * 3 + [whole] + [outside] * 3,
        out_specs=(outside,) * 2
        + (whole,)
        + (outside,) * 3
        + (whole,) * 5
        + (outside,) * 3,
        scratch_shapes=[
            pltpu.VMEM((columns, rows), F32),
            pltpu.VMEM((rows, CHUNK), F32),
            pltpu.SemaphoreType.DMA((24,)),
        ],
        compiler_params=pltpu.CompilerParams(vmem_limit_bytes=VMEM_LIMIT),
        cost_estimate=pl.CostEstimate(flops=0, bytes_accessed=12 << 20, transcendentals=0),
    )(block, ingrad, piece, sums, first, second, third)
def turn_column(column):
    diagonal = lax.broadcasted_iota(jnp.int32, (128, 128), 0) == lax.broadcasted_iota(jnp.int32, (128, 128), 1)
    lines = []
    for block in range(column.shape[0] // 128):
        lines.append(jnp.sum(jnp.where(diagonal, column[block * 128 : (block + 1) * 128], 0.0), 0, keepdims=True))
    return jnp.concatenate(lines, 1)


def piece_gather(full_ref, send, recv, members):
    member = lax.axis_index("seq")
    parts = full_ref.shape[0]
    stages = (members - 1).bit_length()

    def give(part, r, stage):
        owner = flip(member, r)
        mark = r ^ (1 << stage)
        return push(
            full_ref.at[part, owner],
            full_ref.at[part, owner],
            send.at[part, mark],
            recv.at[part, mark],
            "seq",
            flip(member, 1 << stage),
        )

    def take(part, r):
        owner = flip(member, r)
        return push(
            full_ref.at[part, owner],
            full_ref.at[part, owner],
            send.at[part, r],
            recv.at[part, r],
            "seq",
            flip(member, r & -r),
        )

    def begin(part=0, levels=None):
        for stage in reversed(range(stages)) if levels is None else levels:
            give(part, 0, stage).start()

    def relay(part, r):
        take(part, r).wait_recv()
        for stage in reversed(range(zeros_below(r))):
            give(part, r, stage).start()
        if r == 1 << (stages - 1) and part + 1 < parts:
            begin(part + 1)

    order = sorted([r for r in range(1, members) if r % 2 == 0], key=lambda r: (-zeros_below(r), r))
    def when(part, r):
        return 2 * part + 3 * (bin(r).count("1") - 1), part, -zeros_below(r), r

    relays = sorted([(part, r) for r in order for part in range(parts)], key=lambda job: when(*job))

    def arrive():
        for part in range(parts):
            for r in range(1, members, 2):
                take(part, r).wait_recv()

    def finish():
        for part in range(parts):
            for r in [0] + order:
                for stage in range(zeros_below(r) if r else stages):
                    give(part, r, stage).wait_send()

    return begin, relay, relays, arrive, finish


def greet_seq(members):
    member = lax.axis_index("seq")
    stages = (members - 1).bit_length()
    barrier = pltpu.get_barrier_semaphore()
    for stage in range(stages):
        pl.semaphore_signal(barrier, inc=1, device_id={"seq": flip(member, 1 << stage)}, device_id_type=MESH)
    return barrier, stages


FRONT_REFS = 64


def front_kernel(
    members,
    heads,
    lengths_ref,
    input_ref,
    query_ref,
    key_ref,
    value_ref,
    beta_ref,
    first_gain_ref,
    second_gain_ref,
    out_weight_ref,
    conv_ref,
    head_gain_ref,
    *refs,
):
    own_refs, refs = refs[:-FRONT_REFS], refs[-FRONT_REFS:]
    front_body(
        members,
        heads,
        lengths_ref,
        input_ref,
        query_ref,
        key_ref,
        value_ref,
        beta_ref,
        first_gain_ref,
        second_gain_ref,
        out_weight_ref,
        conv_ref,
        head_gain_ref,
        own_refs,
        *refs,
    )


def front_body(
    members,
    heads,
    lengths_ref,
    input_ref,
    query_ref,
    key_ref,
    value_ref,
    beta_ref,
    first_gain_ref,
    second_gain_ref,
    out_weight_ref,
    conv_ref,
    head_gain_ref,
    own_refs,
    pack_hbm,
    first_hbm,
    pre_hbm,
    logits_hbm,
    halo_ref,
    scale_hbm,
    gains_ref,
    turned_hbm,
    full_hbm,
    others_hbm,
    qkv_hbm,
    inv_hbm,
    wu_hbm,
    mq_hbm,
    total_ref,
    delta_hbm,
    rows_hbm,
    far_rows_hbm,
    states_hbm,
    pack_ref,
    first_ref,
    pre_ref,
    logits_ref,
    scale_ref,
    turned_ref,
    full_ref,
    others_ref,
    qkv_ref,
    inv_ref,
    wu_ref,
    mq_ref,
    delta_ref,
    rows_ref,
    far_rows_ref,
    states_ref,
    store_sem,
    resets_ref,
    taps_ref,
    extra_ref,
    start_ref,
    out0_ref,
    state_ref,
    part_ref,
    slots_ref,
    pad_ref,
    edge_ref,
    pack_send,
    pack_recv,
    edge_send,
    edge_recv,
    turned_send,
    turned_recv,
    full_send,
    full_recv,
    head_send,
    head_recv,
    state_send,
    state_recv,
    row_near_send,
    row_near_recv,
    row_far_send,
    row_far_recv,
    row_pass_send,
    row_pass_recv,
):
    tokens, width = input_ref.shape
    columns = heads * CHUNK
    leaving = (
        (pack_ref, pack_hbm),
        (first_ref, first_hbm),
        (pre_ref, pre_hbm),
        (logits_ref, logits_hbm),
        (scale_ref, scale_hbm),
        (turned_ref, turned_hbm),
        (qkv_ref, qkv_hbm),
        (inv_ref, inv_hbm),
        (wu_ref, wu_hbm),
        (mq_ref, mq_hbm),
        (delta_ref, delta_hbm),
        (rows_ref, rows_hbm),
        (states_ref, states_hbm),
        (others_ref, others_hbm),
        (far_rows_ref, far_rows_hbm),
        (full_ref, full_hbm),
    )

    def store(number):
        return pltpu.make_async_copy(*leaving[number], store_sem.at[number])

    member = lax.axis_index("seq")
    _, _, near, far = head_peers()
    barrier, stages = greet_seq(members)
    for target in (near, far):
        pl.semaphore_signal(barrier, inc=1, device_id={"head": target}, device_id_type=MESH)

    @pl.when(member > 0)
    def _():
        pl.semaphore_signal(barrier, inc=1, device_id={"seq": member - 1}, device_id_type=MESH)

    window = slots_ref.shape[0]
    behind = members - 1 - member
    for hop in range(1, window + 1):

        @pl.when(member >= hop)
        def _():
            pl.semaphore_signal(barrier, inc=1, device_id={"seq": member - hop}, device_id_type=MESH)

    def state_copy(hop):
        return push(
            part_ref, slots_ref.at[hop - 1], state_send.at[hop - 1], state_recv.at[hop - 1], "seq", member + hop
        )

    pack_ref[0, member, :, :columns] = query_ref[...]
    pack_ref[0, member, :, columns : 2 * columns] = key_ref[...]
    pack_ref[0, member, :, 2 * columns : 3 * columns] = value_ref[...]
    extra_ref[...] = jnp.zeros_like(extra_ref)
    extra_ref[0:heads] = beta_ref[...].astype(F32)
    extra_ref[heads : heads + 1] = first_gain_ref[...].astype(F32)
    extra_ref[heads + 1 : heads + 2] = second_gain_ref[...].astype(F32)
    pack_ref[0, member, :, 3 * columns :] = extra_ref[...].T.astype(BF)
    turned_ref[0, member] = out_weight_ref[...].T
    for part, own_ref in enumerate(own_refs):
        full_ref[part, member] = own_ref[...]
    pack = piece_gather(pack_ref, pack_send, pack_recv, members)
    turned = piece_gather(turned_ref, turned_send, turned_recv, members)
    full = piece_gather(full_ref, full_send, full_recv, members)
    near_copy = push(turned_ref.at[0], others_ref.at[0], head_send.at[0], head_recv.at[0], "head", near)
    far_copy = push(turned_ref.at[0], others_ref.at[1], head_send.at[1], head_recv.at[1], "head", far)
    pass_copy = push(others_ref.at[1], others_ref.at[2], head_send.at[2], head_recv.at[2], "head", near)
    pl.semaphore_wait(barrier, stages + 2 + jnp.minimum(behind, 1) + jnp.minimum(behind, window))
    pack[0]()
    turned[0]()
    full[0](0, [stages - 1, 0])
    fill_resets(lengths_ref, resets_ref, tokens)
    fill_taps(conv_ref, taps_ref)

    last_rows = pl.ds(tokens - 16, 16)

    def edge(target):
        return push(input_ref.at[last_rows], edge_ref, edge_send, edge_recv, "seq", target)

    @pl.when(member + 1 < members)
    def _():
        edge(member + 1).start()

    chunk = 256

    def at(index):
        return pl.ds(pl.multiple_of(index * chunk, chunk), chunk)

    def measure(index):
        block = input_ref[at(index)].astype(F32)
        scale_ref[at(index)] = lax.rsqrt(jnp.mean(block * block, axis=-1, keepdims=True) + 1e-06)

    pl.loop(0, tokens // chunk)(measure)
    for job in pack[2]:
        pack[1](*job)
    for job in turned[2]:
        turned[1](*job)
    full[0](0, range(1, stages - 1))
    pack[3]()
    projection = pack_ref[0].reshape(width, pack_ref.shape[3])
    extras = projection[:, 3 * columns :].astype(F32)
    gains_ref[0:1] = turn_column(extras[:, heads : heads + 1])
    gains_ref[1:2] = turn_column(extras[:, heads + 1 : heads + 2])

    def project(index):
        first = (input_ref[at(index)].astype(F32) * scale_ref[at(index)] * gains_ref[0:1]).astype(BF)
        first_ref[at(index)] = first
        both = nn(first, pack_ref[0].reshape(width, pack_ref.shape[3]))
        pre_ref[at(index)] = both[:, : 3 * columns].astype(BF)
        logits_ref[at(index)] = both[:, 3 * columns :]

    pl.loop(0, tokens // chunk)(project)

    @pl.when(member == 0)
    def _():
        halo_ref[...] = jnp.zeros_like(halo_ref)

    @pl.when(member > 0)
    def _():
        edge(member).wait_recv()
        block = edge_ref[...].astype(F32)
        scale = lax.rsqrt(jnp.mean(block * block, axis=-1, keepdims=True) + 1e-06)
        first = (block * scale * gains_ref[0:1]).astype(BF)
        halo_ref[...] = nn(first, pack_ref[0].reshape(width, pack_ref.shape[3])[:, : 3 * columns]).astype(BF)

    turned[3]()
    for number in range(6):
        store(number).start()
    near_copy.start()
    far_copy.start()
    rows, cols = grid_indices()
    eye = jnp.where(rows == cols, 1.0, 0.0)
    top = lax.broadcasted_iota(jnp.int32, (CHUNK, 1), 0) < GROUP
    for head in range(heads):
        total_ref[head] = side(eye, jnp.zeros_like(eye))
    batch = pad_ref.shape[0]

    def one(step, carry):
        units = []
        for lane in range(batch):
            chunk = step * batch + lane
            pad = pad_ref.at[lane]
            load_padded(pad, pre_ref, halo_ref, chunk, resets_ref)
            mixed = convolve(pad, taps_ref)
            silued = mixed * sigmoid(mixed)
            keep0 = 1.0 - resets_ref[2 * chunk]
            keep1 = 1.0 - resets_ref[2 * chunk + 1]
            both = keep0 * keep1
            enter = jnp.where(top, keep0, both)
            leave = jnp.where(top, keep1, 1.0)
            at = pl.ds(pl.multiple_of(chunk * CHUNK, CHUNK), CHUNK)
            beta_rows = sigmoid(logits_ref[at, :])
            for head in range(heads):
                window = slice(head * CHUNK, (head + 1) * CHUNK)
                parts = []
                for kind in range(3):
                    part = silued[:, kind * columns + head * CHUNK : kind * columns + (head + 1) * CHUNK]
                    if kind < 2:
                        part = part * lax.rsqrt(jnp.sum(part * part, axis=-1, keepdims=True) + 1e-06)
                    part = part.astype(BF)
                    qkv_ref[at, kind * columns + head * CHUNK : kind * columns + (head + 1) * CHUNK] = part
                    parts.append(part)
                units.append((chunk, head, *parts, beta_rows[:, head : head + 1], keep1, both, enter, leave))
        turned = [u[3].T for u in units]
        strict = [
            jnp.where(rows > cols, u[5] * nn(u[3], t), 0.0) for u, t in zip(units, turned)
        ]
        inverses = [r.astype(BF) for r in inverse_levels(strict, rows, cols, [u[6] for u in units])]
        factors = []
        for u, inverse in zip(units, inverses):
            beta = u[5]
            factors.append(nn(inverse, side(u[3].astype(F32) * beta, u[4].astype(F32) * beta)))
        for u, inverse, factor, t in zip(units, inverses, factors, turned):
            chunk, head, query, key, value, beta, keep1, both, enter, leave = u
            weight, update = factor[:, :CHUNK], factor[:, CHUNK:]
            entering_weight = weight * enter
            inv_ref[chunk, head] = inverse
            wu_ref[chunk, head] = side(entering_weight, update).astype(BF)
            gathered = nn(t, side(weight, update * leave))
            device_map = (both * (eye - gathered[:, :CHUNK])).astype(BF)
            shift = gathered[:, CHUNK:]
            scores = jnp.where(rows >= cols, nn(query, t), 0.0)
            scores = jnp.where((rows >= GROUP) & (cols < GROUP), scores * keep1, scores)
            seen = nn(scores, side(entering_weight, update))
            effective = query.astype(F32) * enter - seen[:, :CHUNK]
            mq_ref[chunk, head] = stack(device_map, effective.astype(BF))
            out0_ref[chunk, head] = seen[:, CHUNK:]
            running = total_ref[head]
            start_ref[chunk, head] = running.astype(BF)
            total_ref[head] = nn(device_map, running) + side(jnp.zeros_like(shift), shift)
        return carry

    count = resets_ref.shape[0] // 2 // batch
    held = 3 if len(full[2]) > 3 else 0
    relays = full[2][: len(full[2]) - held]

    def pumped(step, carry):
        carry = one(step, carry)
        for turn in range(count):
            jobs = [job for place, job in enumerate(relays) if place * count // len(relays) == turn]
            if not jobs and turn != count // 2:
                continue

            @pl.when(step == turn)
            def _():
                for job in jobs:
                    full[1](*job)
                if turn == count // 2:
                    far_copy.wait_recv()
                    pass_copy.start()

        return carry

    lax.fori_loop(0, count, pumped, 0)
    for number in range(6, 10):
        store(number).start()
    part_ref[...] = total_ref[...].astype(BF)
    for hop in range(1, window + 1):

        @pl.when(behind >= hop)
        def _():
            state_copy(hop).start()

    for job in full[2][len(full[2]) - held :]:
        full[1](*job)
    state_ref[...] = jnp.zeros_like(state_ref)
    for hop in range(window, 0, -1):

        @pl.when(member >= hop)
        def _():
            state_copy(hop).wait_recv()
            for head in range(heads):
                part = slots_ref[hop - 1, head]
                state_ref[head] = nn(part[:, :CHUNK], state_ref[head]) + part[:, CHUNK:].astype(F32)

    def near_rows(index):
        return push(
            rows_ref.at[at(index)], far_rows_ref.at[0, at(index)], row_near_send.at[index], row_near_recv.at[index], "head", near
        )

    def far_rows(index):
        return push(
            rows_ref.at[at(index)], far_rows_ref.at[1, at(index)], row_far_send.at[index], row_far_recv.at[index], "head", far
        )

    def pass_rows(index):
        return push(
            far_rows_ref.at[1, at(index)], far_rows_ref.at[2, at(index)], row_pass_send.at[index], row_pass_recv.at[index], "head", near
        )

    def finished(index):
        for lane in range(chunk // CHUNK):
            place_ = index * (chunk // CHUNK) + lane
            rows_at = pl.ds(pl.multiple_of(place_ * CHUNK, CHUNK), CHUNK)
            begins = [start_ref[place_, head] for head in range(heads)]
            states = [
                (nn(begins[head][:, :CHUNK], state_ref[head]) + begins[head][:, CHUNK:].astype(F32)).astype(BF)
                for head in range(heads)
            ]
            outs = [out0_ref[place_, head] + nn(mq_ref[place_, head, CHUNK:], states[head]) for head in range(heads)]
            for head in range(heads):
                lanes = slice(head * CHUNK, (head + 1) * CHUNK)
                states_ref[place_, head] = states[head]
                delta_ref[rows_at, lanes] = outs[head]
                scale = lax.rsqrt(jnp.mean(outs[head] * outs[head], axis=-1, keepdims=True) + 1e-05)
                rows_ref[rows_at, lanes] = (outs[head] * scale * head_gain_ref[...]).astype(BF)
        far_rows(index).start()
        near_rows(index).start()

    pl.loop(0, tokens // chunk)(finished)
    for number in range(10, 13):
        store(number).start()

    @pl.loop(0, tokens // chunk)
    def _(index):
        far_rows(index).wait_recv()
        pass_rows(index).start()

    near_copy.wait()
    far_copy.wait_send()
    pass_copy.wait()
    store(13).start()

    @pl.when(member + 1 < members)
    def _():
        edge(member + 1).wait_send()

    for hop in range(1, window + 1):

        @pl.when(behind >= hop)
        def _():
            state_copy(hop).wait_send()

    @pl.loop(0, tokens // chunk)
    def _(index):
        near_rows(index).wait()
        far_rows(index).wait_send()
        pass_rows(index).wait()

    store(14).start()
    full[3]()
    store(15).start()
    for gather in (pack, turned, full):
        gather[4]()
    for number in range(len(leaving)):
        store(number).wait()


def front_stage(lengths, inputs, mixer_weights, conv, head_gain, own, members, heads, collective):
    tokens, width = inputs.shape
    columns = heads * CHUNK
    chunks = tokens // CHUNK
    whole = pl.BlockSpec(memory_space=pltpu.VMEM)
    piece = width // members
    window = min(members - 1, members // 2)

    def units(wide, kind):
        return jax.ShapeDtypeStruct((chunks, heads, *wide), kind)

    def dma(*shape):
        return [pltpu.SemaphoreType.DMA(shape)] * 2

    outside = pl.BlockSpec(memory_space=pl.ANY)
    made = (
        jax.ShapeDtypeStruct((1, members, piece, 3 * columns + CHUNK), BF),
        jax.ShapeDtypeStruct((tokens, width), BF),
        jax.ShapeDtypeStruct((tokens, 3 * columns), BF),
        jax.ShapeDtypeStruct((tokens, CHUNK), F32),
        jax.ShapeDtypeStruct((16, 3 * columns), BF),
        jax.ShapeDtypeStruct((tokens, 1), F32),
        jax.ShapeDtypeStruct((2, width), F32),
        jax.ShapeDtypeStruct((1, members, columns, piece), BF),
        jax.ShapeDtypeStruct((len(own), members, *own[0].shape), BF),
        jax.ShapeDtypeStruct((3, members, columns, piece), BF),
        jax.ShapeDtypeStruct((tokens, 3 * columns), BF),
        units((CHUNK, CHUNK), BF),
        units((CHUNK, 2 * CHUNK), BF),
        units((2 * CHUNK, CHUNK), BF),
        jax.ShapeDtypeStruct((heads, CHUNK, 2 * CHUNK), F32),
        jax.ShapeDtypeStruct((tokens, columns), F32),
        jax.ShapeDtypeStruct((tokens, columns), BF),
        jax.ShapeDtypeStruct((3, tokens, columns), BF),
        units((CHUNK, CHUNK), BF),
    )
    stay = (4, 6, 14)
    return pl.pallas_call(
        functools.partial(front_kernel, members, heads),
        name="front",
        out_shape=made,
        in_specs=[pl.BlockSpec(memory_space=pltpu.SMEM)] + [whole] * (3 + len(mixer_weights) + len(own)),
        out_specs=tuple(whole if number in stay else outside for number in range(len(made))),
        scratch_shapes=[pltpu.VMEM(a.shape, a.dtype) for number, a in enumerate(made) if number not in stay]
        + [
            pltpu.SemaphoreType.DMA((len(made) - len(stay),)),
            pltpu.SMEM((tokens // GROUP,), F32),
            pltpu.VMEM((4, 3 * columns), F32),
            pltpu.VMEM((CHUNK, piece), F32),
            pltpu.VMEM((chunks, heads, CHUNK, 2 * CHUNK), BF),
            pltpu.VMEM((chunks, heads, CHUNK, CHUNK), F32),
            pltpu.VMEM((heads, CHUNK, CHUNK), F32),
            pltpu.VMEM((heads, CHUNK, 2 * CHUNK), BF),
            pltpu.VMEM((window, heads, CHUNK, 2 * CHUNK), BF),
            pltpu.VMEM((2, 144, 3 * columns), F32),
            pltpu.VMEM((16, width), BF),
        ]
        + dma(1, members)
        + dma()
        + dma(1, members)
        + dma(len(own), members)
        + dma(3)
        + dma(window)
        + dma(tokens // 256) * 3,
        compiler_params=pltpu.CompilerParams(
            collective_id=collective, has_side_effects=True, vmem_limit_bytes=VMEM_LIMIT
        ),
        cost_estimate=pl.CostEstimate(flops=8 * 10**9, bytes_accessed=40 << 20, transcendentals=2 << 20),
    )(lengths, inputs, *mixer_weights, conv, head_gain, *own)


def lanes_whole(pieces):
    places, rows, piece = pieces.shape
    if piece >= 128:
        return pieces
    group = 128 // piece
    return pieces.reshape(places // group, group, rows, piece).transpose(0, 2, 1, 3).reshape(places // group, rows, 128)


def lanes_split(blocks, piece):
    count, rows, lanes = blocks.shape
    if piece >= 128:
        return blocks
    group = 128 // piece
    return blocks.reshape(count, rows, group, piece).transpose(0, 2, 1, 3).reshape(count * group, rows, piece)


def body(
    block_input,
    first_gain,
    query_weight,
    key_weight,
    value_weight,
    beta_weight,
    conv_weight,
    head_gain,
    output_weight,
    second_gain,
    gate_weight,
    up_weight,
    down_weight,
    lengths,
    cotangent,
):
    tokens, width = block_input.shape
    heads = beta_weight.shape[1]
    columns = query_weight.shape[1]
    hidden_columns = gate_weight.shape[1]
    members = lax.axis_size("seq")
    piece = width // members
    seq_place = lax.axis_index("seq")

    gain_head = head_gain.astype(F32)[None, :]
    own = [gate_weight.T, up_weight.T, down_weight.T]
    split = piece < 128
    (
        mixer_pack,
        first_rows,
        pre,
        logits,
        halo,
        scale_one,
        gains,
        turned,
        full,
        others,
        qkv,
        inv,
        wu,
        mq,
        total,
        delta,
        head_rows,
        far_rows,
        states,
    ) = front_stage(
        lengths,
        block_input,
        (
            query_weight,
            key_weight,
            value_weight,
            beta_weight.T,
            first_gain[None, :],
            second_gain[None, :],
            output_weight,
        ),
        conv_weight,
        gain_head,
        [own[0][:16]] if split else own,
        members,
        heads,
        5,
    )
    mixer_pack = mixer_pack.reshape(width, -1)
    if split:
        gathered = lax.all_gather(jnp.stack(own), "seq", axis=1)
        full = jnp.stack([lanes_whole(gathered[i]) for i in range(3)])
    turned = lanes_whole(turned[0])
    others = jnp.stack([lanes_whole(others[i]) for i in range(3)]) if split else others
    d_heads, update_part, middle_shard, d_middle_shard, *grads, second_grad = middle_stage(
        head_rows, far_rows, full, turned, others, block_input, cotangent, gains, 2
    )
    second_part = jnp.sum(second_grad, 0)
    if split:
        pieces = jnp.concatenate([part for pair in grads for part in pair], 1)
        whole_sum = lax.psum_scatter(lanes_split(pieces, piece), "seq", scatter_dimension=0, tiled=False).astype(F32)
        grads = [jnp.zeros((1, members, 16, 128), BF)] * 3
    ddelta, gain_part, arrive, block_output, third_sum = state_backward(
        d_heads, delta, gain_head, mq, total, update_part, middle_shard, grads[2], members, 1
    )
    d_pre, taps_part, first_sum = mixer_backward(
        lengths, pre, halo, conv_weight, logits, qkv, inv, wu, mq, states, ddelta, arrive, grads[0], 3
    )
    input_gradient, mixer_sum, sums, second_sum = final_stage(
        first_rows, d_pre, mixer_pack, block_input, scale_one, gains, d_middle_shard, (gain_part, second_grad, taps_part), grads[1], members, 4
    )
    if not split:
        done = finish_stage(
            block_output, input_gradient, mixer_sum, sums, first_sum, second_sum, third_sum, hidden_columns, heads
        )
        block, ingrad, gain_1, grad_q, grad_k, grad_v, grad_b, grad_c, gain_h, grad_o, gain_2, *rest = done
        return (
            block,
            ingrad,
            gain_1.reshape(-1),
            grad_q,
            grad_k,
            grad_v,
            grad_b.T,
            grad_c,
            gain_h.reshape(-1),
            grad_o,
            gain_2.reshape(-1),
            *(grad.T for grad in rest),
        )
    gain_sum = sums[1, :CHUNK]
    conv_gradient = sums[9 : 9 + 12 * columns // width].reshape(4, 3, columns).transpose(1, 0, 2)
    row_start = seq_place * piece
    first_gradient = lax.dynamic_slice_in_dim(sums[0], row_start, piece, 0)
    second_gradient = lax.dynamic_slice_in_dim(sums[8], row_start, piece, 0)
    beta_gradient = mixer_sum[:, 3 * columns : 3 * columns + heads]
    return (
        block_output,
        input_gradient,
        first_gradient,
        mixer_sum[:, :columns],
        mixer_sum[:, columns : 2 * columns],
        mixer_sum[:, 2 * columns : 3 * columns],
        beta_gradient,
        conv_gradient,
        gain_sum,
        whole_sum[3 * hidden_columns :].T,
        second_gradient,
        whole_sum[:hidden_columns].T,
        whole_sum[hidden_columns : 2 * hidden_columns].T,
        whole_sum[2 * hidden_columns : 3 * hidden_columns].T,
    )


def solution(mesh):
    return jax.shard_map(
        body,
        mesh=mesh,
        in_specs=(
            P("seq", None),
            P("seq"),
            P("seq", "head"),
            P("seq", "head"),
            P("seq", "head"),
            P("seq", "head"),
            P(None, None, "head"),
            P(),
            P("seq", "head"),
            P("seq"),
            P("seq", "head"),
            P("seq", "head"),
            P("seq", "head"),
            P(),
            P("seq", None),
        ),
        out_specs=(
            P("seq", "head"),
            P("seq", "head"),
            P("seq"),
            P("seq", "head"),
            P("seq", "head"),
            P("seq", "head"),
            P("seq", "head"),
            P(None, None, "head"),
            P(),
            P("seq", "head"),
            P("seq"),
            P("seq", "head"),
            P("seq", "head"),
            P("seq", "head"),
        ),
        check_vma=False,
    )
```

```python
import functools

import jax
import jax.numpy as jnp
from jax import lax
from jax.experimental import pallas as pl
from jax.experimental.pallas import tpu as pltpu
from jax.sharding import PartitionSpec as P

GROUP = 64
CHUNK = 128
MESH = pl.DeviceIdType.MESH
BF = jnp.bfloat16
F32 = jnp.float32
VMEM_LIMIT = 59 << 20


def nn(left, right):
    return jnp.dot(left.astype(BF), right.astype(BF), preferred_element_type=F32)


def tn(left, right):
    return lax.dot_general(
        left.astype(BF), right.astype(BF), (((0,), (0,)), ((), ())), preferred_element_type=F32
    )


def nt(left, right):
    return lax.dot_general(
        left.astype(BF), right.astype(BF), (((1,), (1,)), ((), ())), preferred_element_type=F32
    )


def sigmoid(v):
    return 0.5 * jnp.tanh(0.5 * v) + 0.5


def side(left, right):
    return jnp.concatenate([left, right], 1)


def stack(top, bottom):
    return jnp.concatenate([top, bottom], 0)


def grid_indices():
    rows = lax.broadcasted_iota(jnp.int32, (CHUNK, CHUNK), 0)
    cols = lax.broadcasted_iota(jnp.int32, (CHUNK, CHUNK), 1)
    return rows, cols


def fill_resets(lengths_ref, resets_ref, tokens):
    base = lax.axis_index("seq") * tokens

    @pl.loop(0, tokens // GROUP)
    def _(block):
        position = base + block * GROUP
        value = jnp.float32(0.0)
        start = jnp.int32(0)
        for index in range(lengths_ref.shape[0]):
            value = jnp.where(start == position, 1.0, value)
            start = start + lengths_ref[index]
        resets_ref[block] = value


def fill_taps(conv_ref, taps_ref):
    columns = conv_ref.shape[2]
    for kind in range(3):
        taps_ref[:, kind * columns : (kind + 1) * columns] = conv_ref[kind].astype(F32)


def load_padded(pad_ref, pre_ref, halo_ref, chunk, resets_ref):
    start = pl.multiple_of(chunk * CHUNK, CHUNK)
    before = pl.multiple_of(jnp.maximum(start - 16, 0), 16)
    own = pre_ref[pl.ds(start, CHUNK), :].astype(F32)
    earlier = pre_ref[pl.ds(before, 16), :].astype(F32)[8:]
    halo = halo_ref[...].astype(F32)[8:]
    first = jnp.where(chunk == 0, halo, earlier)
    keep0 = 1.0 - resets_ref[2 * chunk]
    keep1 = 1.0 - resets_ref[2 * chunk + 1]
    pad_ref[0:8] = first * keep0
    pad_ref[8:72] = own[:GROUP]
    pad_ref[72:80] = own[GROUP - 8 : GROUP] * keep1
    pad_ref[80:144] = own[GROUP:]


def tap_rows(pad_ref, tap):
    return stack(pad_ref[5 + tap : 69 + tap], pad_ref[77 + tap : 141 + tap])


def convolve(pad_ref, taps_ref):
    mixed = None
    for tap in range(4):
        term = taps_ref[tap : tap + 1] * tap_rows(pad_ref, tap)
        mixed = term if mixed is None else mixed + term
    return mixed


def inverse_levels(strict, rows, cols, keep1):
    eye = jnp.where(rows == cols, 1.0, 0.0)
    pair = (rows // 2) == (cols // 2)
    results = [eye - jnp.where(pair, a, 0.0) for a in strict]
    width = 2
    while width < CHUNK:
        off = ((rows // (2 * width)) == (cols // (2 * width))) & ((rows // width) != (cols // width))
        lows = [r.astype(BF) for r in results]
        parts = [jnp.where(off, a, 0.0).astype(BF) for a in strict]
        if width == GROUP:
            parts = [jnp.where(off, a * k, 0.0).astype(BF) for a, k in zip(strict, keep1)]
        steps = [nn(r, p) for r, p in zip(lows, parts)]
        results = [r - nn(s, low) for r, s, low in zip(results, steps, lows)]
        width *= 2
    return results


def state_backward_kernel(
    heads,
    window,
    dheads_ref,
    delta_ref,
    gain_ref,
    mq_ref,
    total_ref,
    update_ref,
    mid_ref,
    grads_ref,
    ddelta_ref,
    gain_grad_ref,
    state_ref,
    block_ref,
    sum_ref,
    shift_ref,
    part_ref,
    slots_ref,
    send_sem,
    recv_sem,
    near_ref,
    relay_ref,
    far_ref,
    near_send,
    near_recv,
    far_send,
    far_recv,
    piece_relay,
    piece_slots,
    piece_send,
    piece_recv,
):
    member, members = lax.axis_index("seq"), lax.axis_size("seq")
    _, _, near, far = head_peers()
    chunk = 256
    steps = update_ref.shape[0] // chunk
    chunks = mq_ref.shape[0]
    behind = members - 1 - member
    at, _, start_pair, pass_on, own_sum, finish = head_scatter_copies(
        chunk, update_ref, near_ref, relay_ref, far_ref, (near_send, near_recv, far_send, far_recv)
    )
    begin, receive, jobs, end = piece_scatter(
        grads_ref, piece_relay, piece_slots, sum_ref, piece_send, piece_recv, members
    )
    barrier, stages = greet_seq(members)
    for hop in range(1, window + 1):

        @pl.when(behind >= hop)
        def _():
            pl.semaphore_signal(barrier, inc=1, device_id={"seq": member + hop}, device_id_type=MESH)

    for target in (near, far):
        pl.semaphore_signal(barrier, inc=1, device_id={"head": target}, device_id_type=MESH)
    pl.semaphore_wait(barrier, stages + 2 + jnp.minimum(member, window))

    @pl.loop(0, steps)
    def _(index):
        start_pair(index)

    for head in range(heads):
        part_ref[0, head] = total_ref[head, :, :CHUNK].T.astype(BF)

    def copy(kind, hop):
        return push(
            part_ref.at[kind],
            slots_ref.at[kind, hop - 1],
            send_sem.at[kind, hop - 1],
            recv_sem.at[kind, hop - 1],
            "seq",
            member - hop,
        )

    def send(kind):
        for hop in range(1, window + 1):

            @pl.when(member >= hop)
            def _():
                copy(kind, hop).start()

    send(0)
    half = len(jobs) // 4
    begin(jobs[:half])
    shift_ref[...] = jnp.zeros_like(shift_ref)
    gain_grad_ref[...] = jnp.zeros_like(gain_grad_ref)

    def one(step, carry):
        index = chunks - 1 - step
        rows = pl.ds(pl.multiple_of(index * CHUNK, CHUNK), CHUNK)
        for head in range(heads):
            lanes = slice(head * CHUNK, (head + 1) * CHUNK)
            out = delta_ref[rows, lanes]
            grad = dheads_ref[rows, lanes].astype(F32)
            scale = lax.rsqrt(jnp.mean(out * out, axis=-1, keepdims=True) + 1e-05)
            unit = out * scale
            gain_grad_ref[...] += jnp.sum((grad * unit).reshape(CHUNK // 8, 8, CHUNK), 0)
            scaled = grad * gain_ref[...]
            back = scale * (scaled - unit * jnp.mean(scaled * unit, axis=-1, keepdims=True))
            back = back.astype(BF)
            ddelta_ref[rows, lanes] = back
            shift_ref[head] = tn(mq_ref[index, head], stack(shift_ref[head].astype(BF), back))

        @pl.when(lax.rem(step, 2) == 1)
        def _():
            pass_on(lax.div(step, 2))

        return carry

    lax.fori_loop(0, chunks, one, 0)
    for head in range(heads):
        part_ref[1, head] = shift_ref[head].astype(BF)
    send(1)
    begin(jobs[half:])
    for job in jobs[: len(jobs) // 2]:
        receive(*job)
    state_ref[...] = jnp.zeros_like(state_ref)
    for hop in range(window, 0, -1):

        @pl.when(behind >= hop)
        def _():
            copy(0, hop).wait_recv()
            copy(1, hop).wait_recv()
            for head in range(heads):
                state_ref[head] = nn(slots_ref[0, hop - 1, head], state_ref[head]) + slots_ref[1, hop - 1, head].astype(F32)

    for job in jobs[len(jobs) // 2 :]:
        receive(*job)

    @pl.loop(0, steps)
    def _(index):
        block_ref[at(index)] = (mid_ref[at(index)] + own_sum(index)).astype(BF)
        finish(index)

    end()
    for hop in range(1, window + 1):

        @pl.when(member >= hop)
        def _():
            copy(0, hop).wait_send()
            copy(1, hop).wait_send()


def state_backward(dheads, delta, gain, mq, total, update, mid, grads, members, collective):
    chunks, heads = mq.shape[:2]
    tokens, columns = mid.shape
    window = min(members - 1, members // 2)
    whole = pl.BlockSpec(memory_space=pltpu.VMEM)
    parts, _, *piece = grads.shape
    return pl.pallas_call(
        functools.partial(state_backward_kernel, heads, window),
        name="state_backward",
        out_shape=(
            jax.ShapeDtypeStruct((tokens, columns), BF),
            jax.ShapeDtypeStruct((8, CHUNK), F32),
            jax.ShapeDtypeStruct((heads, CHUNK, CHUNK), F32),
            jax.ShapeDtypeStruct((tokens, columns), BF),
            jax.ShapeDtypeStruct((parts, *piece), F32),
        ),
        in_specs=[whole] * 8,
        out_specs=(whole,) * 5,
        scratch_shapes=[
            pltpu.VMEM((heads, CHUNK, CHUNK), F32),
            pltpu.VMEM((2, heads, CHUNK, CHUNK), BF),
            pltpu.VMEM((2, window, heads, CHUNK, CHUNK), BF),
            pltpu.SemaphoreType.DMA((2, window)),
            pltpu.SemaphoreType.DMA((2, window)),
        ]
        + head_scatter_scratch(tokens, columns, tokens // 256)
        + piece_scatter_scratch(parts, members, piece),
        compiler_params=pltpu.CompilerParams(
            collective_id=collective, has_side_effects=True, vmem_limit_bytes=VMEM_LIMIT
        ),
        cost_estimate=pl.CostEstimate(flops=10**9, bytes_accessed=30 << 20, transcendentals=0),
    )(dheads, delta, gain, mq, total, update, mid, grads)


def piece_scatter_scratch(parts, members, piece):
    return [
        pltpu.VMEM((parts, max(members // 2 - 1, 1), *piece), BF),
        pltpu.VMEM((parts, members - 1, *piece), BF),
        pltpu.SemaphoreType.DMA((parts, members)),
        pltpu.SemaphoreType.DMA((parts, members)),
    ]


def piece_scatter(own_ref, relay_ref, slots_ref, total_ref, send, recv, members):
    member = lax.axis_index("seq")
    parts = own_ref.shape[0]
    stages = (members - 1).bit_length()
    order = sorted(range(members), key=lambda r: zeros_below(r) if r else stages)
    levels = {r: list(range(zeros_below(r) if r else stages)) for r in order}
    events = {}
    for r in order:
        for stage in levels[r]:
            events[r, stage] = len(events)
    kept = [r for r in order if r and r % 2 == 0]

    def source(part, r):
        return own_ref.at[part, flip(member, r)] if r % 2 else relay_ref.at[part, kept.index(r)]

    def give(part, r):
        stage = zeros_below(r)
        slot = events[r ^ (1 << stage), stage]
        return push(
            source(part, r), slots_ref.at[part, slot], send.at[part, r], recv.at[part, slot], "seq", flip(member, 1 << stage)
        )

    def take(part, r, stage):
        slot = events[r, stage]
        return push(
            own_ref.at[part, flip(member, 1)], slots_ref.at[part, slot], send.at[part, 0], recv.at[part, slot], "seq", flip(member, 1 << stage)
        )

    jobs = [(part, r) for r in order if r % 2 == 0 for part in range(parts)]

    def begin(some=None):
        for part, r in jobs if some is None else some:
            give(part, r ^ 1).start()

    def receive(part, r):
        total = own_ref[part, flip(member, r)].astype(F32)
        for stage in levels[r]:
            take(part, r, stage).wait_recv()
            total = total + slots_ref[part, events[r, stage]].astype(F32)
        if r:
            relay_ref[part, kept.index(r)] = total.astype(BF)
            give(part, r).start()
        else:
            total_ref[part] = total

    def finish():
        for part in range(parts):
            for r in order:
                if r:
                    give(part, r).wait_send()

    return begin, receive, jobs, finish


def mixer_backward_kernel(
    heads,
    lengths_ref,
    pre_hbm,
    halo_ref,
    conv_ref,
    logits_hbm,
    qkv_hbm,
    inv_hbm,
    wu_hbm,
    mq_hbm,
    states_hbm,
    ddelta_hbm,
    arrive_ref,
    grads_ref,
    dpre_ref,
    taps_grad_ref,
    total_ref,
    pre_ref,
    logits_ref,
    qkv_ref,
    inv_ref,
    wu_ref,
    mq_ref,
    states_ref,
    ddelta_ref,
    load_sem,
    resets_ref,
    taps_ref,
    carry_ref,
    pad_ref,
    dpad_ref,
    tail_ref,
    lead_ref,
    edge_ref,
    send_sem,
    recv_sem,
    relay_ref,
    slots_ref,
    piece_send,
    piece_recv,
):
    member, members = lax.axis_index("seq"), lax.axis_size("seq")
    barrier, stages = greet_seq(members)
    begin, receive, order, finish = piece_scatter(
        grads_ref, relay_ref, slots_ref, total_ref, piece_send, piece_recv, members
    )

    @pl.when(member + 1 < members)
    def _():
        pl.semaphore_signal(barrier, inc=1, device_id={"seq": member + 1}, device_id_type=MESH)

    columns = heads * CHUNK
    chunks = mq_ref.shape[0]
    fill_resets(lengths_ref, resets_ref, pre_ref.shape[0])
    fill_taps(conv_ref, taps_ref)
    quarter = chunks // 4
    sources = (pre_hbm, logits_hbm, qkv_hbm, ddelta_hbm, inv_hbm, wu_hbm, mq_hbm, states_hbm)
    targets = (pre_ref, logits_ref, qkv_ref, ddelta_ref, inv_ref, wu_ref, mq_ref, states_ref)

    def load(number, turn):
        unit = CHUNK if number < 4 else 1
        reach = pl.ds((chunks - (turn + 1) * quarter) * unit, quarter * unit)
        return pltpu.make_async_copy(
            sources[number].at[reach], targets[number].at[reach], load_sem.at[number, turn]
        )

    for turn in range(4):
        for number in range(8):
            load(number, turn).start()
    load(0, 0).wait()
    rows, cols = grid_indices()
    top = lax.broadcasted_iota(jnp.int32, (CHUNK, 1), 0) < GROUP
    pl.semaphore_wait(barrier, stages + jnp.minimum(member, 1))
    begin()
    carry_ref[...] = arrive_ref[...]
    taps_grad_ref[...] = jnp.zeros_like(taps_grad_ref)
    dpad_ref[136:144] = jnp.zeros_like(dpad_ref[136:144])

    def one(step, carry):
        chunk = chunks - 1 - step
        at = pl.ds(pl.multiple_of(chunk * CHUNK, CHUNK), CHUNK)
        for turn in range(4):

            @pl.when(step == turn * quarter)
            def _():
                for number in range(1, 8):
                    load(number, turn).wait()
                if turn < 3:
                    load(0, turn + 1).wait()

        keep0 = 1.0 - resets_ref[2 * chunk]
        keep1 = 1.0 - resets_ref[2 * chunk + 1]
        both = keep0 * keep1
        enter = jnp.where(top, keep0, both)
        leave = jnp.where(top, keep1, 1.0)
        load_padded(pad_ref, pre_ref, halo_ref, chunk, resets_ref)
        mixed = convolve(pad_ref, taps_ref)
        gate = sigmoid(mixed)
        slope = gate * (1.0 + mixed * (1.0 - gate))
        silued = mixed * gate
        beta_rows = sigmoid(logits_ref[at, :])
        grads = [[None] * heads for _ in range(3)]
        dlogits = []
        cross = (rows >= GROUP) & (cols < GROUP)

        def part(kind, head):
            return slice(kind * columns + head * CHUNK, kind * columns + (head + 1) * CHUNK)

        def masked(product, keep):
            lower = jnp.where(keep, product, 0.0)
            return jnp.where(cross, lower * keep1, lower).astype(BF)

        every = range(heads)
        query = [qkv_ref[at, part(0, h)] for h in every]
        key = [qkv_ref[at, part(1, h)] for h in every]
        value = [qkv_ref[at, part(2, h)] for h in every]
        key32 = [k.astype(F32) for k in key]
        beta = [beta_rows[:, h : h + 1] for h in every]
        inverse = [inv_ref[chunk, h] for h in every]
        weight = [wu_ref[chunk, h, :, :CHUNK] for h in every]
        factors = [wu_ref[chunk, h] for h in every]
        update = [wu_ref[chunk, h, :, CHUNK:] for h in every]
        state = [states_ref[chunk, h] for h in every]
        out_grad = [ddelta_ref[at, h * CHUNK : (h + 1) * CHUNK] for h in every]
        later = [carry_ref[h].astype(BF) for h in every]
        carried = [tn(mq_ref[chunk, h], stack(later[h], out_grad[h])) for h in every]
        scores = [masked(nt(query[h], key[h]), rows >= cols) for h in every]
        fresh = [(update[h].astype(F32) - nn(weight[h], state[h])).astype(BF) for h in every]
        fresh_low = [(tn(scores[h], out_grad[h]) + leave * nn(key[h], later[h])).astype(BF) for h in every]
        score_grad = [masked(nt(out_grad[h], fresh[h]), rows >= cols) for h in every]
        through = [nt(stack(out_grad[h], fresh_low[h]), state[h]) for h in every]
        weight_grad = [(-enter * through[h][CHUNK:]).astype(BF) for h in every]
        back = [tn(inverse[h], side(weight_grad[h], fresh_low[h])) for h in every]
        query_grad = [enter * through[h][:CHUNK] + nn(score_grad[h], key[h]) for h in every]
        key_grad = [tn(score_grad[h], query[h]) + leave * nt(fresh[h], later[h]) for h in every]
        strict = [masked(-nt(back[h].astype(BF), factors[h]), rows > cols) for h in every]
        strict_key = [nn(strict[h], key[h]) for h in every]
        turned = [tn(strict[h], (beta[h] * key32[h]).astype(BF)) for h in every]
        for h in every:
            carry_ref[h] = carried[h]
            yk, zv = back[h][:, :CHUNK], back[h][:, CHUNK:]
            both_key = yk + strict_key[h]
            key_grad[h] = key_grad[h] + beta[h] * both_key + turned[h]
            grads[2][h] = beta[h] * zv
            beta_grad = jnp.sum(both_key * key32[h] + zv * value[h].astype(F32), axis=-1, keepdims=True)
            dlogits.append(beta_grad * beta[h] * (1.0 - beta[h]))
        for kind, grad in ((0, query_grad), (1, key_grad)):
            raw = [silued[:, part(kind, h)] for h in every]
            norm = [lax.rsqrt(jnp.sum(raw[h] * raw[h], axis=-1, keepdims=True) + 1e-06) for h in every]
            unit = [raw[h] * norm[h] for h in every]
            inner = [jnp.sum(unit[h] * grad[h], axis=-1, keepdims=True) for h in every]
            grads[kind] = [(grad[h] - unit[h] * inner[h]) * norm[h] for h in every]
        lanes = lax.broadcasted_iota(jnp.int32, (CHUNK, CHUNK), 1)
        spread = jnp.zeros((CHUNK, CHUNK), F32)
        for head in range(heads):
            spread = jnp.where(lanes == head, dlogits[head], spread)
        dpre_ref[at, 3 * columns :] = spread.astype(BF)
        dmixed = jnp.concatenate([g for kind in grads for g in kind], 1) * slope
        dpad_ref[0:GROUP] = dmixed[:GROUP]
        dpad_ref[GROUP : GROUP + 8] = dmixed[GROUP : GROUP + 8] * keep1
        dpad_ref[72 : 72 + GROUP] = dmixed[GROUP:]
        dpre = None
        for tap in range(4):
            back = 3 - tap
            shifted = stack(dpad_ref[back : back + GROUP], dpad_ref[72 + back : 72 + back + GROUP])
            term = taps_ref[tap : tap + 1] * shifted
            dpre = term if dpre is None else dpre + term
            seen = (dmixed * tap_rows(pad_ref, tap)).reshape(CHUNK // 8, 8, 3 * columns)
            taps_grad_ref[tap] += jnp.sum(seen, 0)
        dpre_ref[at, : 3 * columns] = dpre.astype(BF)

        @pl.when(step == 0)
        def _():
            tail_ref[...] = dpre[CHUNK - 16 :]

        dpad_ref[136:144] = dmixed[:8] * keep0
        for place, job in enumerate(order):

            @pl.when(step == (place + 1) * (chunks - 1) // len(order))
            def _():
                receive(*job)

        return carry

    lax.fori_loop(0, chunks, one, 0)
    index = lax.broadcasted_iota(jnp.int32, (8, 1), 0)
    lead = jnp.zeros((8, 3 * columns), F32)
    dpad_ref[0:128] = jnp.zeros_like(dpad_ref[0:128])
    dpad_ref[8:16] = dpad_ref[136:144]
    for tap in range(3):
        back = 3 - tap
        lead = lead + taps_ref[tap : tap + 1] * dpad_ref[back : back + 8]
    lead_ref[...] = lead

    def to_previous(target):
        return push(lead_ref, edge_ref, send_sem, recv_sem, "seq", target)

    @pl.when(member > 0)
    def _():
        to_previous(member - 1).start()

    @pl.when(member + 1 < members)
    def _():
        to_previous(member).wait_recv()
        last = pl.ds(dpre_ref.shape[0] - 16, 16)
        late = stack(tail_ref[0:8], tail_ref[8:16] + edge_ref[...])
        dpre_ref[last, : 3 * columns] = late.astype(BF)

    @pl.when(member > 0)
    def _():
        to_previous(member - 1).wait_send()

    finish()


def mixer_backward(lengths, pre, halo, conv, logits, qkv, inv, wu, mq, states, ddelta, arrive, grads, collective):
    chunks, heads = mq.shape[:2]
    tokens = chunks * CHUNK
    columns = heads * CHUNK
    parts, members = grads.shape[:2]
    piece = grads.shape[2:]
    whole, outside = pl.BlockSpec(memory_space=pltpu.VMEM), pl.BlockSpec(memory_space=pl.ANY)
    streamed = (pre, logits, qkv, inv, wu, mq, states, ddelta)
    return pl.pallas_call(
        functools.partial(mixer_backward_kernel, heads),
        name="mixer_backward",
        out_shape=(
            jax.ShapeDtypeStruct((tokens, 3 * columns + CHUNK), BF),
            jax.ShapeDtypeStruct((4, 8, 3 * columns), F32),
            jax.ShapeDtypeStruct((parts, *piece), F32),
        ),
        in_specs=[pl.BlockSpec(memory_space=pltpu.SMEM), outside, whole, whole] + [outside] * 7 + [whole] * 2,
        out_specs=tuple([pl.BlockSpec(memory_space=pltpu.VMEM)] * 3),
        scratch_shapes=[pltpu.VMEM(a.shape, a.dtype) for a in streamed]
        + [
            pltpu.SemaphoreType.DMA((8, 4)),
            pltpu.SMEM((tokens // GROUP,), F32),
            pltpu.VMEM((4, 3 * columns), F32),
            pltpu.VMEM((heads, CHUNK, CHUNK), F32),
            pltpu.VMEM((144, 3 * columns), F32),
            pltpu.VMEM((144, 3 * columns), F32),
            pltpu.VMEM((16, 3 * columns), F32),
            pltpu.VMEM((8, 3 * columns), F32),
            pltpu.VMEM((8, 3 * columns), F32),
            pltpu.SemaphoreType.DMA,
            pltpu.SemaphoreType.DMA,
        ]
        + piece_scatter_scratch(parts, members, piece),
        compiler_params=pltpu.CompilerParams(
            collective_id=collective, has_side_effects=True, vmem_limit_bytes=VMEM_LIMIT
        ),
        cost_estimate=pl.CostEstimate(flops=3 * 10**9, bytes_accessed=20 << 20, transcendentals=2 << 20),
    )(lengths, pre, halo, conv, logits, qkv, inv, wu, mq, states, ddelta, arrive, grads)


def head_peers():
    place = lax.axis_index("head")
    low = lax.rem(place, 2)
    high = lax.rem(lax.div(place, 2), 2)
    return place, low, place + 1 - 2 * low, place + 2 - 4 * high


def push(src, dst, send_sem, recv_sem, axis, target):
    return pltpu.make_async_remote_copy(
        src_ref=src,
        dst_ref=dst,
        send_sem=send_sem,
        recv_sem=recv_sem,
        device_id={axis: target},
        device_id_type=MESH,
    )


def greet(axis, targets):
    barrier = pltpu.get_barrier_semaphore()
    for target in targets:
        pl.semaphore_signal(barrier, inc=1, device_id={axis: target}, device_id_type=MESH)
    pl.semaphore_wait(barrier, len(targets))


def middle_kernel(
    steps,
    rows_ref,
    late_rows_ref,
    far_rows_ref,
    full_hbm,
    turned_hbm,
    others_hbm,
    input_ref,
    ct_ref,
    late_ct_ref,
    gain_ref,
    dheads_ref,
    update_ref,
    mid_ref,
    dmid_ref,
    first_grads_ref,
    second_grads_ref,
    third_grads_ref,
    gain_grad_ref,
    gate_ref,
    up_ref,
    down_ref,
    turned_ref,
    others_ref,
    load_sem,
    acc_ref,
    part_ref,
    pair_ref,
    far_ref,
    sum_ref,
    keep_ref,
    scale_ref,
    shard_ref,
    pair_send,
    pair_recv,
    far_send,
    far_recv,
    last_send,
    last_recv,
):
    step = pl.program_id(0)
    place, low, near, far = head_peers()
    chunk, width = input_ref.shape
    columns = rows_ref.shape[1]
    hidden = gate_ref.shape[0]
    half = width // 2
    mine = pl.ds(pl.multiple_of(low * half, 128), half)
    theirs = pl.ds(pl.multiple_of((1 - low) * half, 128), half)
    own_columns = pl.ds(pl.multiple_of(place * columns, 128), columns)

    def pair(index):
        return push(
            part_ref.at[lax.rem(index, 2), :, theirs], pair_ref.at[index], pair_send.at[index], pair_recv.at[index], "head", near
        )

    def across(index):
        return push(pair_ref.at[index], far_ref.at[index], far_send.at[index], far_recv.at[index], "head", far)

    def last(index):
        return push(
            sum_ref.at[index, :, mine], sum_ref.at[index, :, mine], last_send.at[index], last_recv.at[index], "head", near
        )

    def loads():
        targets = [
            (full_hbm.at[0], gate_ref),
            (full_hbm.at[1], up_ref),
            (full_hbm.at[2], down_ref),
            (turned_hbm, turned_ref),
        ] + [(others_hbm.at[other], others_ref.at[other]) for other in range(3)]
        for number, (source, target) in enumerate(targets):
            for piece in range(width // 128):
                yield pltpu.make_async_copy(
                    source.at[piece], target.at[:, piece * 128 : (piece + 1) * 128], load_sem.at[number, piece]
                )

    @pl.when(step == 0)
    def _():
        for load in loads():
            load.start()
        greet("head", (near, far))

        acc_ref[...] = jnp.zeros_like(acc_ref)
        gain_grad_ref[...] = jnp.zeros_like(gain_grad_ref)
        for load in loads():
            load.wait()

    @pl.when(step < steps)
    def _():
        ct = ct_ref[...]
        d_hidden = nt(ct, down_ref[...])

        branch = nn(rows_ref[...], turned_ref[...])
        for other in range(3):
            branch = branch + nn(far_rows_ref[other], others_ref[other])
        middle = input_ref[...].astype(F32) + branch
        keep_ref[lax.rem(step, 4)] = middle
        mid_ref[...] = keep_ref[lax.rem(step, 4), :, own_columns]
        scale = lax.rsqrt(jnp.mean(middle * middle, axis=-1, keepdims=True) + 1e-06)
        scale_ref[lax.rem(step, 4)] = scale
        second = (middle * scale * gain_ref[1:2]).astype(BF)
        gate, up = nt(second, gate_ref[...]), nt(second, up_ref[...])
        sig = sigmoid(gate)
        silu = gate * sig
        active = (silu * up).astype(BF)
        d_gate = (d_hidden * up * (sig + silu * (1.0 - sig))).astype(BF)
        d_up = (d_hidden * silu).astype(BF)

        @pl.when(step >= 2)
        def _():
            pair(step - 2).wait_send()

        part_ref[lax.rem(step, 2)] = (nn(d_gate, gate_ref[...]) + nn(d_up, up_ref[...])).astype(BF)
        pair(step).start()

        update_ref[...] = nn(active, down_ref[...]).astype(BF)
        acc_ref[:hidden] += tn(d_gate, second)
        acc_ref[hidden : 2 * hidden] += tn(d_up, second)
        acc_ref[2 * hidden : 3 * hidden] += tn(active, ct)

    @pl.when(step < steps)
    def _():
        pair(step).wait_recv()
        both = part_ref[lax.rem(step, 2), :, mine].astype(F32) + pair_ref[step].astype(F32)
        pair_ref[step] = both.astype(BF)
        across(step).start()

    @pl.when((step > 1) & (step < steps + 2))
    def _():
        done = step - 2
        across(done).wait_recv()
        across(done).wait_send()
        total = pair_ref[done].astype(F32) + far_ref[done].astype(F32)
        sum_ref[done, :, mine] = total.astype(BF)
        last(done).start()

    @pl.when(step > 2)
    def _():
        done = step - 3
        last(done).wait_recv()
        grad = sum_ref[done].astype(F32)
        middle = keep_ref[lax.rem(done, 4)]
        scale = scale_ref[lax.rem(done, 4)]
        unit = middle * scale
        gain_grad_ref[...] += jnp.sum((grad * unit).reshape(chunk // 8, 8, width), 0)
        scaled = grad * gain_ref[1:2]
        d_middle = late_ct_ref[...].astype(F32) + scale * (
            scaled - unit * jnp.mean(scaled * unit, axis=-1, keepdims=True)
        )
        shard_ref[...] = d_middle
        dmid_ref[...] = shard_ref[:, own_columns]
        d_branch = d_middle.astype(BF)
        dheads_ref[...] = nt(d_branch, turned_ref[...]).astype(BF)
        acc_ref[3 * hidden :] += tn(late_rows_ref[...], d_branch)

    @pl.when(step == steps + 2)
    def _():
        for piece in range(width // 128):
            lanes = slice(piece * 128, (piece + 1) * 128)
            begin = 0
            for grads_ref in (first_grads_ref, second_grads_ref, third_grads_ref):
                rows = grads_ref.shape[2]
                for part in range(2):
                    grads_ref[part, piece] = acc_ref[begin : begin + rows, lanes].astype(BF)
                    begin += rows

        @pl.loop(0, steps)
        def _(index):
            last(index).wait_send()

        for index in range(max(steps - 2, 0), steps):
            pair(index).wait_send()


def middle_stage(head_rows, far_rows, full, turned, others, inputs, cotangent, gain, collective):
    tokens, width = inputs.shape
    columns = head_rows.shape[1]
    chunk = min(256, tokens // 2)
    steps = tokens // chunk
    whole = pl.BlockSpec(memory_space=pltpu.VMEM)
    outside = pl.BlockSpec(memory_space=pl.ANY)
    hidden = full.shape[2]
    units = (3 * hidden + columns) // 32
    shares = [16 * (units * 36 // 74), 0, 16 * (units * 25 // 74)]
    shares[1] = 16 * units - sum(shares)

    def early(wide):
        return pl.BlockSpec((chunk, wide), lambda s: (jnp.minimum(s, steps - 1), 0))

    def late(wide):
        return pl.BlockSpec((chunk, wide), lambda s: (jnp.maximum(s - 3, 0), 0))

    far = pl.BlockSpec((3, chunk, columns), lambda s: (0, jnp.minimum(s, steps - 1), 0))
    dma = pltpu.SemaphoreType.DMA((steps,))
    return pl.pallas_call(
        functools.partial(middle_kernel, steps),
        name="middle",
        grid=(steps + 3,),
        out_shape=(
            jax.ShapeDtypeStruct((tokens, columns), BF),
            jax.ShapeDtypeStruct((tokens, width), BF),
            jax.ShapeDtypeStruct((tokens, columns), F32),
            jax.ShapeDtypeStruct((tokens, columns), F32),
            *(jax.ShapeDtypeStruct((2, width // 128, rows, 128), BF) for rows in shares),
            jax.ShapeDtypeStruct((8, width), F32),
        ),
        in_specs=[early(columns), late(columns), far] + [outside] * 3 + [early(width), early(width), late(width), whole],
        out_specs=(late(columns), early(width), early(columns), late(columns), whole, whole, whole, whole),
        scratch_shapes=[
            pltpu.VMEM((hidden, width), BF),
            pltpu.VMEM((hidden, width), BF),
            pltpu.VMEM((hidden, width), BF),
            pltpu.VMEM((columns, width), BF),
            pltpu.VMEM((3, columns, width), BF),
            pltpu.SemaphoreType.DMA((7, width // 128)),
            pltpu.VMEM((3 * hidden + columns, width), F32),
            pltpu.VMEM((2, chunk, width), BF),
            pltpu.VMEM((steps, chunk, width // 2), BF),
            pltpu.VMEM((steps, chunk, width // 2), BF),
            pltpu.VMEM((steps, chunk, width), BF),
            pltpu.VMEM((4, chunk, width), F32),
            pltpu.VMEM((4, chunk, 1), F32),
            pltpu.VMEM((chunk, width), F32),
        ]
        + [dma] * 6,
        compiler_params=pltpu.CompilerParams(
            collective_id=collective,
            has_side_effects=True,
            vmem_limit_bytes=VMEM_LIMIT,
            dimension_semantics=("arbitrary",),
        ),
        cost_estimate=pl.CostEstimate(flops=30 * 10**9, bytes_accessed=30 << 20, transcendentals=2 << 20),
    )(head_rows, head_rows, far_rows, full, turned, others, inputs, cotangent, cotangent, gain)


def zeros_below(value):
    return (value & -value).bit_length() - 1


def flip(place, mask):
    bit = 1
    while bit <= mask:
        if mask & bit:
            place = place + bit - 2 * bit * lax.rem(lax.div(place, bit), 2)
        bit *= 2
    return place


def head_scatter_copies(chunk, part_ref, near_ref, send_ref, far_ref, sems):
    place, low, near, far = head_peers()
    high = lax.rem(lax.div(place, 2), 2)
    columns = far_ref.shape[-1]
    near_send, near_recv, far_send, far_recv = sems

    def at(index):
        return pl.ds(pl.multiple_of(index * chunk, chunk), chunk)

    def cols(owner):
        return pl.ds(pl.multiple_of(owner * columns, 128), columns)

    def pair(index, side_):
        return push(
            part_ref.at[at(index), cols(2 * side_ + 1 - low)],
            near_ref.at[side_, at(index)],
            near_send.at[side_, index],
            near_recv.at[side_, index],
            "head",
            near,
        )

    def across(index):
        return push(send_ref.at[at(index)], far_ref.at[at(index)], far_send.at[index], far_recv.at[index], "head", far)

    def start_pair(index):
        pair(index, 0).start()
        pair(index, 1).start()

    def pass_on(index):
        pair(index, 0).wait_recv()
        pair(index, 1).wait_recv()
        total = part_ref[at(index), cols(2 * (1 - high) + low)].astype(F32) + near_ref[1 - high, at(index)].astype(F32)
        send_ref[at(index)] = total.astype(BF)
        across(index).start()

    def own_sum(index):
        across(index).wait_recv()
        near_part = part_ref[at(index), cols(place)].astype(F32) + near_ref[high, at(index)].astype(F32)
        return near_part + far_ref[at(index)].astype(F32)

    def finish(index):
        pair(index, 0).wait_send()
        pair(index, 1).wait_send()
        across(index).wait_send()

    return at, cols, start_pair, pass_on, own_sum, finish


def head_scatter_scratch(tokens, columns, steps):
    return [
        pltpu.VMEM((2, tokens, columns), BF),
        pltpu.VMEM((tokens, columns), BF),
        pltpu.VMEM((tokens, columns), BF),
        pltpu.SemaphoreType.DMA((2, steps)),
        pltpu.SemaphoreType.DMA((2, steps)),
        pltpu.SemaphoreType.DMA((steps,)),
        pltpu.SemaphoreType.DMA((steps,)),
    ]


def final_kernel(
    members,
    chunk,
    rows_ref,
    dpre_ref,
    pack_hbm,
    input_hbm,
    scale_hbm,
    gain_ref,
    dmid_hbm,
    head_part_ref,
    second_part_ref,
    taps_part_ref,
    rest_ref,
    ingrad_ref,
    piece_ref,
    sums_ref,
    total_ref,
    pack_ref,
    input_ref,
    scale_ref,
    dmid_ref,
    load_sem,
    acc_ref,
    out_ref,
    slots_ref,
    part_ref,
    near_ref,
    send_ref,
    far_ref,
    near_send,
    near_recv,
    far_send,
    far_recv,
    stat_ref,
    stat_slots,
    small_slots,
    piece_send,
    piece_recv,
    stat_send,
    stat_recv,
    small_send,
    small_recv,
    rest_relay,
    rest_slots,
    rest_send,
    rest_recv,
):
    tokens, width = input_ref.shape
    steps = tokens // chunk
    loads = [
        pltpu.make_async_copy(source, target, load_sem.at[number])
        for number, (source, target) in enumerate(
            ((pack_hbm, pack_ref), (input_hbm, input_ref), (scale_hbm, scale_ref), (dmid_hbm, dmid_ref))
        )
    ]
    for load in loads:
        load.start()
    place, low, near, far = head_peers()
    member = lax.axis_index("seq")
    rows = width // members
    stages = (members - 1).bit_length()
    at, cols, start_pair, pass_on, own_sum, finish = head_scatter_copies(
        chunk, part_ref, near_ref, send_ref, far_ref, (near_send, near_recv, far_send, far_recv)
    )

    barrier = pltpu.get_barrier_semaphore()
    opposite = near + far - place
    for target in (near, far, opposite):
        pl.semaphore_signal(barrier, inc=1, device_id={"head": target}, device_id_type=MESH)
    for stage in range(stages):
        pl.semaphore_signal(barrier, inc=1, device_id={"seq": flip(member, 1 << stage)}, device_id_type=MESH)
    begin, rest_receive, rest_jobs, rest_end = piece_scatter(
        rest_ref, rest_relay, rest_slots, total_ref, rest_send, rest_recv, members
    )
    pl.semaphore_wait(barrier, 3 + stages)
    order = sorted(range(members), key=lambda r: zeros_below(r) if r else stages)
    sent = [r for r in order if r]
    events = {}
    for r in order:
        for stage in range(zeros_below(r) if r else stages):
            events[stage, r] = len(events)

    def give(r):
        stage = zeros_below(r)
        slot = events[stage, r ^ (1 << stage)]
        return push(
            out_ref.at[r],
            slots_ref.at[slot],
            piece_send.at[r],
            piece_recv.at[slot],
            "seq",
            flip(member, 1 << stage),
        )

    def take(stage, r):
        slot = events[stage, r]
        return push(
            out_ref.at[0], slots_ref.at[slot], piece_send.at[0], piece_recv.at[slot], "seq", flip(member, 1 << stage)
        )

    def send_piece(r):
        out_ref[r] = acc_ref[flip(member, r)].astype(BF)
        give(r).start()

    def receive(r):
        index = flip(member, r)
        for stage in range(zeros_below(r) if r else stages):
            take(stage, r).wait_recv()
            acc_ref[index] += slots_ref[events[stage, r]].astype(F32)
        if r:
            send_piece(r)

    first = sorted([r for r in range(members) if r % 2], key=lambda r: order.index(r ^ 1))
    evens = [r for r in order if r % 2 == 0]
    if rows % 128 == 0:
        for r in first:
            even = 2 * lax.div(flip(member, r), 2)
            columns = pl.ds(pl.multiple_of(even * rows, 128), 2 * rows)
            block = tn(rows_ref[:, columns], dpre_ref[...])
            acc_ref[even] = block[:rows]
            acc_ref[even + 1] = block[rows:]
            send_piece(r)
        begin()
    else:
        per = 128 // rows
        for unit in range(width // 128):
            block = tn(rows_ref[:, unit * 128 : (unit + 1) * 128], dpre_ref[...])
            acc_ref[unit * per : (unit + 1) * per] = block.reshape(per, rows, block.shape[1])
        for r in first:
            send_piece(r)
        begin()

    small_slots[0] = jnp.zeros_like(small_slots[0])
    small_slots[0, 1:2, :CHUNK] = jnp.sum(head_part_ref[...], 0, keepdims=True)
    small_slots[0, 8:9] = jnp.sum(second_part_ref[...], 0, keepdims=True)
    columns3 = taps_part_ref.shape[2]
    for tap in range(4):
        taps_sum = jnp.sum(taps_part_ref[tap], 0, keepdims=True)
        for block in range(3):
            flat = tap * columns3 + block * (columns3 // 3)
            line, lane = 9 + flat // width, flat % width
            small_slots[0, line : line + 1, lane : lane + columns3 // 3] = taps_sum[
                :, block * (columns3 // 3) : (block + 1) * (columns3 // 3)
            ]
    for load in loads:
        load.wait()
    diagonal = lax.broadcasted_iota(jnp.int32, (128, 128), 0) == lax.broadcasted_iota(jnp.int32, (128, 128), 1)

    def project(index):
        part = nt(dpre_ref[at(index)], pack_ref[...])
        part_ref[at(index)] = part.astype(BF)
        start_pair(index)
        seen = part * (input_ref[at(index)].astype(F32) * scale_ref[at(index)])
        small_slots[0, 0:1] += jnp.sum(seen, 0, keepdims=True)
        stat = jnp.sum(seen * gain_ref[0:1], axis=-1, keepdims=True)
        for block in range(chunk // 128):
            line = jnp.where(diagonal, stat[block * 128 : (block + 1) * 128], 0.0)
            stat_ref[index * (chunk // 128) + block] = jnp.sum(line, 0, keepdims=True)

    early = steps // 2
    receives = list(evens)
    for half in range(2):

        @pl.loop(half * early, (half + 1) * early)
        def _(index):
            project(index)

            @pl.when(lax.rem(index, 2) == 1)
            def _():
                pass_on(lax.div(index, 2))

        if len(receives) > 1:
            receive(receives.pop(0))

    def stat_copy(turn):
        target = (near, far, opposite)[turn]
        return push(stat_ref, stat_slots.at[turn], stat_send.at[turn], stat_recv.at[turn], "head", target)

    def head_copy(turn):
        target = (near, far, opposite)[turn]
        return push(
            small_slots.at[0, pl.ds(0, 8)],
            small_slots.at[1 + turn, pl.ds(0, 8)],
            small_send.at[turn],
            small_recv.at[turn],
            "head",
            target,
        )

    for turn in (1, 2, 0):
        head_copy(turn).start()
        stat_copy(turn).start()
    for index in range(early, steps):
        pass_on(index)
    while len(receives) > 1:
        receive(receives.pop(0))
    for turn in range(3):
        head_copy(turn).wait()
    small_slots[4] = small_slots[0]
    small_slots[4, 0:8] += small_slots[1, 0:8] + small_slots[2, 0:8] + small_slots[3, 0:8]

    bits = list(range(1, stages)) + [0]

    def seq_copy(turn):
        return push(
            small_slots.at[4 + 2 * turn],
            small_slots.at[5 + 2 * turn],
            small_send.at[3 + turn],
            small_recv.at[3 + turn],
            "seq",
            flip(member, 1 << bits[turn]),
        )

    def seq_add(turn):
        seq_copy(turn).wait()
        small_slots[6 + 2 * turn] = small_slots[4 + 2 * turn] + small_slots[5 + 2 * turn]

    seq_copy(0).start()
    for turn in range(3):
        stat_copy(turn).wait()
    stat_ref[...] += stat_slots[0] + stat_slots[1] + stat_slots[2]

    def result(index):
        grad = own_sum(index)
        scale = scale_ref[at(index)]
        unit = input_ref[at(index), cols(place)].astype(F32) * scale
        means = []
        for block in range(chunk // 128):
            line = jnp.where(diagonal, stat_ref[index * (chunk // 128) + block], 0.0)
            means.append(jnp.sum(line, axis=-1, keepdims=True))
        mean = jnp.concatenate(means, 0) * (1.0 / width)
        ingrad_ref[at(index)] = dmid_ref[at(index)] + scale * (grad * gain_ref[0:1, cols(place)] - unit * mean)

    rests = list(rest_jobs)
    for turn in range(stages):
        start, stop = turn * steps // stages, (turn + 1) * steps // stages
        if stop > start:

            @pl.loop(start, stop)
            def _(index):
                result(index)

        share = (len(rests) - 1) // (stages - turn)
        for job in rests[:share]:
            rest_receive(*job)
        rests = rests[share:]
        seq_add(turn)
        if turn + 1 < stages:
            seq_copy(turn + 1).start()
    receive(0)
    for job in rests:
        rest_receive(*job)
    piece_ref[...] = acc_ref[member]
    sums_ref[...] = small_slots[4 + 2 * stages]

    @pl.loop(0, steps)
    def _(index):
        finish(index)

    for r in sent:
        give(r).wait_send()
    rest_end()


def final_stage(first_rows, dpre, pack, inputs, scale, gain, dmid, parts, rest, members, collective):
    tokens, width = inputs.shape
    columns = dmid.shape[1]
    chunk = 256
    steps = tokens // chunk
    stages = (members - 1).bit_length()
    rows = width // members
    wide = dpre.shape[1]
    whole, outside = pl.BlockSpec(memory_space=pltpu.VMEM), pl.BlockSpec(memory_space=pl.ANY)
    return pl.pallas_call(
        functools.partial(final_kernel, members, chunk),
        name="final",
        out_shape=(
            jax.ShapeDtypeStruct((tokens, columns), F32),
            jax.ShapeDtypeStruct((rows, wide), F32),
            jax.ShapeDtypeStruct((16, width), F32),
            jax.ShapeDtypeStruct((rest.shape[0], *rest.shape[2:]), F32),
        ),
        in_specs=[whole, whole, outside, outside, outside, whole, outside] + [whole] * 4,
        out_specs=(whole,) * 4,
        scratch_shapes=[pltpu.VMEM(a.shape, a.dtype) for a in (pack, inputs, scale, dmid)]
        + [
            pltpu.SemaphoreType.DMA((4,)),
            pltpu.VMEM((members, rows, wide), F32),
            pltpu.VMEM((members, rows, wide), BF),
            pltpu.VMEM((members - 1, rows, wide), BF),
            pltpu.VMEM((tokens, width), BF),
        ]
        + head_scatter_scratch(tokens, columns, steps)
        + [
            pltpu.VMEM((tokens // 128, 1, 128), F32),
            pltpu.VMEM((3, tokens // 128, 1, 128), F32),
            pltpu.VMEM((5 + 2 * stages, 16, width), F32),
            pltpu.SemaphoreType.DMA((members,)),
            pltpu.SemaphoreType.DMA((members - 1,)),
            pltpu.SemaphoreType.DMA((3,)),
            pltpu.SemaphoreType.DMA((3,)),
            pltpu.SemaphoreType.DMA((3 + stages,)),
            pltpu.SemaphoreType.DMA((3 + stages,)),
        ]
        + piece_scatter_scratch(rest.shape[0], members, rest.shape[2:]),
        compiler_params=pltpu.CompilerParams(
            collective_id=collective, has_side_effects=True, vmem_limit_bytes=VMEM_LIMIT
        ),
        cost_estimate=pl.CostEstimate(flops=8 * 10**9, bytes_accessed=30 << 20, transcendentals=0),
    )(first_rows, dpre, pack, inputs, scale, gain, dmid, *parts, rest)


def finish_kernel(
    hidden,
    block_ref,
    ingrad_ref,
    piece_ref,
    sums_ref,
    first_ref,
    second_ref,
    third_ref,
    block_out,
    ingrad_out,
    first_gain_out,
    query_out,
    key_out,
    value_out,
    beta_out,
    conv_out,
    head_gain_out,
    output_out,
    second_gain_out,
    gate_out,
    up_out,
    down_out,
    turn_ref,
    strip_ref,
    sems,
):
    rows, columns = query_out.shape
    member = lax.axis_index("seq")
    pieces = [(block_ref, block_out), (ingrad_ref, ingrad_out)]
    for kind, target in enumerate((query_out, key_out, value_out)):
        pieces.append((piece_ref.at[:, pl.ds(kind * columns, columns)], target))
    pieces.append((piece_ref.at[:, pl.ds(3 * columns, CHUNK)], strip_ref))
    spans = []
    place = 0
    for source in (first_ref, second_ref, third_ref):
        for part in range(2):
            spans.append((place, source, part))
            place += source.shape[1]
    goal = 0
    for target, count in ((gate_out, hidden), (up_out, hidden), (down_out, hidden), (turn_ref, columns)):
        for begin, source, part in spans:
            low, high = max(begin, goal), min(begin + source.shape[1], goal + count)
            if low < high:
                pieces.append(
                    (source.at[part, pl.ds(low - begin, high - low)], target.at[pl.ds(low - goal, high - low)])
                )
        goal += count
    copies = [pltpu.make_async_copy(source, target, sems.at[number]) for number, (source, target) in enumerate(pieces)]
    for copy in copies:
        copy.start()
    window = pl.ds(pl.multiple_of(member * rows, 128), rows)
    first_gain_out[...] = sums_ref[0:1, window]
    second_gain_out[...] = sums_ref[8:9, window]
    head_gain_out[...] = sums_ref[1:2, :CHUNK]
    width = sums_ref.shape[1]
    for kind in range(3):
        for tap in range(4):
            flat = (3 * tap + kind) * columns
            line, lane = 9 + flat // width, flat % width
            conv_out[kind, tap : tap + 1] = sums_ref[line : line + 1, lane : lane + columns]
    for copy in copies:
        copy.wait()
    output_out[...] = turn_ref[...].T
    beta_out[...] = strip_ref[...].T[: beta_out.shape[0]]


def finish_stage(block, ingrad, piece, sums, first, second, third, hidden, heads):
    tokens, columns = ingrad.shape
    rows = piece.shape[0]
    whole, outside = pl.BlockSpec(memory_space=pltpu.VMEM), pl.BlockSpec(memory_space=pl.ANY)

    def made(*shape):
        return jax.ShapeDtypeStruct(shape, F32)

    return pl.pallas_call(
        functools.partial(finish_kernel, hidden),
        name="finish",
        out_shape=(
            jax.ShapeDtypeStruct((tokens, columns), BF),
            made(tokens, columns),
            made(1, rows),
            made(rows, columns),
            made(rows, columns),
            made(rows, columns),
            made(heads, rows),
            made(3, 4, columns),
            made(1, CHUNK),
            made(rows, columns),
            made(1, rows),
            made(hidden, rows),
            made(hidden, rows),
            made(hidden, rows),
        ),
        in_specs=[whole] * 7,
        out_specs=(outside,) * 2
        + (whole,)
        + (outside,) * 3
        + (whole,) * 5
        + (outside,) * 3,
        scratch_shapes=[
            pltpu.VMEM((columns, rows), F32),
            pltpu.VMEM((rows, CHUNK), F32),
            pltpu.SemaphoreType.DMA((24,)),
        ],
        compiler_params=pltpu.CompilerParams(vmem_limit_bytes=VMEM_LIMIT),
        cost_estimate=pl.CostEstimate(flops=0, bytes_accessed=12 << 20, transcendentals=0),
    )(block, ingrad, piece, sums, first, second, third)
def turn_column(column):
    diagonal = lax.broadcasted_iota(jnp.int32, (128, 128), 0) == lax.broadcasted_iota(jnp.int32, (128, 128), 1)
    lines = []
    for block in range(column.shape[0] // 128):
        lines.append(jnp.sum(jnp.where(diagonal, column[block * 128 : (block + 1) * 128], 0.0), 0, keepdims=True))
    return jnp.concatenate(lines, 1)


def piece_gather(full_ref, send, recv, members):
    member = lax.axis_index("seq")
    parts = full_ref.shape[0]
    stages = (members - 1).bit_length()

    def give(part, r, stage):
        owner = flip(member, r)
        mark = r ^ (1 << stage)
        return push(
            full_ref.at[part, owner],
            full_ref.at[part, owner],
            send.at[part, mark],
            recv.at[part, mark],
            "seq",
            flip(member, 1 << stage),
        )

    def take(part, r):
        owner = flip(member, r)
        return push(
            full_ref.at[part, owner],
            full_ref.at[part, owner],
            send.at[part, r],
            recv.at[part, r],
            "seq",
            flip(member, r & -r),
        )

    def begin(part=0, levels=None):
        for stage in reversed(range(stages)) if levels is None else levels:
            give(part, 0, stage).start()

    def relay(part, r):
        take(part, r).wait_recv()
        for stage in reversed(range(zeros_below(r))):
            give(part, r, stage).start()
        if r == 1 << (stages - 1) and part + 1 < parts:
            begin(part + 1)

    order = sorted([r for r in range(1, members) if r % 2 == 0], key=lambda r: (-zeros_below(r), r))
    def when(part, r):
        return 2 * part + 3 * (bin(r).count("1") - 1), part, -zeros_below(r), r

    relays = sorted([(part, r) for r in order for part in range(parts)], key=lambda job: when(*job))

    def arrive():
        for part in range(parts):
            for r in range(1, members, 2):
                take(part, r).wait_recv()

    def finish():
        for part in range(parts):
            for r in [0] + order:
                for stage in range(zeros_below(r) if r else stages):
                    give(part, r, stage).wait_send()

    return begin, relay, relays, arrive, finish


def greet_seq(members):
    member = lax.axis_index("seq")
    stages = (members - 1).bit_length()
    barrier = pltpu.get_barrier_semaphore()
    for stage in range(stages):
        pl.semaphore_signal(barrier, inc=1, device_id={"seq": flip(member, 1 << stage)}, device_id_type=MESH)
    return barrier, stages


FRONT_REFS = 64


def front_kernel(
    members,
    heads,
    lengths_ref,
    input_ref,
    query_ref,
    key_ref,
    value_ref,
    beta_ref,
    first_gain_ref,
    second_gain_ref,
    out_weight_ref,
    conv_ref,
    head_gain_ref,
    *refs,
):
    own_refs, refs = refs[:-FRONT_REFS], refs[-FRONT_REFS:]
    front_body(
        members,
        heads,
        lengths_ref,
        input_ref,
        query_ref,
        key_ref,
        value_ref,
        beta_ref,
        first_gain_ref,
        second_gain_ref,
        out_weight_ref,
        conv_ref,
        head_gain_ref,
        own_refs,
        *refs,
    )


def front_body(
    members,
    heads,
    lengths_ref,
    input_ref,
    query_ref,
    key_ref,
    value_ref,
    beta_ref,
    first_gain_ref,
    second_gain_ref,
    out_weight_ref,
    conv_ref,
    head_gain_ref,
    own_refs,
    pack_hbm,
    first_hbm,
    pre_hbm,
    logits_hbm,
    halo_ref,
    scale_hbm,
    gains_ref,
    turned_hbm,
    full_hbm,
    others_hbm,
    qkv_hbm,
    inv_hbm,
    wu_hbm,
    mq_hbm,
    total_ref,
    delta_hbm,
    rows_hbm,
    far_rows_hbm,
    states_hbm,
    pack_ref,
    first_ref,
    pre_ref,
    logits_ref,
    scale_ref,
    turned_ref,
    full_ref,
    others_ref,
    qkv_ref,
    inv_ref,
    wu_ref,
    mq_ref,
    delta_ref,
    rows_ref,
    far_rows_ref,
    states_ref,
    store_sem,
    resets_ref,
    taps_ref,
    extra_ref,
    start_ref,
    out0_ref,
    state_ref,
    part_ref,
    slots_ref,
    pad_ref,
    edge_ref,
    pack_send,
    pack_recv,
    edge_send,
    edge_recv,
    turned_send,
    turned_recv,
    full_send,
    full_recv,
    head_send,
    head_recv,
    state_send,
    state_recv,
    row_near_send,
    row_near_recv,
    row_far_send,
    row_far_recv,
    row_pass_send,
    row_pass_recv,
):
    tokens, width = input_ref.shape
    columns = heads * CHUNK
    leaving = (
        (pack_ref, pack_hbm),
        (first_ref, first_hbm),
        (pre_ref, pre_hbm),
        (logits_ref, logits_hbm),
        (scale_ref, scale_hbm),
        (turned_ref, turned_hbm),
        (qkv_ref, qkv_hbm),
        (inv_ref, inv_hbm),
        (wu_ref, wu_hbm),
        (mq_ref, mq_hbm),
        (delta_ref, delta_hbm),
        (rows_ref, rows_hbm),
        (states_ref, states_hbm),
        (others_ref, others_hbm),
        (far_rows_ref, far_rows_hbm),
        (full_ref, full_hbm),
    )

    def store(number):
        return pltpu.make_async_copy(*leaving[number], store_sem.at[number])

    member = lax.axis_index("seq")
    _, _, near, far = head_peers()
    barrier, stages = greet_seq(members)
    for target in (near, far):
        pl.semaphore_signal(barrier, inc=1, device_id={"head": target}, device_id_type=MESH)

    @pl.when(member > 0)
    def _():
        pl.semaphore_signal(barrier, inc=1, device_id={"seq": member - 1}, device_id_type=MESH)

    window = slots_ref.shape[0]
    behind = members - 1 - member
    for hop in range(1, window + 1):

        @pl.when(member >= hop)
        def _():
            pl.semaphore_signal(barrier, inc=1, device_id={"seq": member - hop}, device_id_type=MESH)

    def state_copy(hop):
        return push(
            part_ref, slots_ref.at[hop - 1], state_send.at[hop - 1], state_recv.at[hop - 1], "seq", member + hop
        )

    pack_ref[0, member, :, :columns] = query_ref[...]
    pack_ref[0, member, :, columns : 2 * columns] = key_ref[...]
    pack_ref[0, member, :, 2 * columns : 3 * columns] = value_ref[...]
    extra_ref[...] = jnp.zeros_like(extra_ref)
    extra_ref[0:heads] = beta_ref[...].astype(F32)
    extra_ref[heads : heads + 1] = first_gain_ref[...].astype(F32)
    extra_ref[heads + 1 : heads + 2] = second_gain_ref[...].astype(F32)
    pack_ref[0, member, :, 3 * columns :] = extra_ref[...].T.astype(BF)
    turned_ref[0, member] = out_weight_ref[...].T
    for part, own_ref in enumerate(own_refs):
        full_ref[part, member] = own_ref[...]
    pack = piece_gather(pack_ref, pack_send, pack_recv, members)
    turned = piece_gather(turned_ref, turned_send, turned_recv, members)
    full = piece_gather(full_ref, full_send, full_recv, members)
    near_copy = push(turned_ref.at[0], others_ref.at[0], head_send.at[0], head_recv.at[0], "head", near)
    far_copy = push(turned_ref.at[0], others_ref.at[1], head_send.at[1], head_recv.at[1], "head", far)
    pass_copy = push(others_ref.at[1], others_ref.at[2], head_send.at[2], head_recv.at[2], "head", near)
    pl.semaphore_wait(barrier, stages + 2 + jnp.minimum(behind, 1) + jnp.minimum(behind, window))
    pack[0]()
    turned[0]()
    full[0](0, [stages - 1, 0])
    fill_resets(lengths_ref, resets_ref, tokens)
    fill_taps(conv_ref, taps_ref)

    last_rows = pl.ds(tokens - 16, 16)

    def edge(target):
        return push(input_ref.at[last_rows], edge_ref, edge_send, edge_recv, "seq", target)

    @pl.when(member + 1 < members)
    def _():
        edge(member + 1).start()

    chunk = 256

    def at(index):
        return pl.ds(pl.multiple_of(index * chunk, chunk), chunk)

    def measure(index):
        block = input_ref[at(index)].astype(F32)
        scale_ref[at(index)] = lax.rsqrt(jnp.mean(block * block, axis=-1, keepdims=True) + 1e-06)

    pl.loop(0, tokens // chunk)(measure)
    for job in pack[2]:
        pack[1](*job)
    for job in turned[2]:
        turned[1](*job)
    full[0](0, range(1, stages - 1))
    pack[3]()
    projection = pack_ref[0].reshape(width, pack_ref.shape[3])
    extras = projection[:, 3 * columns :].astype(F32)
    gains_ref[0:1] = turn_column(extras[:, heads : heads + 1])
    gains_ref[1:2] = turn_column(extras[:, heads + 1 : heads + 2])

    def project(index):
        first = (input_ref[at(index)].astype(F32) * scale_ref[at(index)] * gains_ref[0:1]).astype(BF)
        first_ref[at(index)] = first
        both = nn(first, pack_ref[0].reshape(width, pack_ref.shape[3]))
        pre_ref[at(index)] = both[:, : 3 * columns].astype(BF)
        logits_ref[at(index)] = both[:, 3 * columns :]

    pl.loop(0, tokens // chunk)(project)

    @pl.when(member == 0)
    def _():
        halo_ref[...] = jnp.zeros_like(halo_ref)

    @pl.when(member > 0)
    def _():
        edge(member).wait_recv()
        block = edge_ref[...].astype(F32)
        scale = lax.rsqrt(jnp.mean(block * block, axis=-1, keepdims=True) + 1e-06)
        first = (block * scale * gains_ref[0:1]).astype(BF)
        halo_ref[...] = nn(first, pack_ref[0].reshape(width, pack_ref.shape[3])[:, : 3 * columns]).astype(BF)

    turned[3]()
    for number in range(6):
        store(number).start()
    near_copy.start()
    far_copy.start()
    rows, cols = grid_indices()
    eye = jnp.where(rows == cols, 1.0, 0.0)
    top = lax.broadcasted_iota(jnp.int32, (CHUNK, 1), 0) < GROUP
    for head in range(heads):
        total_ref[head] = side(eye, jnp.zeros_like(eye))
    batch = pad_ref.shape[0]

    def one(step, carry):
        units = []
        for lane in range(batch):
            chunk = step * batch + lane
            pad = pad_ref.at[lane]
            load_padded(pad, pre_ref, halo_ref, chunk, resets_ref)
            mixed = convolve(pad, taps_ref)
            silued = mixed * sigmoid(mixed)
            keep0 = 1.0 - resets_ref[2 * chunk]
            keep1 = 1.0 - resets_ref[2 * chunk + 1]
            both = keep0 * keep1
            enter = jnp.where(top, keep0, both)
            leave = jnp.where(top, keep1, 1.0)
            at = pl.ds(pl.multiple_of(chunk * CHUNK, CHUNK), CHUNK)
            beta_rows = sigmoid(logits_ref[at, :])
            for head in range(heads):
                window = slice(head * CHUNK, (head + 1) * CHUNK)
                parts = []
                for kind in range(3):
                    part = silued[:, kind * columns + head * CHUNK : kind * columns + (head + 1) * CHUNK]
                    if kind < 2:
                        part = part * lax.rsqrt(jnp.sum(part * part, axis=-1, keepdims=True) + 1e-06)
                    part = part.astype(BF)
                    qkv_ref[at, kind * columns + head * CHUNK : kind * columns + (head + 1) * CHUNK] = part
                    parts.append(part)
                units.append((chunk, head, *parts, beta_rows[:, head : head + 1], keep1, both, enter, leave))
        turned = [u[3].T for u in units]
        strict = [
            jnp.where(rows > cols, u[5] * nn(u[3], t), 0.0) for u, t in zip(units, turned)
        ]
        inverses = [r.astype(BF) for r in inverse_levels(strict, rows, cols, [u[6] for u in units])]
        factors = []
        for u, inverse in zip(units, inverses):
            beta = u[5]
            factors.append(nn(inverse, side(u[3].astype(F32) * beta, u[4].astype(F32) * beta)))
        for u, inverse, factor, t in zip(units, inverses, factors, turned):
            chunk, head, query, key, value, beta, keep1, both, enter, leave = u
            weight, update = factor[:, :CHUNK], factor[:, CHUNK:]
            entering_weight = weight * enter
            inv_ref[chunk, head] = inverse
            wu_ref[chunk, head] = side(entering_weight, update).astype(BF)
            gathered = nn(t, side(weight, update * leave))
            device_map = (both * (eye - gathered[:, :CHUNK])).astype(BF)
            shift = gathered[:, CHUNK:]
            scores = jnp.where(rows >= cols, nn(query, t), 0.0)
            scores = jnp.where((rows >= GROUP) & (cols < GROUP), scores * keep1, scores)
            seen = nn(scores, side(entering_weight, update))
            effective = query.astype(F32) * enter - seen[:, :CHUNK]
            mq_ref[chunk, head] = stack(device_map, effective.astype(BF))
            out0_ref[chunk, head] = seen[:, CHUNK:]
            running = total_ref[head]
            start_ref[chunk, head] = running.astype(BF)
            total_ref[head] = nn(device_map, running) + side(jnp.zeros_like(shift), shift)
        return carry

    count = resets_ref.shape[0] // 2 // batch
    held = 3 if len(full[2]) > 3 else 0
    relays = full[2][: len(full[2]) - held]

    def pumped(step, carry):
        carry = one(step, carry)
        for turn in range(count):
            jobs = [job for place, job in enumerate(relays) if place * count // len(relays) == turn]
            if not jobs and turn != count // 2:
                continue

            @pl.when(step == turn)
            def _():
                for job in jobs:
                    full[1](*job)
                if turn == count // 2:
                    far_copy.wait_recv()
                    pass_copy.start()

        return carry

    lax.fori_loop(0, count, pumped, 0)
    for number in range(6, 10):
        store(number).start()
    part_ref[...] = total_ref[...].astype(BF)
    for hop in range(1, window + 1):

        @pl.when(behind >= hop)
        def _():
            state_copy(hop).start()

    for job in full[2][len(full[2]) - held :]:
        full[1](*job)
    state_ref[...] = jnp.zeros_like(state_ref)
    for hop in range(window, 0, -1):

        @pl.when(member >= hop)
        def _():
            state_copy(hop).wait_recv()
            for head in range(heads):
                part = slots_ref[hop - 1, head]
                state_ref[head] = nn(part[:, :CHUNK], state_ref[head]) + part[:, CHUNK:].astype(F32)

    def near_rows(index):
        return push(
            rows_ref.at[at(index)], far_rows_ref.at[0, at(index)], row_near_send.at[index], row_near_recv.at[index], "head", near
        )

    def far_rows(index):
        return push(
            rows_ref.at[at(index)], far_rows_ref.at[1, at(index)], row_far_send.at[index], row_far_recv.at[index], "head", far
        )

    def pass_rows(index):
        return push(
            far_rows_ref.at[1, at(index)], far_rows_ref.at[2, at(index)], row_pass_send.at[index], row_pass_recv.at[index], "head", near
        )

    def finished(index):
        for lane in range(chunk // CHUNK):
            place_ = index * (chunk // CHUNK) + lane
            rows_at = pl.ds(pl.multiple_of(place_ * CHUNK, CHUNK), CHUNK)
            begins = [start_ref[place_, head] for head in range(heads)]
            states = [
                (nn(begins[head][:, :CHUNK], state_ref[head]) + begins[head][:, CHUNK:].astype(F32)).astype(BF)
                for head in range(heads)
            ]
            outs = [out0_ref[place_, head] + nn(mq_ref[place_, head, CHUNK:], states[head]) for head in range(heads)]
            for head in range(heads):
                lanes = slice(head * CHUNK, (head + 1) * CHUNK)
                states_ref[place_, head] = states[head]
                delta_ref[rows_at, lanes] = outs[head]
                scale = lax.rsqrt(jnp.mean(outs[head] * outs[head], axis=-1, keepdims=True) + 1e-05)
                rows_ref[rows_at, lanes] = (outs[head] * scale * head_gain_ref[...]).astype(BF)
        far_rows(index).start()
        near_rows(index).start()

    pl.loop(0, tokens // chunk)(finished)
    for number in range(10, 13):
        store(number).start()

    @pl.loop(0, tokens // chunk)
    def _(index):
        far_rows(index).wait_recv()
        pass_rows(index).start()

    near_copy.wait()
    far_copy.wait_send()
    pass_copy.wait()
    store(13).start()

    @pl.when(member + 1 < members)
    def _():
        edge(member + 1).wait_send()

    for hop in range(1, window + 1):

        @pl.when(behind >= hop)
        def _():
            state_copy(hop).wait_send()

    @pl.loop(0, tokens // chunk)
    def _(index):
        near_rows(index).wait()
        far_rows(index).wait_send()
        pass_rows(index).wait()

    store(14).start()
    full[3]()
    store(15).start()
    for gather in (pack, turned, full):
        gather[4]()
    for number in range(len(leaving)):
        store(number).wait()


def front_stage(lengths, inputs, mixer_weights, conv, head_gain, own, members, heads, collective):
    tokens, width = inputs.shape
    columns = heads * CHUNK
    chunks = tokens // CHUNK
    whole = pl.BlockSpec(memory_space=pltpu.VMEM)
    piece = width // members
    window = min(members - 1, members // 2)

    def units(wide, kind):
        return jax.ShapeDtypeStruct((chunks, heads, *wide), kind)

    def dma(*shape):
        return [pltpu.SemaphoreType.DMA(shape)] * 2

    outside = pl.BlockSpec(memory_space=pl.ANY)
    made = (
        jax.ShapeDtypeStruct((1, members, piece, 3 * columns + CHUNK), BF),
        jax.ShapeDtypeStruct((tokens, width), BF),
        jax.ShapeDtypeStruct((tokens, 3 * columns), BF),
        jax.ShapeDtypeStruct((tokens, CHUNK), F32),
        jax.ShapeDtypeStruct((16, 3 * columns), BF),
        jax.ShapeDtypeStruct((tokens, 1), F32),
        jax.ShapeDtypeStruct((2, width), F32),
        jax.ShapeDtypeStruct((1, members, columns, piece), BF),
        jax.ShapeDtypeStruct((len(own), members, *own[0].shape), BF),
        jax.ShapeDtypeStruct((3, members, columns, piece), BF),
        jax.ShapeDtypeStruct((tokens, 3 * columns), BF),
        units((CHUNK, CHUNK), BF),
        units((CHUNK, 2 * CHUNK), BF),
        units((2 * CHUNK, CHUNK), BF),
        jax.ShapeDtypeStruct((heads, CHUNK, 2 * CHUNK), F32),
        jax.ShapeDtypeStruct((tokens, columns), F32),
        jax.ShapeDtypeStruct((tokens, columns), BF),
        jax.ShapeDtypeStruct((3, tokens, columns), BF),
        units((CHUNK, CHUNK), BF),
    )
    stay = (4, 6, 14)
    return pl.pallas_call(
        functools.partial(front_kernel, members, heads),
        name="front",
        out_shape=made,
        in_specs=[pl.BlockSpec(memory_space=pltpu.SMEM)] + [whole] * (3 + len(mixer_weights) + len(own)),
        out_specs=tuple(whole if number in stay else outside for number in range(len(made))),
        scratch_shapes=[pltpu.VMEM(a.shape, a.dtype) for number, a in enumerate(made) if number not in stay]
        + [
            pltpu.SemaphoreType.DMA((len(made) - len(stay),)),
            pltpu.SMEM((tokens // GROUP,), F32),
            pltpu.VMEM((4, 3 * columns), F32),
            pltpu.VMEM((CHUNK, piece), F32),
            pltpu.VMEM((chunks, heads, CHUNK, 2 * CHUNK), BF),
            pltpu.VMEM((chunks, heads, CHUNK, CHUNK), F32),
            pltpu.VMEM((heads, CHUNK, CHUNK), F32),
            pltpu.VMEM((heads, CHUNK, 2 * CHUNK), BF),
            pltpu.VMEM((window, heads, CHUNK, 2 * CHUNK), BF),
            pltpu.VMEM((2, 144, 3 * columns), F32),
            pltpu.VMEM((16, width), BF),
        ]
        + dma(1, members)
        + dma()
        + dma(1, members)
        + dma(len(own), members)
        + dma(3)
        + dma(window)
        + dma(tokens // 256) * 3,
        compiler_params=pltpu.CompilerParams(
            collective_id=collective, has_side_effects=True, vmem_limit_bytes=VMEM_LIMIT
        ),
        cost_estimate=pl.CostEstimate(flops=8 * 10**9, bytes_accessed=40 << 20, transcendentals=2 << 20),
    )(lengths, inputs, *mixer_weights, conv, head_gain, *own)


def lanes_whole(pieces):
    places, rows, piece = pieces.shape
    if piece >= 128:
        return pieces
    group = 128 // piece
    return pieces.reshape(places // group, group, rows, piece).transpose(0, 2, 1, 3).reshape(places // group, rows, 128)


def lanes_split(blocks, piece):
    count, rows, lanes = blocks.shape
    if piece >= 128:
        return blocks
    group = 128 // piece
    return blocks.reshape(count, rows, group, piece).transpose(0, 2, 1, 3).reshape(count * group, rows, piece)


def body(
    block_input,
    first_gain,
    query_weight,
    key_weight,
    value_weight,
    beta_weight,
    conv_weight,
    head_gain,
    output_weight,
    second_gain,
    gate_weight,
    up_weight,
    down_weight,
    lengths,
    cotangent,
):
    tokens, width = block_input.shape
    heads = beta_weight.shape[1]
    columns = query_weight.shape[1]
    hidden_columns = gate_weight.shape[1]
    members = lax.axis_size("seq")
    piece = width // members
    seq_place = lax.axis_index("seq")

    gain_head = head_gain.astype(F32)[None, :]
    own = [gate_weight.T, up_weight.T, down_weight.T]
    split = piece < 128
    (
        mixer_pack,
        first_rows,
        pre,
        logits,
        halo,
        scale_one,
        gains,
        turned,
        full,
        others,
        qkv,
        inv,
        wu,
        mq,
        total,
        delta,
        head_rows,
        far_rows,
        states,
    ) = front_stage(
        lengths,
        block_input,
        (
            query_weight,
            key_weight,
            value_weight,
            beta_weight.T,
            first_gain[None, :],
            second_gain[None, :],
            output_weight,
        ),
        conv_weight,
        gain_head,
        [own[0][:16]] if split else own,
        members,
        heads,
        5,
    )
    mixer_pack = mixer_pack.reshape(width, -1)
    if split:
        gathered = lax.all_gather(jnp.stack(own), "seq", axis=1)
        full = jnp.stack([lanes_whole(gathered[i]) for i in range(3)])
    turned = lanes_whole(turned[0])
    others = jnp.stack([lanes_whole(others[i]) for i in range(3)]) if split else others
    d_heads, update_part, middle_shard, d_middle_shard, *grads, second_grad = middle_stage(
        head_rows, far_rows, full, turned, others, block_input, cotangent, gains, 2
    )
    second_part = jnp.sum(second_grad, 0)
    if split:
        pieces = jnp.concatenate([part for pair in grads for part in pair], 1)
        whole_sum = lax.psum_scatter(lanes_split(pieces, piece), "seq", scatter_dimension=0, tiled=False).astype(F32)
        grads = [jnp.zeros((1, members, 16, 128), BF)] * 3
    ddelta, gain_part, arrive, block_output, third_sum = state_backward(
        d_heads, delta, gain_head, mq, total, update_part, middle_shard, grads[2], members, 1
    )
    d_pre, taps_part, first_sum = mixer_backward(
        lengths, pre, halo, conv_weight, logits, qkv, inv, wu, mq, states, ddelta, arrive, grads[0], 3
    )
    input_gradient, mixer_sum, sums, second_sum = final_stage(
        first_rows, d_pre, mixer_pack, block_input, scale_one, gains, d_middle_shard, (gain_part, second_grad, taps_part), grads[1], members, 4
    )
    if not split:
        done = finish_stage(
            block_output, input_gradient, mixer_sum, sums, first_sum, second_sum, third_sum, hidden_columns, heads
        )
        block, ingrad, gain_1, grad_q, grad_k, grad_v, grad_b, grad_c, gain_h, grad_o, gain_2, *rest = done
        return (
            block,
            ingrad,
            gain_1.reshape(-1),
            grad_q,
            grad_k,
            grad_v,
            grad_b.T,
            grad_c,
            gain_h.reshape(-1),
            grad_o,
            gain_2.reshape(-1),
            *(grad.T for grad in rest),
        )
    gain_sum = sums[1, :CHUNK]
    conv_gradient = sums[9 : 9 + 12 * columns // width].reshape(4, 3, columns).transpose(1, 0, 2)
    row_start = seq_place * piece
    first_gradient = lax.dynamic_slice_in_dim(sums[0], row_start, piece, 0)
    second_gradient = lax.dynamic_slice_in_dim(sums[8], row_start, piece, 0)
    beta_gradient = mixer_sum[:, 3 * columns : 3 * columns + heads]
    return (
        block_output,
        input_gradient,
        first_gradient,
        mixer_sum[:, :columns],
        mixer_sum[:, columns : 2 * columns],
        mixer_sum[:, 2 * columns : 3 * columns],
        beta_gradient,
        conv_gradient,
        gain_sum,
        whole_sum[3 * hidden_columns :].T,
        second_gradient,
        whole_sum[:hidden_columns].T,
        whole_sum[hidden_columns : 2 * hidden_columns].T,
        whole_sum[2 * hidden_columns : 3 * hidden_columns].T,
    )


def solution(mesh):
    return jax.shard_map(
        body,
        mesh=mesh,
        in_specs=(
            P("seq", None),
            P("seq"),
            P("seq", "head"),
            P("seq", "head"),
            P("seq", "head"),
            P("seq", "head"),
            P(None, None, "head"),
            P(),
            P("seq", "head"),
            P("seq"),
            P("seq", "head"),
            P("seq", "head"),
            P("seq", "head"),
            P(),
            P("seq", None),
        ),
        out_specs=(
            P("seq", "head"),
            P("seq", "head"),
            P("seq"),
            P("seq", "head"),
            P("seq", "head"),
            P("seq", "head"),
            P("seq", "head"),
            P(None, None, "head"),
            P(),
            P("seq", "head"),
            P("seq"),
            P("seq", "head"),
            P("seq", "head"),
            P("seq", "head"),
        ),
        check_vma=False,
    )
```

```python
import functools

import jax
import jax.numpy as jnp
from jax import lax
from jax.experimental import pallas as pl
from jax.experimental.pallas import tpu as pltpu
from jax.sharding import PartitionSpec as P

GROUP = 64
CHUNK = 128
MESH = pl.DeviceIdType.MESH
BF = jnp.bfloat16
F32 = jnp.float32
VMEM_LIMIT = 59 << 20


def nn(left, right):
    return jnp.dot(left.astype(BF), right.astype(BF), preferred_element_type=F32)


def tn(left, right):
    return lax.dot_general(
        left.astype(BF), right.astype(BF), (((0,), (0,)), ((), ())), preferred_element_type=F32
    )


def nt(left, right):
    return lax.dot_general(
        left.astype(BF), right.astype(BF), (((1,), (1,)), ((), ())), preferred_element_type=F32
    )


def sigmoid(v):
    return 0.5 * jnp.tanh(0.5 * v) + 0.5


def side(left, right):
    return jnp.concatenate([left, right], 1)


def stack(top, bottom):
    return jnp.concatenate([top, bottom], 0)


def grid_indices():
    rows = lax.broadcasted_iota(jnp.int32, (CHUNK, CHUNK), 0)
    cols = lax.broadcasted_iota(jnp.int32, (CHUNK, CHUNK), 1)
    return rows, cols


def fill_resets(lengths_ref, resets_ref, tokens):
    base = lax.axis_index("seq") * tokens

    @pl.loop(0, tokens // GROUP)
    def _(block):
        position = base + block * GROUP
        value = jnp.float32(0.0)
        start = jnp.int32(0)
        for index in range(lengths_ref.shape[0]):
            value = jnp.where(start == position, 1.0, value)
            start = start + lengths_ref[index]
        resets_ref[block] = value


def fill_taps(conv_ref, taps_ref):
    columns = conv_ref.shape[2]
    for kind in range(3):
        taps_ref[:, kind * columns : (kind + 1) * columns] = conv_ref[kind].astype(F32)


def load_padded(pad_ref, pre_ref, halo_ref, chunk, resets_ref):
    start = pl.multiple_of(chunk * CHUNK, CHUNK)
    before = pl.multiple_of(jnp.maximum(start - 16, 0), 16)
    own = pre_ref[pl.ds(start, CHUNK), :].astype(F32)
    earlier = pre_ref[pl.ds(before, 16), :].astype(F32)[8:]
    halo = halo_ref[...].astype(F32)[8:]
    first = jnp.where(chunk == 0, halo, earlier)
    keep0 = 1.0 - resets_ref[2 * chunk]
    keep1 = 1.0 - resets_ref[2 * chunk + 1]
    pad_ref[0:8] = first * keep0
    pad_ref[8:72] = own[:GROUP]
    pad_ref[72:80] = own[GROUP - 8 : GROUP] * keep1
    pad_ref[80:144] = own[GROUP:]


def tap_rows(pad_ref, tap):
    return stack(pad_ref[5 + tap : 69 + tap], pad_ref[77 + tap : 141 + tap])


def convolve(pad_ref, taps_ref):
    mixed = None
    for tap in range(4):
        term = taps_ref[tap : tap + 1] * tap_rows(pad_ref, tap)
        mixed = term if mixed is None else mixed + term
    return mixed


def inverse_levels(strict, rows, cols, keep1):
    eye = jnp.where(rows == cols, 1.0, 0.0)
    pair = (rows // 2) == (cols // 2)
    results = [eye - jnp.where(pair, a, 0.0) for a in strict]
    width = 2
    while width < CHUNK:
        off = ((rows // (2 * width)) == (cols // (2 * width))) & ((rows // width) != (cols // width))
        lows = [r.astype(BF) for r in results]
        parts = [jnp.where(off, a, 0.0).astype(BF) for a in strict]
        if width == GROUP:
            parts = [jnp.where(off, a * k, 0.0).astype(BF) for a, k in zip(strict, keep1)]
        steps = [nn(r, p) for r, p in zip(lows, parts)]
        results = [r - nn(s, low) for r, s, low in zip(results, steps, lows)]
        width *= 2
    return results


def state_backward_kernel(
    heads,
    window,
    dheads_ref,
    delta_ref,
    gain_ref,
    mq_ref,
    total_ref,
    update_ref,
    mid_ref,
    grads_ref,
    ddelta_ref,
    gain_grad_ref,
    state_ref,
    block_ref,
    sum_ref,
    shift_ref,
    part_ref,
    slots_ref,
    send_sem,
    recv_sem,
    near_ref,
    relay_ref,
    far_ref,
    near_send,
    near_recv,
    far_send,
    far_recv,
    piece_relay,
    piece_slots,
    piece_send,
    piece_recv,
):
    member, members = lax.axis_index("seq"), lax.axis_size("seq")
    _, _, near, far = head_peers()
    chunk = 256
    steps = update_ref.shape[0] // chunk
    chunks = mq_ref.shape[0]
    behind = members - 1 - member
    at, _, start_pair, pass_on, own_sum, finish = head_scatter_copies(
        chunk, update_ref, near_ref, relay_ref, far_ref, (near_send, near_recv, far_send, far_recv)
    )
    begin, receive, jobs, end = piece_scatter(
        grads_ref, piece_relay, piece_slots, sum_ref, piece_send, piece_recv, members
    )
    barrier, stages = greet_seq(members)
    for hop in range(1, window + 1):

        @pl.when(behind >= hop)
        def _():
            pl.semaphore_signal(barrier, inc=1, device_id={"seq": member + hop}, device_id_type=MESH)

    for target in (near, far):
        pl.semaphore_signal(barrier, inc=1, device_id={"head": target}, device_id_type=MESH)
    pl.semaphore_wait(barrier, stages + 2 + jnp.minimum(member, window))

    @pl.loop(0, steps)
    def _(index):
        start_pair(index)

    for head in range(heads):
        part_ref[0, head] = total_ref[head, :, :CHUNK].T.astype(BF)

    def copy(kind, hop):
        return push(
            part_ref.at[kind],
            slots_ref.at[kind, hop - 1],
            send_sem.at[kind, hop - 1],
            recv_sem.at[kind, hop - 1],
            "seq",
            member - hop,
        )

    def send(kind):
        for hop in range(1, window + 1):

            @pl.when(member >= hop)
            def _():
                copy(kind, hop).start()

    send(0)
    half = len(jobs) // 4
    begin(jobs[:half])
    shift_ref[...] = jnp.zeros_like(shift_ref)
    gain_grad_ref[...] = jnp.zeros_like(gain_grad_ref)

    def one(step, carry):
        index = chunks - 1 - step
        rows = pl.ds(pl.multiple_of(index * CHUNK, CHUNK), CHUNK)
        for head in range(heads):
            lanes = slice(head * CHUNK, (head + 1) * CHUNK)
            out = delta_ref[rows, lanes]
            grad = dheads_ref[rows, lanes].astype(F32)
            scale = lax.rsqrt(jnp.mean(out * out, axis=-1, keepdims=True) + 1e-05)
            unit = out * scale
            gain_grad_ref[...] += jnp.sum((grad * unit).reshape(CHUNK // 8, 8, CHUNK), 0)
            scaled = grad * gain_ref[...]
            back = scale * (scaled - unit * jnp.mean(scaled * unit, axis=-1, keepdims=True))
            back = back.astype(BF)
            ddelta_ref[rows, lanes] = back
            shift_ref[head] = tn(mq_ref[index, head], stack(shift_ref[head].astype(BF), back))

        @pl.when(lax.rem(step, 2) == 1)
        def _():
            pass_on(lax.div(step, 2))

        return carry

    lax.fori_loop(0, chunks, one, 0)
    for head in range(heads):
        part_ref[1, head] = shift_ref[head].astype(BF)
    send(1)
    begin(jobs[half:])
    for job in jobs[: len(jobs) // 2]:
        receive(*job)
    state_ref[...] = jnp.zeros_like(state_ref)
    for hop in range(window, 0, -1):

        @pl.when(behind >= hop)
        def _():
            copy(0, hop).wait_recv()
            copy(1, hop).wait_recv()
            for head in range(heads):
                state_ref[head] = nn(slots_ref[0, hop - 1, head], state_ref[head]) + slots_ref[1, hop - 1, head].astype(F32)

    for job in jobs[len(jobs) // 2 :]:
        receive(*job)

    @pl.loop(0, steps)
    def _(index):
        block_ref[at(index)] = (mid_ref[at(index)] + own_sum(index)).astype(BF)
        finish(index)

    end()
    for hop in range(1, window + 1):

        @pl.when(member >= hop)
        def _():
            copy(0, hop).wait_send()
            copy(1, hop).wait_send()


def state_backward(dheads, delta, gain, mq, total, update, mid, grads, members, collective):
    chunks, heads = mq.shape[:2]
    tokens, columns = mid.shape
    window = min(members - 1, members // 2)
    whole = pl.BlockSpec(memory_space=pltpu.VMEM)
    parts, _, *piece = grads.shape
    return pl.pallas_call(
        functools.partial(state_backward_kernel, heads, window),
        name="state_backward",
        out_shape=(
            jax.ShapeDtypeStruct((tokens, columns), BF),
            jax.ShapeDtypeStruct((8, CHUNK), F32),
            jax.ShapeDtypeStruct((heads, CHUNK, CHUNK), F32),
            jax.ShapeDtypeStruct((tokens, columns), BF),
            jax.ShapeDtypeStruct((parts, *piece), F32),
        ),
        in_specs=[whole] * 8,
        out_specs=(whole,) * 5,
        scratch_shapes=[
            pltpu.VMEM((heads, CHUNK, CHUNK), F32),
            pltpu.VMEM((2, heads, CHUNK, CHUNK), BF),
            pltpu.VMEM((2, window, heads, CHUNK, CHUNK), BF),
            pltpu.SemaphoreType.DMA((2, window)),
            pltpu.SemaphoreType.DMA((2, window)),
        ]
        + head_scatter_scratch(tokens, columns, tokens // 256)
        + piece_scatter_scratch(parts, members, piece),
        compiler_params=pltpu.CompilerParams(
            collective_id=collective, has_side_effects=True, vmem_limit_bytes=VMEM_LIMIT
        ),
        cost_estimate=pl.CostEstimate(flops=10**9, bytes_accessed=30 << 20, transcendentals=0),
    )(dheads, delta, gain, mq, total, update, mid, grads)


def piece_scatter_scratch(parts, members, piece):
    return [
        pltpu.VMEM((parts, max(members // 2 - 1, 1), *piece), BF),
        pltpu.VMEM((parts, members - 1, *piece), BF),
        pltpu.SemaphoreType.DMA((parts, members)),
        pltpu.SemaphoreType.DMA((parts, members)),
    ]


def piece_scatter(own_ref, relay_ref, slots_ref, total_ref, send, recv, members):
    member = lax.axis_index("seq")
    parts = own_ref.shape[0]
    stages = (members - 1).bit_length()
    order = sorted(range(members), key=lambda r: zeros_below(r) if r else stages)
    levels = {r: list(range(zeros_below(r) if r else stages)) for r in order}
    events = {}
    for r in order:
        for stage in levels[r]:
            events[r, stage] = len(events)
    kept = [r for r in order if r and r % 2 == 0]

    def source(part, r):
        return own_ref.at[part, flip(member, r)] if r % 2 else relay_ref.at[part, kept.index(r)]

    def give(part, r):
        stage = zeros_below(r)
        slot = events[r ^ (1 << stage), stage]
        return push(
            source(part, r), slots_ref.at[part, slot], send.at[part, r], recv.at[part, slot], "seq", flip(member, 1 << stage)
        )

    def take(part, r, stage):
        slot = events[r, stage]
        return push(
            own_ref.at[part, flip(member, 1)], slots_ref.at[part, slot], send.at[part, 0], recv.at[part, slot], "seq", flip(member, 1 << stage)
        )

    jobs = [(part, r) for r in order if r % 2 == 0 for part in range(parts)]

    def begin(some=None):
        for part, r in jobs if some is None else some:
            give(part, r ^ 1).start()

    def receive(part, r):
        total = own_ref[part, flip(member, r)].astype(F32)
        for stage in levels[r]:
            take(part, r, stage).wait_recv()
            total = total + slots_ref[part, events[r, stage]].astype(F32)
        if r:
            relay_ref[part, kept.index(r)] = total.astype(BF)
            give(part, r).start()
        else:
            total_ref[part] = total

    def finish():
        for part in range(parts):
            for r in order:
                if r:
                    give(part, r).wait_send()

    return begin, receive, jobs, finish


def mixer_backward_kernel(
    heads,
    lengths_ref,
    pre_hbm,
    halo_ref,
    conv_ref,
    logits_hbm,
    qkv_hbm,
    inv_hbm,
    wu_hbm,
    mq_hbm,
    states_hbm,
    ddelta_hbm,
    arrive_ref,
    grads_ref,
    dpre_ref,
    taps_grad_ref,
    total_ref,
    pre_ref,
    logits_ref,
    qkv_ref,
    inv_ref,
    wu_ref,
    mq_ref,
    states_ref,
    ddelta_ref,
    load_sem,
    resets_ref,
    taps_ref,
    carry_ref,
    pad_ref,
    dpad_ref,
    tail_ref,
    lead_ref,
    edge_ref,
    send_sem,
    recv_sem,
    relay_ref,
    slots_ref,
    piece_send,
    piece_recv,
):
    member, members = lax.axis_index("seq"), lax.axis_size("seq")
    barrier, stages = greet_seq(members)
    begin, receive, order, finish = piece_scatter(
        grads_ref, relay_ref, slots_ref, total_ref, piece_send, piece_recv, members
    )

    @pl.when(member + 1 < members)
    def _():
        pl.semaphore_signal(barrier, inc=1, device_id={"seq": member + 1}, device_id_type=MESH)

    columns = heads * CHUNK
    chunks = mq_ref.shape[0]
    fill_resets(lengths_ref, resets_ref, pre_ref.shape[0])
    fill_taps(conv_ref, taps_ref)
    quarter = chunks // 4
    sources = (pre_hbm, logits_hbm, qkv_hbm, ddelta_hbm, inv_hbm, wu_hbm, mq_hbm, states_hbm)
    targets = (pre_ref, logits_ref, qkv_ref, ddelta_ref, inv_ref, wu_ref, mq_ref, states_ref)

    def load(number, turn):
        unit = CHUNK if number < 4 else 1
        reach = pl.ds((chunks - (turn + 1) * quarter) * unit, quarter * unit)
        return pltpu.make_async_copy(
            sources[number].at[reach], targets[number].at[reach], load_sem.at[number, turn]
        )

    for turn in range(4):
        for number in range(8):
            load(number, turn).start()
    load(0, 0).wait()
    rows, cols = grid_indices()
    top = lax.broadcasted_iota(jnp.int32, (CHUNK, 1), 0) < GROUP
    pl.semaphore_wait(barrier, stages + jnp.minimum(member, 1))
    begin()
    carry_ref[...] = arrive_ref[...]
    taps_grad_ref[...] = jnp.zeros_like(taps_grad_ref)
    dpad_ref[136:144] = jnp.zeros_like(dpad_ref[136:144])

    def one(step, carry):
        chunk = chunks - 1 - step
        at = pl.ds(pl.multiple_of(chunk * CHUNK, CHUNK), CHUNK)
        for turn in range(4):

            @pl.when(step == turn * quarter)
            def _():
                for number in range(1, 8):
                    load(number, turn).wait()
                if turn < 3:
                    load(0, turn + 1).wait()

        keep0 = 1.0 - resets_ref[2 * chunk]
        keep1 = 1.0 - resets_ref[2 * chunk + 1]
        both = keep0 * keep1
        enter = jnp.where(top, keep0, both)
        leave = jnp.where(top, keep1, 1.0)
        load_padded(pad_ref, pre_ref, halo_ref, chunk, resets_ref)
        mixed = convolve(pad_ref, taps_ref)
        gate = sigmoid(mixed)
        slope = gate * (1.0 + mixed * (1.0 - gate))
        silued = mixed * gate
        beta_rows = sigmoid(logits_ref[at, :])
        grads = [[None] * heads for _ in range(3)]
        dlogits = []
        cross = (rows >= GROUP) & (cols < GROUP)

        def part(kind, head):
            return slice(kind * columns + head * CHUNK, kind * columns + (head + 1) * CHUNK)

        def masked(product, keep):
            lower = jnp.where(keep, product, 0.0)
            return jnp.where(cross, lower * keep1, lower).astype(BF)

        every = range(heads)
        query = [qkv_ref[at, part(0, h)] for h in every]
        key = [qkv_ref[at, part(1, h)] for h in every]
        value = [qkv_ref[at, part(2, h)] for h in every]
        key32 = [k.astype(F32) for k in key]
        beta = [beta_rows[:, h : h + 1] for h in every]
        inverse = [inv_ref[chunk, h] for h in every]
        weight = [wu_ref[chunk, h, :, :CHUNK] for h in every]
        factors = [wu_ref[chunk, h] for h in every]
        update = [wu_ref[chunk, h, :, CHUNK:] for h in every]
        state = [states_ref[chunk, h] for h in every]
        out_grad = [ddelta_ref[at, h * CHUNK : (h + 1) * CHUNK] for h in every]
        later = [carry_ref[h].astype(BF) for h in every]
        carried = [tn(mq_ref[chunk, h], stack(later[h], out_grad[h])) for h in every]
        scores = [masked(nt(query[h], key[h]), rows >= cols) for h in every]
        fresh = [(update[h].astype(F32) - nn(weight[h], state[h])).astype(BF) for h in every]
        fresh_low = [(tn(scores[h], out_grad[h]) + leave * nn(key[h], later[h])).astype(BF) for h in every]
        score_grad = [masked(nt(out_grad[h], fresh[h]), rows >= cols) for h in every]
        through = [nt(stack(out_grad[h], fresh_low[h]), state[h]) for h in every]
        weight_grad = [(-enter * through[h][CHUNK:]).astype(BF) for h in every]
        back = [tn(inverse[h], side(weight_grad[h], fresh_low[h])) for h in every]
        query_grad = [enter * through[h][:CHUNK] + nn(score_grad[h], key[h]) for h in every]
        key_grad = [tn(score_grad[h], query[h]) + leave * nt(fresh[h], later[h]) for h in every]
        strict = [masked(-nt(back[h].astype(BF), factors[h]), rows > cols) for h in every]
        strict_key = [nn(strict[h], key[h]) for h in every]
        turned = [tn(strict[h], (beta[h] * key32[h]).astype(BF)) for h in every]
        for h in every:
            carry_ref[h] = carried[h]
            yk, zv = back[h][:, :CHUNK], back[h][:, CHUNK:]
            both_key = yk + strict_key[h]
            key_grad[h] = key_grad[h] + beta[h] * both_key + turned[h]
            grads[2][h] = beta[h] * zv
            beta_grad = jnp.sum(both_key * key32[h] + zv * value[h].astype(F32), axis=-1, keepdims=True)
            dlogits.append(beta_grad * beta[h] * (1.0 - beta[h]))
        for kind, grad in ((0, query_grad), (1, key_grad)):
            raw = [silued[:, part(kind, h)] for h in every]
            norm = [lax.rsqrt(jnp.sum(raw[h] * raw[h], axis=-1, keepdims=True) + 1e-06) for h in every]
            unit = [raw[h] * norm[h] for h in every]
            inner = [jnp.sum(unit[h] * grad[h], axis=-1, keepdims=True) for h in every]
            grads[kind] = [(grad[h] - unit[h] * inner[h]) * norm[h] for h in every]
        lanes = lax.broadcasted_iota(jnp.int32, (CHUNK, CHUNK), 1)
        spread = jnp.zeros((CHUNK, CHUNK), F32)
        for head in range(heads):
            spread = jnp.where(lanes == head, dlogits[head], spread)
        dpre_ref[at, 3 * columns :] = spread.astype(BF)
        dmixed = jnp.concatenate([g for kind in grads for g in kind], 1) * slope
        dpad_ref[0:GROUP] = dmixed[:GROUP]
        dpad_ref[GROUP : GROUP + 8] = dmixed[GROUP : GROUP + 8] * keep1
        dpad_ref[72 : 72 + GROUP] = dmixed[GROUP:]
        dpre = None
        for tap in range(4):
            back = 3 - tap
            shifted = stack(dpad_ref[back : back + GROUP], dpad_ref[72 + back : 72 + back + GROUP])
            term = taps_ref[tap : tap + 1] * shifted
            dpre = term if dpre is None else dpre + term
            seen = (dmixed * tap_rows(pad_ref, tap)).reshape(CHUNK // 8, 8, 3 * columns)
            taps_grad_ref[tap] += jnp.sum(seen, 0)
        dpre_ref[at, : 3 * columns] = dpre.astype(BF)

        @pl.when(step == 0)
        def _():
            tail_ref[...] = dpre[CHUNK - 16 :]

        dpad_ref[136:144] = dmixed[:8] * keep0
        for place, job in enumerate(order):

            @pl.when(step == (place + 1) * (chunks - 1) // len(order))
            def _():
                receive(*job)

        return carry

    lax.fori_loop(0, chunks, one, 0)
    index = lax.broadcasted_iota(jnp.int32, (8, 1), 0)
    lead = jnp.zeros((8, 3 * columns), F32)
    dpad_ref[0:128] = jnp.zeros_like(dpad_ref[0:128])
    dpad_ref[8:16] = dpad_ref[136:144]
    for tap in range(3):
        back = 3 - tap
        lead = lead + taps_ref[tap : tap + 1] * dpad_ref[back : back + 8]
    lead_ref[...] = lead

    def to_previous(target):
        return push(lead_ref, edge_ref, send_sem, recv_sem, "seq", target)

    @pl.when(member > 0)
    def _():
        to_previous(member - 1).start()

    @pl.when(member + 1 < members)
    def _():
        to_previous(member).wait_recv()
        last = pl.ds(dpre_ref.shape[0] - 16, 16)
        late = stack(tail_ref[0:8], tail_ref[8:16] + edge_ref[...])
        dpre_ref[last, : 3 * columns] = late.astype(BF)

    @pl.when(member > 0)
    def _():
        to_previous(member - 1).wait_send()

    finish()


def mixer_backward(lengths, pre, halo, conv, logits, qkv, inv, wu, mq, states, ddelta, arrive, grads, collective):
    chunks, heads = mq.shape[:2]
    tokens = chunks * CHUNK
    columns = heads * CHUNK
    parts, members = grads.shape[:2]
    piece = grads.shape[2:]
    whole, outside = pl.BlockSpec(memory_space=pltpu.VMEM), pl.BlockSpec(memory_space=pl.ANY)
    streamed = (pre, logits, qkv, inv, wu, mq, states, ddelta)
    return pl.pallas_call(
        functools.partial(mixer_backward_kernel, heads),
        name="mixer_backward",
        out_shape=(
            jax.ShapeDtypeStruct((tokens, 3 * columns + CHUNK), BF),
            jax.ShapeDtypeStruct((4, 8, 3 * columns), F32),
            jax.ShapeDtypeStruct((parts, *piece), F32),
        ),
        in_specs=[pl.BlockSpec(memory_space=pltpu.SMEM), outside, whole, whole] + [outside] * 7 + [whole] * 2,
        out_specs=tuple([pl.BlockSpec(memory_space=pltpu.VMEM)] * 3),
        scratch_shapes=[pltpu.VMEM(a.shape, a.dtype) for a in streamed]
        + [
            pltpu.SemaphoreType.DMA((8, 4)),
            pltpu.SMEM((tokens // GROUP,), F32),
            pltpu.VMEM((4, 3 * columns), F32),
            pltpu.VMEM((heads, CHUNK, CHUNK), F32),
            pltpu.VMEM((144, 3 * columns), F32),
            pltpu.VMEM((144, 3 * columns), F32),
            pltpu.VMEM((16, 3 * columns), F32),
            pltpu.VMEM((8, 3 * columns), F32),
            pltpu.VMEM((8, 3 * columns), F32),
            pltpu.SemaphoreType.DMA,
            pltpu.SemaphoreType.DMA,
        ]
        + piece_scatter_scratch(parts, members, piece),
        compiler_params=pltpu.CompilerParams(
            collective_id=collective, has_side_effects=True, vmem_limit_bytes=VMEM_LIMIT
        ),
        cost_estimate=pl.CostEstimate(flops=3 * 10**9, bytes_accessed=20 << 20, transcendentals=2 << 20),
    )(lengths, pre, halo, conv, logits, qkv, inv, wu, mq, states, ddelta, arrive, grads)


def head_peers():
    place = lax.axis_index("head")
    low = lax.rem(place, 2)
    high = lax.rem(lax.div(place, 2), 2)
    return place, low, place + 1 - 2 * low, place + 2 - 4 * high


def push(src, dst, send_sem, recv_sem, axis, target):
    return pltpu.make_async_remote_copy(
        src_ref=src,
        dst_ref=dst,
        send_sem=send_sem,
        recv_sem=recv_sem,
        device_id={axis: target},
        device_id_type=MESH,
    )


def greet(axis, targets):
    barrier = pltpu.get_barrier_semaphore()
    for target in targets:
        pl.semaphore_signal(barrier, inc=1, device_id={axis: target}, device_id_type=MESH)
    pl.semaphore_wait(barrier, len(targets))


def middle_kernel(
    steps,
    rows_ref,
    far_rows_ref,
    full_hbm,
    turned_hbm,
    others_hbm,
    input_ref,
    ct_ref,
    late_ct_ref,
    gain_ref,
    dheads_ref,
    update_ref,
    mid_ref,
    dmid_ref,
    first_grads_ref,
    second_grads_ref,
    third_grads_ref,
    gain_grad_ref,
    gate_ref,
    up_ref,
    down_ref,
    turned_ref,
    others_ref,
    load_sem,
    own_rows_ref,
    stage_ref,
    acc_ref,
    part_ref,
    pair_ref,
    far_ref,
    sum_ref,
    keep_ref,
    scale_ref,
    shard_ref,
    pair_send,
    pair_recv,
    far_send,
    far_recv,
    last_send,
    last_recv,
    row_near_send,
    row_near_recv,
    row_far_send,
    row_far_recv,
    row_pass_send,
    row_pass_recv,
):
    step = pl.program_id(0)
    place, low, near, far = head_peers()
    chunk, width = input_ref.shape
    columns = rows_ref.shape[1]
    hidden = gate_ref.shape[0]
    half = width // 2
    mine = pl.ds(pl.multiple_of(low * half, 128), half)
    theirs = pl.ds(pl.multiple_of((1 - low) * half, 128), half)
    own_columns = pl.ds(pl.multiple_of(place * columns, 128), columns)

    known = steps // 2

    def at(index):
        return pl.ds(pl.multiple_of(index * chunk, chunk), chunk)

    def near_rows(index):
        place_ = at(index - known)
        return push(
            rows_ref.at[at(index)], own_rows_ref.at[0, place_], row_near_send.at[index], row_near_recv.at[index], "head", near
        )

    def far_rows(index):
        place_ = at(index - known)
        return push(
            rows_ref.at[at(index)], own_rows_ref.at[1, place_], row_far_send.at[index], row_far_recv.at[index], "head", far
        )

    def pass_rows(index):
        place_ = at(index - known)
        return push(
            own_rows_ref.at[1, place_], own_rows_ref.at[2, place_], row_pass_send.at[index], row_pass_recv.at[index], "head", near
        )

    def pair(index):
        return push(
            part_ref.at[lax.rem(index, 2), :, theirs], pair_ref.at[index], pair_send.at[index], pair_recv.at[index], "head", near
        )

    def across(index):
        return push(pair_ref.at[index], far_ref.at[index], far_send.at[index], far_recv.at[index], "head", far)

    def last(index):
        return push(
            sum_ref.at[index, :, mine], sum_ref.at[index, :, mine], last_send.at[index], last_recv.at[index], "head", near
        )

    def loads():
        targets = [
            (full_hbm.at[0], gate_ref),
            (full_hbm.at[1], up_ref),
            (full_hbm.at[2], down_ref),
            (turned_hbm, turned_ref),
        ] + [(others_hbm.at[other], others_ref.at[other]) for other in range(3)]
        for number, (source, target) in enumerate(targets):
            for piece in range(width // 128):
                yield pltpu.make_async_copy(
                    source.at[piece], target.at[:, piece * 128 : (piece + 1) * 128], load_sem.at[number, piece]
                )

    @pl.when(step == 0)
    def _():
        for load in loads():
            load.start()
        greet("head", (near, far))

        @pl.loop(known, steps)
        def _(index):
            far_rows(index).start()
            near_rows(index).start()


        acc_ref[...] = jnp.zeros_like(acc_ref)
        gain_grad_ref[...] = jnp.zeros_like(gain_grad_ref)
        for load in loads():
            load.wait()

    @pl.when(step < steps)
    def _():
        ct = ct_ref[...]
        d_hidden = nt(ct, down_ref[...])

        @pl.when(step < known)
        def _():
            stage_ref[...] = far_rows_ref[...]

        @pl.when(step >= known)
        def _():
            near_rows(step).wait_recv()
            pass_rows(step).wait_recv()
            stage_ref[...] = own_rows_ref[:, at(step - known)]

        branch = nn(rows_ref[at(step)], turned_ref[...])
        for other in range(3):
            branch = branch + nn(stage_ref[other], others_ref[other])
        middle = input_ref[...].astype(F32) + branch
        keep_ref[lax.rem(step, 4)] = middle
        mid_ref[...] = keep_ref[lax.rem(step, 4), :, own_columns]
        scale = lax.rsqrt(jnp.mean(middle * middle, axis=-1, keepdims=True) + 1e-06)
        scale_ref[lax.rem(step, 4)] = scale
        second = (middle * scale * gain_ref[1:2]).astype(BF)
        gate, up = nt(second, gate_ref[...]), nt(second, up_ref[...])
        sig = sigmoid(gate)
        silu = gate * sig
        active = (silu * up).astype(BF)
        d_gate = (d_hidden * up * (sig + silu * (1.0 - sig))).astype(BF)
        d_up = (d_hidden * silu).astype(BF)

        @pl.when(step >= 2)
        def _():
            pair(step - 2).wait_send()

        part_ref[lax.rem(step, 2)] = (nn(d_gate, gate_ref[...]) + nn(d_up, up_ref[...])).astype(BF)
        pair(step).start()

        @pl.when((step + 2 >= known) & (step + 2 < steps))
        def _():
            far_rows(step + 2).wait_recv()
            pass_rows(step + 2).start()

        update_ref[...] = nn(active, down_ref[...]).astype(BF)
        acc_ref[:hidden] += tn(d_gate, second)
        acc_ref[hidden : 2 * hidden] += tn(d_up, second)
        acc_ref[2 * hidden : 3 * hidden] += tn(active, ct)

    @pl.when(step < steps)
    def _():
        pair(step).wait_recv()
        both = part_ref[lax.rem(step, 2), :, mine].astype(F32) + pair_ref[step].astype(F32)
        pair_ref[step] = both.astype(BF)
        across(step).start()

    @pl.when((step > 1) & (step < steps + 2))
    def _():
        done = step - 2
        across(done).wait_recv()
        across(done).wait_send()
        total = pair_ref[done].astype(F32) + far_ref[done].astype(F32)
        sum_ref[done, :, mine] = total.astype(BF)
        last(done).start()

    @pl.when(step > 2)
    def _():
        done = step - 3
        last(done).wait_recv()
        grad = sum_ref[done].astype(F32)
        middle = keep_ref[lax.rem(done, 4)]
        scale = scale_ref[lax.rem(done, 4)]
        unit = middle * scale
        gain_grad_ref[...] += jnp.sum((grad * unit).reshape(chunk // 8, 8, width), 0)
        scaled = grad * gain_ref[1:2]
        d_middle = late_ct_ref[...].astype(F32) + scale * (
            scaled - unit * jnp.mean(scaled * unit, axis=-1, keepdims=True)
        )
        shard_ref[...] = d_middle
        dmid_ref[...] = shard_ref[:, own_columns]
        d_branch = d_middle.astype(BF)
        dheads_ref[...] = nt(d_branch, turned_ref[...]).astype(BF)
        acc_ref[3 * hidden :] += tn(rows_ref[at(done)], d_branch)

    @pl.when(step == steps + 2)
    def _():
        for piece in range(width // 128):
            lanes = slice(piece * 128, (piece + 1) * 128)
            begin = 0
            for grads_ref in (first_grads_ref, second_grads_ref, third_grads_ref):
                rows = grads_ref.shape[2]
                for part in range(2):
                    grads_ref[part, piece] = acc_ref[begin : begin + rows, lanes].astype(BF)
                    begin += rows

        @pl.loop(0, steps)
        def _(index):
            last(index).wait_send()

        @pl.loop(known, steps)
        def _(index):
            near_rows(index).wait_send()
            far_rows(index).wait_send()
            pass_rows(index).wait_send()

        for index in range(max(steps - 2, 0), steps):
            pair(index).wait_send()


def middle_stage(head_rows, far_rows, full, turned, others, inputs, cotangent, gain, collective):
    tokens, width = inputs.shape
    columns = head_rows.shape[1]
    chunk = min(256, tokens // 2)
    steps = tokens // chunk
    whole = pl.BlockSpec(memory_space=pltpu.VMEM)
    outside = pl.BlockSpec(memory_space=pl.ANY)
    hidden = full.shape[2]
    units = (3 * hidden + columns) // 32
    shares = [16 * (units * 36 // 74), 0, 16 * (units * 25 // 74)]
    shares[1] = 16 * units - sum(shares)

    def early(wide):
        return pl.BlockSpec((chunk, wide), lambda s: (jnp.minimum(s, steps - 1), 0))

    def late(wide):
        return pl.BlockSpec((chunk, wide), lambda s: (jnp.maximum(s - 3, 0), 0))

    far = pl.BlockSpec((3, chunk, columns), lambda s: (0, jnp.minimum(s, steps // 2 - 1), 0))
    dma = pltpu.SemaphoreType.DMA((steps,))
    return pl.pallas_call(
        functools.partial(middle_kernel, steps),
        name="middle",
        grid=(steps + 3,),
        out_shape=(
            jax.ShapeDtypeStruct((tokens, columns), BF),
            jax.ShapeDtypeStruct((tokens, width), BF),
            jax.ShapeDtypeStruct((tokens, columns), F32),
            jax.ShapeDtypeStruct((tokens, columns), F32),
            *(jax.ShapeDtypeStruct((2, width // 128, rows, 128), BF) for rows in shares),
            jax.ShapeDtypeStruct((8, width), F32),
        ),
        in_specs=[whole, far] + [outside] * 3 + [early(width), early(width), late(width), whole],
        out_specs=(late(columns), early(width), early(columns), late(columns), whole, whole, whole, whole),
        scratch_shapes=[
            pltpu.VMEM((hidden, width), BF),
            pltpu.VMEM((hidden, width), BF),
            pltpu.VMEM((hidden, width), BF),
            pltpu.VMEM((columns, width), BF),
            pltpu.VMEM((3, columns, width), BF),
            pltpu.SemaphoreType.DMA((7, width // 128)),
            pltpu.VMEM((3, tokens // 2, columns), BF),
            pltpu.VMEM((3, chunk, columns), BF),
            pltpu.VMEM((3 * hidden + columns, width), F32),
            pltpu.VMEM((2, chunk, width), BF),
            pltpu.VMEM((steps, chunk, width // 2), BF),
            pltpu.VMEM((steps, chunk, width // 2), BF),
            pltpu.VMEM((steps, chunk, width), BF),
            pltpu.VMEM((4, chunk, width), F32),
            pltpu.VMEM((4, chunk, 1), F32),
            pltpu.VMEM((chunk, width), F32),
        ]
        + [dma] * 12,
        compiler_params=pltpu.CompilerParams(
            collective_id=collective,
            has_side_effects=True,
            vmem_limit_bytes=VMEM_LIMIT,
            dimension_semantics=("arbitrary",),
        ),
        cost_estimate=pl.CostEstimate(flops=30 * 10**9, bytes_accessed=30 << 20, transcendentals=2 << 20),
    )(head_rows, far_rows, full, turned, others, inputs, cotangent, cotangent, gain)


def zeros_below(value):
    return (value & -value).bit_length() - 1


def flip(place, mask):
    bit = 1
    while bit <= mask:
        if mask & bit:
            place = place + bit - 2 * bit * lax.rem(lax.div(place, bit), 2)
        bit *= 2
    return place


def head_scatter_copies(chunk, part_ref, near_ref, send_ref, far_ref, sems):
    place, low, near, far = head_peers()
    high = lax.rem(lax.div(place, 2), 2)
    columns = far_ref.shape[-1]
    near_send, near_recv, far_send, far_recv = sems

    def at(index):
        return pl.ds(pl.multiple_of(index * chunk, chunk), chunk)

    def cols(owner):
        return pl.ds(pl.multiple_of(owner * columns, 128), columns)

    def pair(index, side_):
        return push(
            part_ref.at[at(index), cols(2 * side_ + 1 - low)],
            near_ref.at[side_, at(index)],
            near_send.at[side_, index],
            near_recv.at[side_, index],
            "head",
            near,
        )

    def across(index):
        return push(send_ref.at[at(index)], far_ref.at[at(index)], far_send.at[index], far_recv.at[index], "head", far)

    def start_pair(index):
        pair(index, 0).start()
        pair(index, 1).start()

    def pass_on(index):
        pair(index, 0).wait_recv()
        pair(index, 1).wait_recv()
        total = part_ref[at(index), cols(2 * (1 - high) + low)].astype(F32) + near_ref[1 - high, at(index)].astype(F32)
        send_ref[at(index)] = total.astype(BF)
        across(index).start()

    def own_sum(index):
        across(index).wait_recv()
        near_part = part_ref[at(index), cols(place)].astype(F32) + near_ref[high, at(index)].astype(F32)
        return near_part + far_ref[at(index)].astype(F32)

    def finish(index):
        pair(index, 0).wait_send()
        pair(index, 1).wait_send()
        across(index).wait_send()

    return at, cols, start_pair, pass_on, own_sum, finish


def head_scatter_scratch(tokens, columns, steps):
    return [
        pltpu.VMEM((2, tokens, columns), BF),
        pltpu.VMEM((tokens, columns), BF),
        pltpu.VMEM((tokens, columns), BF),
        pltpu.SemaphoreType.DMA((2, steps)),
        pltpu.SemaphoreType.DMA((2, steps)),
        pltpu.SemaphoreType.DMA((steps,)),
        pltpu.SemaphoreType.DMA((steps,)),
    ]


def final_kernel(
    members,
    chunk,
    rows_ref,
    dpre_ref,
    pack_hbm,
    input_hbm,
    scale_hbm,
    gain_ref,
    dmid_hbm,
    head_part_ref,
    second_part_ref,
    taps_part_ref,
    rest_ref,
    ingrad_ref,
    piece_ref,
    sums_ref,
    total_ref,
    pack_ref,
    input_ref,
    scale_ref,
    dmid_ref,
    load_sem,
    acc_ref,
    out_ref,
    slots_ref,
    part_ref,
    near_ref,
    send_ref,
    far_ref,
    near_send,
    near_recv,
    far_send,
    far_recv,
    stat_ref,
    stat_slots,
    small_slots,
    piece_send,
    piece_recv,
    stat_send,
    stat_recv,
    small_send,
    small_recv,
    rest_relay,
    rest_slots,
    rest_send,
    rest_recv,
):
    tokens, width = input_ref.shape
    steps = tokens // chunk
    loads = [
        pltpu.make_async_copy(source, target, load_sem.at[number])
        for number, (source, target) in enumerate(
            ((pack_hbm, pack_ref), (input_hbm, input_ref), (scale_hbm, scale_ref), (dmid_hbm, dmid_ref))
        )
    ]
    for load in loads:
        load.start()
    place, low, near, far = head_peers()
    member = lax.axis_index("seq")
    rows = width // members
    stages = (members - 1).bit_length()
    at, cols, start_pair, pass_on, own_sum, finish = head_scatter_copies(
        chunk, part_ref, near_ref, send_ref, far_ref, (near_send, near_recv, far_send, far_recv)
    )

    barrier = pltpu.get_barrier_semaphore()
    opposite = near + far - place
    for target in (near, far, opposite):
        pl.semaphore_signal(barrier, inc=1, device_id={"head": target}, device_id_type=MESH)
    for stage in range(stages):
        pl.semaphore_signal(barrier, inc=1, device_id={"seq": flip(member, 1 << stage)}, device_id_type=MESH)
    begin, rest_receive, rest_jobs, rest_end = piece_scatter(
        rest_ref, rest_relay, rest_slots, total_ref, rest_send, rest_recv, members
    )
    pl.semaphore_wait(barrier, 3 + stages)
    order = sorted(range(members), key=lambda r: zeros_below(r) if r else stages)
    sent = [r for r in order if r]
    events = {}
    for r in order:
        for stage in range(zeros_below(r) if r else stages):
            events[stage, r] = len(events)

    def give(r):
        stage = zeros_below(r)
        slot = events[stage, r ^ (1 << stage)]
        return push(
            out_ref.at[r],
            slots_ref.at[slot],
            piece_send.at[r],
            piece_recv.at[slot],
            "seq",
            flip(member, 1 << stage),
        )

    def take(stage, r):
        slot = events[stage, r]
        return push(
            out_ref.at[0], slots_ref.at[slot], piece_send.at[0], piece_recv.at[slot], "seq", flip(member, 1 << stage)
        )

    def send_piece(r):
        out_ref[r] = acc_ref[flip(member, r)].astype(BF)
        give(r).start()

    def receive(r):
        index = flip(member, r)
        for stage in range(zeros_below(r) if r else stages):
            take(stage, r).wait_recv()
            acc_ref[index] += slots_ref[events[stage, r]].astype(F32)
        if r:
            send_piece(r)

    first = sorted([r for r in range(members) if r % 2], key=lambda r: order.index(r ^ 1))
    evens = [r for r in order if r % 2 == 0]
    if rows % 128 == 0:
        for r in first:
            even = 2 * lax.div(flip(member, r), 2)
            columns = pl.ds(pl.multiple_of(even * rows, 128), 2 * rows)
            block = tn(rows_ref[:, columns], dpre_ref[...])
            acc_ref[even] = block[:rows]
            acc_ref[even + 1] = block[rows:]
            send_piece(r)
        begin()
    else:
        per = 128 // rows
        for unit in range(width // 128):
            block = tn(rows_ref[:, unit * 128 : (unit + 1) * 128], dpre_ref[...])
            acc_ref[unit * per : (unit + 1) * per] = block.reshape(per, rows, block.shape[1])
        for r in first:
            send_piece(r)
        begin()

    small_slots[0] = jnp.zeros_like(small_slots[0])
    small_slots[0, 1:2, :CHUNK] = jnp.sum(head_part_ref[...], 0, keepdims=True)
    small_slots[0, 8:9] = jnp.sum(second_part_ref[...], 0, keepdims=True)
    columns3 = taps_part_ref.shape[2]
    for tap in range(4):
        taps_sum = jnp.sum(taps_part_ref[tap], 0, keepdims=True)
        for block in range(3):
            flat = tap * columns3 + block * (columns3 // 3)
            line, lane = 9 + flat // width, flat % width
            small_slots[0, line : line + 1, lane : lane + columns3 // 3] = taps_sum[
                :, block * (columns3 // 3) : (block + 1) * (columns3 // 3)
            ]
    for load in loads:
        load.wait()
    diagonal = lax.broadcasted_iota(jnp.int32, (128, 128), 0) == lax.broadcasted_iota(jnp.int32, (128, 128), 1)

    def project(index):
        part = nt(dpre_ref[at(index)], pack_ref[...])
        part_ref[at(index)] = part.astype(BF)
        start_pair(index)
        seen = part * (input_ref[at(index)].astype(F32) * scale_ref[at(index)])
        small_slots[0, 0:1] += jnp.sum(seen, 0, keepdims=True)
        stat = jnp.sum(seen * gain_ref[0:1], axis=-1, keepdims=True)
        for block in range(chunk // 128):
            line = jnp.where(diagonal, stat[block * 128 : (block + 1) * 128], 0.0)
            stat_ref[index * (chunk // 128) + block] = jnp.sum(line, 0, keepdims=True)

    early = steps // 2
    receives = list(evens)
    for half in range(2):

        @pl.loop(half * early, (half + 1) * early)
        def _(index):
            project(index)

            @pl.when(lax.rem(index, 2) == 1)
            def _():
                pass_on(lax.div(index, 2))

        if len(receives) > 1:
            receive(receives.pop(0))

    def stat_copy(turn):
        target = (near, far, opposite)[turn]
        return push(stat_ref, stat_slots.at[turn], stat_send.at[turn], stat_recv.at[turn], "head", target)

    def head_copy(turn):
        target = (near, far, opposite)[turn]
        return push(
            small_slots.at[0, pl.ds(0, 8)],
            small_slots.at[1 + turn, pl.ds(0, 8)],
            small_send.at[turn],
            small_recv.at[turn],
            "head",
            target,
        )

    for turn in (1, 2, 0):
        head_copy(turn).start()
        stat_copy(turn).start()
    for index in range(early, steps):
        pass_on(index)
    while len(receives) > 1:
        receive(receives.pop(0))
    for turn in range(3):
        head_copy(turn).wait()
    small_slots[4] = small_slots[0]
    small_slots[4, 0:8] += small_slots[1, 0:8] + small_slots[2, 0:8] + small_slots[3, 0:8]

    bits = list(range(1, stages)) + [0]

    def seq_copy(turn):
        return push(
            small_slots.at[4 + 2 * turn],
            small_slots.at[5 + 2 * turn],
            small_send.at[3 + turn],
            small_recv.at[3 + turn],
            "seq",
            flip(member, 1 << bits[turn]),
        )

    def seq_add(turn):
        seq_copy(turn).wait()
        small_slots[6 + 2 * turn] = small_slots[4 + 2 * turn] + small_slots[5 + 2 * turn]

    seq_copy(0).start()
    for turn in range(3):
        stat_copy(turn).wait()
    stat_ref[...] += stat_slots[0] + stat_slots[1] + stat_slots[2]

    def result(index):
        grad = own_sum(index)
        scale = scale_ref[at(index)]
        unit = input_ref[at(index), cols(place)].astype(F32) * scale
        means = []
        for block in range(chunk // 128):
            line = jnp.where(diagonal, stat_ref[index * (chunk // 128) + block], 0.0)
            means.append(jnp.sum(line, axis=-1, keepdims=True))
        mean = jnp.concatenate(means, 0) * (1.0 / width)
        ingrad_ref[at(index)] = dmid_ref[at(index)] + scale * (grad * gain_ref[0:1, cols(place)] - unit * mean)

    rests = list(rest_jobs)
    for turn in range(stages):
        start, stop = turn * steps // stages, (turn + 1) * steps // stages
        if stop > start:

            @pl.loop(start, stop)
            def _(index):
                result(index)

        share = (len(rests) - 1) // (stages - turn)
        for job in rests[:share]:
            rest_receive(*job)
        rests = rests[share:]
        seq_add(turn)
        if turn + 1 < stages:
            seq_copy(turn + 1).start()
    receive(0)
    for job in rests:
        rest_receive(*job)
    piece_ref[...] = acc_ref[member]
    sums_ref[...] = small_slots[4 + 2 * stages]

    @pl.loop(0, steps)
    def _(index):
        finish(index)

    for r in sent:
        give(r).wait_send()
    rest_end()


def final_stage(first_rows, dpre, pack, inputs, scale, gain, dmid, parts, rest, members, collective):
    tokens, width = inputs.shape
    columns = dmid.shape[1]
    chunk = 256
    steps = tokens // chunk
    stages = (members - 1).bit_length()
    rows = width // members
    wide = dpre.shape[1]
    whole, outside = pl.BlockSpec(memory_space=pltpu.VMEM), pl.BlockSpec(memory_space=pl.ANY)
    return pl.pallas_call(
        functools.partial(final_kernel, members, chunk),
        name="final",
        out_shape=(
            jax.ShapeDtypeStruct((tokens, columns), F32),
            jax.ShapeDtypeStruct((rows, wide), F32),
            jax.ShapeDtypeStruct((16, width), F32),
            jax.ShapeDtypeStruct((rest.shape[0], *rest.shape[2:]), F32),
        ),
        in_specs=[whole, whole, outside, outside, outside, whole, outside] + [whole] * 4,
        out_specs=(whole,) * 4,
        scratch_shapes=[pltpu.VMEM(a.shape, a.dtype) for a in (pack, inputs, scale, dmid)]
        + [
            pltpu.SemaphoreType.DMA((4,)),
            pltpu.VMEM((members, rows, wide), F32),
            pltpu.VMEM((members, rows, wide), BF),
            pltpu.VMEM((members - 1, rows, wide), BF),
            pltpu.VMEM((tokens, width), BF),
        ]
        + head_scatter_scratch(tokens, columns, steps)
        + [
            pltpu.VMEM((tokens // 128, 1, 128), F32),
            pltpu.VMEM((3, tokens // 128, 1, 128), F32),
            pltpu.VMEM((5 + 2 * stages, 16, width), F32),
            pltpu.SemaphoreType.DMA((members,)),
            pltpu.SemaphoreType.DMA((members - 1,)),
            pltpu.SemaphoreType.DMA((3,)),
            pltpu.SemaphoreType.DMA((3,)),
            pltpu.SemaphoreType.DMA((3 + stages,)),
            pltpu.SemaphoreType.DMA((3 + stages,)),
        ]
        + piece_scatter_scratch(rest.shape[0], members, rest.shape[2:]),
        compiler_params=pltpu.CompilerParams(
            collective_id=collective, has_side_effects=True, vmem_limit_bytes=VMEM_LIMIT
        ),
        cost_estimate=pl.CostEstimate(flops=8 * 10**9, bytes_accessed=30 << 20, transcendentals=0),
    )(first_rows, dpre, pack, inputs, scale, gain, dmid, *parts, rest)


def finish_kernel(
    hidden,
    block_ref,
    ingrad_ref,
    piece_ref,
    sums_ref,
    first_ref,
    second_ref,
    third_ref,
    block_out,
    ingrad_out,
    first_gain_out,
    query_out,
    key_out,
    value_out,
    beta_out,
    conv_out,
    head_gain_out,
    output_out,
    second_gain_out,
    gate_out,
    up_out,
    down_out,
    turn_ref,
    strip_ref,
    sems,
):
    rows, columns = query_out.shape
    member = lax.axis_index("seq")
    pieces = [(block_ref, block_out), (ingrad_ref, ingrad_out)]
    for kind, target in enumerate((query_out, key_out, value_out)):
        pieces.append((piece_ref.at[:, pl.ds(kind * columns, columns)], target))
    pieces.append((piece_ref.at[:, pl.ds(3 * columns, CHUNK)], strip_ref))
    spans = []
    place = 0
    for source in (first_ref, second_ref, third_ref):
        for part in range(2):
            spans.append((place, source, part))
            place += source.shape[1]
    goal = 0
    for target, count in ((gate_out, hidden), (up_out, hidden), (down_out, hidden), (turn_ref, columns)):
        for begin, source, part in spans:
            low, high = max(begin, goal), min(begin + source.shape[1], goal + count)
            if low < high:
                pieces.append(
                    (source.at[part, pl.ds(low - begin, high - low)], target.at[pl.ds(low - goal, high - low)])
                )
        goal += count
    copies = [pltpu.make_async_copy(source, target, sems.at[number]) for number, (source, target) in enumerate(pieces)]
    for copy in copies:
        copy.start()
    window = pl.ds(pl.multiple_of(member * rows, 128), rows)
    first_gain_out[...] = sums_ref[0:1, window]
    second_gain_out[...] = sums_ref[8:9, window]
    head_gain_out[...] = sums_ref[1:2, :CHUNK]
    width = sums_ref.shape[1]
    for kind in range(3):
        for tap in range(4):
            flat = (3 * tap + kind) * columns
            line, lane = 9 + flat // width, flat % width
            conv_out[kind, tap : tap + 1] = sums_ref[line : line + 1, lane : lane + columns]
    for copy in copies:
        copy.wait()
    output_out[...] = turn_ref[...].T
    beta_out[...] = strip_ref[...].T[: beta_out.shape[0]]


def finish_stage(block, ingrad, piece, sums, first, second, third, hidden, heads):
    tokens, columns = ingrad.shape
    rows = piece.shape[0]
    whole, outside = pl.BlockSpec(memory_space=pltpu.VMEM), pl.BlockSpec(memory_space=pl.ANY)

    def made(*shape):
        return jax.ShapeDtypeStruct(shape, F32)

    return pl.pallas_call(
        functools.partial(finish_kernel, hidden),
        name="finish",
        out_shape=(
            jax.ShapeDtypeStruct((tokens, columns), BF),
            made(tokens, columns),
            made(1, rows),
            made(rows, columns),
            made(rows, columns),
            made(rows, columns),
            made(heads, rows),
            made(3, 4, columns),
            made(1, CHUNK),
            made(rows, columns),
            made(1, rows),
            made(hidden, rows),
            made(hidden, rows),
            made(hidden, rows),
        ),
        in_specs=[whole] * 7,
        out_specs=(outside,) * 2
        + (whole,)
        + (outside,) * 3
        + (whole,) * 5
        + (outside,) * 3,
        scratch_shapes=[
            pltpu.VMEM((columns, rows), F32),
            pltpu.VMEM((rows, CHUNK), F32),
            pltpu.SemaphoreType.DMA((24,)),
        ],
        compiler_params=pltpu.CompilerParams(vmem_limit_bytes=VMEM_LIMIT),
        cost_estimate=pl.CostEstimate(flops=0, bytes_accessed=12 << 20, transcendentals=0),
    )(block, ingrad, piece, sums, first, second, third)
def turn_column(column):
    diagonal = lax.broadcasted_iota(jnp.int32, (128, 128), 0) == lax.broadcasted_iota(jnp.int32, (128, 128), 1)
    lines = []
    for block in range(column.shape[0] // 128):
        lines.append(jnp.sum(jnp.where(diagonal, column[block * 128 : (block + 1) * 128], 0.0), 0, keepdims=True))
    return jnp.concatenate(lines, 1)


def piece_gather(full_ref, send, recv, members):
    member = lax.axis_index("seq")
    parts = full_ref.shape[0]
    stages = (members - 1).bit_length()

    def give(part, r, stage):
        owner = flip(member, r)
        mark = r ^ (1 << stage)
        return push(
            full_ref.at[part, owner],
            full_ref.at[part, owner],
            send.at[part, mark],
            recv.at[part, mark],
            "seq",
            flip(member, 1 << stage),
        )

    def take(part, r):
        owner = flip(member, r)
        return push(
            full_ref.at[part, owner],
            full_ref.at[part, owner],
            send.at[part, r],
            recv.at[part, r],
            "seq",
            flip(member, r & -r),
        )

    def begin(part=0, levels=None):
        for stage in reversed(range(stages)) if levels is None else levels:
            give(part, 0, stage).start()

    def relay(part, r):
        take(part, r).wait_recv()
        for stage in reversed(range(zeros_below(r))):
            give(part, r, stage).start()
        if r == 1 << (stages - 1) and part + 1 < parts:
            begin(part + 1)

    order = sorted([r for r in range(1, members) if r % 2 == 0], key=lambda r: (-zeros_below(r), r))
    def when(part, r):
        return 2 * part + 3 * (bin(r).count("1") - 1), part, -zeros_below(r), r

    relays = sorted([(part, r) for r in order for part in range(parts)], key=lambda job: when(*job))

    def arrive():
        for part in range(parts):
            for r in range(1, members, 2):
                take(part, r).wait_recv()

    def finish():
        for part in range(parts):
            for r in [0] + order:
                for stage in range(zeros_below(r) if r else stages):
                    give(part, r, stage).wait_send()

    return begin, relay, relays, arrive, finish


def greet_seq(members):
    member = lax.axis_index("seq")
    stages = (members - 1).bit_length()
    barrier = pltpu.get_barrier_semaphore()
    for stage in range(stages):
        pl.semaphore_signal(barrier, inc=1, device_id={"seq": flip(member, 1 << stage)}, device_id_type=MESH)
    return barrier, stages


FRONT_REFS = 64


def front_kernel(
    members,
    heads,
    lengths_ref,
    input_ref,
    query_ref,
    key_ref,
    value_ref,
    beta_ref,
    first_gain_ref,
    second_gain_ref,
    out_weight_ref,
    conv_ref,
    head_gain_ref,
    *refs,
):
    own_refs, refs = refs[:-FRONT_REFS], refs[-FRONT_REFS:]
    front_body(
        members,
        heads,
        lengths_ref,
        input_ref,
        query_ref,
        key_ref,
        value_ref,
        beta_ref,
        first_gain_ref,
        second_gain_ref,
        out_weight_ref,
        conv_ref,
        head_gain_ref,
        own_refs,
        *refs,
    )


def front_body(
    members,
    heads,
    lengths_ref,
    input_ref,
    query_ref,
    key_ref,
    value_ref,
    beta_ref,
    first_gain_ref,
    second_gain_ref,
    out_weight_ref,
    conv_ref,
    head_gain_ref,
    own_refs,
    pack_hbm,
    first_hbm,
    pre_hbm,
    logits_hbm,
    halo_ref,
    scale_hbm,
    gains_ref,
    turned_hbm,
    full_hbm,
    others_hbm,
    qkv_hbm,
    inv_hbm,
    wu_hbm,
    mq_hbm,
    total_ref,
    delta_hbm,
    rows_hbm,
    far_rows_hbm,
    states_hbm,
    pack_ref,
    first_ref,
    pre_ref,
    logits_ref,
    scale_ref,
    turned_ref,
    full_ref,
    others_ref,
    qkv_ref,
    inv_ref,
    wu_ref,
    mq_ref,
    delta_ref,
    rows_ref,
    far_rows_ref,
    states_ref,
    store_sem,
    resets_ref,
    taps_ref,
    extra_ref,
    start_ref,
    out0_ref,
    state_ref,
    part_ref,
    slots_ref,
    pad_ref,
    edge_ref,
    pack_send,
    pack_recv,
    edge_send,
    edge_recv,
    turned_send,
    turned_recv,
    full_send,
    full_recv,
    head_send,
    head_recv,
    state_send,
    state_recv,
    row_near_send,
    row_near_recv,
    row_far_send,
    row_far_recv,
    row_pass_send,
    row_pass_recv,
):
    tokens, width = input_ref.shape
    columns = heads * CHUNK
    leaving = (
        (pack_ref, pack_hbm),
        (first_ref, first_hbm),
        (pre_ref, pre_hbm),
        (logits_ref, logits_hbm),
        (scale_ref, scale_hbm),
        (turned_ref, turned_hbm),
        (qkv_ref, qkv_hbm),
        (inv_ref, inv_hbm),
        (wu_ref, wu_hbm),
        (mq_ref, mq_hbm),
        (delta_ref, delta_hbm),
        (rows_ref, rows_hbm),
        (states_ref, states_hbm),
        (others_ref, others_hbm),
        (far_rows_ref, far_rows_hbm),
        (full_ref, full_hbm),
    )

    def store(number):
        return pltpu.make_async_copy(*leaving[number], store_sem.at[number])

    member = lax.axis_index("seq")
    _, _, near, far = head_peers()
    barrier, stages = greet_seq(members)
    for target in (near, far):
        pl.semaphore_signal(barrier, inc=1, device_id={"head": target}, device_id_type=MESH)

    @pl.when(member > 0)
    def _():
        pl.semaphore_signal(barrier, inc=1, device_id={"seq": member - 1}, device_id_type=MESH)

    window = slots_ref.shape[0]
    behind = members - 1 - member
    for hop in range(1, window + 1):

        @pl.when(member >= hop)
        def _():
            pl.semaphore_signal(barrier, inc=1, device_id={"seq": member - hop}, device_id_type=MESH)

    def state_copy(hop):
        return push(
            part_ref, slots_ref.at[hop - 1], state_send.at[hop - 1], state_recv.at[hop - 1], "seq", member + hop
        )

    pack_ref[0, member, :, :columns] = query_ref[...]
    pack_ref[0, member, :, columns : 2 * columns] = key_ref[...]
    pack_ref[0, member, :, 2 * columns : 3 * columns] = value_ref[...]
    extra_ref[...] = jnp.zeros_like(extra_ref)
    extra_ref[0:heads] = beta_ref[...].astype(F32)
    extra_ref[heads : heads + 1] = first_gain_ref[...].astype(F32)
    extra_ref[heads + 1 : heads + 2] = second_gain_ref[...].astype(F32)
    pack_ref[0, member, :, 3 * columns :] = extra_ref[...].T.astype(BF)
    turned_ref[0, member] = out_weight_ref[...].T
    for part, own_ref in enumerate(own_refs):
        full_ref[part, member] = own_ref[...]
    pack = piece_gather(pack_ref, pack_send, pack_recv, members)
    turned = piece_gather(turned_ref, turned_send, turned_recv, members)
    full = piece_gather(full_ref, full_send, full_recv, members)
    near_copy = push(turned_ref.at[0], others_ref.at[0], head_send.at[0], head_recv.at[0], "head", near)
    far_copy = push(turned_ref.at[0], others_ref.at[1], head_send.at[1], head_recv.at[1], "head", far)
    pass_copy = push(others_ref.at[1], others_ref.at[2], head_send.at[2], head_recv.at[2], "head", near)
    pl.semaphore_wait(barrier, stages + 2 + jnp.minimum(behind, 1) + jnp.minimum(behind, window))
    pack[0]()
    full[0](0, [stages - 1, 0])
    fill_resets(lengths_ref, resets_ref, tokens)
    fill_taps(conv_ref, taps_ref)

    last_rows = pl.ds(tokens - 16, 16)

    def edge(target):
        return push(input_ref.at[last_rows], edge_ref, edge_send, edge_recv, "seq", target)

    @pl.when(member + 1 < members)
    def _():
        edge(member + 1).start()

    chunk = 256

    def at(index):
        return pl.ds(pl.multiple_of(index * chunk, chunk), chunk)

    def measure(index):
        block = input_ref[at(index)].astype(F32)
        scale_ref[at(index)] = lax.rsqrt(jnp.mean(block * block, axis=-1, keepdims=True) + 1e-06)

    pl.loop(0, tokens // chunk)(measure)
    for job in pack[2]:
        pack[1](*job)
    full[0](0, range(1, stages - 1))
    turned[0]()
    pack[3]()
    projection = pack_ref[0].reshape(width, pack_ref.shape[3])
    extras = projection[:, 3 * columns :].astype(F32)
    gains_ref[0:1] = turn_column(extras[:, heads : heads + 1])
    gains_ref[1:2] = turn_column(extras[:, heads + 1 : heads + 2])

    def project(index):
        first = (input_ref[at(index)].astype(F32) * scale_ref[at(index)] * gains_ref[0:1]).astype(BF)
        first_ref[at(index)] = first
        both = nn(first, pack_ref[0].reshape(width, pack_ref.shape[3]))
        pre_ref[at(index)] = both[:, : 3 * columns].astype(BF)
        logits_ref[at(index)] = both[:, 3 * columns :]

    pl.loop(0, tokens // chunk)(project)

    @pl.when(member == 0)
    def _():
        halo_ref[...] = jnp.zeros_like(halo_ref)

    @pl.when(member > 0)
    def _():
        edge(member).wait_recv()
        block = edge_ref[...].astype(F32)
        scale = lax.rsqrt(jnp.mean(block * block, axis=-1, keepdims=True) + 1e-06)
        first = (block * scale * gains_ref[0:1]).astype(BF)
        halo_ref[...] = nn(first, pack_ref[0].reshape(width, pack_ref.shape[3])[:, : 3 * columns]).astype(BF)

    for number in range(5):
        store(number).start()
    rows, cols = grid_indices()
    eye = jnp.where(rows == cols, 1.0, 0.0)
    top = lax.broadcasted_iota(jnp.int32, (CHUNK, 1), 0) < GROUP
    for head in range(heads):
        total_ref[head] = side(eye, jnp.zeros_like(eye))
    batch = pad_ref.shape[0]

    def one(step, carry):
        units = []
        for lane in range(batch):
            chunk = step * batch + lane
            pad = pad_ref.at[lane]
            load_padded(pad, pre_ref, halo_ref, chunk, resets_ref)
            mixed = convolve(pad, taps_ref)
            silued = mixed * sigmoid(mixed)
            keep0 = 1.0 - resets_ref[2 * chunk]
            keep1 = 1.0 - resets_ref[2 * chunk + 1]
            both = keep0 * keep1
            enter = jnp.where(top, keep0, both)
            leave = jnp.where(top, keep1, 1.0)
            at = pl.ds(pl.multiple_of(chunk * CHUNK, CHUNK), CHUNK)
            beta_rows = sigmoid(logits_ref[at, :])
            for head in range(heads):
                window = slice(head * CHUNK, (head + 1) * CHUNK)
                parts = []
                for kind in range(3):
                    part = silued[:, kind * columns + head * CHUNK : kind * columns + (head + 1) * CHUNK]
                    if kind < 2:
                        part = part * lax.rsqrt(jnp.sum(part * part, axis=-1, keepdims=True) + 1e-06)
                    part = part.astype(BF)
                    qkv_ref[at, kind * columns + head * CHUNK : kind * columns + (head + 1) * CHUNK] = part
                    parts.append(part)
                units.append((chunk, head, *parts, beta_rows[:, head : head + 1], keep1, both, enter, leave))
        turned = [u[3].T for u in units]
        strict = [
            jnp.where(rows > cols, u[5] * nn(u[3], t), 0.0) for u, t in zip(units, turned)
        ]
        inverses = [r.astype(BF) for r in inverse_levels(strict, rows, cols, [u[6] for u in units])]
        factors = []
        for u, inverse in zip(units, inverses):
            beta = u[5]
            factors.append(nn(inverse, side(u[3].astype(F32) * beta, u[4].astype(F32) * beta)))
        for u, inverse, factor, t in zip(units, inverses, factors, turned):
            chunk, head, query, key, value, beta, keep1, both, enter, leave = u
            weight, update = factor[:, :CHUNK], factor[:, CHUNK:]
            entering_weight = weight * enter
            inv_ref[chunk, head] = inverse
            wu_ref[chunk, head] = side(entering_weight, update).astype(BF)
            gathered = nn(t, side(weight, update * leave))
            device_map = (both * (eye - gathered[:, :CHUNK])).astype(BF)
            shift = gathered[:, CHUNK:]
            scores = jnp.where(rows >= cols, nn(query, t), 0.0)
            scores = jnp.where((rows >= GROUP) & (cols < GROUP), scores * keep1, scores)
            seen = nn(scores, side(entering_weight, update))
            effective = query.astype(F32) * enter - seen[:, :CHUNK]
            mq_ref[chunk, head] = stack(device_map, effective.astype(BF))
            out0_ref[chunk, head] = seen[:, CHUNK:]
            running = total_ref[head]
            start_ref[chunk, head] = running.astype(BF)
            total_ref[head] = nn(device_map, running) + side(jnp.zeros_like(shift), shift)
        return carry

    count = resets_ref.shape[0] // 2 // batch
    held = 3 if len(full[2]) > 3 else 0
    relays = full[2][: len(full[2]) - held]

    def pumped(step, carry):
        carry = one(step, carry)
        for turn in range(count):
            jobs = [job for place, job in enumerate(relays) if place * count // len(relays) == turn]
            if not jobs and turn not in (0, 2, count - 2):
                continue

            @pl.when(step == turn)
            def _():
                if turn == 0:
                    for job in turned[2]:
                        turned[1](*job)
                for job in jobs:
                    full[1](*job)
                if turn == 2:
                    turned[3]()
                    store(5).start()
                    near_copy.start()
                    far_copy.start()
                if turn == count - 2:
                    far_copy.wait_recv()
                    pass_copy.start()

        return carry

    lax.fori_loop(0, count, pumped, 0)
    for number in range(6, 10):
        store(number).start()
    part_ref[...] = total_ref[...].astype(BF)
    for hop in range(1, window + 1):

        @pl.when(behind >= hop)
        def _():
            state_copy(hop).start()

    for job in full[2][len(full[2]) - held :]:
        full[1](*job)
    state_ref[...] = jnp.zeros_like(state_ref)
    for hop in range(window, 0, -1):

        @pl.when(member >= hop)
        def _():
            state_copy(hop).wait_recv()
            for head in range(heads):
                part = slots_ref[hop - 1, head]
                state_ref[head] = nn(part[:, :CHUNK], state_ref[head]) + part[:, CHUNK:].astype(F32)

    def near_rows(index):
        return push(
            rows_ref.at[at(index)], far_rows_ref.at[0, at(index)], row_near_send.at[index], row_near_recv.at[index], "head", near
        )

    def far_rows(index):
        return push(
            rows_ref.at[at(index)], far_rows_ref.at[1, at(index)], row_far_send.at[index], row_far_recv.at[index], "head", far
        )

    def pass_rows(index):
        return push(
            far_rows_ref.at[1, at(index)], far_rows_ref.at[2, at(index)], row_pass_send.at[index], row_pass_recv.at[index], "head", near
        )

    def finished(index):
        for lane in range(chunk // CHUNK):
            place_ = index * (chunk // CHUNK) + lane
            rows_at = pl.ds(pl.multiple_of(place_ * CHUNK, CHUNK), CHUNK)
            begins = [start_ref[place_, head] for head in range(heads)]
            states = [
                (nn(begins[head][:, :CHUNK], state_ref[head]) + begins[head][:, CHUNK:].astype(F32)).astype(BF)
                for head in range(heads)
            ]
            outs = [out0_ref[place_, head] + nn(mq_ref[place_, head, CHUNK:], states[head]) for head in range(heads)]
            for head in range(heads):
                lanes = slice(head * CHUNK, (head + 1) * CHUNK)
                states_ref[place_, head] = states[head]
                delta_ref[rows_at, lanes] = outs[head]
                scale = lax.rsqrt(jnp.mean(outs[head] * outs[head], axis=-1, keepdims=True) + 1e-05)
                rows_ref[rows_at, lanes] = (outs[head] * scale * head_gain_ref[...]).astype(BF)

    sent = far_rows_ref.shape[1] // chunk

    def finished_and_sent(index):
        finished(index)
        far_rows(index).start()
        near_rows(index).start()

    pl.loop(0, sent)(finished_and_sent)
    pl.loop(sent, tokens // chunk)(finished)
    for number in range(10, 13):
        store(number).start()

    @pl.loop(0, sent)
    def _(index):
        far_rows(index).wait_recv()
        pass_rows(index).start()

    near_copy.wait()
    far_copy.wait_send()
    pass_copy.wait()
    store(13).start()

    @pl.when(member + 1 < members)
    def _():
        edge(member + 1).wait_send()

    for hop in range(1, window + 1):

        @pl.when(behind >= hop)
        def _():
            state_copy(hop).wait_send()

    @pl.loop(0, sent)
    def _(index):
        near_rows(index).wait()
        far_rows(index).wait_send()
        pass_rows(index).wait()

    store(14).start()
    full[3]()
    store(15).start()
    for gather in (pack, turned, full):
        gather[4]()
    for number in range(len(leaving)):
        store(number).wait()


def front_stage(lengths, inputs, mixer_weights, conv, head_gain, own, members, heads, collective):
    tokens, width = inputs.shape
    columns = heads * CHUNK
    chunks = tokens // CHUNK
    whole = pl.BlockSpec(memory_space=pltpu.VMEM)
    piece = width // members
    window = min(members - 1, members // 2)

    def units(wide, kind):
        return jax.ShapeDtypeStruct((chunks, heads, *wide), kind)

    def dma(*shape):
        return [pltpu.SemaphoreType.DMA(shape)] * 2

    outside = pl.BlockSpec(memory_space=pl.ANY)
    made = (
        jax.ShapeDtypeStruct((1, members, piece, 3 * columns + CHUNK), BF),
        jax.ShapeDtypeStruct((tokens, width), BF),
        jax.ShapeDtypeStruct((tokens, 3 * columns), BF),
        jax.ShapeDtypeStruct((tokens, CHUNK), F32),
        jax.ShapeDtypeStruct((16, 3 * columns), BF),
        jax.ShapeDtypeStruct((tokens, 1), F32),
        jax.ShapeDtypeStruct((2, width), F32),
        jax.ShapeDtypeStruct((1, members, columns, piece), BF),
        jax.ShapeDtypeStruct((len(own), members, *own[0].shape), BF),
        jax.ShapeDtypeStruct((3, members, columns, piece), BF),
        jax.ShapeDtypeStruct((tokens, 3 * columns), BF),
        units((CHUNK, CHUNK), BF),
        units((CHUNK, 2 * CHUNK), BF),
        units((2 * CHUNK, CHUNK), BF),
        jax.ShapeDtypeStruct((heads, CHUNK, 2 * CHUNK), F32),
        jax.ShapeDtypeStruct((tokens, columns), F32),
        jax.ShapeDtypeStruct((tokens, columns), BF),
        jax.ShapeDtypeStruct((3, tokens // 2, columns), BF),
        units((CHUNK, CHUNK), BF),
    )
    stay = (4, 6, 14)
    return pl.pallas_call(
        functools.partial(front_kernel, members, heads),
        name="front",
        out_shape=made,
        in_specs=[pl.BlockSpec(memory_space=pltpu.SMEM)] + [whole] * (3 + len(mixer_weights) + len(own)),
        out_specs=tuple(whole if number in stay else outside for number in range(len(made))),
        scratch_shapes=[pltpu.VMEM(a.shape, a.dtype) for number, a in enumerate(made) if number not in stay]
        + [
            pltpu.SemaphoreType.DMA((len(made) - len(stay),)),
            pltpu.SMEM((tokens // GROUP,), F32),
            pltpu.VMEM((4, 3 * columns), F32),
            pltpu.VMEM((CHUNK, piece), F32),
            pltpu.VMEM((chunks, heads, CHUNK, 2 * CHUNK), BF),
            pltpu.VMEM((chunks, heads, CHUNK, CHUNK), F32),
            pltpu.VMEM((heads, CHUNK, CHUNK), F32),
            pltpu.VMEM((heads, CHUNK, 2 * CHUNK), BF),
            pltpu.VMEM((window, heads, CHUNK, 2 * CHUNK), BF),
            pltpu.VMEM((2, 144, 3 * columns), F32),
            pltpu.VMEM((16, width), BF),
        ]
        + dma(1, members)
        + dma()
        + dma(1, members)
        + dma(len(own), members)
        + dma(3)
        + dma(window)
        + dma(tokens // 256) * 3,
        compiler_params=pltpu.CompilerParams(
            collective_id=collective, has_side_effects=True, vmem_limit_bytes=VMEM_LIMIT
        ),
        cost_estimate=pl.CostEstimate(flops=8 * 10**9, bytes_accessed=40 << 20, transcendentals=2 << 20),
    )(lengths, inputs, *mixer_weights, conv, head_gain, *own)


def lanes_whole(pieces):
    places, rows, piece = pieces.shape
    if piece >= 128:
        return pieces
    group = 128 // piece
    return pieces.reshape(places // group, group, rows, piece).transpose(0, 2, 1, 3).reshape(places // group, rows, 128)


def lanes_split(blocks, piece):
    count, rows, lanes = blocks.shape
    if piece >= 128:
        return blocks
    group = 128 // piece
    return blocks.reshape(count, rows, group, piece).transpose(0, 2, 1, 3).reshape(count * group, rows, piece)


def body(
    block_input,
    first_gain,
    query_weight,
    key_weight,
    value_weight,
    beta_weight,
    conv_weight,
    head_gain,
    output_weight,
    second_gain,
    gate_weight,
    up_weight,
    down_weight,
    lengths,
    cotangent,
):
    tokens, width = block_input.shape
    heads = beta_weight.shape[1]
    columns = query_weight.shape[1]
    hidden_columns = gate_weight.shape[1]
    members = lax.axis_size("seq")
    piece = width // members
    seq_place = lax.axis_index("seq")

    gain_head = head_gain.astype(F32)[None, :]
    own = [gate_weight.T, up_weight.T, down_weight.T]
    split = piece < 128
    (
        mixer_pack,
        first_rows,
        pre,
        logits,
        halo,
        scale_one,
        gains,
        turned,
        full,
        others,
        qkv,
        inv,
        wu,
        mq,
        total,
        delta,
        head_rows,
        far_rows,
        states,
    ) = front_stage(
        lengths,
        block_input,
        (
            query_weight,
            key_weight,
            value_weight,
            beta_weight.T,
            first_gain[None, :],
            second_gain[None, :],
            output_weight,
        ),
        conv_weight,
        gain_head,
        [own[0][:16]] if split else own,
        members,
        heads,
        5,
    )
    mixer_pack = mixer_pack.reshape(width, -1)
    if split:
        gathered = lax.all_gather(jnp.stack(own), "seq", axis=1)
        full = jnp.stack([lanes_whole(gathered[i]) for i in range(3)])
    turned = lanes_whole(turned[0])
    others = jnp.stack([lanes_whole(others[i]) for i in range(3)]) if split else others
    d_heads, update_part, middle_shard, d_middle_shard, *grads, second_grad = middle_stage(
        head_rows, far_rows, full, turned, others, block_input, cotangent, gains, 2
    )
    second_part = jnp.sum(second_grad, 0)
    if split:
        pieces = jnp.concatenate([part for pair in grads for part in pair], 1)
        whole_sum = lax.psum_scatter(lanes_split(pieces, piece), "seq", scatter_dimension=0, tiled=False).astype(F32)
        grads = [jnp.zeros((1, members, 16, 128), BF)] * 3
    ddelta, gain_part, arrive, block_output, third_sum = state_backward(
        d_heads, delta, gain_head, mq, total, update_part, middle_shard, grads[2], members, 1
    )
    d_pre, taps_part, first_sum = mixer_backward(
        lengths, pre, halo, conv_weight, logits, qkv, inv, wu, mq, states, ddelta, arrive, grads[0], 3
    )
    input_gradient, mixer_sum, sums, second_sum = final_stage(
        first_rows, d_pre, mixer_pack, block_input, scale_one, gains, d_middle_shard, (gain_part, second_grad, taps_part), grads[1], members, 4
    )
    if not split:
        done = finish_stage(
            block_output, input_gradient, mixer_sum, sums, first_sum, second_sum, third_sum, hidden_columns, heads
        )
        block, ingrad, gain_1, grad_q, grad_k, grad_v, grad_b, grad_c, gain_h, grad_o, gain_2, *rest = done
        return (
            block,
            ingrad,
            gain_1.reshape(-1),
            grad_q,
            grad_k,
            grad_v,
            grad_b.T,
            grad_c,
            gain_h.reshape(-1),
            grad_o,
            gain_2.reshape(-1),
            *(grad.T for grad in rest),
        )
    gain_sum = sums[1, :CHUNK]
    conv_gradient = sums[9 : 9 + 12 * columns // width].reshape(4, 3, columns).transpose(1, 0, 2)
    row_start = seq_place * piece
    first_gradient = lax.dynamic_slice_in_dim(sums[0], row_start, piece, 0)
    second_gradient = lax.dynamic_slice_in_dim(sums[8], row_start, piece, 0)
    beta_gradient = mixer_sum[:, 3 * columns : 3 * columns + heads]
    return (
        block_output,
        input_gradient,
        first_gradient,
        mixer_sum[:, :columns],
        mixer_sum[:, columns : 2 * columns],
        mixer_sum[:, 2 * columns : 3 * columns],
        beta_gradient,
        conv_gradient,
        gain_sum,
        whole_sum[3 * hidden_columns :].T,
        second_gradient,
        whole_sum[:hidden_columns].T,
        whole_sum[hidden_columns : 2 * hidden_columns].T,
        whole_sum[2 * hidden_columns : 3 * hidden_columns].T,
    )


def solution(mesh):
    return jax.shard_map(
        body,
        mesh=mesh,
        in_specs=(
            P("seq", None),
            P("seq"),
            P("seq", "head"),
            P("seq", "head"),
            P("seq", "head"),
            P("seq", "head"),
            P(None, None, "head"),
            P(),
            P("seq", "head"),
            P("seq"),
            P("seq", "head"),
            P("seq", "head"),
            P("seq", "head"),
            P(),
            P("seq", None),
        ),
        out_specs=(
            P("seq", "head"),
            P("seq", "head"),
            P("seq"),
            P("seq", "head"),
            P("seq", "head"),
            P("seq", "head"),
            P("seq", "head"),
            P(None, None, "head"),
            P(),
            P("seq", "head"),
            P("seq"),
            P("seq", "head"),
            P("seq", "head"),
            P("seq", "head"),
        ),
        check_vma=False,
    )
```

```python
import functools

import jax
import jax.numpy as jnp
from jax import lax
from jax.experimental import pallas as pl
from jax.experimental.pallas import tpu as pltpu
from jax.sharding import PartitionSpec as P

GROUP = 64
CHUNK = 128
MESH = pl.DeviceIdType.MESH
BF = jnp.bfloat16
F32 = jnp.float32
VMEM_LIMIT = 59 << 20


def nn(left, right):
    return jnp.dot(left.astype(BF), right.astype(BF), preferred_element_type=F32)


def tn(left, right):
    return lax.dot_general(
        left.astype(BF), right.astype(BF), (((0,), (0,)), ((), ())), preferred_element_type=F32
    )


def nt(left, right):
    return lax.dot_general(
        left.astype(BF), right.astype(BF), (((1,), (1,)), ((), ())), preferred_element_type=F32
    )


def sigmoid(v):
    return 0.5 * jnp.tanh(0.5 * v) + 0.5


def side(left, right):
    return jnp.concatenate([left, right], 1)


def stack(top, bottom):
    return jnp.concatenate([top, bottom], 0)


def grid_indices():
    rows = lax.broadcasted_iota(jnp.int32, (CHUNK, CHUNK), 0)
    cols = lax.broadcasted_iota(jnp.int32, (CHUNK, CHUNK), 1)
    return rows, cols


def fill_resets(lengths_ref, resets_ref, tokens):
    base = lax.axis_index("seq") * tokens

    @pl.loop(0, tokens // GROUP)
    def _(block):
        position = base + block * GROUP
        value = jnp.float32(0.0)
        start = jnp.int32(0)
        for index in range(lengths_ref.shape[0]):
            value = jnp.where(start == position, 1.0, value)
            start = start + lengths_ref[index]
        resets_ref[block] = value


def fill_taps(conv_ref, taps_ref):
    columns = conv_ref.shape[2]
    for kind in range(3):
        taps_ref[:, kind * columns : (kind + 1) * columns] = conv_ref[kind].astype(F32)


def load_padded(pad_ref, pre_ref, halo_ref, chunk, resets_ref):
    start = pl.multiple_of(chunk * CHUNK, CHUNK)
    before = pl.multiple_of(jnp.maximum(start - 16, 0), 16)
    own = pre_ref[pl.ds(start, CHUNK), :].astype(F32)
    earlier = pre_ref[pl.ds(before, 16), :].astype(F32)[8:]
    halo = halo_ref[...].astype(F32)[8:]
    first = jnp.where(chunk == 0, halo, earlier)
    keep0 = 1.0 - resets_ref[2 * chunk]
    keep1 = 1.0 - resets_ref[2 * chunk + 1]
    pad_ref[0:8] = first * keep0
    pad_ref[8:72] = own[:GROUP]
    pad_ref[72:80] = own[GROUP - 8 : GROUP] * keep1
    pad_ref[80:144] = own[GROUP:]


def tap_rows(pad_ref, tap):
    return stack(pad_ref[5 + tap : 69 + tap], pad_ref[77 + tap : 141 + tap])


def convolve(pad_ref, taps_ref):
    mixed = None
    for tap in range(4):
        term = taps_ref[tap : tap + 1] * tap_rows(pad_ref, tap)
        mixed = term if mixed is None else mixed + term
    return mixed


def inverse_levels(strict, rows, cols, keep1):
    eye = jnp.where(rows == cols, 1.0, 0.0)
    pair = (rows // 2) == (cols // 2)
    results = [eye - jnp.where(pair, a, 0.0) for a in strict]
    width = 2
    while width < CHUNK:
        off = ((rows // (2 * width)) == (cols // (2 * width))) & ((rows // width) != (cols // width))
        lows = [r.astype(BF) for r in results]
        parts = [jnp.where(off, a, 0.0).astype(BF) for a in strict]
        if width == GROUP:
            parts = [jnp.where(off, a * k, 0.0).astype(BF) for a, k in zip(strict, keep1)]
        steps = [nn(r, p) for r, p in zip(lows, parts)]
        results = [r - nn(s, low) for r, s, low in zip(results, steps, lows)]
        width *= 2
    return results


def state_backward_kernel(
    heads,
    window,
    dheads_ref,
    delta_ref,
    gain_ref,
    mq_ref,
    total_ref,
    update_ref,
    mid_ref,
    grads_ref,
    ddelta_ref,
    gain_grad_ref,
    state_ref,
    block_ref,
    sum_ref,
    shift_ref,
    part_ref,
    slots_ref,
    send_sem,
    recv_sem,
    near_ref,
    relay_ref,
    far_ref,
    near_send,
    near_recv,
    far_send,
    far_recv,
    piece_relay,
    piece_slots,
    piece_send,
    piece_recv,
):
    member, members = lax.axis_index("seq"), lax.axis_size("seq")
    _, _, near, far = head_peers()
    chunk = 256
    steps = update_ref.shape[0] // chunk
    chunks = mq_ref.shape[0]
    behind = members - 1 - member
    at, _, start_pair, pass_on, own_sum, finish = head_scatter_copies(
        chunk, update_ref, near_ref, relay_ref, far_ref, (near_send, near_recv, far_send, far_recv)
    )
    begin, receive, jobs, end = piece_scatter(
        grads_ref, piece_relay, piece_slots, sum_ref, piece_send, piece_recv, members
    )
    barrier, stages = greet_seq(members)
    for hop in range(1, window + 1):

        @pl.when(behind >= hop)
        def _():
            pl.semaphore_signal(barrier, inc=1, device_id={"seq": member + hop}, device_id_type=MESH)

    for target in (near, far):
        pl.semaphore_signal(barrier, inc=1, device_id={"head": target}, device_id_type=MESH)
    pl.semaphore_wait(barrier, stages + 2 + jnp.minimum(member, window))

    @pl.loop(0, steps)
    def _(index):
        start_pair(index)

    for head in range(heads):
        part_ref[0, head] = total_ref[head, :, :CHUNK].T.astype(BF)

    def copy(kind, hop):
        return push(
            part_ref.at[kind],
            slots_ref.at[kind, hop - 1],
            send_sem.at[kind, hop - 1],
            recv_sem.at[kind, hop - 1],
            "seq",
            member - hop,
        )

    def send(kind):
        for hop in range(1, window + 1):

            @pl.when(member >= hop)
            def _():
                copy(kind, hop).start()

    send(0)
    half = len(jobs) // 4
    begin(jobs[:half])
    shift_ref[...] = jnp.zeros_like(shift_ref)
    gain_grad_ref[...] = jnp.zeros_like(gain_grad_ref)

    def one(step, carry):
        index = chunks - 1 - step
        rows = pl.ds(pl.multiple_of(index * CHUNK, CHUNK), CHUNK)
        for head in range(heads):
            lanes = slice(head * CHUNK, (head + 1) * CHUNK)
            out = delta_ref[rows, lanes]
            grad = dheads_ref[rows, lanes].astype(F32)
            scale = lax.rsqrt(jnp.mean(out * out, axis=-1, keepdims=True) + 1e-05)
            unit = out * scale
            gain_grad_ref[...] += jnp.sum((grad * unit).reshape(CHUNK // 8, 8, CHUNK), 0)
            scaled = grad * gain_ref[...]
            back = scale * (scaled - unit * jnp.mean(scaled * unit, axis=-1, keepdims=True))
            back = back.astype(BF)
            ddelta_ref[rows, lanes] = back
            shift_ref[head] = tn(mq_ref[index, head], stack(shift_ref[head].astype(BF), back))

        @pl.when(lax.rem(step, 2) == 1)
        def _():
            pass_on(lax.div(step, 2))

        return carry

    lax.fori_loop(0, chunks, one, 0)
    for head in range(heads):
        part_ref[1, head] = shift_ref[head].astype(BF)
    send(1)
    begin(jobs[half:])
    for job in jobs[: len(jobs) // 2]:
        receive(*job)
    state_ref[...] = jnp.zeros_like(state_ref)
    for hop in range(window, 0, -1):

        @pl.when(behind >= hop)
        def _():
            copy(0, hop).wait_recv()
            copy(1, hop).wait_recv()
            for head in range(heads):
                state_ref[head] = nn(slots_ref[0, hop - 1, head], state_ref[head]) + slots_ref[1, hop - 1, head].astype(F32)

    for job in jobs[len(jobs) // 2 :]:
        receive(*job)

    @pl.loop(0, steps)
    def _(index):
        block_ref[at(index)] = (mid_ref[at(index)] + own_sum(index)).astype(BF)
        finish(index)

    end()
    for hop in range(1, window + 1):

        @pl.when(member >= hop)
        def _():
            copy(0, hop).wait_send()
            copy(1, hop).wait_send()


def state_backward(dheads, delta, gain, mq, total, update, mid, grads, members, collective):
    chunks, heads = mq.shape[:2]
    tokens, columns = mid.shape
    window = min(members - 1, members // 2)
    whole = pl.BlockSpec(memory_space=pltpu.VMEM)
    parts, _, *piece = grads.shape
    return pl.pallas_call(
        functools.partial(state_backward_kernel, heads, window),
        name="state_backward",
        out_shape=(
            jax.ShapeDtypeStruct((tokens, columns), BF),
            jax.ShapeDtypeStruct((8, CHUNK), F32),
            jax.ShapeDtypeStruct((heads, CHUNK, CHUNK), F32),
            jax.ShapeDtypeStruct((tokens, columns), BF),
            jax.ShapeDtypeStruct((parts, *piece), F32),
        ),
        in_specs=[whole] * 8,
        out_specs=(whole,) * 5,
        scratch_shapes=[
            pltpu.VMEM((heads, CHUNK, CHUNK), F32),
            pltpu.VMEM((2, heads, CHUNK, CHUNK), BF),
            pltpu.VMEM((2, window, heads, CHUNK, CHUNK), BF),
            pltpu.SemaphoreType.DMA((2, window)),
            pltpu.SemaphoreType.DMA((2, window)),
        ]
        + head_scatter_scratch(tokens, columns, tokens // 256)
        + piece_scatter_scratch(parts, members, piece),
        compiler_params=pltpu.CompilerParams(
            collective_id=collective, has_side_effects=True, vmem_limit_bytes=VMEM_LIMIT
        ),
        cost_estimate=pl.CostEstimate(flops=10**9, bytes_accessed=30 << 20, transcendentals=0),
    )(dheads, delta, gain, mq, total, update, mid, grads)


def piece_scatter_scratch(parts, members, piece):
    return [
        pltpu.VMEM((parts, max(members // 2 - 1, 1), *piece), BF),
        pltpu.VMEM((parts, members - 1, *piece), BF),
        pltpu.SemaphoreType.DMA((parts, members)),
        pltpu.SemaphoreType.DMA((parts, members)),
    ]


def piece_scatter(own_ref, relay_ref, slots_ref, total_ref, send, recv, members):
    member = lax.axis_index("seq")
    parts = own_ref.shape[0]
    stages = (members - 1).bit_length()
    order = sorted(range(members), key=lambda r: zeros_below(r) if r else stages)
    levels = {r: list(range(zeros_below(r) if r else stages)) for r in order}
    events = {}
    for r in order:
        for stage in levels[r]:
            events[r, stage] = len(events)
    kept = [r for r in order if r and r % 2 == 0]

    def source(part, r):
        return own_ref.at[part, flip(member, r)] if r % 2 else relay_ref.at[part, kept.index(r)]

    def give(part, r):
        stage = zeros_below(r)
        slot = events[r ^ (1 << stage), stage]
        return push(
            source(part, r), slots_ref.at[part, slot], send.at[part, r], recv.at[part, slot], "seq", flip(member, 1 << stage)
        )

    def take(part, r, stage):
        slot = events[r, stage]
        return push(
            own_ref.at[part, flip(member, 1)], slots_ref.at[part, slot], send.at[part, 0], recv.at[part, slot], "seq", flip(member, 1 << stage)
        )

    jobs = [(part, r) for r in order if r % 2 == 0 for part in range(parts)]

    def begin(some=None):
        for part, r in jobs if some is None else some:
            give(part, r ^ 1).start()

    def receive(part, r):
        total = own_ref[part, flip(member, r)].astype(F32)
        for stage in levels[r]:
            take(part, r, stage).wait_recv()
            total = total + slots_ref[part, events[r, stage]].astype(F32)
        if r:
            relay_ref[part, kept.index(r)] = total.astype(BF)
            give(part, r).start()
        else:
            total_ref[part] = total

    def finish():
        for part in range(parts):
            for r in order:
                if r:
                    give(part, r).wait_send()

    return begin, receive, jobs, finish


def mixer_backward_kernel(
    heads,
    lengths_ref,
    pre_hbm,
    halo_ref,
    conv_ref,
    logits_hbm,
    qkv_hbm,
    inv_hbm,
    wu_hbm,
    mq_hbm,
    states_hbm,
    ddelta_hbm,
    arrive_ref,
    grads_ref,
    dpre_ref,
    taps_grad_ref,
    total_ref,
    pre_ref,
    logits_ref,
    qkv_ref,
    inv_ref,
    wu_ref,
    mq_ref,
    states_ref,
    ddelta_ref,
    load_sem,
    resets_ref,
    taps_ref,
    carry_ref,
    pad_ref,
    dpad_ref,
    tail_ref,
    lead_ref,
    edge_ref,
    send_sem,
    recv_sem,
    relay_ref,
    slots_ref,
    piece_send,
    piece_recv,
):
    member, members = lax.axis_index("seq"), lax.axis_size("seq")
    barrier, stages = greet_seq(members)
    begin, receive, order, finish = piece_scatter(
        grads_ref, relay_ref, slots_ref, total_ref, piece_send, piece_recv, members
    )

    @pl.when(member + 1 < members)
    def _():
        pl.semaphore_signal(barrier, inc=1, device_id={"seq": member + 1}, device_id_type=MESH)

    columns = heads * CHUNK
    chunks = mq_ref.shape[0]
    fill_resets(lengths_ref, resets_ref, pre_ref.shape[0])
    fill_taps(conv_ref, taps_ref)
    quarter = chunks // 4
    sources = (pre_hbm, logits_hbm, qkv_hbm, ddelta_hbm, inv_hbm, wu_hbm, mq_hbm, states_hbm)
    targets = (pre_ref, logits_ref, qkv_ref, ddelta_ref, inv_ref, wu_ref, mq_ref, states_ref)

    def load(number, turn):
        unit = CHUNK if number < 4 else 1
        reach = pl.ds((chunks - (turn + 1) * quarter) * unit, quarter * unit)
        return pltpu.make_async_copy(
            sources[number].at[reach], targets[number].at[reach], load_sem.at[number, turn]
        )

    for turn in range(4):
        for number in range(8):
            load(number, turn).start()
    load(0, 0).wait()
    rows, cols = grid_indices()
    top = lax.broadcasted_iota(jnp.int32, (CHUNK, 1), 0) < GROUP
    pl.semaphore_wait(barrier, stages + jnp.minimum(member, 1))
    begin()
    carry_ref[...] = arrive_ref[...]
    taps_grad_ref[...] = jnp.zeros_like(taps_grad_ref)
    dpad_ref[136:144] = jnp.zeros_like(dpad_ref[136:144])

    lanes_ = 2
    cross = (rows >= GROUP) & (cols < GROUP)
    columns_of = lax.broadcasted_iota(jnp.int32, (CHUNK, CHUNK), 1)

    def part(kind, head):
        return slice(kind * columns + head * CHUNK, kind * columns + (head + 1) * CHUNK)

    def one(step, carry):
        for turn in range(4):

            @pl.when(step * lanes_ == turn * quarter)
            def _():
                for number in range(1, 8):
                    load(number, turn).wait()
                if turn < 3:
                    load(0, turn + 1).wait()

        at, keep0, keep1, enter, leave, slope, silued, beta_rows, place = [], [], [], [], [], [], [], [], []
        for lane in range(lanes_):
            chunk = chunks - 1 - lanes_ * step - lane
            place.append(chunk)
            at.append(pl.ds(pl.multiple_of(chunk * CHUNK, CHUNK), CHUNK))
            keep0.append(1.0 - resets_ref[2 * chunk])
            keep1.append(1.0 - resets_ref[2 * chunk + 1])
            enter.append(jnp.where(top, keep0[lane], keep0[lane] * keep1[lane]))
            leave.append(jnp.where(top, keep1[lane], 1.0))
            load_padded(pad_ref.at[lane], pre_ref, halo_ref, chunk, resets_ref)
            mixed = convolve(pad_ref.at[lane], taps_ref)
            gate = sigmoid(mixed)
            slope.append(gate * (1.0 + mixed * (1.0 - gate)))
            silued.append(mixed * gate)
            beta_rows.append(sigmoid(logits_ref[at[lane], :]))

        units = [(lane, h) for lane in range(lanes_) for h in range(heads)]
        every = range(len(units))

        def masked(product, keep, u):
            lower = jnp.where(keep, product, 0.0)
            return jnp.where(cross, lower * keep1[units[u][0]], lower).astype(BF)

        query = [qkv_ref[at[l], part(0, h)] for l, h in units]
        key = [qkv_ref[at[l], part(1, h)] for l, h in units]
        value = [qkv_ref[at[l], part(2, h)] for l, h in units]
        key32 = [k.astype(F32) for k in key]
        beta = [beta_rows[l][:, h : h + 1] for l, h in units]
        inverse = [inv_ref[place[l], h] for l, h in units]
        factors = [wu_ref[place[l], h] for l, h in units]
        weight = [f[:, :CHUNK] for f in factors]
        update = [f[:, CHUNK:] for f in factors]
        state = [states_ref[place[l], h] for l, h in units]
        out_grad = [ddelta_ref[at[l], h * CHUNK : (h + 1) * CHUNK] for l, h in units]
        later = []
        carried = [carry_ref[h] for h in range(heads)]
        for u, (l, h) in enumerate(units):
            later.append(carried[h].astype(BF))
            carried[h] = tn(mq_ref[place[l], h], stack(later[u], out_grad[u]))
        scores = [masked(nt(query[u], key[u]), rows >= cols, u) for u in every]
        fresh = [(update[u].astype(F32) - nn(weight[u], state[u])).astype(BF) for u in every]
        fresh_low = [
            (tn(scores[u], out_grad[u]) + leave[units[u][0]] * nn(key[u], later[u])).astype(BF) for u in every
        ]
        score_grad = [masked(nt(out_grad[u], fresh[u]), rows >= cols, u) for u in every]
        through = [nt(stack(out_grad[u], fresh_low[u]), state[u]) for u in every]
        weight_grad = [(-enter[units[u][0]] * through[u][CHUNK:]).astype(BF) for u in every]
        back = [tn(inverse[u], side(weight_grad[u], fresh_low[u])) for u in every]
        query_grad = [enter[units[u][0]] * through[u][:CHUNK] + nn(score_grad[u], key[u]) for u in every]
        key_grad = [tn(score_grad[u], query[u]) + leave[units[u][0]] * nt(fresh[u], later[u]) for u in every]
        strict = [masked(-nt(back[u].astype(BF), factors[u]), rows > cols, u) for u in every]
        strict_key = [nn(strict[u], key[u]) for u in every]
        turned = [tn(strict[u], (beta[u] * key32[u]).astype(BF)) for u in every]
        for h in range(heads):
            carry_ref[h] = carried[h]
        value_grad, dlogits = [], []
        for u in every:
            yk, zv = back[u][:, :CHUNK], back[u][:, CHUNK:]
            both_key = yk + strict_key[u]
            key_grad[u] = key_grad[u] + beta[u] * both_key + turned[u]
            value_grad.append(beta[u] * zv)
            beta_grad = jnp.sum(both_key * key32[u] + zv * value[u].astype(F32), axis=-1, keepdims=True)
            dlogits.append(beta_grad * beta[u] * (1.0 - beta[u]))
        unit_grads = []
        for kind, grad in ((0, query_grad), (1, key_grad)):
            raw = [silued[l][:, part(kind, h)] for l, h in units]
            norm = [lax.rsqrt(jnp.sum(r * r, axis=-1, keepdims=True) + 1e-06) for r in raw]
            unit = [raw[u] * norm[u] for u in every]
            inner = [jnp.sum(unit[u] * grad[u], axis=-1, keepdims=True) for u in every]
            unit_grads.append([(grad[u] - unit[u] * inner[u]) * norm[u] for u in every])
        unit_grads.append(value_grad)
        for lane in range(lanes_):
            spread = jnp.zeros((CHUNK, CHUNK), F32)
            for head in range(heads):
                spread = jnp.where(columns_of == head, dlogits[lane * heads + head], spread)
            dpre_ref[at[lane], 3 * columns :] = spread.astype(BF)
            mine = [g[lane * heads + head] for g in unit_grads for head in range(heads)]
            dmixed = jnp.concatenate(mine, 1) * slope[lane]
            dpad_ref[0:GROUP] = dmixed[:GROUP]
            dpad_ref[GROUP : GROUP + 8] = dmixed[GROUP : GROUP + 8] * keep1[lane]
            dpad_ref[72 : 72 + GROUP] = dmixed[GROUP:]
            dpre = None
            for tap in range(4):
                reach = 3 - tap
                shifted = stack(dpad_ref[reach : reach + GROUP], dpad_ref[72 + reach : 72 + reach + GROUP])
                term = taps_ref[tap : tap + 1] * shifted
                dpre = term if dpre is None else dpre + term
                seen = (dmixed * tap_rows(pad_ref.at[lane], tap)).reshape(CHUNK // 8, 8, 3 * columns)
                taps_grad_ref[tap] += jnp.sum(seen, 0)
            dpre_ref[at[lane], : 3 * columns] = dpre.astype(BF)
            if lane == 0:

                @pl.when(step == 0)
                def _():
                    tail_ref[...] = dpre[CHUNK - 16 :]

            dpad_ref[136:144] = dmixed[:8] * keep0[lane]
        turns = chunks // lanes_
        for number, job in enumerate(order):

            @pl.when(step == (number + 1) * (turns - 1) // len(order))
            def _():
                receive(*job)

        return carry

    lax.fori_loop(0, chunks // lanes_, one, 0)
    index = lax.broadcasted_iota(jnp.int32, (8, 1), 0)
    lead = jnp.zeros((8, 3 * columns), F32)
    dpad_ref[0:128] = jnp.zeros_like(dpad_ref[0:128])
    dpad_ref[8:16] = dpad_ref[136:144]
    for tap in range(3):
        back = 3 - tap
        lead = lead + taps_ref[tap : tap + 1] * dpad_ref[back : back + 8]
    lead_ref[...] = lead

    def to_previous(target):
        return push(lead_ref, edge_ref, send_sem, recv_sem, "seq", target)

    @pl.when(member > 0)
    def _():
        to_previous(member - 1).start()

    @pl.when(member + 1 < members)
    def _():
        to_previous(member).wait_recv()
        last = pl.ds(dpre_ref.shape[0] - 16, 16)
        late = stack(tail_ref[0:8], tail_ref[8:16] + edge_ref[...])
        dpre_ref[last, : 3 * columns] = late.astype(BF)

    @pl.when(member > 0)
    def _():
        to_previous(member - 1).wait_send()

    finish()


def mixer_backward(lengths, pre, halo, conv, logits, qkv, inv, wu, mq, states, ddelta, arrive, grads, collective):
    chunks, heads = mq.shape[:2]
    tokens = chunks * CHUNK
    columns = heads * CHUNK
    parts, members = grads.shape[:2]
    piece = grads.shape[2:]
    whole, outside = pl.BlockSpec(memory_space=pltpu.VMEM), pl.BlockSpec(memory_space=pl.ANY)
    streamed = (pre, logits, qkv, inv, wu, mq, states, ddelta)
    return pl.pallas_call(
        functools.partial(mixer_backward_kernel, heads),
        name="mixer_backward",
        out_shape=(
            jax.ShapeDtypeStruct((tokens, 3 * columns + CHUNK), BF),
            jax.ShapeDtypeStruct((4, 8, 3 * columns), F32),
            jax.ShapeDtypeStruct((parts, *piece), F32),
        ),
        in_specs=[pl.BlockSpec(memory_space=pltpu.SMEM), outside, whole, whole] + [outside] * 7 + [whole] * 2,
        out_specs=tuple([pl.BlockSpec(memory_space=pltpu.VMEM)] * 3),
        scratch_shapes=[pltpu.VMEM(a.shape, a.dtype) for a in streamed]
        + [
            pltpu.SemaphoreType.DMA((8, 4)),
            pltpu.SMEM((tokens // GROUP,), F32),
            pltpu.VMEM((4, 3 * columns), F32),
            pltpu.VMEM((heads, CHUNK, CHUNK), F32),
            pltpu.VMEM((2, 144, 3 * columns), F32),
            pltpu.VMEM((144, 3 * columns), F32),
            pltpu.VMEM((16, 3 * columns), F32),
            pltpu.VMEM((8, 3 * columns), F32),
            pltpu.VMEM((8, 3 * columns), F32),
            pltpu.SemaphoreType.DMA,
            pltpu.SemaphoreType.DMA,
        ]
        + piece_scatter_scratch(parts, members, piece),
        compiler_params=pltpu.CompilerParams(
            collective_id=collective, has_side_effects=True, vmem_limit_bytes=VMEM_LIMIT
        ),
        cost_estimate=pl.CostEstimate(flops=3 * 10**9, bytes_accessed=20 << 20, transcendentals=2 << 20),
    )(lengths, pre, halo, conv, logits, qkv, inv, wu, mq, states, ddelta, arrive, grads)


def head_peers():
    place = lax.axis_index("head")
    low = lax.rem(place, 2)
    high = lax.rem(lax.div(place, 2), 2)
    return place, low, place + 1 - 2 * low, place + 2 - 4 * high


def push(src, dst, send_sem, recv_sem, axis, target):
    return pltpu.make_async_remote_copy(
        src_ref=src,
        dst_ref=dst,
        send_sem=send_sem,
        recv_sem=recv_sem,
        device_id={axis: target},
        device_id_type=MESH,
    )


def greet(axis, targets):
    barrier = pltpu.get_barrier_semaphore()
    for target in targets:
        pl.semaphore_signal(barrier, inc=1, device_id={axis: target}, device_id_type=MESH)
    pl.semaphore_wait(barrier, len(targets))


def middle_kernel(
    steps,
    rows_ref,
    far_rows_ref,
    full_hbm,
    turned_hbm,
    others_hbm,
    input_ref,
    ct_ref,
    late_ct_ref,
    gain_ref,
    dheads_ref,
    update_ref,
    mid_ref,
    dmid_ref,
    first_grads_ref,
    second_grads_ref,
    third_grads_ref,
    gain_grad_ref,
    gate_ref,
    up_ref,
    down_ref,
    turned_ref,
    others_ref,
    load_sem,
    own_rows_ref,
    stage_ref,
    acc_ref,
    part_ref,
    pair_ref,
    far_ref,
    sum_ref,
    keep_ref,
    scale_ref,
    shard_ref,
    pair_send,
    pair_recv,
    far_send,
    far_recv,
    last_send,
    last_recv,
    row_near_send,
    row_near_recv,
    row_far_send,
    row_far_recv,
    row_pass_send,
    row_pass_recv,
):
    step = pl.program_id(0)
    place, low, near, far = head_peers()
    chunk, width = input_ref.shape
    columns = rows_ref.shape[1]
    hidden = gate_ref.shape[0]
    half = width // 2
    mine = pl.ds(pl.multiple_of(low * half, 128), half)
    theirs = pl.ds(pl.multiple_of((1 - low) * half, 128), half)
    own_columns = pl.ds(pl.multiple_of(place * columns, 128), columns)

    known = steps // 2

    def at(index):
        return pl.ds(pl.multiple_of(index * chunk, chunk), chunk)

    def near_rows(index):
        place_ = at(index - known)
        return push(
            rows_ref.at[at(index)], own_rows_ref.at[0, place_], row_near_send.at[index], row_near_recv.at[index], "head", near
        )

    def far_rows(index):
        place_ = at(index - known)
        return push(
            rows_ref.at[at(index)], own_rows_ref.at[1, place_], row_far_send.at[index], row_far_recv.at[index], "head", far
        )

    def pass_rows(index):
        place_ = at(index - known)
        return push(
            own_rows_ref.at[1, place_], own_rows_ref.at[2, place_], row_pass_send.at[index], row_pass_recv.at[index], "head", near
        )

    def pair(index):
        return push(
            part_ref.at[lax.rem(index, 2), :, theirs], pair_ref.at[index], pair_send.at[index], pair_recv.at[index], "head", near
        )

    def across(index):
        return push(pair_ref.at[index], far_ref.at[index], far_send.at[index], far_recv.at[index], "head", far)

    def last(index):
        return push(
            sum_ref.at[index, :, mine], sum_ref.at[index, :, mine], last_send.at[index], last_recv.at[index], "head", near
        )

    def loads():
        targets = [
            (full_hbm.at[0], gate_ref),
            (full_hbm.at[1], up_ref),
            (full_hbm.at[2], down_ref),
            (turned_hbm, turned_ref),
        ] + [(others_hbm.at[other], others_ref.at[other]) for other in range(3)]
        for number, (source, target) in enumerate(targets):
            for piece in range(width // 128):
                yield pltpu.make_async_copy(
                    source.at[piece], target.at[:, piece * 128 : (piece + 1) * 128], load_sem.at[number, piece]
                )

    @pl.when(step == 0)
    def _():
        for load in loads():
            load.start()
        greet("head", (near, far))

        @pl.loop(known, steps)
        def _(index):
            far_rows(index).start()
            near_rows(index).start()


        acc_ref[...] = jnp.zeros_like(acc_ref)
        gain_grad_ref[...] = jnp.zeros_like(gain_grad_ref)
        for load in loads():
            load.wait()

    @pl.when(step < steps)
    def _():
        ct = ct_ref[...]
        d_hidden = nt(ct, down_ref[...])

        @pl.when(step < known)
        def _():
            stage_ref[...] = far_rows_ref[...]

        @pl.when(step >= known)
        def _():
            near_rows(step).wait_recv()
            pass_rows(step).wait_recv()
            stage_ref[...] = own_rows_ref[:, at(step - known)]

        branch = nn(rows_ref[at(step)], turned_ref[...])
        for other in range(3):
            branch = branch + nn(stage_ref[other], others_ref[other])
        middle = input_ref[...].astype(F32) + branch
        keep_ref[lax.rem(step, 4)] = middle
        mid_ref[...] = keep_ref[lax.rem(step, 4), :, own_columns]
        scale = lax.rsqrt(jnp.mean(middle * middle, axis=-1, keepdims=True) + 1e-06)
        scale_ref[lax.rem(step, 4)] = scale
        second = (middle * scale * gain_ref[1:2]).astype(BF)
        gate, up = nt(second, gate_ref[...]), nt(second, up_ref[...])
        sig = sigmoid(gate)
        silu = gate * sig
        active = (silu * up).astype(BF)
        d_gate = (d_hidden * up * (sig + silu * (1.0 - sig))).astype(BF)
        d_up = (d_hidden * silu).astype(BF)

        @pl.when(step >= 2)
        def _():
            pair(step - 2).wait_send()

        part_ref[lax.rem(step, 2)] = (nn(d_gate, gate_ref[...]) + nn(d_up, up_ref[...])).astype(BF)
        pair(step).start()

        @pl.when((step + 2 >= known) & (step + 2 < steps))
        def _():
            far_rows(step + 2).wait_recv()
            pass_rows(step + 2).start()

        update_ref[...] = nn(active, down_ref[...]).astype(BF)
        acc_ref[:hidden] += tn(d_gate, second)
        acc_ref[hidden : 2 * hidden] += tn(d_up, second)
        acc_ref[2 * hidden : 3 * hidden] += tn(active, ct)

    @pl.when(step < steps)
    def _():
        pair(step).wait_recv()
        both = part_ref[lax.rem(step, 2), :, mine].astype(F32) + pair_ref[step].astype(F32)
        pair_ref[step] = both.astype(BF)
        across(step).start()

    @pl.when((step > 1) & (step < steps + 2))
    def _():
        done = step - 2
        across(done).wait_recv()
        across(done).wait_send()
        total = pair_ref[done].astype(F32) + far_ref[done].astype(F32)
        sum_ref[done, :, mine] = total.astype(BF)
        last(done).start()

    @pl.when(step > 2)
    def _():
        done = step - 3
        last(done).wait_recv()
        grad = sum_ref[done].astype(F32)
        middle = keep_ref[lax.rem(done, 4)]
        scale = scale_ref[lax.rem(done, 4)]
        unit = middle * scale
        gain_grad_ref[...] += jnp.sum((grad * unit).reshape(chunk // 8, 8, width), 0)
        scaled = grad * gain_ref[1:2]
        d_middle = late_ct_ref[...].astype(F32) + scale * (
            scaled - unit * jnp.mean(scaled * unit, axis=-1, keepdims=True)
        )
        shard_ref[...] = d_middle
        dmid_ref[...] = shard_ref[:, own_columns]
        d_branch = d_middle.astype(BF)
        dheads_ref[...] = nt(d_branch, turned_ref[...]).astype(BF)
        acc_ref[3 * hidden :] += tn(rows_ref[at(done)], d_branch)

    @pl.when(step == steps + 2)
    def _():
        for piece in range(width // 128):
            lanes = slice(piece * 128, (piece + 1) * 128)
            begin = 0
            for grads_ref in (first_grads_ref, second_grads_ref, third_grads_ref):
                rows = grads_ref.shape[2]
                for part in range(2):
                    grads_ref[part, piece] = acc_ref[begin : begin + rows, lanes].astype(BF)
                    begin += rows

        @pl.loop(0, steps)
        def _(index):
            last(index).wait_send()

        @pl.loop(known, steps)
        def _(index):
            near_rows(index).wait_send()
            far_rows(index).wait_send()
            pass_rows(index).wait_send()

        for index in range(max(steps - 2, 0), steps):
            pair(index).wait_send()


def middle_stage(head_rows, far_rows, full, turned, others, inputs, cotangent, gain, collective):
    tokens, width = inputs.shape
    columns = head_rows.shape[1]
    chunk = min(256, tokens // 2)
    steps = tokens // chunk
    whole = pl.BlockSpec(memory_space=pltpu.VMEM)
    outside = pl.BlockSpec(memory_space=pl.ANY)
    hidden = full.shape[2]
    units = (3 * hidden + columns) // 32
    shares = [16 * (units * 36 // 74), 0, 16 * (units * 25 // 74)]
    shares[1] = 16 * units - sum(shares)

    def early(wide):
        return pl.BlockSpec((chunk, wide), lambda s: (jnp.minimum(s, steps - 1), 0))

    def late(wide):
        return pl.BlockSpec((chunk, wide), lambda s: (jnp.maximum(s - 3, 0), 0))

    far = pl.BlockSpec((3, chunk, columns), lambda s: (0, jnp.minimum(s, steps // 2 - 1), 0))
    dma = pltpu.SemaphoreType.DMA((steps,))
    return pl.pallas_call(
        functools.partial(middle_kernel, steps),
        name="middle",
        grid=(steps + 3,),
        out_shape=(
            jax.ShapeDtypeStruct((tokens, columns), BF),
            jax.ShapeDtypeStruct((tokens, width), BF),
            jax.ShapeDtypeStruct((tokens, columns), F32),
            jax.ShapeDtypeStruct((tokens, columns), F32),
            *(jax.ShapeDtypeStruct((2, width // 128, rows, 128), BF) for rows in shares),
            jax.ShapeDtypeStruct((8, width), F32),
        ),
        in_specs=[whole, far] + [outside] * 3 + [early(width), early(width), late(width), whole],
        out_specs=(late(columns), early(width), early(columns), late(columns), whole, whole, whole, whole),
        scratch_shapes=[
            pltpu.VMEM((hidden, width), BF),
            pltpu.VMEM((hidden, width), BF),
            pltpu.VMEM((hidden, width), BF),
            pltpu.VMEM((columns, width), BF),
            pltpu.VMEM((3, columns, width), BF),
            pltpu.SemaphoreType.DMA((7, width // 128)),
            pltpu.VMEM((3, tokens // 2, columns), BF),
            pltpu.VMEM((3, chunk, columns), BF),
            pltpu.VMEM((3 * hidden + columns, width), F32),
            pltpu.VMEM((2, chunk, width), BF),
            pltpu.VMEM((steps, chunk, width // 2), BF),
            pltpu.VMEM((steps, chunk, width // 2), BF),
            pltpu.VMEM((steps, chunk, width), BF),
            pltpu.VMEM((4, chunk, width), F32),
            pltpu.VMEM((4, chunk, 1), F32),
            pltpu.VMEM((chunk, width), F32),
        ]
        + [dma] * 12,
        compiler_params=pltpu.CompilerParams(
            collective_id=collective,
            has_side_effects=True,
            vmem_limit_bytes=VMEM_LIMIT,
            dimension_semantics=("arbitrary",),
        ),
        cost_estimate=pl.CostEstimate(flops=30 * 10**9, bytes_accessed=30 << 20, transcendentals=2 << 20),
    )(head_rows, far_rows, full, turned, others, inputs, cotangent, cotangent, gain)


def zeros_below(value):
    return (value & -value).bit_length() - 1


def flip(place, mask):
    bit = 1
    while bit <= mask:
        if mask & bit:
            place = place + bit - 2 * bit * lax.rem(lax.div(place, bit), 2)
        bit *= 2
    return place


def head_scatter_copies(chunk, part_ref, near_ref, send_ref, far_ref, sems):
    place, low, near, far = head_peers()
    high = lax.rem(lax.div(place, 2), 2)
    columns = far_ref.shape[-1]
    near_send, near_recv, far_send, far_recv = sems

    def at(index):
        return pl.ds(pl.multiple_of(index * chunk, chunk), chunk)

    def cols(owner):
        return pl.ds(pl.multiple_of(owner * columns, 128), columns)

    def pair(index, side_):
        return push(
            part_ref.at[at(index), cols(2 * side_ + 1 - low)],
            near_ref.at[side_, at(index)],
            near_send.at[side_, index],
            near_recv.at[side_, index],
            "head",
            near,
        )

    def across(index):
        return push(send_ref.at[at(index)], far_ref.at[at(index)], far_send.at[index], far_recv.at[index], "head", far)

    def start_pair(index):
        pair(index, 0).start()
        pair(index, 1).start()

    def pass_on(index):
        pair(index, 0).wait_recv()
        pair(index, 1).wait_recv()
        total = part_ref[at(index), cols(2 * (1 - high) + low)].astype(F32) + near_ref[1 - high, at(index)].astype(F32)
        send_ref[at(index)] = total.astype(BF)
        across(index).start()

    def own_sum(index):
        across(index).wait_recv()
        near_part = part_ref[at(index), cols(place)].astype(F32) + near_ref[high, at(index)].astype(F32)
        return near_part + far_ref[at(index)].astype(F32)

    def finish(index):
        pair(index, 0).wait_send()
        pair(index, 1).wait_send()
        across(index).wait_send()

    return at, cols, start_pair, pass_on, own_sum, finish


def head_scatter_scratch(tokens, columns, steps):
    return [
        pltpu.VMEM((2, tokens, columns), BF),
        pltpu.VMEM((tokens, columns), BF),
        pltpu.VMEM((tokens, columns), BF),
        pltpu.SemaphoreType.DMA((2, steps)),
        pltpu.SemaphoreType.DMA((2, steps)),
        pltpu.SemaphoreType.DMA((steps,)),
        pltpu.SemaphoreType.DMA((steps,)),
    ]


def final_kernel(
    members,
    chunk,
    rows_ref,
    dpre_ref,
    pack_hbm,
    input_hbm,
    scale_hbm,
    gain_ref,
    dmid_hbm,
    head_part_ref,
    second_part_ref,
    taps_part_ref,
    rest_ref,
    ingrad_ref,
    piece_ref,
    sums_ref,
    total_ref,
    pack_ref,
    input_ref,
    scale_ref,
    dmid_ref,
    load_sem,
    acc_ref,
    out_ref,
    slots_ref,
    part_ref,
    near_ref,
    send_ref,
    far_ref,
    near_send,
    near_recv,
    far_send,
    far_recv,
    stat_ref,
    stat_slots,
    small_slots,
    piece_send,
    piece_recv,
    stat_send,
    stat_recv,
    small_send,
    small_recv,
    rest_relay,
    rest_slots,
    rest_send,
    rest_recv,
):
    tokens, width = input_ref.shape
    steps = tokens // chunk
    loads = [
        pltpu.make_async_copy(source, target, load_sem.at[number])
        for number, (source, target) in enumerate(
            ((pack_hbm, pack_ref), (input_hbm, input_ref), (scale_hbm, scale_ref), (dmid_hbm, dmid_ref))
        )
    ]
    for load in loads:
        load.start()
    place, low, near, far = head_peers()
    member = lax.axis_index("seq")
    rows = width // members
    stages = (members - 1).bit_length()
    at, cols, start_pair, pass_on, own_sum, finish = head_scatter_copies(
        chunk, part_ref, near_ref, send_ref, far_ref, (near_send, near_recv, far_send, far_recv)
    )

    barrier = pltpu.get_barrier_semaphore()
    opposite = near + far - place
    for target in (near, far, opposite):
        pl.semaphore_signal(barrier, inc=1, device_id={"head": target}, device_id_type=MESH)
    for stage in range(stages):
        pl.semaphore_signal(barrier, inc=1, device_id={"seq": flip(member, 1 << stage)}, device_id_type=MESH)
    begin, rest_receive, rest_jobs, rest_end = piece_scatter(
        rest_ref, rest_relay, rest_slots, total_ref, rest_send, rest_recv, members
    )
    pl.semaphore_wait(barrier, 3 + stages)
    order = sorted(range(members), key=lambda r: zeros_below(r) if r else stages)
    sent = [r for r in order if r]
    events = {}
    for r in order:
        for stage in range(zeros_below(r) if r else stages):
            events[stage, r] = len(events)

    def give(r):
        stage = zeros_below(r)
        slot = events[stage, r ^ (1 << stage)]
        return push(
            out_ref.at[r],
            slots_ref.at[slot],
            piece_send.at[r],
            piece_recv.at[slot],
            "seq",
            flip(member, 1 << stage),
        )

    def take(stage, r):
        slot = events[stage, r]
        return push(
            out_ref.at[0], slots_ref.at[slot], piece_send.at[0], piece_recv.at[slot], "seq", flip(member, 1 << stage)
        )

    def send_piece(r):
        out_ref[r] = acc_ref[flip(member, r)].astype(BF)
        give(r).start()

    def receive(r):
        index = flip(member, r)
        for stage in range(zeros_below(r) if r else stages):
            take(stage, r).wait_recv()
            acc_ref[index] += slots_ref[events[stage, r]].astype(F32)
        if r:
            send_piece(r)

    first = sorted([r for r in range(members) if r % 2], key=lambda r: order.index(r ^ 1))
    evens = [r for r in order if r % 2 == 0]
    if rows % 128 == 0:
        for r in first:
            even = 2 * lax.div(flip(member, r), 2)
            columns = pl.ds(pl.multiple_of(even * rows, 128), 2 * rows)
            block = tn(rows_ref[:, columns], dpre_ref[...])
            acc_ref[even] = block[:rows]
            acc_ref[even + 1] = block[rows:]
            send_piece(r)
        begin()
    else:
        per = 128 // rows
        for unit in range(width // 128):
            block = tn(rows_ref[:, unit * 128 : (unit + 1) * 128], dpre_ref[...])
            acc_ref[unit * per : (unit + 1) * per] = block.reshape(per, rows, block.shape[1])
        for r in first:
            send_piece(r)
        begin()

    small_slots[0] = jnp.zeros_like(small_slots[0])
    small_slots[0, 1:2, :CHUNK] = jnp.sum(head_part_ref[...], 0, keepdims=True)
    small_slots[0, 8:9] = jnp.sum(second_part_ref[...], 0, keepdims=True)
    columns3 = taps_part_ref.shape[2]
    for tap in range(4):
        taps_sum = jnp.sum(taps_part_ref[tap], 0, keepdims=True)
        for block in range(3):
            flat = tap * columns3 + block * (columns3 // 3)
            line, lane = 9 + flat // width, flat % width
            small_slots[0, line : line + 1, lane : lane + columns3 // 3] = taps_sum[
                :, block * (columns3 // 3) : (block + 1) * (columns3 // 3)
            ]
    for load in loads:
        load.wait()
    diagonal = lax.broadcasted_iota(jnp.int32, (128, 128), 0) == lax.broadcasted_iota(jnp.int32, (128, 128), 1)

    def project(index):
        part = nt(dpre_ref[at(index)], pack_ref[...])
        part_ref[at(index)] = part.astype(BF)
        start_pair(index)
        seen = part * (input_ref[at(index)].astype(F32) * scale_ref[at(index)])
        small_slots[0, 0:1] += jnp.sum(seen, 0, keepdims=True)
        stat = jnp.sum(seen * gain_ref[0:1], axis=-1, keepdims=True)
        for block in range(chunk // 128):
            line = jnp.where(diagonal, stat[block * 128 : (block + 1) * 128], 0.0)
            stat_ref[index * (chunk // 128) + block] = jnp.sum(line, 0, keepdims=True)

    early = steps // 2
    receives = list(evens)
    for half in range(2):

        @pl.loop(half * early, (half + 1) * early)
        def _(index):
            project(index)

            @pl.when(lax.rem(index, 2) == 1)
            def _():
                pass_on(lax.div(index, 2))

        if len(receives) > 1:
            receive(receives.pop(0))

    def stat_copy(turn):
        target = (near, far, opposite)[turn]
        return push(stat_ref, stat_slots.at[turn], stat_send.at[turn], stat_recv.at[turn], "head", target)

    def head_copy(turn):
        target = (near, far, opposite)[turn]
        return push(
            small_slots.at[0, pl.ds(0, 8)],
            small_slots.at[1 + turn, pl.ds(0, 8)],
            small_send.at[turn],
            small_recv.at[turn],
            "head",
            target,
        )

    for turn in (1, 2, 0):
        head_copy(turn).start()
        stat_copy(turn).start()
    for index in range(early, steps):
        pass_on(index)
    while len(receives) > 1:
        receive(receives.pop(0))
    for turn in range(3):
        head_copy(turn).wait()
    small_slots[4] = small_slots[0]
    small_slots[4, 0:8] += small_slots[1, 0:8] + small_slots[2, 0:8] + small_slots[3, 0:8]

    bits = list(range(1, stages)) + [0]

    def seq_copy(turn):
        return push(
            small_slots.at[4 + 2 * turn],
            small_slots.at[5 + 2 * turn],
            small_send.at[3 + turn],
            small_recv.at[3 + turn],
            "seq",
            flip(member, 1 << bits[turn]),
        )

    def seq_add(turn):
        seq_copy(turn).wait()
        small_slots[6 + 2 * turn] = small_slots[4 + 2 * turn] + small_slots[5 + 2 * turn]

    seq_copy(0).start()
    for turn in range(3):
        stat_copy(turn).wait()
    stat_ref[...] += stat_slots[0] + stat_slots[1] + stat_slots[2]

    def result(index):
        grad = own_sum(index)
        scale = scale_ref[at(index)]
        unit = input_ref[at(index), cols(place)].astype(F32) * scale
        means = []
        for block in range(chunk // 128):
            line = jnp.where(diagonal, stat_ref[index * (chunk // 128) + block], 0.0)
            means.append(jnp.sum(line, axis=-1, keepdims=True))
        mean = jnp.concatenate(means, 0) * (1.0 / width)
        ingrad_ref[at(index)] = dmid_ref[at(index)] + scale * (grad * gain_ref[0:1, cols(place)] - unit * mean)

    rests = list(rest_jobs)
    for turn in range(stages):
        start, stop = turn * steps // stages, (turn + 1) * steps // stages
        if stop > start:

            @pl.loop(start, stop)
            def _(index):
                result(index)

        share = (len(rests) - 1) // (stages - turn)
        for job in rests[:share]:
            rest_receive(*job)
        rests = rests[share:]
        seq_add(turn)
        if turn + 1 < stages:
            seq_copy(turn + 1).start()
    receive(0)
    for job in rests:
        rest_receive(*job)
    piece_ref[...] = acc_ref[member]
    sums_ref[...] = small_slots[4 + 2 * stages]

    @pl.loop(0, steps)
    def _(index):
        finish(index)

    for r in sent:
        give(r).wait_send()
    rest_end()


def final_stage(first_rows, dpre, pack, inputs, scale, gain, dmid, parts, rest, members, collective):
    tokens, width = inputs.shape
    columns = dmid.shape[1]
    chunk = 256
    steps = tokens // chunk
    stages = (members - 1).bit_length()
    rows = width // members
    wide = dpre.shape[1]
    whole, outside = pl.BlockSpec(memory_space=pltpu.VMEM), pl.BlockSpec(memory_space=pl.ANY)
    return pl.pallas_call(
        functools.partial(final_kernel, members, chunk),
        name="final",
        out_shape=(
            jax.ShapeDtypeStruct((tokens, columns), F32),
            jax.ShapeDtypeStruct((rows, wide), F32),
            jax.ShapeDtypeStruct((16, width), F32),
            jax.ShapeDtypeStruct((rest.shape[0], *rest.shape[2:]), F32),
        ),
        in_specs=[whole, whole, outside, outside, outside, whole, outside] + [whole] * 4,
        out_specs=(whole,) * 4,
        scratch_shapes=[pltpu.VMEM(a.shape, a.dtype) for a in (pack, inputs, scale, dmid)]
        + [
            pltpu.SemaphoreType.DMA((4,)),
            pltpu.VMEM((members, rows, wide), F32),
            pltpu.VMEM((members, rows, wide), BF),
            pltpu.VMEM((members - 1, rows, wide), BF),
            pltpu.VMEM((tokens, width), BF),
        ]
        + head_scatter_scratch(tokens, columns, steps)
        + [
            pltpu.VMEM((tokens // 128, 1, 128), F32),
            pltpu.VMEM((3, tokens // 128, 1, 128), F32),
            pltpu.VMEM((5 + 2 * stages, 16, width), F32),
            pltpu.SemaphoreType.DMA((members,)),
            pltpu.SemaphoreType.DMA((members - 1,)),
            pltpu.SemaphoreType.DMA((3,)),
            pltpu.SemaphoreType.DMA((3,)),
            pltpu.SemaphoreType.DMA((3 + stages,)),
            pltpu.SemaphoreType.DMA((3 + stages,)),
        ]
        + piece_scatter_scratch(rest.shape[0], members, rest.shape[2:]),
        compiler_params=pltpu.CompilerParams(
            collective_id=collective, has_side_effects=True, vmem_limit_bytes=VMEM_LIMIT
        ),
        cost_estimate=pl.CostEstimate(flops=8 * 10**9, bytes_accessed=30 << 20, transcendentals=0),
    )(first_rows, dpre, pack, inputs, scale, gain, dmid, *parts, rest)


def finish_kernel(
    hidden,
    block_ref,
    ingrad_ref,
    piece_ref,
    sums_ref,
    first_ref,
    second_ref,
    third_ref,
    block_out,
    ingrad_out,
    first_gain_out,
    query_out,
    key_out,
    value_out,
    beta_out,
    conv_out,
    head_gain_out,
    output_out,
    second_gain_out,
    gate_out,
    up_out,
    down_out,
    turn_ref,
    strip_ref,
    sems,
):
    rows, columns = query_out.shape
    member = lax.axis_index("seq")
    pieces = [(block_ref, block_out), (ingrad_ref, ingrad_out)]
    for kind, target in enumerate((query_out, key_out, value_out)):
        pieces.append((piece_ref.at[:, pl.ds(kind * columns, columns)], target))
    pieces.append((piece_ref.at[:, pl.ds(3 * columns, CHUNK)], strip_ref))
    spans = []
    place = 0
    for source in (first_ref, second_ref, third_ref):
        for part in range(2):
            spans.append((place, source, part))
            place += source.shape[1]
    goal = 0
    for target, count in ((gate_out, hidden), (up_out, hidden), (down_out, hidden), (turn_ref, columns)):
        for begin, source, part in spans:
            low, high = max(begin, goal), min(begin + source.shape[1], goal + count)
            if low < high:
                pieces.append(
                    (source.at[part, pl.ds(low - begin, high - low)], target.at[pl.ds(low - goal, high - low)])
                )
        goal += count
    copies = [pltpu.make_async_copy(source, target, sems.at[number]) for number, (source, target) in enumerate(pieces)]
    for copy in copies:
        copy.start()
    window = pl.ds(pl.multiple_of(member * rows, 128), rows)
    first_gain_out[...] = sums_ref[0:1, window]
    second_gain_out[...] = sums_ref[8:9, window]
    head_gain_out[...] = sums_ref[1:2, :CHUNK]
    width = sums_ref.shape[1]
    for kind in range(3):
        for tap in range(4):
            flat = (3 * tap + kind) * columns
            line, lane = 9 + flat // width, flat % width
            conv_out[kind, tap : tap + 1] = sums_ref[line : line + 1, lane : lane + columns]
    for copy in copies:
        copy.wait()
    output_out[...] = turn_ref[...].T
    beta_out[...] = strip_ref[...].T[: beta_out.shape[0]]


def finish_stage(block, ingrad, piece, sums, first, second, third, hidden, heads):
    tokens, columns = ingrad.shape
    rows = piece.shape[0]
    whole, outside = pl.BlockSpec(memory_space=pltpu.VMEM), pl.BlockSpec(memory_space=pl.ANY)

    def made(*shape):
        return jax.ShapeDtypeStruct(shape, F32)

    return pl.pallas_call(
        functools.partial(finish_kernel, hidden),
        name="finish",
        out_shape=(
            jax.ShapeDtypeStruct((tokens, columns), BF),
            made(tokens, columns),
            made(1, rows),
            made(rows, columns),
            made(rows, columns),
            made(rows, columns),
            made(heads, rows),
            made(3, 4, columns),
            made(1, CHUNK),
            made(rows, columns),
            made(1, rows),
            made(hidden, rows),
            made(hidden, rows),
            made(hidden, rows),
        ),
        in_specs=[whole] * 7,
        out_specs=(outside,) * 2
        + (whole,)
        + (outside,) * 3
        + (whole,) * 5
        + (outside,) * 3,
        scratch_shapes=[
            pltpu.VMEM((columns, rows), F32),
            pltpu.VMEM((rows, CHUNK), F32),
            pltpu.SemaphoreType.DMA((24,)),
        ],
        compiler_params=pltpu.CompilerParams(vmem_limit_bytes=VMEM_LIMIT),
        cost_estimate=pl.CostEstimate(flops=0, bytes_accessed=12 << 20, transcendentals=0),
    )(block, ingrad, piece, sums, first, second, third)
def turn_column(column):
    diagonal = lax.broadcasted_iota(jnp.int32, (128, 128), 0) == lax.broadcasted_iota(jnp.int32, (128, 128), 1)
    lines = []
    for block in range(column.shape[0] // 128):
        lines.append(jnp.sum(jnp.where(diagonal, column[block * 128 : (block + 1) * 128], 0.0), 0, keepdims=True))
    return jnp.concatenate(lines, 1)


def piece_gather(full_ref, send, recv, members):
    member = lax.axis_index("seq")
    parts = full_ref.shape[0]
    stages = (members - 1).bit_length()

    def give(part, r, stage):
        owner = flip(member, r)
        mark = r ^ (1 << stage)
        return push(
            full_ref.at[part, owner],
            full_ref.at[part, owner],
            send.at[part, mark],
            recv.at[part, mark],
            "seq",
            flip(member, 1 << stage),
        )

    def take(part, r):
        owner = flip(member, r)
        return push(
            full_ref.at[part, owner],
            full_ref.at[part, owner],
            send.at[part, r],
            recv.at[part, r],
            "seq",
            flip(member, r & -r),
        )

    def begin(part=0, levels=None):
        for stage in reversed(range(stages)) if levels is None else levels:
            give(part, 0, stage).start()

    def relay(part, r):
        take(part, r).wait_recv()
        for stage in reversed(range(zeros_below(r))):
            give(part, r, stage).start()
        if r == 1 << (stages - 1) and part + 1 < parts:
            begin(part + 1)

    order = sorted([r for r in range(1, members) if r % 2 == 0], key=lambda r: (-zeros_below(r), r))
    def when(part, r):
        return 2 * part + 3 * (bin(r).count("1") - 1), part, -zeros_below(r), r

    relays = sorted([(part, r) for r in order for part in range(parts)], key=lambda job: when(*job))

    def arrive():
        for part in range(parts):
            for r in range(1, members, 2):
                take(part, r).wait_recv()

    def finish():
        for part in range(parts):
            for r in [0] + order:
                for stage in range(zeros_below(r) if r else stages):
                    give(part, r, stage).wait_send()

    return begin, relay, relays, arrive, finish


def greet_seq(members):
    member = lax.axis_index("seq")
    stages = (members - 1).bit_length()
    barrier = pltpu.get_barrier_semaphore()
    for stage in range(stages):
        pl.semaphore_signal(barrier, inc=1, device_id={"seq": flip(member, 1 << stage)}, device_id_type=MESH)
    return barrier, stages


FRONT_REFS = 64


def front_kernel(
    members,
    heads,
    lengths_ref,
    input_ref,
    query_ref,
    key_ref,
    value_ref,
    beta_ref,
    first_gain_ref,
    second_gain_ref,
    out_weight_ref,
    conv_ref,
    head_gain_ref,
    *refs,
):
    own_refs, refs = refs[:-FRONT_REFS], refs[-FRONT_REFS:]
    front_body(
        members,
        heads,
        lengths_ref,
        input_ref,
        query_ref,
        key_ref,
        value_ref,
        beta_ref,
        first_gain_ref,
        second_gain_ref,
        out_weight_ref,
        conv_ref,
        head_gain_ref,
        own_refs,
        *refs,
    )


def front_body(
    members,
    heads,
    lengths_ref,
    input_ref,
    query_ref,
    key_ref,
    value_ref,
    beta_ref,
    first_gain_ref,
    second_gain_ref,
    out_weight_ref,
    conv_ref,
    head_gain_ref,
    own_refs,
    pack_hbm,
    first_hbm,
    pre_hbm,
    logits_hbm,
    halo_ref,
    scale_hbm,
    gains_ref,
    turned_hbm,
    full_hbm,
    others_hbm,
    qkv_hbm,
    inv_hbm,
    wu_hbm,
    mq_hbm,
    total_ref,
    delta_hbm,
    rows_hbm,
    far_rows_hbm,
    states_hbm,
    pack_ref,
    first_ref,
    pre_ref,
    logits_ref,
    scale_ref,
    turned_ref,
    full_ref,
    others_ref,
    qkv_ref,
    inv_ref,
    wu_ref,
    mq_ref,
    delta_ref,
    rows_ref,
    far_rows_ref,
    states_ref,
    store_sem,
    resets_ref,
    taps_ref,
    extra_ref,
    start_ref,
    out0_ref,
    state_ref,
    part_ref,
    slots_ref,
    pad_ref,
    edge_ref,
    pack_send,
    pack_recv,
    edge_send,
    edge_recv,
    turned_send,
    turned_recv,
    full_send,
    full_recv,
    head_send,
    head_recv,
    state_send,
    state_recv,
    row_near_send,
    row_near_recv,
    row_far_send,
    row_far_recv,
    row_pass_send,
    row_pass_recv,
):
    tokens, width = input_ref.shape
    columns = heads * CHUNK
    leaving = (
        (pack_ref, pack_hbm),
        (first_ref, first_hbm),
        (pre_ref, pre_hbm),
        (logits_ref, logits_hbm),
        (scale_ref, scale_hbm),
        (turned_ref, turned_hbm),
        (qkv_ref, qkv_hbm),
        (inv_ref, inv_hbm),
        (wu_ref, wu_hbm),
        (mq_ref, mq_hbm),
        (delta_ref, delta_hbm),
        (rows_ref, rows_hbm),
        (states_ref, states_hbm),
        (others_ref, others_hbm),
        (far_rows_ref, far_rows_hbm),
        (full_ref, full_hbm),
    )

    def store(number):
        return pltpu.make_async_copy(*leaving[number], store_sem.at[number])

    member = lax.axis_index("seq")
    _, _, near, far = head_peers()
    barrier, stages = greet_seq(members)
    for target in (near, far):
        pl.semaphore_signal(barrier, inc=1, device_id={"head": target}, device_id_type=MESH)

    @pl.when(member > 0)
    def _():
        pl.semaphore_signal(barrier, inc=1, device_id={"seq": member - 1}, device_id_type=MESH)

    window = slots_ref.shape[0]
    behind = members - 1 - member
    for hop in range(1, window + 1):

        @pl.when(member >= hop)
        def _():
            pl.semaphore_signal(barrier, inc=1, device_id={"seq": member - hop}, device_id_type=MESH)

    def state_copy(hop):
        return push(
            part_ref, slots_ref.at[hop - 1], state_send.at[hop - 1], state_recv.at[hop - 1], "seq", member + hop
        )

    pack_ref[0, member, :, :columns] = query_ref[...]
    pack_ref[0, member, :, columns : 2 * columns] = key_ref[...]
    pack_ref[0, member, :, 2 * columns : 3 * columns] = value_ref[...]
    extra_ref[...] = jnp.zeros_like(extra_ref)
    extra_ref[0:heads] = beta_ref[...].astype(F32)
    extra_ref[heads : heads + 1] = first_gain_ref[...].astype(F32)
    extra_ref[heads + 1 : heads + 2] = second_gain_ref[...].astype(F32)
    pack_ref[0, member, :, 3 * columns :] = extra_ref[...].T.astype(BF)
    turned_ref[0, member] = out_weight_ref[...].T
    for part, own_ref in enumerate(own_refs):
        full_ref[part, member] = own_ref[...]
    pack = piece_gather(pack_ref, pack_send, pack_recv, members)
    turned = piece_gather(turned_ref, turned_send, turned_recv, members)
    full = piece_gather(full_ref, full_send, full_recv, members)
    near_copy = push(turned_ref.at[0], others_ref.at[0], head_send.at[0], head_recv.at[0], "head", near)
    far_copy = push(turned_ref.at[0], others_ref.at[1], head_send.at[1], head_recv.at[1], "head", far)
    pass_copy = push(others_ref.at[1], others_ref.at[2], head_send.at[2], head_recv.at[2], "head", near)
    pl.semaphore_wait(barrier, stages + 2 + jnp.minimum(behind, 1) + jnp.minimum(behind, window))
    pack[0]()
    fill_resets(lengths_ref, resets_ref, tokens)
    fill_taps(conv_ref, taps_ref)

    last_rows = pl.ds(tokens - 16, 16)

    def edge(target):
        return push(input_ref.at[last_rows], edge_ref, edge_send, edge_recv, "seq", target)

    @pl.when(member + 1 < members)
    def _():
        edge(member + 1).start()

    chunk = 256

    def at(index):
        return pl.ds(pl.multiple_of(index * chunk, chunk), chunk)

    def measure(index):
        block = input_ref[at(index)].astype(F32)
        scale_ref[at(index)] = lax.rsqrt(jnp.mean(block * block, axis=-1, keepdims=True) + 1e-06)

    pl.loop(0, tokens // chunk)(measure)
    for job in pack[2]:
        pack[1](*job)
    full[0](0)
    turned[0]()
    pack[3]()
    projection = pack_ref[0].reshape(width, pack_ref.shape[3])
    extras = projection[:, 3 * columns :].astype(F32)
    gains_ref[0:1] = turn_column(extras[:, heads : heads + 1])
    gains_ref[1:2] = turn_column(extras[:, heads + 1 : heads + 2])

    def project(index):
        first = (input_ref[at(index)].astype(F32) * scale_ref[at(index)] * gains_ref[0:1]).astype(BF)
        first_ref[at(index)] = first
        both = nn(first, pack_ref[0].reshape(width, pack_ref.shape[3]))
        pre_ref[at(index)] = both[:, : 3 * columns].astype(BF)
        logits_ref[at(index)] = both[:, 3 * columns :]

    pl.loop(0, tokens // chunk)(project)

    @pl.when(member == 0)
    def _():
        halo_ref[...] = jnp.zeros_like(halo_ref)

    @pl.when(member > 0)
    def _():
        edge(member).wait_recv()
        block = edge_ref[...].astype(F32)
        scale = lax.rsqrt(jnp.mean(block * block, axis=-1, keepdims=True) + 1e-06)
        first = (block * scale * gains_ref[0:1]).astype(BF)
        halo_ref[...] = nn(first, pack_ref[0].reshape(width, pack_ref.shape[3])[:, : 3 * columns]).astype(BF)

    for number in range(5):
        store(number).start()
    rows, cols = grid_indices()
    eye = jnp.where(rows == cols, 1.0, 0.0)
    top = lax.broadcasted_iota(jnp.int32, (CHUNK, 1), 0) < GROUP
    for head in range(heads):
        total_ref[head] = side(eye, jnp.zeros_like(eye))
    batch = pad_ref.shape[0]

    def one(step, carry):
        units = []
        for lane in range(batch):
            chunk = step * batch + lane
            pad = pad_ref.at[lane]
            load_padded(pad, pre_ref, halo_ref, chunk, resets_ref)
            mixed = convolve(pad, taps_ref)
            silued = mixed * sigmoid(mixed)
            keep0 = 1.0 - resets_ref[2 * chunk]
            keep1 = 1.0 - resets_ref[2 * chunk + 1]
            both = keep0 * keep1
            enter = jnp.where(top, keep0, both)
            leave = jnp.where(top, keep1, 1.0)
            at = pl.ds(pl.multiple_of(chunk * CHUNK, CHUNK), CHUNK)
            beta_rows = sigmoid(logits_ref[at, :])
            for head in range(heads):
                window = slice(head * CHUNK, (head + 1) * CHUNK)
                parts = []
                for kind in range(3):
                    part = silued[:, kind * columns + head * CHUNK : kind * columns + (head + 1) * CHUNK]
                    if kind < 2:
                        part = part * lax.rsqrt(jnp.sum(part * part, axis=-1, keepdims=True) + 1e-06)
                    part = part.astype(BF)
                    qkv_ref[at, kind * columns + head * CHUNK : kind * columns + (head + 1) * CHUNK] = part
                    parts.append(part)
                units.append((chunk, head, *parts, beta_rows[:, head : head + 1], keep1, both, enter, leave))
        turned = [u[3].T for u in units]
        strict = [
            jnp.where(rows > cols, u[5] * nn(u[3], t), 0.0) for u, t in zip(units, turned)
        ]
        inverses = [r.astype(BF) for r in inverse_levels(strict, rows, cols, [u[6] for u in units])]
        factors = []
        for u, inverse in zip(units, inverses):
            beta = u[5]
            factors.append(nn(inverse, side(u[3].astype(F32) * beta, u[4].astype(F32) * beta)))
        for u, inverse, factor, t in zip(units, inverses, factors, turned):
            chunk, head, query, key, value, beta, keep1, both, enter, leave = u
            weight, update = factor[:, :CHUNK], factor[:, CHUNK:]
            entering_weight = weight * enter
            inv_ref[chunk, head] = inverse
            wu_ref[chunk, head] = side(entering_weight, update).astype(BF)
            gathered = nn(t, side(weight, update * leave))
            device_map = (both * (eye - gathered[:, :CHUNK])).astype(BF)
            shift = gathered[:, CHUNK:]
            scores = jnp.where(rows >= cols, nn(query, t), 0.0)
            scores = jnp.where((rows >= GROUP) & (cols < GROUP), scores * keep1, scores)
            seen = nn(scores, side(entering_weight, update))
            effective = query.astype(F32) * enter - seen[:, :CHUNK]
            mq_ref[chunk, head] = stack(device_map, effective.astype(BF))
            out0_ref[chunk, head] = seen[:, CHUNK:]
            running = total_ref[head]
            start_ref[chunk, head] = running.astype(BF)
            total_ref[head] = nn(device_map, running) + side(jnp.zeros_like(shift), shift)
        return carry

    count = resets_ref.shape[0] // 2 // batch
    held = 4 if len(full[2]) > 4 else 0
    relays = full[2][: len(full[2]) - held]

    def pumped(step, carry):
        carry = one(step, carry)
        for turn in range(count):
            jobs = [job for place, job in enumerate(relays) if place * count // len(relays) == turn]
            if not jobs and turn not in (0, 2, count - 2):
                continue

            @pl.when(step == turn)
            def _():
                if turn == 0:
                    for job in turned[2]:
                        turned[1](*job)
                for job in jobs:
                    full[1](*job)
                if turn == 2:
                    turned[3]()
                    store(5).start()
                    near_copy.start()
                    far_copy.start()
                if turn == count - 2:
                    far_copy.wait_recv()
                    pass_copy.start()

        return carry

    lax.fori_loop(0, count, pumped, 0)
    for number in range(6, 10):
        store(number).start()
    part_ref[...] = total_ref[...].astype(BF)
    for hop in range(1, window + 1):

        @pl.when(behind >= hop)
        def _():
            state_copy(hop).start()

    for job in full[2][len(full[2]) - held :]:
        full[1](*job)
    state_ref[...] = jnp.zeros_like(state_ref)
    for hop in range(window, 0, -1):

        @pl.when(member >= hop)
        def _():
            state_copy(hop).wait_recv()
            for head in range(heads):
                part = slots_ref[hop - 1, head]
                state_ref[head] = nn(part[:, :CHUNK], state_ref[head]) + part[:, CHUNK:].astype(F32)

    def near_rows(index):
        return push(
            rows_ref.at[at(index)], far_rows_ref.at[0, at(index)], row_near_send.at[index], row_near_recv.at[index], "head", near
        )

    def far_rows(index):
        return push(
            rows_ref.at[at(index)], far_rows_ref.at[1, at(index)], row_far_send.at[index], row_far_recv.at[index], "head", far
        )

    def pass_rows(index):
        return push(
            far_rows_ref.at[1, at(index)], far_rows_ref.at[2, at(index)], row_pass_send.at[index], row_pass_recv.at[index], "head", near
        )

    def finished(index):
        for lane in range(chunk // CHUNK):
            place_ = index * (chunk // CHUNK) + lane
            rows_at = pl.ds(pl.multiple_of(place_ * CHUNK, CHUNK), CHUNK)
            begins = [start_ref[place_, head] for head in range(heads)]
            states = [
                (nn(begins[head][:, :CHUNK], state_ref[head]) + begins[head][:, CHUNK:].astype(F32)).astype(BF)
                for head in range(heads)
            ]
            outs = [out0_ref[place_, head] + nn(mq_ref[place_, head, CHUNK:], states[head]) for head in range(heads)]
            for head in range(heads):
                lanes = slice(head * CHUNK, (head + 1) * CHUNK)
                states_ref[place_, head] = states[head]
                delta_ref[rows_at, lanes] = outs[head]
                scale = lax.rsqrt(jnp.mean(outs[head] * outs[head], axis=-1, keepdims=True) + 1e-05)
                rows_ref[rows_at, lanes] = (outs[head] * scale * head_gain_ref[...]).astype(BF)

    sent = far_rows_ref.shape[1] // chunk

    def finished_and_sent(index):
        finished(index)
        far_rows(index).start()
        near_rows(index).start()

    pl.loop(0, sent)(finished_and_sent)
    pl.loop(sent, tokens // chunk)(finished)
    for number in range(10, 13):
        store(number).start()

    @pl.loop(0, sent)
    def _(index):
        far_rows(index).wait_recv()
        pass_rows(index).start()

    near_copy.wait()
    far_copy.wait_send()
    pass_copy.wait()
    store(13).start()

    @pl.when(member + 1 < members)
    def _():
        edge(member + 1).wait_send()

    for hop in range(1, window + 1):

        @pl.when(behind >= hop)
        def _():
            state_copy(hop).wait_send()

    @pl.loop(0, sent)
    def _(index):
        near_rows(index).wait()
        far_rows(index).wait_send()
        pass_rows(index).wait()

    store(14).start()
    full[3]()
    store(15).start()
    for gather in (pack, turned, full):
        gather[4]()
    for number in range(len(leaving)):
        store(number).wait()


def front_stage(lengths, inputs, mixer_weights, conv, head_gain, own, members, heads, collective):
    tokens, width = inputs.shape
    columns = heads * CHUNK
    chunks = tokens // CHUNK
    whole = pl.BlockSpec(memory_space=pltpu.VMEM)
    piece = width // members
    window = min(members - 1, members // 2)

    def units(wide, kind):
        return jax.ShapeDtypeStruct((chunks, heads, *wide), kind)

    def dma(*shape):
        return [pltpu.SemaphoreType.DMA(shape)] * 2

    outside = pl.BlockSpec(memory_space=pl.ANY)
    made = (
        jax.ShapeDtypeStruct((1, members, piece, 3 * columns + CHUNK), BF),
        jax.ShapeDtypeStruct((tokens, width), BF),
        jax.ShapeDtypeStruct((tokens, 3 * columns), BF),
        jax.ShapeDtypeStruct((tokens, CHUNK), F32),
        jax.ShapeDtypeStruct((16, 3 * columns), BF),
        jax.ShapeDtypeStruct((tokens, 1), F32),
        jax.ShapeDtypeStruct((2, width), F32),
        jax.ShapeDtypeStruct((1, members, columns, piece), BF),
        jax.ShapeDtypeStruct((len(own), members, *own[0].shape), BF),
        jax.ShapeDtypeStruct((3, members, columns, piece), BF),
        jax.ShapeDtypeStruct((tokens, 3 * columns), BF),
        units((CHUNK, CHUNK), BF),
        units((CHUNK, 2 * CHUNK), BF),
        units((2 * CHUNK, CHUNK), BF),
        jax.ShapeDtypeStruct((heads, CHUNK, 2 * CHUNK), F32),
        jax.ShapeDtypeStruct((tokens, columns), F32),
        jax.ShapeDtypeStruct((tokens, columns), BF),
        jax.ShapeDtypeStruct((3, tokens // 2, columns), BF),
        units((CHUNK, CHUNK), BF),
    )
    stay = (4, 6, 14)
    return pl.pallas_call(
        functools.partial(front_kernel, members, heads),
        name="front",
        out_shape=made,
        in_specs=[pl.BlockSpec(memory_space=pltpu.SMEM)] + [whole] * (3 + len(mixer_weights) + len(own)),
        out_specs=tuple(whole if number in stay else outside for number in range(len(made))),
        scratch_shapes=[pltpu.VMEM(a.shape, a.dtype) for number, a in enumerate(made) if number not in stay]
        + [
            pltpu.SemaphoreType.DMA((len(made) - len(stay),)),
            pltpu.SMEM((tokens // GROUP,), F32),
            pltpu.VMEM((4, 3 * columns), F32),
            pltpu.VMEM((CHUNK, piece), F32),
            pltpu.VMEM((chunks, heads, CHUNK, 2 * CHUNK), BF),
            pltpu.VMEM((chunks, heads, CHUNK, CHUNK), F32),
            pltpu.VMEM((heads, CHUNK, CHUNK), F32),
            pltpu.VMEM((heads, CHUNK, 2 * CHUNK), BF),
            pltpu.VMEM((window, heads, CHUNK, 2 * CHUNK), BF),
            pltpu.VMEM((2, 144, 3 * columns), F32),
            pltpu.VMEM((16, width), BF),
        ]
        + dma(1, members)
        + dma()
        + dma(1, members)
        + dma(len(own), members)
        + dma(3)
        + dma(window)
        + dma(tokens // 256) * 3,
        compiler_params=pltpu.CompilerParams(
            collective_id=collective, has_side_effects=True, vmem_limit_bytes=VMEM_LIMIT
        ),
        cost_estimate=pl.CostEstimate(flops=8 * 10**9, bytes_accessed=40 << 20, transcendentals=2 << 20),
    )(lengths, inputs, *mixer_weights, conv, head_gain, *own)


def lanes_whole(pieces):
    places, rows, piece = pieces.shape
    if piece >= 128:
        return pieces
    group = 128 // piece
    return pieces.reshape(places // group, group, rows, piece).transpose(0, 2, 1, 3).reshape(places // group, rows, 128)


def lanes_split(blocks, piece):
    count, rows, lanes = blocks.shape
    if piece >= 128:
        return blocks
    group = 128 // piece
    return blocks.reshape(count, rows, group, piece).transpose(0, 2, 1, 3).reshape(count * group, rows, piece)


def body(
    block_input,
    first_gain,
    query_weight,
    key_weight,
    value_weight,
    beta_weight,
    conv_weight,
    head_gain,
    output_weight,
    second_gain,
    gate_weight,
    up_weight,
    down_weight,
    lengths,
    cotangent,
):
    tokens, width = block_input.shape
    heads = beta_weight.shape[1]
    columns = query_weight.shape[1]
    hidden_columns = gate_weight.shape[1]
    members = lax.axis_size("seq")
    piece = width // members
    seq_place = lax.axis_index("seq")

    gain_head = head_gain.astype(F32)[None, :]
    own = [gate_weight.T, up_weight.T, down_weight.T]
    split = piece < 128
    (
        mixer_pack,
        first_rows,
        pre,
        logits,
        halo,
        scale_one,
        gains,
        turned,
        full,
        others,
        qkv,
        inv,
        wu,
        mq,
        total,
        delta,
        head_rows,
        far_rows,
        states,
    ) = front_stage(
        lengths,
        block_input,
        (
            query_weight,
            key_weight,
            value_weight,
            beta_weight.T,
            first_gain[None, :],
            second_gain[None, :],
            output_weight,
        ),
        conv_weight,
        gain_head,
        [own[0][:16]] if split else own,
        members,
        heads,
        5,
    )
    mixer_pack = mixer_pack.reshape(width, -1)
    if split:
        gathered = lax.all_gather(jnp.stack(own), "seq", axis=1)
        full = jnp.stack([lanes_whole(gathered[i]) for i in range(3)])
    turned = lanes_whole(turned[0])
    others = jnp.stack([lanes_whole(others[i]) for i in range(3)]) if split else others
    d_heads, update_part, middle_shard, d_middle_shard, *grads, second_grad = middle_stage(
        head_rows, far_rows, full, turned, others, block_input, cotangent, gains, 2
    )
    second_part = jnp.sum(second_grad, 0)
    if split:
        pieces = jnp.concatenate([part for pair in grads for part in pair], 1)
        whole_sum = lax.psum_scatter(lanes_split(pieces, piece), "seq", scatter_dimension=0, tiled=False).astype(F32)
        grads = [jnp.zeros((1, members, 16, 128), BF)] * 3
    ddelta, gain_part, arrive, block_output, third_sum = state_backward(
        d_heads, delta, gain_head, mq, total, update_part, middle_shard, grads[2], members, 1
    )
    d_pre, taps_part, first_sum = mixer_backward(
        lengths, pre, halo, conv_weight, logits, qkv, inv, wu, mq, states, ddelta, arrive, grads[0], 3
    )
    input_gradient, mixer_sum, sums, second_sum = final_stage(
        first_rows, d_pre, mixer_pack, block_input, scale_one, gains, d_middle_shard, (gain_part, second_grad, taps_part), grads[1], members, 4
    )
    if not split:
        done = finish_stage(
            block_output, input_gradient, mixer_sum, sums, first_sum, second_sum, third_sum, hidden_columns, heads
        )
        block, ingrad, gain_1, grad_q, grad_k, grad_v, grad_b, grad_c, gain_h, grad_o, gain_2, *rest = done
        return (
            block,
            ingrad,
            gain_1.reshape(-1),
            grad_q,
            grad_k,
            grad_v,
            grad_b.T,
            grad_c,
            gain_h.reshape(-1),
            grad_o,
            gain_2.reshape(-1),
            *(grad.T for grad in rest),
        )
    gain_sum = sums[1, :CHUNK]
    conv_gradient = sums[9 : 9 + 12 * columns // width].reshape(4, 3, columns).transpose(1, 0, 2)
    row_start = seq_place * piece
    first_gradient = lax.dynamic_slice_in_dim(sums[0], row_start, piece, 0)
    second_gradient = lax.dynamic_slice_in_dim(sums[8], row_start, piece, 0)
    beta_gradient = mixer_sum[:, 3 * columns : 3 * columns + heads]
    return (
        block_output,
        input_gradient,
        first_gradient,
        mixer_sum[:, :columns],
        mixer_sum[:, columns : 2 * columns],
        mixer_sum[:, 2 * columns : 3 * columns],
        beta_gradient,
        conv_gradient,
        gain_sum,
        whole_sum[3 * hidden_columns :].T,
        second_gradient,
        whole_sum[:hidden_columns].T,
        whole_sum[hidden_columns : 2 * hidden_columns].T,
        whole_sum[2 * hidden_columns : 3 * hidden_columns].T,
    )


def solution(mesh):
    return jax.shard_map(
        body,
        mesh=mesh,
        in_specs=(
            P("seq", None),
            P("seq"),
            P("seq", "head"),
            P("seq", "head"),
            P("seq", "head"),
            P("seq", "head"),
            P(None, None, "head"),
            P(),
            P("seq", "head"),
            P("seq"),
            P("seq", "head"),
            P("seq", "head"),
            P("seq", "head"),
            P(),
            P("seq", None),
        ),
        out_specs=(
            P("seq", "head"),
            P("seq", "head"),
            P("seq"),
            P("seq", "head"),
            P("seq", "head"),
            P("seq", "head"),
            P("seq", "head"),
            P(None, None, "head"),
            P(),
            P("seq", "head"),
            P("seq"),
            P("seq", "head"),
            P("seq", "head"),
            P("seq", "head"),
        ),
        check_vma=False,
    )
```

```python
import functools

import jax
import jax.numpy as jnp
from jax import lax
from jax.experimental import pallas as pl
from jax.experimental.pallas import tpu as pltpu
from jax.sharding import PartitionSpec as P

GROUP = 64
CHUNK = 128
MESH = pl.DeviceIdType.MESH
BF = jnp.bfloat16
F32 = jnp.float32
VMEM_LIMIT = 59 << 20


def nn(left, right):
    return jnp.dot(left.astype(BF), right.astype(BF), preferred_element_type=F32)


def tn(left, right):
    return lax.dot_general(
        left.astype(BF), right.astype(BF), (((0,), (0,)), ((), ())), preferred_element_type=F32
    )


def nt(left, right):
    return lax.dot_general(
        left.astype(BF), right.astype(BF), (((1,), (1,)), ((), ())), preferred_element_type=F32
    )


def sigmoid(v):
    return 0.5 * jnp.tanh(0.5 * v) + 0.5


def side(left, right):
    return jnp.concatenate([left, right], 1)


def stack(top, bottom):
    return jnp.concatenate([top, bottom], 0)


def grid_indices():
    rows = lax.broadcasted_iota(jnp.int32, (CHUNK, CHUNK), 0)
    cols = lax.broadcasted_iota(jnp.int32, (CHUNK, CHUNK), 1)
    return rows, cols


def fill_resets(lengths_ref, resets_ref, tokens):
    base = lax.axis_index("seq") * tokens

    @pl.loop(0, tokens // GROUP)
    def _(block):
        position = base + block * GROUP
        value = jnp.float32(0.0)
        start = jnp.int32(0)
        for index in range(lengths_ref.shape[0]):
            value = jnp.where(start == position, 1.0, value)
            start = start + lengths_ref[index]
        resets_ref[block] = value


def fill_taps(conv_ref, taps_ref):
    columns = conv_ref.shape[2]
    for kind in range(3):
        taps_ref[:, kind * columns : (kind + 1) * columns] = conv_ref[kind].astype(F32)


def load_padded(pad_ref, pre_ref, halo_ref, chunk, resets_ref):
    start = pl.multiple_of(chunk * CHUNK, CHUNK)
    before = pl.multiple_of(jnp.maximum(start - 16, 0), 16)
    own = pre_ref[pl.ds(start, CHUNK), :].astype(F32)
    earlier = pre_ref[pl.ds(before, 16), :].astype(F32)[8:]
    halo = halo_ref[...].astype(F32)[8:]
    first = jnp.where(chunk == 0, halo, earlier)
    keep0 = 1.0 - resets_ref[2 * chunk]
    keep1 = 1.0 - resets_ref[2 * chunk + 1]
    pad_ref[0:8] = first * keep0
    pad_ref[8:72] = own[:GROUP]
    pad_ref[72:80] = own[GROUP - 8 : GROUP] * keep1
    pad_ref[80:144] = own[GROUP:]


def tap_rows(pad_ref, tap):
    return stack(pad_ref[5 + tap : 69 + tap], pad_ref[77 + tap : 141 + tap])


def convolve(pad_ref, taps_ref):
    mixed = None
    for tap in range(4):
        term = taps_ref[tap : tap + 1] * tap_rows(pad_ref, tap)
        mixed = term if mixed is None else mixed + term
    return mixed


def inverse_levels(strict, rows, cols, keep1):
    eye = jnp.where(rows == cols, 1.0, 0.0)
    pair = (rows // 2) == (cols // 2)
    results = [eye - jnp.where(pair, a, 0.0) for a in strict]
    width = 2
    while width < CHUNK:
        off = ((rows // (2 * width)) == (cols // (2 * width))) & ((rows // width) != (cols // width))
        lows = [r.astype(BF) for r in results]
        parts = [jnp.where(off, a, 0.0).astype(BF) for a in strict]
        if width == GROUP:
            parts = [jnp.where(off, a * k, 0.0).astype(BF) for a, k in zip(strict, keep1)]
        steps = [nn(r, p) for r, p in zip(lows, parts)]
        results = [r - nn(s, low) for r, s, low in zip(results, steps, lows)]
        width *= 2
    return results


def state_backward_kernel(
    heads,
    window,
    dheads_ref,
    delta_ref,
    gain_ref,
    mq_ref,
    total_ref,
    update_ref,
    mid_ref,
    grads_ref,
    ddelta_ref,
    gain_grad_ref,
    state_ref,
    block_ref,
    sum_ref,
    shift_ref,
    part_ref,
    slots_ref,
    send_sem,
    recv_sem,
    near_ref,
    relay_ref,
    far_ref,
    near_send,
    near_recv,
    far_send,
    far_recv,
    piece_relay,
    piece_slots,
    piece_send,
    piece_recv,
):
    member, members = lax.axis_index("seq"), lax.axis_size("seq")
    _, _, near, far = head_peers()
    chunk = 256
    steps = update_ref.shape[0] // chunk
    chunks = mq_ref.shape[0]
    behind = members - 1 - member
    at, _, start_pair, pass_on, own_sum, finish = head_scatter_copies(
        chunk, update_ref, near_ref, relay_ref, far_ref, (near_send, near_recv, far_send, far_recv)
    )
    begin, receive, jobs, end = piece_scatter(
        grads_ref, piece_relay, piece_slots, sum_ref, piece_send, piece_recv, members
    )
    barrier, stages = greet_seq(members)
    for hop in range(1, window + 1):

        @pl.when(behind >= hop)
        def _():
            pl.semaphore_signal(barrier, inc=1, device_id={"seq": member + hop}, device_id_type=MESH)

    for target in (near, far):
        pl.semaphore_signal(barrier, inc=1, device_id={"head": target}, device_id_type=MESH)
    pl.semaphore_wait(barrier, stages + 2 + jnp.minimum(member, window))

    @pl.loop(0, steps)
    def _(index):
        start_pair(index)

    for head in range(heads):
        part_ref[0, head] = total_ref[head, :, :CHUNK].T.astype(BF)

    def copy(kind, hop):
        return push(
            part_ref.at[kind],
            slots_ref.at[kind, hop - 1],
            send_sem.at[kind, hop - 1],
            recv_sem.at[kind, hop - 1],
            "seq",
            member - hop,
        )

    def send(kind):
        for hop in range(1, window + 1):

            @pl.when(member >= hop)
            def _():
                copy(kind, hop).start()

    send(0)
    half = len(jobs) // 4
    begin(jobs[:half])
    shift_ref[...] = jnp.zeros_like(shift_ref)
    gain_grad_ref[...] = jnp.zeros_like(gain_grad_ref)

    def one(step, carry):
        index = chunks - 1 - step
        rows = pl.ds(pl.multiple_of(index * CHUNK, CHUNK), CHUNK)
        for head in range(heads):
            lanes = slice(head * CHUNK, (head + 1) * CHUNK)
            out = delta_ref[rows, lanes]
            grad = dheads_ref[rows, lanes].astype(F32)
            scale = lax.rsqrt(jnp.mean(out * out, axis=-1, keepdims=True) + 1e-05)
            unit = out * scale
            gain_grad_ref[...] += jnp.sum((grad * unit).reshape(CHUNK // 8, 8, CHUNK), 0)
            scaled = grad * gain_ref[...].astype(F32)
            back = scale * (scaled - unit * jnp.mean(scaled * unit, axis=-1, keepdims=True))
            back = back.astype(BF)
            ddelta_ref[rows, lanes] = back
            shift_ref[head] = tn(mq_ref[index, head], stack(shift_ref[head].astype(BF), back))

        @pl.when(lax.rem(step, 2) == 1)
        def _():
            pass_on(lax.div(step, 2))

        return carry

    lax.fori_loop(0, chunks, one, 0)
    for head in range(heads):
        part_ref[1, head] = shift_ref[head].astype(BF)
    send(1)
    begin(jobs[half:])
    for job in jobs[: len(jobs) // 2]:
        receive(*job)
    state_ref[...] = jnp.zeros_like(state_ref)
    for hop in range(window, 0, -1):

        @pl.when(behind >= hop)
        def _():
            copy(0, hop).wait_recv()
            copy(1, hop).wait_recv()
            for head in range(heads):
                state_ref[head] = nn(slots_ref[0, hop - 1, head], state_ref[head]) + slots_ref[1, hop - 1, head].astype(F32)

    for job in jobs[len(jobs) // 2 :]:
        receive(*job)

    @pl.loop(0, steps)
    def _(index):
        block_ref[at(index)] = (mid_ref[at(index)] + own_sum(index)).astype(BF)
        finish(index)

    end()
    for hop in range(1, window + 1):

        @pl.when(member >= hop)
        def _():
            copy(0, hop).wait_send()
            copy(1, hop).wait_send()


def state_backward(dheads, delta, gain, mq, total, update, mid, grads, members, collective):
    chunks, heads = mq.shape[:2]
    tokens, columns = mid.shape
    window = min(members - 1, members // 2)
    whole = pl.BlockSpec(memory_space=pltpu.VMEM)
    parts, _, *piece = grads.shape
    return pl.pallas_call(
        functools.partial(state_backward_kernel, heads, window),
        name="state_backward",
        out_shape=(
            jax.ShapeDtypeStruct((tokens, columns), BF),
            jax.ShapeDtypeStruct((8, CHUNK), F32),
            jax.ShapeDtypeStruct((heads, CHUNK, CHUNK), F32),
            jax.ShapeDtypeStruct((tokens, columns), BF),
            jax.ShapeDtypeStruct((parts, *piece), F32),
        ),
        in_specs=[whole] * 8,
        out_specs=(whole,) * 5,
        scratch_shapes=[
            pltpu.VMEM((heads, CHUNK, CHUNK), F32),
            pltpu.VMEM((2, heads, CHUNK, CHUNK), BF),
            pltpu.VMEM((2, window, heads, CHUNK, CHUNK), BF),
            pltpu.SemaphoreType.DMA((2, window)),
            pltpu.SemaphoreType.DMA((2, window)),
        ]
        + head_scatter_scratch(tokens, columns, tokens // 256)
        + piece_scatter_scratch(parts, members, piece),
        compiler_params=pltpu.CompilerParams(
            collective_id=collective, has_side_effects=True, vmem_limit_bytes=VMEM_LIMIT
        ),
        cost_estimate=pl.CostEstimate(flops=10**9, bytes_accessed=30 << 20, transcendentals=0),
    )(dheads, delta, gain, mq, total, update, mid, grads)


def piece_scatter_scratch(parts, members, piece):
    return [
        pltpu.VMEM((parts, max(members // 2 - 1, 1), *piece), BF),
        pltpu.VMEM((parts, members - 1, *piece), BF),
        pltpu.SemaphoreType.DMA((parts, members)),
        pltpu.SemaphoreType.DMA((parts, members)),
    ]


def piece_scatter(own_ref, relay_ref, slots_ref, total_ref, send, recv, members):
    member = lax.axis_index("seq")
    parts = own_ref.shape[0]
    stages = (members - 1).bit_length()
    order = sorted(range(members), key=lambda r: zeros_below(r) if r else stages)
    levels = {r: list(range(zeros_below(r) if r else stages)) for r in order}
    events = {}
    for r in order:
        for stage in levels[r]:
            events[r, stage] = len(events)
    kept = [r for r in order if r and r % 2 == 0]

    def source(part, r):
        return own_ref.at[part, flip(member, r)] if r % 2 else relay_ref.at[part, kept.index(r)]

    def give(part, r):
        stage = zeros_below(r)
        slot = events[r ^ (1 << stage), stage]
        return push(
            source(part, r), slots_ref.at[part, slot], send.at[part, r], recv.at[part, slot], "seq", flip(member, 1 << stage)
        )

    def take(part, r, stage):
        slot = events[r, stage]
        return push(
            own_ref.at[part, flip(member, 1)], slots_ref.at[part, slot], send.at[part, 0], recv.at[part, slot], "seq", flip(member, 1 << stage)
        )

    jobs = [(part, r) for r in order if r % 2 == 0 for part in range(parts)]

    def begin(some=None):
        for part, r in jobs if some is None else some:
            give(part, r ^ 1).start()

    def receive(part, r):
        total = own_ref[part, flip(member, r)].astype(F32)
        for stage in levels[r]:
            take(part, r, stage).wait_recv()
            total = total + slots_ref[part, events[r, stage]].astype(F32)
        if r:
            relay_ref[part, kept.index(r)] = total.astype(BF)
            give(part, r).start()
        else:
            total_ref[part] = total

    def finish():
        for part in range(parts):
            for r in order:
                if r:
                    give(part, r).wait_send()

    return begin, receive, jobs, finish


def mixer_backward_kernel(
    heads,
    lengths_ref,
    pre_hbm,
    halo_ref,
    conv_ref,
    logits_hbm,
    qkv_hbm,
    inv_hbm,
    wu_hbm,
    mq_hbm,
    states_hbm,
    ddelta_hbm,
    arrive_ref,
    grads_ref,
    dpre_ref,
    taps_grad_ref,
    total_ref,
    pre_ref,
    logits_ref,
    qkv_ref,
    inv_ref,
    wu_ref,
    mq_ref,
    states_ref,
    ddelta_ref,
    load_sem,
    resets_ref,
    taps_ref,
    carry_ref,
    pad_ref,
    dpad_ref,
    tail_ref,
    lead_ref,
    edge_ref,
    send_sem,
    recv_sem,
    relay_ref,
    slots_ref,
    piece_send,
    piece_recv,
):
    member, members = lax.axis_index("seq"), lax.axis_size("seq")
    barrier, stages = greet_seq(members)
    begin, receive, order, finish = piece_scatter(
        grads_ref, relay_ref, slots_ref, total_ref, piece_send, piece_recv, members
    )

    @pl.when(member + 1 < members)
    def _():
        pl.semaphore_signal(barrier, inc=1, device_id={"seq": member + 1}, device_id_type=MESH)

    columns = heads * CHUNK
    chunks = mq_ref.shape[0]
    fill_resets(lengths_ref, resets_ref, pre_ref.shape[0])
    fill_taps(conv_ref, taps_ref)
    quarter = chunks // 4
    sources = (pre_hbm, logits_hbm, qkv_hbm, ddelta_hbm, inv_hbm, wu_hbm, mq_hbm, states_hbm)
    targets = (pre_ref, logits_ref, qkv_ref, ddelta_ref, inv_ref, wu_ref, mq_ref, states_ref)

    def load(number, turn):
        unit = CHUNK if number < 4 else 1
        reach = pl.ds((chunks - (turn + 1) * quarter) * unit, quarter * unit)
        return pltpu.make_async_copy(
            sources[number].at[reach], targets[number].at[reach], load_sem.at[number, turn]
        )

    for turn in range(4):
        for number in range(8):
            load(number, turn).start()
    load(0, 0).wait()
    rows, cols = grid_indices()
    top = lax.broadcasted_iota(jnp.int32, (CHUNK, 1), 0) < GROUP
    pl.semaphore_wait(barrier, stages + jnp.minimum(member, 1))
    begin()
    carry_ref[...] = arrive_ref[...]
    taps_grad_ref[...] = jnp.zeros_like(taps_grad_ref)
    dpad_ref[136:144] = jnp.zeros_like(dpad_ref[136:144])

    lanes_ = 2
    cross = (rows >= GROUP) & (cols < GROUP)
    columns_of = lax.broadcasted_iota(jnp.int32, (CHUNK, CHUNK), 1)

    def part(kind, head):
        return slice(kind * columns + head * CHUNK, kind * columns + (head + 1) * CHUNK)

    def one(step, carry):
        for turn in range(4):

            @pl.when(step * lanes_ == turn * quarter)
            def _():
                for number in range(1, 8):
                    load(number, turn).wait()
                if turn < 3:
                    load(0, turn + 1).wait()

        at, keep0, keep1, enter, leave, slope, silued, beta_rows, place = [], [], [], [], [], [], [], [], []
        for lane in range(lanes_):
            chunk = chunks - 1 - lanes_ * step - lane
            place.append(chunk)
            at.append(pl.ds(pl.multiple_of(chunk * CHUNK, CHUNK), CHUNK))
            keep0.append(1.0 - resets_ref[2 * chunk])
            keep1.append(1.0 - resets_ref[2 * chunk + 1])
            enter.append(jnp.where(top, keep0[lane], keep0[lane] * keep1[lane]))
            leave.append(jnp.where(top, keep1[lane], 1.0))
            load_padded(pad_ref.at[lane], pre_ref, halo_ref, chunk, resets_ref)
            mixed = convolve(pad_ref.at[lane], taps_ref)
            gate = sigmoid(mixed)
            slope.append(gate * (1.0 + mixed * (1.0 - gate)))
            silued.append(mixed * gate)
            beta_rows.append(sigmoid(logits_ref[at[lane], :]))

        units = [(lane, h) for lane in range(lanes_) for h in range(heads)]
        every = range(len(units))

        def masked(product, keep, u):
            lower = jnp.where(keep, product, 0.0)
            return jnp.where(cross, lower * keep1[units[u][0]], lower).astype(BF)

        query = [qkv_ref[at[l], part(0, h)] for l, h in units]
        key = [qkv_ref[at[l], part(1, h)] for l, h in units]
        value = [qkv_ref[at[l], part(2, h)] for l, h in units]
        key32 = [k.astype(F32) for k in key]
        beta = [beta_rows[l][:, h : h + 1] for l, h in units]
        inverse = [inv_ref[place[l], h] for l, h in units]
        factors = [wu_ref[place[l], h] for l, h in units]
        weight = [f[:, :CHUNK] for f in factors]
        update = [f[:, CHUNK:] for f in factors]
        state = [states_ref[place[l], h] for l, h in units]
        out_grad = [ddelta_ref[at[l], h * CHUNK : (h + 1) * CHUNK] for l, h in units]
        later = []
        carried = [carry_ref[h] for h in range(heads)]
        for u, (l, h) in enumerate(units):
            later.append(carried[h].astype(BF))
            carried[h] = tn(mq_ref[place[l], h], stack(later[u], out_grad[u]))
        scores = [masked(nt(query[u], key[u]), rows >= cols, u) for u in every]
        fresh = [(update[u].astype(F32) - nn(weight[u], state[u])).astype(BF) for u in every]
        fresh_low = [
            (tn(scores[u], out_grad[u]) + leave[units[u][0]] * nn(key[u], later[u])).astype(BF) for u in every
        ]
        score_grad = [masked(nt(out_grad[u], fresh[u]), rows >= cols, u) for u in every]
        through = [nt(stack(out_grad[u], fresh_low[u]), state[u]) for u in every]
        weight_grad = [(-enter[units[u][0]] * through[u][CHUNK:]).astype(BF) for u in every]
        back = [tn(inverse[u], side(weight_grad[u], fresh_low[u])) for u in every]
        query_grad = [enter[units[u][0]] * through[u][:CHUNK] + nn(score_grad[u], key[u]) for u in every]
        key_grad = [tn(score_grad[u], query[u]) + leave[units[u][0]] * nt(fresh[u], later[u]) for u in every]
        strict = [masked(-nt(back[u].astype(BF), factors[u]), rows > cols, u) for u in every]
        strict_key = [nn(strict[u], key[u]) for u in every]
        turned = [tn(strict[u], (beta[u] * key32[u]).astype(BF)) for u in every]
        for h in range(heads):
            carry_ref[h] = carried[h]
        value_grad, dlogits = [], []
        for u in every:
            yk, zv = back[u][:, :CHUNK], back[u][:, CHUNK:]
            both_key = yk + strict_key[u]
            key_grad[u] = key_grad[u] + beta[u] * both_key + turned[u]
            value_grad.append(beta[u] * zv)
            beta_grad = jnp.sum(both_key * key32[u] + zv * value[u].astype(F32), axis=-1, keepdims=True)
            dlogits.append(beta_grad * beta[u] * (1.0 - beta[u]))
        unit_grads = []
        for kind, grad in ((0, query_grad), (1, key_grad)):
            raw = [silued[l][:, part(kind, h)] for l, h in units]
            norm = [lax.rsqrt(jnp.sum(r * r, axis=-1, keepdims=True) + 1e-06) for r in raw]
            unit = [raw[u] * norm[u] for u in every]
            inner = [jnp.sum(unit[u] * grad[u], axis=-1, keepdims=True) for u in every]
            unit_grads.append([(grad[u] - unit[u] * inner[u]) * norm[u] for u in every])
        unit_grads.append(value_grad)
        for lane in range(lanes_):
            spread = jnp.zeros((CHUNK, CHUNK), F32)
            for head in range(heads):
                spread = jnp.where(columns_of == head, dlogits[lane * heads + head], spread)
            dpre_ref[at[lane], 3 * columns :] = spread.astype(BF)
            mine = [g[lane * heads + head] for g in unit_grads for head in range(heads)]
            dmixed = jnp.concatenate(mine, 1) * slope[lane]
            dpad_ref[0:GROUP] = dmixed[:GROUP]
            dpad_ref[GROUP : GROUP + 8] = dmixed[GROUP : GROUP + 8] * keep1[lane]
            dpad_ref[72 : 72 + GROUP] = dmixed[GROUP:]
            dpre = None
            for tap in range(4):
                reach = 3 - tap
                shifted = stack(dpad_ref[reach : reach + GROUP], dpad_ref[72 + reach : 72 + reach + GROUP])
                term = taps_ref[tap : tap + 1] * shifted
                dpre = term if dpre is None else dpre + term
                seen = (dmixed * tap_rows(pad_ref.at[lane], tap)).reshape(CHUNK // 8, 8, 3 * columns)
                taps_grad_ref[tap] += jnp.sum(seen, 0)
            dpre_ref[at[lane], : 3 * columns] = dpre.astype(BF)
            if lane == 0:

                @pl.when(step == 0)
                def _():
                    tail_ref[...] = dpre[CHUNK - 16 :]

            dpad_ref[136:144] = dmixed[:8] * keep0[lane]
        turns = chunks // lanes_
        for number, job in enumerate(order):

            @pl.when(step == (number + 1) * (turns - 1) // len(order))
            def _():
                receive(*job)

        return carry

    lax.fori_loop(0, chunks // lanes_, one, 0)
    index = lax.broadcasted_iota(jnp.int32, (8, 1), 0)
    lead = jnp.zeros((8, 3 * columns), F32)
    dpad_ref[0:128] = jnp.zeros_like(dpad_ref[0:128])
    dpad_ref[8:16] = dpad_ref[136:144]
    for tap in range(3):
        back = 3 - tap
        lead = lead + taps_ref[tap : tap + 1] * dpad_ref[back : back + 8]
    lead_ref[...] = lead

    def to_previous(target):
        return push(lead_ref, edge_ref, send_sem, recv_sem, "seq", target)

    @pl.when(member > 0)
    def _():
        to_previous(member - 1).start()

    @pl.when(member + 1 < members)
    def _():
        to_previous(member).wait_recv()
        last = pl.ds(dpre_ref.shape[0] - 16, 16)
        late = stack(tail_ref[0:8], tail_ref[8:16] + edge_ref[...])
        dpre_ref[last, : 3 * columns] = late.astype(BF)

    @pl.when(member > 0)
    def _():
        to_previous(member - 1).wait_send()

    finish()


def mixer_backward(lengths, pre, halo, conv, logits, qkv, inv, wu, mq, states, ddelta, arrive, grads, collective):
    chunks, heads = mq.shape[:2]
    tokens = chunks * CHUNK
    columns = heads * CHUNK
    parts, members = grads.shape[:2]
    piece = grads.shape[2:]
    whole, outside = pl.BlockSpec(memory_space=pltpu.VMEM), pl.BlockSpec(memory_space=pl.ANY)
    streamed = (pre, logits, qkv, inv, wu, mq, states, ddelta)
    return pl.pallas_call(
        functools.partial(mixer_backward_kernel, heads),
        name="mixer_backward",
        out_shape=(
            jax.ShapeDtypeStruct((tokens, 3 * columns + CHUNK), BF),
            jax.ShapeDtypeStruct((4, 8, 3 * columns), F32),
            jax.ShapeDtypeStruct((parts, *piece), F32),
        ),
        in_specs=[pl.BlockSpec(memory_space=pltpu.SMEM), outside, whole, whole] + [outside] * 7 + [whole] * 2,
        out_specs=tuple([pl.BlockSpec(memory_space=pltpu.VMEM)] * 3),
        scratch_shapes=[pltpu.VMEM(a.shape, a.dtype) for a in streamed]
        + [
            pltpu.SemaphoreType.DMA((8, 4)),
            pltpu.SMEM((tokens // GROUP,), F32),
            pltpu.VMEM((4, 3 * columns), F32),
            pltpu.VMEM((heads, CHUNK, CHUNK), F32),
            pltpu.VMEM((2, 144, 3 * columns), F32),
            pltpu.VMEM((144, 3 * columns), F32),
            pltpu.VMEM((16, 3 * columns), F32),
            pltpu.VMEM((8, 3 * columns), F32),
            pltpu.VMEM((8, 3 * columns), F32),
            pltpu.SemaphoreType.DMA,
            pltpu.SemaphoreType.DMA,
        ]
        + piece_scatter_scratch(parts, members, piece),
        compiler_params=pltpu.CompilerParams(
            collective_id=collective, has_side_effects=True, vmem_limit_bytes=VMEM_LIMIT
        ),
        cost_estimate=pl.CostEstimate(flops=3 * 10**9, bytes_accessed=20 << 20, transcendentals=2 << 20),
    )(lengths, pre, halo, conv, logits, qkv, inv, wu, mq, states, ddelta, arrive, grads)


def head_peers():
    place = lax.axis_index("head")
    low = lax.rem(place, 2)
    high = lax.rem(lax.div(place, 2), 2)
    return place, low, place + 1 - 2 * low, place + 2 - 4 * high


def push(src, dst, send_sem, recv_sem, axis, target):
    return pltpu.make_async_remote_copy(
        src_ref=src,
        dst_ref=dst,
        send_sem=send_sem,
        recv_sem=recv_sem,
        device_id={axis: target},
        device_id_type=MESH,
    )


def greet(axis, targets):
    barrier = pltpu.get_barrier_semaphore()
    for target in targets:
        pl.semaphore_signal(barrier, inc=1, device_id={axis: target}, device_id_type=MESH)
    pl.semaphore_wait(barrier, len(targets))


def middle_kernel(
    steps,
    rows_ref,
    far_rows_ref,
    full_hbm,
    turned_hbm,
    others_hbm,
    input_ref,
    ct_ref,
    late_ct_ref,
    gain_ref,
    dheads_ref,
    update_ref,
    mid_ref,
    dmid_ref,
    first_grads_ref,
    second_grads_ref,
    third_grads_ref,
    gain_grad_ref,
    gate_ref,
    up_ref,
    down_ref,
    turned_ref,
    others_ref,
    load_sem,
    own_rows_ref,
    stage_ref,
    acc_ref,
    part_ref,
    pair_ref,
    far_ref,
    sum_ref,
    keep_ref,
    scale_ref,
    shard_ref,
    pair_send,
    pair_recv,
    far_send,
    far_recv,
    last_send,
    last_recv,
    row_near_send,
    row_near_recv,
    row_far_send,
    row_far_recv,
    row_pass_send,
    row_pass_recv,
):
    step = pl.program_id(0)
    place, low, near, far = head_peers()
    chunk, width = input_ref.shape
    columns = rows_ref.shape[1]
    hidden = gate_ref.shape[0]
    half = width // 2
    mine = pl.ds(pl.multiple_of(low * half, 128), half)
    theirs = pl.ds(pl.multiple_of((1 - low) * half, 128), half)
    own_columns = pl.ds(pl.multiple_of(place * columns, 128), columns)

    known = steps // 2

    def at(index):
        return pl.ds(pl.multiple_of(index * chunk, chunk), chunk)

    def near_rows(index):
        place_ = at(index - known)
        return push(
            rows_ref.at[at(index)], own_rows_ref.at[0, place_], row_near_send.at[index], row_near_recv.at[index], "head", near
        )

    def far_rows(index):
        place_ = at(index - known)
        return push(
            rows_ref.at[at(index)], own_rows_ref.at[1, place_], row_far_send.at[index], row_far_recv.at[index], "head", far
        )

    def pass_rows(index):
        place_ = at(index - known)
        return push(
            own_rows_ref.at[1, place_], own_rows_ref.at[2, place_], row_pass_send.at[index], row_pass_recv.at[index], "head", near
        )

    def pair(index):
        return push(
            part_ref.at[lax.rem(index, 2), :, theirs], pair_ref.at[index], pair_send.at[index], pair_recv.at[index], "head", near
        )

    def across(index):
        return push(pair_ref.at[index], far_ref.at[index], far_send.at[index], far_recv.at[index], "head", far)

    def last(index):
        return push(
            sum_ref.at[index, :, mine], sum_ref.at[index, :, mine], last_send.at[index], last_recv.at[index], "head", near
        )

    def loads():
        targets = [
            (full_hbm.at[0], gate_ref),
            (full_hbm.at[1], up_ref),
            (full_hbm.at[2], down_ref),
            (turned_hbm, turned_ref),
        ] + [(others_hbm.at[other], others_ref.at[other]) for other in range(3)]
        for number, (source, target) in enumerate(targets):
            for piece in range(width // 128):
                yield pltpu.make_async_copy(
                    source.at[piece], target.at[:, piece * 128 : (piece + 1) * 128], load_sem.at[number, piece]
                )

    @pl.when(step == 0)
    def _():
        for load in loads():
            load.start()
        greet("head", (near, far))

        @pl.loop(known, steps)
        def _(index):
            far_rows(index).start()
            near_rows(index).start()


        acc_ref[...] = jnp.zeros_like(acc_ref)
        gain_grad_ref[...] = jnp.zeros_like(gain_grad_ref)
        for load in loads():
            load.wait()

    @pl.when(step < steps)
    def _():
        ct = ct_ref[...]
        d_hidden = nt(ct, down_ref[...])

        @pl.when(step < known)
        def _():
            stage_ref[...] = far_rows_ref[...]

        @pl.when(step >= known)
        def _():
            near_rows(step).wait_recv()
            pass_rows(step).wait_recv()
            stage_ref[...] = own_rows_ref[:, at(step - known)]

        branch = nn(rows_ref[at(step)], turned_ref[...])
        for other in range(3):
            branch = branch + nn(stage_ref[other], others_ref[other])
        middle = input_ref[...].astype(F32) + branch
        keep_ref[lax.rem(step, 4)] = middle
        mid_ref[...] = keep_ref[lax.rem(step, 4), :, own_columns]
        scale = lax.rsqrt(jnp.mean(middle * middle, axis=-1, keepdims=True) + 1e-06)
        scale_ref[lax.rem(step, 4)] = scale
        second = (middle * scale * gain_ref[1:2]).astype(BF)
        gate, up = nt(second, gate_ref[...]), nt(second, up_ref[...])
        sig = sigmoid(gate)
        silu = gate * sig
        active = (silu * up).astype(BF)
        d_gate = (d_hidden * up * (sig + silu * (1.0 - sig))).astype(BF)
        d_up = (d_hidden * silu).astype(BF)

        @pl.when(step >= 2)
        def _():
            pair(step - 2).wait_send()

        part_ref[lax.rem(step, 2)] = (nn(d_gate, gate_ref[...]) + nn(d_up, up_ref[...])).astype(BF)
        pair(step).start()

        @pl.when((step + 2 >= known) & (step + 2 < steps))
        def _():
            far_rows(step + 2).wait_recv()
            pass_rows(step + 2).start()

        update_ref[...] = nn(active, down_ref[...]).astype(BF)
        acc_ref[:hidden] += tn(d_gate, second)
        acc_ref[hidden : 2 * hidden] += tn(d_up, second)
        acc_ref[2 * hidden : 3 * hidden] += tn(active, ct)

    @pl.when(step < steps)
    def _():
        pair(step).wait_recv()
        both = part_ref[lax.rem(step, 2), :, mine].astype(F32) + pair_ref[step].astype(F32)
        pair_ref[step] = both.astype(BF)
        across(step).start()

    @pl.when((step > 1) & (step < steps + 2))
    def _():
        done = step - 2
        across(done).wait_recv()
        across(done).wait_send()
        total = pair_ref[done].astype(F32) + far_ref[done].astype(F32)
        sum_ref[done, :, mine] = total.astype(BF)
        last(done).start()

    @pl.when(step > 2)
    def _():
        done = step - 3
        last(done).wait_recv()
        grad = sum_ref[done].astype(F32)
        middle = keep_ref[lax.rem(done, 4)]
        scale = scale_ref[lax.rem(done, 4)]
        unit = middle * scale
        gain_grad_ref[...] += jnp.sum((grad * unit).reshape(chunk // 8, 8, width), 0)
        scaled = grad * gain_ref[1:2]
        d_middle = late_ct_ref[...].astype(F32) + scale * (
            scaled - unit * jnp.mean(scaled * unit, axis=-1, keepdims=True)
        )
        shard_ref[...] = d_middle
        dmid_ref[...] = shard_ref[:, own_columns]
        d_branch = d_middle.astype(BF)
        dheads_ref[...] = nt(d_branch, turned_ref[...]).astype(BF)
        acc_ref[3 * hidden :] += tn(rows_ref[at(done)], d_branch)

    @pl.when(step == steps + 2)
    def _():
        for piece in range(width // 128):
            lanes = slice(piece * 128, (piece + 1) * 128)
            begin = 0
            for grads_ref in (first_grads_ref, second_grads_ref, third_grads_ref):
                rows = grads_ref.shape[2]
                for part in range(2):
                    grads_ref[part, piece] = acc_ref[begin : begin + rows, lanes].astype(BF)
                    begin += rows

        @pl.loop(0, steps)
        def _(index):
            last(index).wait_send()

        @pl.loop(known, steps)
        def _(index):
            near_rows(index).wait_send()
            far_rows(index).wait_send()
            pass_rows(index).wait_send()

        for index in range(max(steps - 2, 0), steps):
            pair(index).wait_send()


def middle_stage(head_rows, far_rows, full, turned, others, inputs, cotangent, gain, collective):
    tokens, width = inputs.shape
    columns = head_rows.shape[1]
    chunk = min(256, tokens // 2)
    steps = tokens // chunk
    whole = pl.BlockSpec(memory_space=pltpu.VMEM)
    outside = pl.BlockSpec(memory_space=pl.ANY)
    hidden = full.shape[2]
    units = (3 * hidden + columns) // 32
    shares = [16 * (units * 36 // 74), 0, 16 * (units * 25 // 74)]
    shares[1] = 16 * units - sum(shares)

    def early(wide):
        return pl.BlockSpec((chunk, wide), lambda s: (jnp.minimum(s, steps - 1), 0))

    def late(wide):
        return pl.BlockSpec((chunk, wide), lambda s: (jnp.maximum(s - 3, 0), 0))

    far = pl.BlockSpec((3, chunk, columns), lambda s: (0, jnp.minimum(s, steps // 2 - 1), 0))
    dma = pltpu.SemaphoreType.DMA((steps,))
    return pl.pallas_call(
        functools.partial(middle_kernel, steps),
        name="middle",
        grid=(steps + 3,),
        out_shape=(
            jax.ShapeDtypeStruct((tokens, columns), BF),
            jax.ShapeDtypeStruct((tokens, width), BF),
            jax.ShapeDtypeStruct((tokens, columns), F32),
            jax.ShapeDtypeStruct((tokens, columns), F32),
            *(jax.ShapeDtypeStruct((2, width // 128, rows, 128), BF) for rows in shares),
            jax.ShapeDtypeStruct((8, width), F32),
        ),
        in_specs=[whole, far] + [outside] * 3 + [early(width), early(width), late(width), whole],
        out_specs=(late(columns), early(width), early(columns), late(columns), whole, whole, whole, whole),
        scratch_shapes=[
            pltpu.VMEM((hidden, width), BF),
            pltpu.VMEM((hidden, width), BF),
            pltpu.VMEM((hidden, width), BF),
            pltpu.VMEM((columns, width), BF),
            pltpu.VMEM((3, columns, width), BF),
            pltpu.SemaphoreType.DMA((7, width // 128)),
            pltpu.VMEM((3, tokens // 2, columns), BF),
            pltpu.VMEM((3, chunk, columns), BF),
            pltpu.VMEM((3 * hidden + columns, width), F32),
            pltpu.VMEM((2, chunk, width), BF),
            pltpu.VMEM((steps, chunk, width // 2), BF),
            pltpu.VMEM((steps, chunk, width // 2), BF),
            pltpu.VMEM((steps, chunk, width), BF),
            pltpu.VMEM((4, chunk, width), F32),
            pltpu.VMEM((4, chunk, 1), F32),
            pltpu.VMEM((chunk, width), F32),
        ]
        + [dma] * 12,
        compiler_params=pltpu.CompilerParams(
            collective_id=collective,
            has_side_effects=True,
            vmem_limit_bytes=VMEM_LIMIT,
            dimension_semantics=("arbitrary",),
        ),
        cost_estimate=pl.CostEstimate(flops=30 * 10**9, bytes_accessed=30 << 20, transcendentals=2 << 20),
    )(head_rows, far_rows, full, turned, others, inputs, cotangent, cotangent, gain)


def zeros_below(value):
    return (value & -value).bit_length() - 1


def flip(place, mask):
    bit = 1
    while bit <= mask:
        if mask & bit:
            place = place + bit - 2 * bit * lax.rem(lax.div(place, bit), 2)
        bit *= 2
    return place


def head_scatter_copies(chunk, part_ref, near_ref, send_ref, far_ref, sems):
    place, low, near, far = head_peers()
    high = lax.rem(lax.div(place, 2), 2)
    columns = far_ref.shape[-1]
    near_send, near_recv, far_send, far_recv = sems

    def at(index):
        return pl.ds(pl.multiple_of(index * chunk, chunk), chunk)

    def cols(owner):
        return pl.ds(pl.multiple_of(owner * columns, 128), columns)

    def pair(index, side_):
        return push(
            part_ref.at[at(index), cols(2 * side_ + 1 - low)],
            near_ref.at[side_, at(index)],
            near_send.at[side_, index],
            near_recv.at[side_, index],
            "head",
            near,
        )

    def across(index):
        return push(send_ref.at[at(index)], far_ref.at[at(index)], far_send.at[index], far_recv.at[index], "head", far)

    def start_pair(index):
        pair(index, 0).start()
        pair(index, 1).start()

    def pass_on(index):
        pair(index, 0).wait_recv()
        pair(index, 1).wait_recv()
        total = part_ref[at(index), cols(2 * (1 - high) + low)].astype(F32) + near_ref[1 - high, at(index)].astype(F32)
        send_ref[at(index)] = total.astype(BF)
        across(index).start()

    def own_sum(index):
        across(index).wait_recv()
        near_part = part_ref[at(index), cols(place)].astype(F32) + near_ref[high, at(index)].astype(F32)
        return near_part + far_ref[at(index)].astype(F32)

    def finish(index):
        pair(index, 0).wait_send()
        pair(index, 1).wait_send()
        across(index).wait_send()

    return at, cols, start_pair, pass_on, own_sum, finish


def head_scatter_scratch(tokens, columns, steps):
    return [
        pltpu.VMEM((2, tokens, columns), BF),
        pltpu.VMEM((tokens, columns), BF),
        pltpu.VMEM((tokens, columns), BF),
        pltpu.SemaphoreType.DMA((2, steps)),
        pltpu.SemaphoreType.DMA((2, steps)),
        pltpu.SemaphoreType.DMA((steps,)),
        pltpu.SemaphoreType.DMA((steps,)),
    ]


def final_kernel(
    members,
    chunk,
    rows_ref,
    dpre_ref,
    pack_hbm,
    input_hbm,
    scale_hbm,
    gain_ref,
    dmid_hbm,
    head_part_ref,
    second_part_ref,
    taps_part_ref,
    rest_ref,
    ingrad_ref,
    piece_ref,
    sums_ref,
    total_ref,
    pack_ref,
    input_ref,
    scale_ref,
    dmid_ref,
    load_sem,
    acc_ref,
    out_ref,
    slots_ref,
    part_ref,
    near_ref,
    send_ref,
    far_ref,
    near_send,
    near_recv,
    far_send,
    far_recv,
    stat_ref,
    stat_slots,
    small_slots,
    piece_send,
    piece_recv,
    stat_send,
    stat_recv,
    small_send,
    small_recv,
    rest_relay,
    rest_slots,
    rest_send,
    rest_recv,
):
    tokens, width = input_ref.shape
    steps = tokens // chunk
    loads = [
        pltpu.make_async_copy(source, target, load_sem.at[number])
        for number, (source, target) in enumerate(
            ((pack_hbm, pack_ref), (input_hbm, input_ref), (scale_hbm, scale_ref), (dmid_hbm, dmid_ref))
        )
    ]
    for load in loads:
        load.start()
    place, low, near, far = head_peers()
    member = lax.axis_index("seq")
    rows = width // members
    stages = (members - 1).bit_length()
    at, cols, start_pair, pass_on, own_sum, finish = head_scatter_copies(
        chunk, part_ref, near_ref, send_ref, far_ref, (near_send, near_recv, far_send, far_recv)
    )

    barrier = pltpu.get_barrier_semaphore()
    opposite = near + far - place
    for target in (near, far, opposite):
        pl.semaphore_signal(barrier, inc=1, device_id={"head": target}, device_id_type=MESH)
    for stage in range(stages):
        pl.semaphore_signal(barrier, inc=1, device_id={"seq": flip(member, 1 << stage)}, device_id_type=MESH)
    begin, rest_receive, rest_jobs, rest_end = piece_scatter(
        rest_ref, rest_relay, rest_slots, total_ref, rest_send, rest_recv, members
    )
    pl.semaphore_wait(barrier, 3 + stages)
    order = sorted(range(members), key=lambda r: zeros_below(r) if r else stages)
    sent = [r for r in order if r]
    events = {}
    for r in order:
        for stage in range(zeros_below(r) if r else stages):
            events[stage, r] = len(events)

    def give(r):
        stage = zeros_below(r)
        slot = events[stage, r ^ (1 << stage)]
        return push(
            out_ref.at[r],
            slots_ref.at[slot],
            piece_send.at[r],
            piece_recv.at[slot],
            "seq",
            flip(member, 1 << stage),
        )

    def take(stage, r):
        slot = events[stage, r]
        return push(
            out_ref.at[0], slots_ref.at[slot], piece_send.at[0], piece_recv.at[slot], "seq", flip(member, 1 << stage)
        )

    def send_piece(r):
        out_ref[r] = acc_ref[flip(member, r)].astype(BF)
        give(r).start()

    def receive(r):
        index = flip(member, r)
        for stage in range(zeros_below(r) if r else stages):
            take(stage, r).wait_recv()
            acc_ref[index] += slots_ref[events[stage, r]].astype(F32)
        if r:
            send_piece(r)

    first = sorted([r for r in range(members) if r % 2], key=lambda r: order.index(r ^ 1))
    evens = [r for r in order if r % 2 == 0]
    if rows % 128 == 0:
        for r in first:
            even = 2 * lax.div(flip(member, r), 2)
            columns = pl.ds(pl.multiple_of(even * rows, 128), 2 * rows)
            block = tn(rows_ref[:, columns], dpre_ref[...])
            acc_ref[even] = block[:rows]
            acc_ref[even + 1] = block[rows:]
            send_piece(r)
        begin()
    else:
        per = 128 // rows
        for unit in range(width // 128):
            block = tn(rows_ref[:, unit * 128 : (unit + 1) * 128], dpre_ref[...])
            acc_ref[unit * per : (unit + 1) * per] = block.reshape(per, rows, block.shape[1])
        for r in first:
            send_piece(r)
        begin()

    small_slots[0] = jnp.zeros_like(small_slots[0])
    small_slots[0, 1:2, :CHUNK] = jnp.sum(head_part_ref[...], 0, keepdims=True)
    small_slots[0, 8:9] = jnp.sum(second_part_ref[...], 0, keepdims=True)
    columns3 = taps_part_ref.shape[2]
    for tap in range(4):
        taps_sum = jnp.sum(taps_part_ref[tap], 0, keepdims=True)
        for block in range(3):
            flat = tap * columns3 + block * (columns3 // 3)
            line, lane = 9 + flat // width, flat % width
            small_slots[0, line : line + 1, lane : lane + columns3 // 3] = taps_sum[
                :, block * (columns3 // 3) : (block + 1) * (columns3 // 3)
            ]
    for load in loads:
        load.wait()
    diagonal = lax.broadcasted_iota(jnp.int32, (128, 128), 0) == lax.broadcasted_iota(jnp.int32, (128, 128), 1)

    def project(index):
        part = nt(dpre_ref[at(index)], pack_ref[...])
        part_ref[at(index)] = part.astype(BF)
        start_pair(index)
        seen = part * (input_ref[at(index)].astype(F32) * scale_ref[at(index)])
        small_slots[0, 0:1] += jnp.sum(seen, 0, keepdims=True)
        stat = jnp.sum(seen * gain_ref[0:1], axis=-1, keepdims=True)
        for block in range(chunk // 128):
            line = jnp.where(diagonal, stat[block * 128 : (block + 1) * 128], 0.0)
            stat_ref[index * (chunk // 128) + block] = jnp.sum(line, 0, keepdims=True)

    early = steps // 2
    receives = list(evens)
    for half in range(2):

        @pl.loop(half * early, (half + 1) * early)
        def _(index):
            project(index)

            @pl.when(lax.rem(index, 2) == 1)
            def _():
                pass_on(lax.div(index, 2))

        if len(receives) > 1:
            receive(receives.pop(0))

    def stat_copy(turn):
        target = (near, far, opposite)[turn]
        return push(stat_ref, stat_slots.at[turn], stat_send.at[turn], stat_recv.at[turn], "head", target)

    def head_copy(turn):
        target = (near, far, opposite)[turn]
        return push(
            small_slots.at[0, pl.ds(0, 8)],
            small_slots.at[1 + turn, pl.ds(0, 8)],
            small_send.at[turn],
            small_recv.at[turn],
            "head",
            target,
        )

    for turn in (1, 2, 0):
        head_copy(turn).start()
        stat_copy(turn).start()
    for index in range(early, steps):
        pass_on(index)
    while len(receives) > 1:
        receive(receives.pop(0))
    for turn in range(3):
        head_copy(turn).wait()
    small_slots[4] = small_slots[0]
    small_slots[4, 0:8] += small_slots[1, 0:8] + small_slots[2, 0:8] + small_slots[3, 0:8]

    bits = list(range(1, stages)) + [0]

    def seq_copy(turn):
        return push(
            small_slots.at[4 + 2 * turn],
            small_slots.at[5 + 2 * turn],
            small_send.at[3 + turn],
            small_recv.at[3 + turn],
            "seq",
            flip(member, 1 << bits[turn]),
        )

    def seq_add(turn):
        seq_copy(turn).wait()
        small_slots[6 + 2 * turn] = small_slots[4 + 2 * turn] + small_slots[5 + 2 * turn]

    seq_copy(0).start()
    for turn in range(3):
        stat_copy(turn).wait()
    stat_ref[...] += stat_slots[0] + stat_slots[1] + stat_slots[2]

    def result(index):
        grad = own_sum(index)
        scale = scale_ref[at(index)]
        unit = input_ref[at(index), cols(place)].astype(F32) * scale
        means = []
        for block in range(chunk // 128):
            line = jnp.where(diagonal, stat_ref[index * (chunk // 128) + block], 0.0)
            means.append(jnp.sum(line, axis=-1, keepdims=True))
        mean = jnp.concatenate(means, 0) * (1.0 / width)
        ingrad_ref[at(index)] = dmid_ref[at(index)] + scale * (grad * gain_ref[0:1, cols(place)] - unit * mean)

    rests = list(rest_jobs)
    for turn in range(stages):
        start, stop = turn * steps // stages, (turn + 1) * steps // stages
        if stop > start:

            @pl.loop(start, stop)
            def _(index):
                result(index)

        share = (len(rests) - 1) // (stages - turn)
        for job in rests[:share]:
            rest_receive(*job)
        rests = rests[share:]
        seq_add(turn)
        if turn + 1 < stages:
            seq_copy(turn + 1).start()
    receive(0)
    for job in rests:
        rest_receive(*job)
    piece_ref[...] = acc_ref[member]
    sums_ref[...] = small_slots[4 + 2 * stages]

    @pl.loop(0, steps)
    def _(index):
        finish(index)

    for r in sent:
        give(r).wait_send()
    rest_end()


def final_stage(first_rows, dpre, pack, inputs, scale, gain, dmid, parts, rest, members, collective):
    tokens, width = inputs.shape
    columns = dmid.shape[1]
    chunk = 256
    steps = tokens // chunk
    stages = (members - 1).bit_length()
    rows = width // members
    wide = dpre.shape[1]
    whole, outside = pl.BlockSpec(memory_space=pltpu.VMEM), pl.BlockSpec(memory_space=pl.ANY)
    return pl.pallas_call(
        functools.partial(final_kernel, members, chunk),
        name="final",
        out_shape=(
            jax.ShapeDtypeStruct((tokens, columns), F32),
            jax.ShapeDtypeStruct((rows, wide), F32),
            jax.ShapeDtypeStruct((16, width), F32),
            jax.ShapeDtypeStruct((rest.shape[0], *rest.shape[2:]), F32),
        ),
        in_specs=[whole, whole, outside, outside, outside, whole, outside] + [whole] * 4,
        out_specs=(whole,) * 4,
        scratch_shapes=[pltpu.VMEM(a.shape, a.dtype) for a in (pack, inputs, scale, dmid)]
        + [
            pltpu.SemaphoreType.DMA((4,)),
            pltpu.VMEM((members, rows, wide), F32),
            pltpu.VMEM((members, rows, wide), BF),
            pltpu.VMEM((members - 1, rows, wide), BF),
            pltpu.VMEM((tokens, width), BF),
        ]
        + head_scatter_scratch(tokens, columns, steps)
        + [
            pltpu.VMEM((tokens // 128, 1, 128), F32),
            pltpu.VMEM((3, tokens // 128, 1, 128), F32),
            pltpu.VMEM((5 + 2 * stages, 16, width), F32),
            pltpu.SemaphoreType.DMA((members,)),
            pltpu.SemaphoreType.DMA((members - 1,)),
            pltpu.SemaphoreType.DMA((3,)),
            pltpu.SemaphoreType.DMA((3,)),
            pltpu.SemaphoreType.DMA((3 + stages,)),
            pltpu.SemaphoreType.DMA((3 + stages,)),
        ]
        + piece_scatter_scratch(rest.shape[0], members, rest.shape[2:]),
        compiler_params=pltpu.CompilerParams(
            collective_id=collective, has_side_effects=True, vmem_limit_bytes=VMEM_LIMIT
        ),
        cost_estimate=pl.CostEstimate(flops=8 * 10**9, bytes_accessed=30 << 20, transcendentals=0),
    )(first_rows, dpre, pack, inputs, scale, gain, dmid, *parts, rest)


def finish_kernel(
    hidden,
    block_ref,
    ingrad_ref,
    piece_ref,
    sums_ref,
    first_ref,
    second_ref,
    third_ref,
    block_out,
    ingrad_out,
    first_gain_out,
    query_out,
    key_out,
    value_out,
    beta_out,
    conv_out,
    head_gain_out,
    output_out,
    second_gain_out,
    gate_out,
    up_out,
    down_out,
    turn_ref,
    strip_ref,
    sems,
):
    rows, columns = query_out.shape
    member = lax.axis_index("seq")
    pieces = [(block_ref, block_out), (ingrad_ref, ingrad_out)]
    for kind, target in enumerate((query_out, key_out, value_out)):
        pieces.append((piece_ref.at[:, pl.ds(kind * columns, columns)], target))
    pieces.append((piece_ref.at[:, pl.ds(3 * columns, CHUNK)], strip_ref))
    spans = []
    place = 0
    for source in (first_ref, second_ref, third_ref):
        for part in range(2):
            spans.append((place, source, part))
            place += source.shape[1]
    goal = 0
    for target, count in ((gate_out, hidden), (up_out, hidden), (down_out, hidden), (turn_ref, columns)):
        for begin, source, part in spans:
            low, high = max(begin, goal), min(begin + source.shape[1], goal + count)
            if low < high:
                pieces.append(
                    (source.at[part, pl.ds(low - begin, high - low)], target.at[pl.ds(low - goal, high - low)])
                )
        goal += count
    copies = [pltpu.make_async_copy(source, target, sems.at[number]) for number, (source, target) in enumerate(pieces)]
    for copy in copies:
        copy.start()
    window = pl.ds(pl.multiple_of(member * rows, 128), rows)
    first_gain_out[...] = sums_ref[0:1, window]
    second_gain_out[...] = sums_ref[8:9, window]
    head_gain_out[...] = sums_ref[1:2, :CHUNK]
    width = sums_ref.shape[1]
    for kind in range(3):
        for tap in range(4):
            flat = (3 * tap + kind) * columns
            line, lane = 9 + flat // width, flat % width
            conv_out[kind, tap : tap + 1] = sums_ref[line : line + 1, lane : lane + columns]
    for copy in copies:
        copy.wait()
    output_out[...] = turn_ref[...].T
    beta_out[...] = strip_ref[...].T[: beta_out.shape[0]]


def finish_stage(block, ingrad, piece, sums, first, second, third, hidden, heads):
    tokens, columns = ingrad.shape
    rows = piece.shape[0]
    whole, outside = pl.BlockSpec(memory_space=pltpu.VMEM), pl.BlockSpec(memory_space=pl.ANY)

    def made(*shape):
        return jax.ShapeDtypeStruct(shape, F32)

    return pl.pallas_call(
        functools.partial(finish_kernel, hidden),
        name="finish",
        out_shape=(
            jax.ShapeDtypeStruct((tokens, columns), BF),
            made(tokens, columns),
            made(1, rows),
            made(rows, columns),
            made(rows, columns),
            made(rows, columns),
            made(heads, rows),
            made(3, 4, columns),
            made(1, CHUNK),
            made(rows, columns),
            made(1, rows),
            made(hidden, rows),
            made(hidden, rows),
            made(hidden, rows),
        ),
        in_specs=[whole] * 7,
        out_specs=(outside,) * 2
        + (whole,)
        + (outside,) * 3
        + (whole,) * 5
        + (outside,) * 3,
        scratch_shapes=[
            pltpu.VMEM((columns, rows), F32),
            pltpu.VMEM((rows, CHUNK), F32),
            pltpu.SemaphoreType.DMA((24,)),
        ],
        compiler_params=pltpu.CompilerParams(vmem_limit_bytes=VMEM_LIMIT),
        cost_estimate=pl.CostEstimate(flops=0, bytes_accessed=12 << 20, transcendentals=0),
    )(block, ingrad, piece, sums, first, second, third)
def turn_column(column):
    diagonal = lax.broadcasted_iota(jnp.int32, (128, 128), 0) == lax.broadcasted_iota(jnp.int32, (128, 128), 1)
    lines = []
    for block in range(column.shape[0] // 128):
        lines.append(jnp.sum(jnp.where(diagonal, column[block * 128 : (block + 1) * 128], 0.0), 0, keepdims=True))
    return jnp.concatenate(lines, 1)


def piece_gather(full_ref, send, recv, members):
    member = lax.axis_index("seq")
    parts = full_ref.shape[0]
    stages = (members - 1).bit_length()

    def give(part, r, stage):
        owner = flip(member, r)
        mark = r ^ (1 << stage)
        return push(
            full_ref.at[part, owner],
            full_ref.at[part, owner],
            send.at[part, mark],
            recv.at[part, mark],
            "seq",
            flip(member, 1 << stage),
        )

    def take(part, r):
        owner = flip(member, r)
        return push(
            full_ref.at[part, owner],
            full_ref.at[part, owner],
            send.at[part, r],
            recv.at[part, r],
            "seq",
            flip(member, r & -r),
        )

    def begin(part=0, levels=None):
        for stage in reversed(range(stages)) if levels is None else levels:
            give(part, 0, stage).start()

    def relay(part, r):
        take(part, r).wait_recv()
        for stage in reversed(range(zeros_below(r))):
            give(part, r, stage).start()
        if r == 1 << (stages - 1) and part + 1 < parts:
            begin(part + 1)

    order = sorted([r for r in range(1, members) if r % 2 == 0], key=lambda r: (-zeros_below(r), r))
    def when(part, r):
        return 2 * part + 3 * (bin(r).count("1") - 1), part, -zeros_below(r), r

    relays = sorted([(part, r) for r in order for part in range(parts)], key=lambda job: when(*job))

    def arrive():
        for part in range(parts):
            for r in range(1, members, 2):
                take(part, r).wait_recv()

    def finish():
        for part in range(parts):
            for r in [0] + order:
                for stage in range(zeros_below(r) if r else stages):
                    give(part, r, stage).wait_send()

    return begin, relay, relays, arrive, finish


def greet_seq(members):
    member = lax.axis_index("seq")
    stages = (members - 1).bit_length()
    barrier = pltpu.get_barrier_semaphore()
    for stage in range(stages):
        pl.semaphore_signal(barrier, inc=1, device_id={"seq": flip(member, 1 << stage)}, device_id_type=MESH)
    return barrier, stages


FRONT_REFS = 64


def front_kernel(
    members,
    heads,
    lengths_ref,
    input_ref,
    query_ref,
    key_ref,
    value_ref,
    beta_ref,
    first_gain_ref,
    second_gain_ref,
    out_weight_ref,
    conv_ref,
    head_gain_ref,
    *refs,
):
    own_refs, refs = refs[:-FRONT_REFS], refs[-FRONT_REFS:]
    front_body(
        members,
        heads,
        lengths_ref,
        input_ref,
        query_ref,
        key_ref,
        value_ref,
        beta_ref,
        first_gain_ref,
        second_gain_ref,
        out_weight_ref,
        conv_ref,
        head_gain_ref,
        own_refs,
        *refs,
    )


def front_body(
    members,
    heads,
    lengths_ref,
    input_ref,
    query_ref,
    key_ref,
    value_ref,
    beta_ref,
    first_gain_ref,
    second_gain_ref,
    out_weight_ref,
    conv_ref,
    head_gain_ref,
    own_refs,
    pack_hbm,
    first_hbm,
    pre_hbm,
    logits_hbm,
    halo_ref,
    scale_hbm,
    gains_ref,
    turned_hbm,
    full_hbm,
    others_hbm,
    qkv_hbm,
    inv_hbm,
    wu_hbm,
    mq_hbm,
    total_ref,
    delta_hbm,
    rows_hbm,
    far_rows_hbm,
    states_hbm,
    pack_ref,
    first_ref,
    pre_ref,
    logits_ref,
    scale_ref,
    turned_ref,
    full_ref,
    others_ref,
    qkv_ref,
    inv_ref,
    wu_ref,
    mq_ref,
    delta_ref,
    rows_ref,
    far_rows_ref,
    states_ref,
    store_sem,
    resets_ref,
    taps_ref,
    extra_ref,
    start_ref,
    out0_ref,
    state_ref,
    part_ref,
    slots_ref,
    pad_ref,
    edge_ref,
    pack_send,
    pack_recv,
    edge_send,
    edge_recv,
    turned_send,
    turned_recv,
    full_send,
    full_recv,
    head_send,
    head_recv,
    state_send,
    state_recv,
    row_near_send,
    row_near_recv,
    row_far_send,
    row_far_recv,
    row_pass_send,
    row_pass_recv,
):
    tokens, width = input_ref.shape
    columns = heads * CHUNK
    leaving = (
        (pack_ref, pack_hbm),
        (first_ref, first_hbm),
        (pre_ref, pre_hbm),
        (logits_ref, logits_hbm),
        (scale_ref, scale_hbm),
        (turned_ref, turned_hbm),
        (qkv_ref, qkv_hbm),
        (inv_ref, inv_hbm),
        (wu_ref, wu_hbm),
        (mq_ref, mq_hbm),
        (delta_ref, delta_hbm),
        (rows_ref, rows_hbm),
        (states_ref, states_hbm),
        (others_ref, others_hbm),
        (far_rows_ref, far_rows_hbm),
        (full_ref, full_hbm),
    )

    def store(number):
        return pltpu.make_async_copy(*leaving[number], store_sem.at[number])

    member = lax.axis_index("seq")
    _, _, near, far = head_peers()
    barrier, stages = greet_seq(members)
    for target in (near, far):
        pl.semaphore_signal(barrier, inc=1, device_id={"head": target}, device_id_type=MESH)

    @pl.when(member > 0)
    def _():
        pl.semaphore_signal(barrier, inc=1, device_id={"seq": member - 1}, device_id_type=MESH)

    window = slots_ref.shape[0]
    behind = members - 1 - member
    for hop in range(1, window + 1):

        @pl.when(member >= hop)
        def _():
            pl.semaphore_signal(barrier, inc=1, device_id={"seq": member - hop}, device_id_type=MESH)

    def state_copy(hop):
        return push(
            part_ref, slots_ref.at[hop - 1], state_send.at[hop - 1], state_recv.at[hop - 1], "seq", member + hop
        )

    pack_ref[0, member, :, :columns] = query_ref[...]
    pack_ref[0, member, :, columns : 2 * columns] = key_ref[...]
    pack_ref[0, member, :, 2 * columns : 3 * columns] = value_ref[...]
    extra_ref[...] = jnp.zeros_like(extra_ref)
    extra_ref[0:heads] = beta_ref[...].astype(F32)
    extra_ref[heads : heads + 1] = first_gain_ref[...].astype(F32)
    extra_ref[heads + 1 : heads + 2] = second_gain_ref[...].astype(F32)
    pack_ref[0, member, :, 3 * columns :] = extra_ref[...].T.astype(BF)
    turned_ref[0, member] = out_weight_ref[...].T
    for part, own_ref in enumerate(own_refs):
        full_ref[part, member] = own_ref[...]
    pack = piece_gather(pack_ref, pack_send, pack_recv, members)
    turned = piece_gather(turned_ref, turned_send, turned_recv, members)
    full = piece_gather(full_ref, full_send, full_recv, members)
    near_copy = push(turned_ref.at[0], others_ref.at[0], head_send.at[0], head_recv.at[0], "head", near)
    far_copy = push(turned_ref.at[0], others_ref.at[1], head_send.at[1], head_recv.at[1], "head", far)
    pass_copy = push(others_ref.at[1], others_ref.at[2], head_send.at[2], head_recv.at[2], "head", near)
    pl.semaphore_wait(barrier, stages + 2 + jnp.minimum(behind, 1) + jnp.minimum(behind, window))
    pack[0]()
    fill_resets(lengths_ref, resets_ref, tokens)
    fill_taps(conv_ref, taps_ref)

    last_rows = pl.ds(tokens - 16, 16)

    def edge(target):
        return push(input_ref.at[last_rows], edge_ref, edge_send, edge_recv, "seq", target)

    @pl.when(member + 1 < members)
    def _():
        edge(member + 1).start()

    chunk = 256

    def at(index):
        return pl.ds(pl.multiple_of(index * chunk, chunk), chunk)

    def measure(index):
        block = input_ref[at(index)].astype(F32)
        scale_ref[at(index)] = lax.rsqrt(jnp.mean(block * block, axis=-1, keepdims=True) + 1e-06)

    pl.loop(0, tokens // chunk)(measure)
    for job in pack[2]:
        pack[1](*job)
    full[0](0)
    turned[0]()
    pack[3]()
    projection = pack_ref[0].reshape(width, pack_ref.shape[3])
    extras = projection[:, 3 * columns :].astype(F32)
    gains_ref[0:1] = turn_column(extras[:, heads : heads + 1])
    gains_ref[1:2] = turn_column(extras[:, heads + 1 : heads + 2])

    def project(index):
        first = (input_ref[at(index)].astype(F32) * scale_ref[at(index)] * gains_ref[0:1]).astype(BF)
        first_ref[at(index)] = first
        both = nn(first, pack_ref[0].reshape(width, pack_ref.shape[3]))
        pre_ref[at(index)] = both[:, : 3 * columns].astype(BF)
        logits_ref[at(index)] = both[:, 3 * columns :]

    pl.loop(0, tokens // chunk)(project)

    @pl.when(member == 0)
    def _():
        halo_ref[...] = jnp.zeros_like(halo_ref)

    @pl.when(member > 0)
    def _():
        edge(member).wait_recv()
        block = edge_ref[...].astype(F32)
        scale = lax.rsqrt(jnp.mean(block * block, axis=-1, keepdims=True) + 1e-06)
        first = (block * scale * gains_ref[0:1]).astype(BF)
        halo_ref[...] = nn(first, pack_ref[0].reshape(width, pack_ref.shape[3])[:, : 3 * columns]).astype(BF)

    for number in range(5):
        store(number).start()
    rows, cols = grid_indices()
    eye = jnp.where(rows == cols, 1.0, 0.0)
    top = lax.broadcasted_iota(jnp.int32, (CHUNK, 1), 0) < GROUP
    for head in range(heads):
        total_ref[head] = side(eye, jnp.zeros_like(eye))
    batch = pad_ref.shape[0]

    def one(step, carry):
        units = []
        for lane in range(batch):
            chunk = step * batch + lane
            pad = pad_ref.at[lane]
            load_padded(pad, pre_ref, halo_ref, chunk, resets_ref)
            mixed = convolve(pad, taps_ref)
            silued = mixed * sigmoid(mixed)
            keep0 = 1.0 - resets_ref[2 * chunk]
            keep1 = 1.0 - resets_ref[2 * chunk + 1]
            both = keep0 * keep1
            enter = jnp.where(top, keep0, both)
            leave = jnp.where(top, keep1, 1.0)
            at = pl.ds(pl.multiple_of(chunk * CHUNK, CHUNK), CHUNK)
            beta_rows = sigmoid(logits_ref[at, :])
            for head in range(heads):
                window = slice(head * CHUNK, (head + 1) * CHUNK)
                parts = []
                for kind in range(3):
                    part = silued[:, kind * columns + head * CHUNK : kind * columns + (head + 1) * CHUNK]
                    if kind < 2:
                        part = part * lax.rsqrt(jnp.sum(part * part, axis=-1, keepdims=True) + 1e-06)
                    part = part.astype(BF)
                    qkv_ref[at, kind * columns + head * CHUNK : kind * columns + (head + 1) * CHUNK] = part
                    parts.append(part)
                units.append((chunk, head, *parts, beta_rows[:, head : head + 1], keep1, both, enter, leave))
        turned = [u[3].T for u in units]
        strict = [
            jnp.where(rows > cols, u[5] * nn(u[3], t), 0.0) for u, t in zip(units, turned)
        ]
        inverses = [r.astype(BF) for r in inverse_levels(strict, rows, cols, [u[6] for u in units])]
        factors = []
        for u, inverse in zip(units, inverses):
            beta = u[5]
            factors.append(nn(inverse, side(u[3].astype(F32) * beta, u[4].astype(F32) * beta)))
        for u, inverse, factor, t in zip(units, inverses, factors, turned):
            chunk, head, query, key, value, beta, keep1, both, enter, leave = u
            weight, update = factor[:, :CHUNK], factor[:, CHUNK:]
            entering_weight = weight * enter
            inv_ref[chunk, head] = inverse
            wu_ref[chunk, head] = side(entering_weight, update).astype(BF)
            gathered = nn(t, side(weight, update * leave))
            device_map = (both * (eye - gathered[:, :CHUNK])).astype(BF)
            shift = gathered[:, CHUNK:]
            scores = jnp.where(rows >= cols, nn(query, t), 0.0)
            scores = jnp.where((rows >= GROUP) & (cols < GROUP), scores * keep1, scores)
            seen = nn(scores, side(entering_weight, update))
            effective = query.astype(F32) * enter - seen[:, :CHUNK]
            mq_ref[chunk, head] = stack(device_map, effective.astype(BF))
            out0_ref[chunk, head] = seen[:, CHUNK:]
            running = total_ref[head]
            start_ref[chunk, head] = running.astype(BF)
            total_ref[head] = nn(device_map, running) + side(jnp.zeros_like(shift), shift)
        return carry

    count = resets_ref.shape[0] // 2 // batch
    held = 4 if len(full[2]) > 4 else 0
    relays = full[2][: len(full[2]) - held]

    def pumped(step, carry):
        carry = one(step, carry)
        for turn in range(count):
            jobs = [job for place, job in enumerate(relays) if place * count // len(relays) == turn]
            if not jobs and turn not in (0, 2, count - 2):
                continue

            @pl.when(step == turn)
            def _():
                if turn == 0:
                    for job in turned[2]:
                        turned[1](*job)
                for job in jobs:
                    full[1](*job)
                if turn == 2:
                    turned[3]()
                    store(5).start()
                    near_copy.start()
                    far_copy.start()
                if turn == count - 2:
                    far_copy.wait_recv()
                    pass_copy.start()

        return carry

    lax.fori_loop(0, count, pumped, 0)
    for number in range(6, 10):
        store(number).start()
    part_ref[...] = total_ref[...].astype(BF)
    for hop in range(1, window + 1):

        @pl.when(behind >= hop)
        def _():
            state_copy(hop).start()

    for job in full[2][len(full[2]) - held :]:
        full[1](*job)
    state_ref[...] = jnp.zeros_like(state_ref)
    for hop in range(window, 0, -1):

        @pl.when(member >= hop)
        def _():
            state_copy(hop).wait_recv()
            for head in range(heads):
                part = slots_ref[hop - 1, head]
                state_ref[head] = nn(part[:, :CHUNK], state_ref[head]) + part[:, CHUNK:].astype(F32)

    def near_rows(index):
        return push(
            rows_ref.at[at(index)], far_rows_ref.at[0, at(index)], row_near_send.at[index], row_near_recv.at[index], "head", near
        )

    def far_rows(index):
        return push(
            rows_ref.at[at(index)], far_rows_ref.at[1, at(index)], row_far_send.at[index], row_far_recv.at[index], "head", far
        )

    def pass_rows(index):
        return push(
            far_rows_ref.at[1, at(index)], far_rows_ref.at[2, at(index)], row_pass_send.at[index], row_pass_recv.at[index], "head", near
        )

    def finished(index):
        for lane in range(chunk // CHUNK):
            place_ = index * (chunk // CHUNK) + lane
            rows_at = pl.ds(pl.multiple_of(place_ * CHUNK, CHUNK), CHUNK)
            begins = [start_ref[place_, head] for head in range(heads)]
            states = [
                (nn(begins[head][:, :CHUNK], state_ref[head]) + begins[head][:, CHUNK:].astype(F32)).astype(BF)
                for head in range(heads)
            ]
            outs = [out0_ref[place_, head] + nn(mq_ref[place_, head, CHUNK:], states[head]) for head in range(heads)]
            for head in range(heads):
                lanes = slice(head * CHUNK, (head + 1) * CHUNK)
                states_ref[place_, head] = states[head]
                delta_ref[rows_at, lanes] = outs[head]
                scale = lax.rsqrt(jnp.mean(outs[head] * outs[head], axis=-1, keepdims=True) + 1e-05)
                rows_ref[rows_at, lanes] = (outs[head] * scale * head_gain_ref[...].astype(F32)).astype(BF)

    sent = far_rows_ref.shape[1] // chunk

    def finished_and_sent(index):
        finished(index)
        far_rows(index).start()
        near_rows(index).start()

    pl.loop(0, sent)(finished_and_sent)
    pl.loop(sent, tokens // chunk)(finished)
    for number in range(10, 13):
        store(number).start()

    @pl.loop(0, sent)
    def _(index):
        far_rows(index).wait_recv()
        pass_rows(index).start()

    near_copy.wait()
    far_copy.wait_send()
    pass_copy.wait()
    store(13).start()

    @pl.when(member + 1 < members)
    def _():
        edge(member + 1).wait_send()

    for hop in range(1, window + 1):

        @pl.when(behind >= hop)
        def _():
            state_copy(hop).wait_send()

    @pl.loop(0, sent)
    def _(index):
        near_rows(index).wait()
        far_rows(index).wait_send()
        pass_rows(index).wait()

    store(14).start()
    full[3]()
    store(15).start()
    for gather in (pack, turned, full):
        gather[4]()
    for number in range(len(leaving)):
        store(number).wait()


def front_stage(lengths, inputs, mixer_weights, conv, head_gain, own, members, heads, collective):
    tokens, width = inputs.shape
    columns = heads * CHUNK
    chunks = tokens // CHUNK
    whole = pl.BlockSpec(memory_space=pltpu.VMEM)
    piece = width // members
    window = min(members - 1, members // 2)

    def units(wide, kind):
        return jax.ShapeDtypeStruct((chunks, heads, *wide), kind)

    def dma(*shape):
        return [pltpu.SemaphoreType.DMA(shape)] * 2

    outside = pl.BlockSpec(memory_space=pl.ANY)
    made = (
        jax.ShapeDtypeStruct((1, members, piece, 3 * columns + CHUNK), BF),
        jax.ShapeDtypeStruct((tokens, width), BF),
        jax.ShapeDtypeStruct((tokens, 3 * columns), BF),
        jax.ShapeDtypeStruct((tokens, CHUNK), F32),
        jax.ShapeDtypeStruct((16, 3 * columns), BF),
        jax.ShapeDtypeStruct((tokens, 1), F32),
        jax.ShapeDtypeStruct((2, width), F32),
        jax.ShapeDtypeStruct((1, members, columns, piece), BF),
        jax.ShapeDtypeStruct((len(own), members, *own[0].shape), BF),
        jax.ShapeDtypeStruct((3, members, columns, piece), BF),
        jax.ShapeDtypeStruct((tokens, 3 * columns), BF),
        units((CHUNK, CHUNK), BF),
        units((CHUNK, 2 * CHUNK), BF),
        units((2 * CHUNK, CHUNK), BF),
        jax.ShapeDtypeStruct((heads, CHUNK, 2 * CHUNK), F32),
        jax.ShapeDtypeStruct((tokens, columns), F32),
        jax.ShapeDtypeStruct((tokens, columns), BF),
        jax.ShapeDtypeStruct((3, tokens // 2, columns), BF),
        units((CHUNK, CHUNK), BF),
    )
    stay = (4, 6, 14)
    return pl.pallas_call(
        functools.partial(front_kernel, members, heads),
        name="front",
        out_shape=made,
        in_specs=[pl.BlockSpec(memory_space=pltpu.SMEM)] + [whole] * (3 + len(mixer_weights) + len(own)),
        out_specs=tuple(whole if number in stay else outside for number in range(len(made))),
        scratch_shapes=[pltpu.VMEM(a.shape, a.dtype) for number, a in enumerate(made) if number not in stay]
        + [
            pltpu.SemaphoreType.DMA((len(made) - len(stay),)),
            pltpu.SMEM((tokens // GROUP,), F32),
            pltpu.VMEM((4, 3 * columns), F32),
            pltpu.VMEM((CHUNK, piece), F32),
            pltpu.VMEM((chunks, heads, CHUNK, 2 * CHUNK), BF),
            pltpu.VMEM((chunks, heads, CHUNK, CHUNK), F32),
            pltpu.VMEM((heads, CHUNK, CHUNK), F32),
            pltpu.VMEM((heads, CHUNK, 2 * CHUNK), BF),
            pltpu.VMEM((window, heads, CHUNK, 2 * CHUNK), BF),
            pltpu.VMEM((2, 144, 3 * columns), F32),
            pltpu.VMEM((16, width), BF),
        ]
        + dma(1, members)
        + dma()
        + dma(1, members)
        + dma(len(own), members)
        + dma(3)
        + dma(window)
        + dma(tokens // 256) * 3,
        compiler_params=pltpu.CompilerParams(
            collective_id=collective, has_side_effects=True, vmem_limit_bytes=VMEM_LIMIT
        ),
        cost_estimate=pl.CostEstimate(flops=8 * 10**9, bytes_accessed=40 << 20, transcendentals=2 << 20),
    )(lengths, inputs, *mixer_weights, conv, head_gain, *own)


def lanes_whole(pieces):
    places, rows, piece = pieces.shape
    if piece >= 128:
        return pieces
    group = 128 // piece
    return pieces.reshape(places // group, group, rows, piece).transpose(0, 2, 1, 3).reshape(places // group, rows, 128)


def lanes_split(blocks, piece):
    count, rows, lanes = blocks.shape
    if piece >= 128:
        return blocks
    group = 128 // piece
    return blocks.reshape(count, rows, group, piece).transpose(0, 2, 1, 3).reshape(count * group, rows, piece)


def body(
    block_input,
    first_gain,
    query_weight,
    key_weight,
    value_weight,
    beta_weight,
    conv_weight,
    head_gain,
    output_weight,
    second_gain,
    gate_weight,
    up_weight,
    down_weight,
    lengths,
    cotangent,
):
    tokens, width = block_input.shape
    heads = beta_weight.shape[1]
    columns = query_weight.shape[1]
    hidden_columns = gate_weight.shape[1]
    members = lax.axis_size("seq")
    piece = width // members
    seq_place = lax.axis_index("seq")

    gain_head = head_gain[None, :]
    own = [gate_weight.T, up_weight.T, down_weight.T]
    split = piece < 128
    (
        mixer_pack,
        first_rows,
        pre,
        logits,
        halo,
        scale_one,
        gains,
        turned,
        full,
        others,
        qkv,
        inv,
        wu,
        mq,
        total,
        delta,
        head_rows,
        far_rows,
        states,
    ) = front_stage(
        lengths,
        block_input,
        (
            query_weight,
            key_weight,
            value_weight,
            beta_weight.T,
            first_gain[None, :],
            second_gain[None, :],
            output_weight,
        ),
        conv_weight,
        gain_head,
        [own[0][:16]] if split else own,
        members,
        heads,
        5,
    )
    mixer_pack = mixer_pack.reshape(width, -1)
    if split:
        gathered = lax.all_gather(jnp.stack(own), "seq", axis=1)
        full = jnp.stack([lanes_whole(gathered[i]) for i in range(3)])
    turned = lanes_whole(turned[0])
    others = jnp.stack([lanes_whole(others[i]) for i in range(3)]) if split else others
    d_heads, update_part, middle_shard, d_middle_shard, *grads, second_grad = middle_stage(
        head_rows, far_rows, full, turned, others, block_input, cotangent, gains, 2
    )
    second_part = jnp.sum(second_grad, 0)
    if split:
        pieces = jnp.concatenate([part for pair in grads for part in pair], 1)
        whole_sum = lax.psum_scatter(lanes_split(pieces, piece), "seq", scatter_dimension=0, tiled=False).astype(F32)
        grads = [jnp.zeros((1, members, 16, 128), BF)] * 3
    ddelta, gain_part, arrive, block_output, third_sum = state_backward(
        d_heads, delta, gain_head, mq, total, update_part, middle_shard, grads[2], members, 1
    )
    d_pre, taps_part, first_sum = mixer_backward(
        lengths, pre, halo, conv_weight, logits, qkv, inv, wu, mq, states, ddelta, arrive, grads[0], 3
    )
    input_gradient, mixer_sum, sums, second_sum = final_stage(
        first_rows, d_pre, mixer_pack, block_input, scale_one, gains, d_middle_shard, (gain_part, second_grad, taps_part), grads[1], members, 4
    )
    if not split:
        done = finish_stage(
            block_output, input_gradient, mixer_sum, sums, first_sum, second_sum, third_sum, hidden_columns, heads
        )
        block, ingrad, gain_1, grad_q, grad_k, grad_v, grad_b, grad_c, gain_h, grad_o, gain_2, *rest = done
        return (
            block,
            ingrad,
            gain_1.reshape(-1),
            grad_q,
            grad_k,
            grad_v,
            grad_b.T,
            grad_c,
            gain_h.reshape(-1),
            grad_o,
            gain_2.reshape(-1),
            *(grad.T for grad in rest),
        )
    gain_sum = sums[1, :CHUNK]
    conv_gradient = sums[9 : 9 + 12 * columns // width].reshape(4, 3, columns).transpose(1, 0, 2)
    row_start = seq_place * piece
    first_gradient = lax.dynamic_slice_in_dim(sums[0], row_start, piece, 0)
    second_gradient = lax.dynamic_slice_in_dim(sums[8], row_start, piece, 0)
    beta_gradient = mixer_sum[:, 3 * columns : 3 * columns + heads]
    return (
        block_output,
        input_gradient,
        first_gradient,
        mixer_sum[:, :columns],
        mixer_sum[:, columns : 2 * columns],
        mixer_sum[:, 2 * columns : 3 * columns],
        beta_gradient,
        conv_gradient,
        gain_sum,
        whole_sum[3 * hidden_columns :].T,
        second_gradient,
        whole_sum[:hidden_columns].T,
        whole_sum[hidden_columns : 2 * hidden_columns].T,
        whole_sum[2 * hidden_columns : 3 * hidden_columns].T,
    )


def solution(mesh):
    return jax.shard_map(
        body,
        mesh=mesh,
        in_specs=(
            P("seq", None),
            P("seq"),
            P("seq", "head"),
            P("seq", "head"),
            P("seq", "head"),
            P("seq", "head"),
            P(None, None, "head"),
            P(),
            P("seq", "head"),
            P("seq"),
            P("seq", "head"),
            P("seq", "head"),
            P("seq", "head"),
            P(),
            P("seq", None),
        ),
        out_specs=(
            P("seq", "head"),
            P("seq", "head"),
            P("seq"),
            P("seq", "head"),
            P("seq", "head"),
            P("seq", "head"),
            P("seq", "head"),
            P(None, None, "head"),
            P(),
            P("seq", "head"),
            P("seq"),
            P("seq", "head"),
            P("seq", "head"),
            P("seq", "head"),
        ),
        check_vma=False,
    )
```
